32 devices in a mesh: dp: 4 (over y, x), seq: 8 (over z, core).
Axes of the slice: x: 2, y: 2, z: 4, core: 2. Of those that a mesh axis runs over, the one named last changes fastest.
Arguments:
- inputs: bfloat16 [2, 4, 1024, 1024], P(None, 'dp', 'seq'), may hold values from -6 to 6
- variate_ids: int32 [2, 4, 1024], P(None, 'dp', 'seq'), may hold values from 0 to 7
- time_ids: int32 [2, 4, 1024], P(None, 'dp', 'seq'), may hold values from 0 to 1023
- attn_gain: float32 [1024], P(('dp', 'seq')), may hold values from 0.5 to 1.5
- query_weight: float32 [1024, 1024], P(('dp', 'seq')), may hold values from -0.1875 to 0.1875
- key_weight: float32 [1024, 1024], P(('dp', 'seq')), may hold values from -0.1875 to 0.1875
- value_weight: float32 [1024, 1024], P(('dp', 'seq')), may hold values from -0.1875 to 0.1875
- out_weight: float32 [1024, 1024], P(('dp', 'seq')), may hold values from -3 to 3
- query_gain: float32 [64], replicated, may hold values from 0.1 to 1.9
- key_gain: float32 [64], replicated, may hold values from 0.1 to 1.9
- variate_bias: float32 [2, 16], replicated, may hold values from -3 to 3
- ffn_gain: float32 [1024], P(('dp', 'seq')), may hold values from 0.5 to 1.5
- gate_weight: float32 [4096, 1024], P(('dp', 'seq')), may hold values from -0.1875 to 0.1875
- up_weight: float32 [4096, 1024], P(('dp', 'seq')), may hold values from -0.1875 to 0.1875
- down_weight: float32 [4096, 1024], P(('dp', 'seq')), may hold values from -0.09375 to 0.09375
- out_grad: bfloat16 [2, 4, 1024, 1024], P(None, 'dp', 'seq'), may hold values from -6 to 6
Outputs:
- output: bfloat16 [2, 4, 1024, 1024], P(None, 'dp', 'seq')
- input_grad: bfloat16 [2, 4, 1024, 1024], P(None, 'dp', 'seq')
- attn_gain_grad: float32 [1024], P(('dp', 'seq'))
- query_weight_grad: float32 [1024, 1024], P(('dp', 'seq'))
- key_weight_grad: float32 [1024, 1024], P(('dp', 'seq'))
- value_weight_grad: float32 [1024, 1024], P(('dp', 'seq'))
- out_weight_grad: float32 [1024, 1024], P(('dp', 'seq'))
- query_gain_grad: float32 [64], replicated
- key_gain_grad: float32 [64], replicated
- variate_bias_grad: float32 [2, 16], replicated
- ffn_gain_grad: float32 [1024], P(('dp', 'seq'))
- gate_weight_grad: float32 [4096, 1024], P(('dp', 'seq'))
- up_weight_grad: float32 [4096, 1024], P(('dp', 'seq'))
- down_weight_grad: float32 [4096, 1024], P(('dp', 'seq'))
The draws below stay inside these ranges and needn't reach their ends.
All inputs are finite; a program needn't handle non-finite values.
Results may differ from the reference program's by a relative error of at most 0.04.
Values may be sent and summed in bfloat16 or wider, within the bound.
No kernel may reach another device: no remote copies, remote signals or barrier semaphores. Data moves between devices by JAX's collectives and lax.ppermute only.
A program may use at most 256 MiB of HBM per device.

```python
import math
import jax
import jax.numpy as jnp
from jax import lax

D = 1024
H = 16
HD = 64
FF = 4096
MB = 2
VARIATES = 8
SEQS = 4
LENGTH = 1024


def plant(array, stream_key, low, largest):
    longest = array.shape.index(max(array.shape))
    spots = []
    for shift in (0, 1):
        where = [jax.random.randint(jax.random.fold_in(stream_key, axis), (), 0, length) for axis, length in enumerate(array.shape)]
        where[longest] = (where[longest] + shift) % array.shape[longest]
        spots.append(tuple(where))
    return array.at[spots[0]].set(low).at[spots[1]].set(largest)


def levels(key, shape, pieces, smallest, high):
    factor_of = 1.0
    for axis_at, parts in pieces:
        steps = jax.random.uniform(jax.random.fold_in(jax.random.fold_in(key, 6), axis_at), (parts,), jnp.float32, smallest / len(pieces), high / len(pieces))
        factor_of = factor_of * jnp.repeat(jnp.exp(steps), shape[axis_at] // parts).reshape((-1,) + (1,) * (len(shape) - 1 - axis_at))
    return factor_of


def gaussian(own_key, shape, deviation, limit, pieces=(), dtype=jnp.bfloat16):
    drawn = deviation * jax.random.normal(own_key, shape, jnp.float32)
    if pieces:
        drawn = drawn * levels(own_key, shape, pieces, -0.22, 0.18)
    return jnp.clip(drawn, -limit, limit).astype(dtype)


def setup_inputs(seed: int = 0) -> dict:
    arg_keys = jax.random.split(jax.random.key(seed), 17)
    return {
        "inputs": gaussian(arg_keys[0], (MB, SEQS, LENGTH, D), 1.0, 6.0, ((1, 4), (2, 8))),
        "variate_ids": plant(jax.random.randint(arg_keys[1], (MB, SEQS, LENGTH), 0, VARIATES), jax.random.fold_in(arg_keys[1], 1), 0, VARIATES - 1).astype(jnp.int32),
        "time_ids": plant(jax.random.randint(arg_keys[2], (MB, SEQS, LENGTH), 0, LENGTH), jax.random.fold_in(arg_keys[2], 1), 0, LENGTH - 1).astype(jnp.int32),
        "attn_gain": jnp.clip(1.0 + 0.1 * jax.random.normal(arg_keys[3], (D,), jnp.float32), 0.5, 1.5),
        "query_weight": gaussian(arg_keys[4], (D, D), D ** -0.5, 0.1875, ((0, 32),), jnp.float32),
        "key_weight": gaussian(arg_keys[5], (D, D), D ** -0.5, 0.1875, ((0, 32),), jnp.float32),
        "value_weight": gaussian(arg_keys[6], (D, D), D ** -0.5, 0.1875, ((0, 32),), jnp.float32),
        "out_weight": gaussian(arg_keys[7], (D, D), (0.5 * LENGTH ** 0.5 * D ** -0.5), 3.0, ((0, 32),), jnp.float32),
        "query_gain": jnp.clip(1.0 + 0.18 * jax.random.normal(arg_keys[8], (HD,), jnp.float32), 0.1, 1.9),
        "key_gain": jnp.clip(1.0 + 0.18 * jax.random.normal(arg_keys[9], (HD,), jnp.float32), 0.1, 1.9),
        "variate_bias": gaussian(arg_keys[10], (2, H), 1.0, 3.0, (), jnp.float32),
        "ffn_gain": jnp.clip(1.0 + 0.1 * jax.random.normal(arg_keys[11], (D,), jnp.float32), 0.5, 1.5),
        "gate_weight": gaussian(arg_keys[12], (FF, D), D ** -0.5, 0.1875, ((0, 32),), jnp.float32),
        "up_weight": gaussian(arg_keys[13], (FF, D), D ** -0.5, 0.1875, ((0, 32),), jnp.float32),
        "down_weight": gaussian(arg_keys[14], (FF, D), FF ** -0.5, 0.09375, ((0, 32),), jnp.float32),
        "out_grad": gaussian(arg_keys[15], (MB, SEQS, LENGTH, D), 1.0, 6.0, ((1, 4), (2, 8))),
    }


@jax.custom_vjp
def low(v):
    return lax.optimization_barrier(v.astype(jnp.bfloat16)).astype(jnp.float32)

@jax.custom_vjp
def low_back(v):
    return v

def low_keep(v):
    return (low(v), None)

def low_pass(kept, grad):
    return (grad,)

def back_keep(v):
    return (v, None)

def back_low(kept, grad):
    return (low(grad),)
low.defvjp(low_keep, low_pass)
low_back.defvjp(back_keep, back_low)
epsilon = 1e-06

def dense(left_side, right_side):
    return jnp.dot(left_side, right_side, precision=lax.Precision.HIGHEST)

def rms_scale(values):
    return lax.rsqrt(lax.optimization_barrier(jnp.mean(values * values, axis=-1, keepdims=True)) + epsilon)

def rotation(positions):
    half_dim = HD // 2
    frequency = 10000.0 ** (-jnp.arange(half_dim).astype(jnp.float32) / half_dim)
    angles = positions.astype(jnp.float32)[..., None] * frequency
    return (jnp.cos(angles)[..., None, :], jnp.sin(angles)[..., None, :])

def rotate(values, cos_part, sin_part):
    half_dim = values.shape[-1] // 2
    first_half = values[..., :half_dim]
    second_half = values[..., half_dim:]
    return jnp.concatenate([first_half * cos_part - second_half * sin_part, first_half * sin_part + second_half * cos_part], axis=-1)

def attend(queries, key_rows, value_rows, kind_ids, bias_table):
    length_now = queries.shape[0]
    block_size = math.gcd(length_now, 512)
    query_blocks = queries.reshape(length_now // block_size, block_size, H, HD)
    kind_blocks = kind_ids.reshape(length_now // block_size, block_size)

    def one_block(args_pair):
        query_rows, query_kinds = args_pair
        raw_scores = low_back(jnp.einsum('qhe,khe->hqk', query_rows, key_rows, precision=lax.Precision.HIGHEST) * HD ** (-0.5))
        same_kind = query_kinds[:, None] == kind_ids[None, :]
        scores = raw_scores + jnp.where(same_kind[None], bias_table[0][:, None, None], bias_table[1][:, None, None])
        top_score = lax.optimization_barrier(jnp.max(scores, axis=-1, keepdims=True))
        exp_scores = jnp.exp(scores - top_score)
        attn_prob = exp_scores / lax.optimization_barrier(jnp.sum(exp_scores, axis=-1, keepdims=True))
        return jnp.einsum('hqk,khe->qhe', low(attn_prob), value_rows, precision=lax.Precision.HIGHEST)
    return lax.map(jax.checkpoint(one_block), (query_blocks, kind_blocks)).reshape(length_now, H, HD)

def reference(inputs, variate_ids, time_ids, attn_gain, query_weight, key_weight, value_weight, out_weight, query_gain, key_gain, variate_bias, ffn_gain, gate_weight, up_weight, down_weight, out_grad):
    seq_total = MB * SEQS
    sequences = inputs.astype(jnp.float32).reshape(seq_total, LENGTH, D)
    kind_all = variate_ids.reshape(seq_total, LENGTH)
    time_all = time_ids.reshape(seq_total, LENGTH)
    params = (attn_gain, query_weight, key_weight, value_weight, out_weight, query_gain, key_gain, variate_bias, ffn_gain, gate_weight, up_weight, down_weight)

    def forward(params_in, sequences_in):
        gain_one, w_query, w_key, w_value, w_out, q_gain, k_gain, bias_table, gain_two, w_gate, w_up, w_down = params_in
        gain_one = low(gain_one)
        w_query = low(w_query)
        w_key = low(w_key)
        w_value = low(w_value)
        w_out = low(w_out)
        gain_two = low(gain_two)
        w_gate = low(w_gate)
        w_up = low(w_up)
        w_down = low(w_down)

        def one_sequence(args_triple):
            seq_in, seq_kinds, seq_times = args_triple
            normed = low(seq_in * rms_scale(seq_in) * gain_one)
            query_raw = low_back(dense(normed, w_query)).reshape(LENGTH, H, HD)
            key_raw = low_back(dense(normed, w_key)).reshape(LENGTH, H, HD)
            value_rows = low(low_back(dense(normed, w_value))).reshape(LENGTH, H, HD)
            cos_part, sin_part = rotation(seq_times)
            query_rot = low(rotate(query_raw * rms_scale(query_raw) * q_gain, cos_part, sin_part))
            key_rot = low(rotate(key_raw * rms_scale(key_raw) * k_gain, cos_part, sin_part))
            attended = attend(query_rot, key_rot, value_rows, seq_kinds, bias_table).reshape(LENGTH, D)
            attended = low(low_back(attended))
            middle = seq_in + low_back(dense(attended, w_out))
            normed_two = low(middle * rms_scale(middle) * gain_two)
            gate_pre = low_back(dense(normed_two, w_gate.T))
            up_pre = low_back(dense(normed_two, w_up.T))
            hidden = low(jax.nn.silu(gate_pre) * up_pre)
            return middle + low_back(dense(hidden, w_down))
        return lax.map(jax.checkpoint(one_sequence), (sequences_in, kind_all, time_all))
    results, pullback = jax.vjp(forward, params, sequences)
    param_grads, input_grad = pullback(out_grad.astype(jnp.float32).reshape(results.shape))
    return (results.astype(jnp.bfloat16).reshape(MB, SEQS, LENGTH, D), input_grad.astype(jnp.bfloat16).reshape(MB, SEQS, LENGTH, D), param_grads[0], param_grads[1], param_grads[2], param_grads[3], param_grads[4], param_grads[5], param_grads[6], param_grads[7], param_grads[8], param_grads[9], param_grads[10], param_grads[11])
```

```python
import math

import jax
import jax.numpy as jnp
from jax import lax
from jax.experimental import pallas as pl
from jax.experimental.pallas import tpu as pltpu
from jax.sharding import PartitionSpec as P

D = 1024
H = 16
HD = 64
FF = 4096


epsilon = 1e-06
lowest = -1e30


def rms_scale(values):
    return lax.rsqrt(jnp.mean(values * values, axis=-1, keepdims=True) + epsilon)


def norm_back(values, inv_rms, gain_vec, upstream):
    weighted = upstream * gain_vec
    inner_mean = jnp.mean(weighted * values, axis=-1, keepdims=True)
    return inv_rms * weighted - values * (inv_rms * inv_rms * inv_rms) * inner_mean


def rotation(positions):
    half_dim = HD // 2
    frequency = 10000.0 ** (-jnp.arange(half_dim).astype(jnp.float32) / half_dim)
    angles = positions.astype(jnp.float32)[..., None] * frequency
    return (jnp.cos(angles)[..., None, :], jnp.sin(angles)[..., None, :])


def rotate(values, cos_part, sin_part):
    half_dim = values.shape[-1] // 2
    first_half = values[..., :half_dim]
    second_half = values[..., half_dim:]
    return jnp.concatenate(
        [
            first_half * cos_part - second_half * sin_part,
            first_half * sin_part + second_half * cos_part,
        ],
        axis=-1,
    )


def rotate_back(upstream, cos_part, sin_part):
    half_dim = upstream.shape[-1] // 2
    first_half = upstream[..., :half_dim]
    second_half = upstream[..., half_dim:]
    return jnp.concatenate(
        [
            first_half * cos_part + second_half * sin_part,
            second_half * cos_part - first_half * sin_part,
        ],
        axis=-1,
    )


def product(left_side, right_side):
    return jnp.dot(left_side, right_side, preferred_element_type=jnp.float32)


def times_transposed(left_side, right_side):
    return lax.dot_general(
        left_side, right_side, (((1,), (1,)), ((), ())), preferred_element_type=jnp.float32
    )


def rows_inner(left_side, right_side):
    return lax.dot_general(
        left_side, right_side, (((0,), (0,)), ((), ())), preferred_element_type=jnp.float32
    )


def score_block(queries, key_rows, query_kinds, key_kinds, variate_bias):
    raw_scores = jnp.einsum(
        "sqhe,skhe->shqk", queries, key_rows, preferred_element_type=jnp.float32
    ) * HD ** (-0.5)
    same_kind = query_kinds[:, None, :, None] == key_kinds[:, None, None, :]
    scores = raw_scores + jnp.where(
        same_kind, variate_bias[0][None, :, None, None], variate_bias[1][None, :, None, None]
    )
    return (scores, same_kind)


def forward_piece(queries, query_kinds, variate_bias, carried, pieces):
    piece_keys, piece_values, piece_kinds = pieces
    seq_count = piece_keys.shape[0]
    piece_len = piece_keys.shape[1]
    block_size = math.gcd(piece_len, 512)

    def forward_advance(block_index, totals):
        running_max, running_total, running_sum = totals
        offset = block_index * block_size
        key_rows = lax.dynamic_slice_in_dim(piece_keys, offset, block_size, 1).reshape(
            seq_count, block_size, H, HD
        )
        value_rows = lax.dynamic_slice_in_dim(piece_values, offset, block_size, 1).reshape(
            seq_count, block_size, H, HD
        )
        kind_rows = lax.dynamic_slice_in_dim(piece_kinds, offset, block_size, 1)
        scores, same_kind = score_block(queries, key_rows, query_kinds, kind_rows, variate_bias)
        new_max = jnp.maximum(running_max, jnp.max(scores, axis=-1))
        factor = jnp.exp(running_max - new_max)
        exp_scores = jnp.exp(scores - new_max[..., None])
        running_total = running_total * factor + jnp.sum(exp_scores, axis=-1)
        running_sum = running_sum * factor[..., None] + jnp.einsum(
            "shqk,skhe->shqe",
            exp_scores.astype(jnp.bfloat16),
            value_rows,
            preferred_element_type=jnp.float32,
        )
        return (new_max, running_total, running_sum)

    return lax.fori_loop(0, piece_len // block_size, forward_advance, carried)


def back_piece(context, carried, pieces):
    queries, query_kinds, grad_out, log_total, delta_row, variate_bias = context
    piece_keys, piece_values, piece_kinds = pieces
    seq_count = piece_keys.shape[0]
    piece_len = piece_keys.shape[1]
    block_size = math.gcd(piece_len, 512)
    score_scale = HD ** (-0.5)

    def back_advance(block_index, totals):
        offset = block_index * block_size
        key_rows = lax.dynamic_slice_in_dim(piece_keys, offset, block_size, 1).reshape(
            seq_count, block_size, H, HD
        )
        value_rows = lax.dynamic_slice_in_dim(piece_values, offset, block_size, 1).reshape(
            seq_count, block_size, H, HD
        )
        kind_rows = lax.dynamic_slice_in_dim(piece_kinds, offset, block_size, 1)
        scores, same_kind = score_block(queries, key_rows, query_kinds, kind_rows, variate_bias)
        attn_prob = jnp.exp(scores - log_total[..., None])
        grad_prob = jnp.einsum(
            "sqhe,skhe->shqk", grad_out, value_rows, preferred_element_type=jnp.float32
        )
        grad_score = attn_prob * (grad_prob - delta_row[..., None])
        bias_step = jnp.stack(
            [
                jnp.sum(jnp.where(same_kind, grad_score, 0.0), axis=(0, 2, 3)),
                jnp.sum(jnp.where(same_kind, 0.0, grad_score), axis=(0, 2, 3)),
            ]
        )
        score_low = grad_score.astype(jnp.bfloat16)
        query_grad = (
            totals[0]
            + jnp.einsum("shqk,skhe->shqe", score_low, key_rows, preferred_element_type=jnp.float32)
            * score_scale
        )
        key_part = (
            jnp.einsum("shqk,sqhe->skhe", score_low, queries, preferred_element_type=jnp.float32)
            * score_scale
        ).reshape(seq_count, block_size, D)
        value_part = jnp.einsum(
            "shqk,sqhe->skhe",
            attn_prob.astype(jnp.bfloat16),
            grad_out,
            preferred_element_type=jnp.float32,
        ).reshape(seq_count, block_size, D)
        key_total = lax.dynamic_update_slice_in_dim(
            totals[2],
            lax.dynamic_slice_in_dim(totals[2], offset, block_size, 1) + key_part,
            offset,
            1,
        )
        value_total = lax.dynamic_update_slice_in_dim(
            totals[3],
            lax.dynamic_slice_in_dim(totals[3], offset, block_size, 1) + value_part,
            offset,
            1,
        )
        return (query_grad, totals[1] + bias_step, key_total, value_total)

    return lax.fori_loop(0, piece_len // block_size, back_advance, carried)


def local(
    inputs,
    variate_ids,
    time_ids,
    attn_gain,
    query_weight,
    key_weight,
    value_weight,
    out_weight,
    query_gain,
    key_gain,
    variate_bias,
    ffn_gain,
    gate_weight,
    up_weight,
    down_weight,
    out_grad,
):
    seq_count = inputs.shape[1]
    tok_count = inputs.shape[2]
    row_count = seq_count * tok_count
    full_grads = [
        jnp.zeros(extent, jnp.float32)
        for extent in ((D,), (D, D), (D, D), (D, D), (D, D), (D,), (FF, D), (FF, D), (FF, D))
    ]
    small_grads = [
        jnp.zeros((HD,), jnp.float32),
        jnp.zeros((HD,), jnp.float32),
        jnp.zeros((2, H), jnp.float32),
    ]
    shard_total = None
    small_total = None
    outputs_list = []
    input_grads = []
    weights_now = None
    for micro_index in range(inputs.shape[0]):
        weights_now = (
            lax.all_gather(attn_gain.astype(jnp.bfloat16), ("dp", "seq"), axis=0, tiled=True),
            lax.all_gather(query_weight.astype(jnp.bfloat16), ("dp", "seq"), axis=0, tiled=True),
            lax.all_gather(key_weight.astype(jnp.bfloat16), ("dp", "seq"), axis=0, tiled=True),
            lax.all_gather(value_weight.astype(jnp.bfloat16), ("dp", "seq"), axis=0, tiled=True),
            lax.all_gather(out_weight.astype(jnp.bfloat16), ("dp", "seq"), axis=0, tiled=True),
            lax.all_gather(ffn_gain.astype(jnp.bfloat16), ("dp", "seq"), axis=0, tiled=True),
            lax.all_gather(gate_weight.astype(jnp.bfloat16), ("dp", "seq"), axis=0, tiled=True),
            lax.all_gather(up_weight.astype(jnp.bfloat16), ("dp", "seq"), axis=0, tiled=True),
            lax.all_gather(down_weight.astype(jnp.bfloat16), ("dp", "seq"), axis=0, tiled=True),
        )
        gain_one, w_query, w_key, w_value, w_out, gain_two, w_gate, w_up, w_down = weights_now
        hidden_in = inputs[micro_index].astype(jnp.float32).reshape(row_count, D)
        kinds_now = variate_ids[micro_index].astype(jnp.bfloat16)
        cos_part, sin_part = rotation(time_ids[micro_index])
        inv_one = rms_scale(hidden_in)
        normed = (hidden_in * inv_one * gain_one.astype(jnp.float32)).astype(jnp.bfloat16)
        query_raw = product(normed, w_query).reshape(seq_count, tok_count, H, HD)
        key_raw = product(normed, w_key).reshape(seq_count, tok_count, H, HD)
        value_flat = product(normed, w_value).astype(jnp.bfloat16).reshape(seq_count, tok_count, D)
        inv_query = rms_scale(query_raw)
        query_rot = rotate(query_raw * inv_query * query_gain, cos_part, sin_part).astype(
            jnp.bfloat16
        )
        inv_key = rms_scale(key_raw)
        key_rot = rotate(key_raw * inv_key * key_gain, cos_part, sin_part).astype(jnp.bfloat16)
        key_flat = key_rot.reshape(seq_count, tok_count, D)
        initial = (
            jnp.full((seq_count, H, tok_count), lowest, jnp.float32),
            jnp.zeros((seq_count, H, tok_count), jnp.float32),
            jnp.zeros((seq_count, H, tok_count, HD), jnp.float32),
        )
        final_max, final_total, final_sum = forward_piece(
            query_rot,
            kinds_now,
            variate_bias,
            initial,
            (
                lax.all_gather(key_flat, "seq", axis=1, tiled=True),
                lax.all_gather(value_flat, "seq", axis=1, tiled=True),
                lax.all_gather(kinds_now, "seq", axis=1, tiled=True),
            ),
        )
        log_total = final_max + jnp.log(final_total)
        attended = jnp.transpose(final_sum / final_total[..., None], (0, 2, 1, 3))
        attended_low = attended.reshape(row_count, D).astype(jnp.bfloat16)
        middle = hidden_in + product(attended_low, w_out)
        inv_two = rms_scale(middle)
        normed_two = (middle * inv_two * gain_two.astype(jnp.float32)).astype(jnp.bfloat16)
        gate_pre = times_transposed(normed_two, w_gate)
        up_pre = times_transposed(normed_two, w_up)
        gate_sig = jax.nn.sigmoid(gate_pre)
        hidden_low = (gate_pre * gate_sig * up_pre).astype(jnp.bfloat16)
        result = middle + product(hidden_low, w_down)
        outputs_list.append(result.reshape(seq_count, tok_count, D).astype(jnp.bfloat16))
        gain_one, w_query, w_key, w_value, w_out, gain_two, w_gate, w_up, w_down = (
            lax.all_gather(attn_gain.astype(jnp.bfloat16), ("dp", "seq"), axis=0, tiled=True),
            lax.all_gather(query_weight.astype(jnp.bfloat16), ("dp", "seq"), axis=0, tiled=True),
            lax.all_gather(key_weight.astype(jnp.bfloat16), ("dp", "seq"), axis=0, tiled=True),
            lax.all_gather(value_weight.astype(jnp.bfloat16), ("dp", "seq"), axis=0, tiled=True),
            lax.all_gather(out_weight.astype(jnp.bfloat16), ("dp", "seq"), axis=0, tiled=True),
            lax.all_gather(ffn_gain.astype(jnp.bfloat16), ("dp", "seq"), axis=0, tiled=True),
            lax.all_gather(gate_weight.astype(jnp.bfloat16), ("dp", "seq"), axis=0, tiled=True),
            lax.all_gather(up_weight.astype(jnp.bfloat16), ("dp", "seq"), axis=0, tiled=True),
            lax.all_gather(down_weight.astype(jnp.bfloat16), ("dp", "seq"), axis=0, tiled=True),
        )
        grad_in = out_grad[micro_index].astype(jnp.float32).reshape(row_count, D)
        grad_low = grad_in.astype(jnp.bfloat16)
        full_grads[8] = rows_inner(hidden_low, grad_low)
        grad_hidden = times_transposed(grad_low, w_down)
        grad_gate = (grad_hidden * up_pre * gate_sig * (1.0 + gate_pre * (1.0 - gate_sig))).astype(
            jnp.bfloat16
        )
        grad_up = (grad_hidden * gate_pre * gate_sig).astype(jnp.bfloat16)
        full_grads[6] = rows_inner(grad_gate, normed_two)
        full_grads[7] = rows_inner(grad_up, normed_two)
        grad_normed_two = product(grad_gate, w_gate) + product(grad_up, w_up)
        full_grads[5] = jnp.sum(grad_normed_two * middle * inv_two, axis=0)
        grad_middle = grad_in + norm_back(
            middle, inv_two, gain_two.astype(jnp.float32), grad_normed_two
        )
        grad_middle_low = grad_middle.astype(jnp.bfloat16)
        full_grads[4] = rows_inner(attended_low, grad_middle_low)
        grad_attended = (
            times_transposed(grad_middle_low, w_out)
            .astype(jnp.bfloat16)
            .reshape(seq_count, tok_count, H, HD)
        )
        delta_row = jnp.transpose(
            jnp.sum(grad_attended.astype(jnp.float32) * attended, axis=-1), (0, 2, 1)
        )
        context = (query_rot, kinds_now, grad_attended, log_total, delta_row, variate_bias)
        base_carry = (
            jnp.zeros((seq_count, H, tok_count, HD), jnp.float32),
            jnp.zeros((2, H), jnp.float32),
        )
        length_all = tok_count * lax.axis_size("seq")
        wide_carry = (
            jnp.zeros((seq_count, length_all, D), jnp.float32),
            jnp.zeros((seq_count, length_all, D), jnp.float32),
        )
        grad_query_heads, grad_bias, key_all, value_all = back_piece(
            context,
            base_carry + wide_carry,
            (
                lax.all_gather(key_flat, "seq", axis=1, tiled=True),
                lax.all_gather(value_flat, "seq", axis=1, tiled=True),
                lax.all_gather(kinds_now, "seq", axis=1, tiled=True),
            ),
        )
        grad_key, grad_value = (
            lax.psum_scatter(
                key_all.astype(jnp.bfloat16), "seq", scatter_dimension=1, tiled=True
            ).astype(jnp.float32),
            lax.psum_scatter(
                value_all.astype(jnp.bfloat16), "seq", scatter_dimension=1, tiled=True
            ).astype(jnp.float32),
        )
        grad_key = grad_key.reshape(seq_count, tok_count, H, HD)
        grad_value_low = grad_value.reshape(row_count, D).astype(jnp.bfloat16)
        small_grads[2] = grad_bias
        grad_query = jnp.transpose(grad_query_heads, (0, 2, 1, 3))
        grad_query_norm = rotate_back(grad_query, cos_part, sin_part)
        small_grads[0] = jnp.sum(grad_query_norm * query_raw * inv_query, axis=(0, 1, 2))
        grad_query_low = (
            norm_back(query_raw, inv_query, query_gain, grad_query_norm)
            .reshape(row_count, D)
            .astype(jnp.bfloat16)
        )
        grad_key_norm = rotate_back(grad_key, cos_part, sin_part)
        small_grads[1] = jnp.sum(grad_key_norm * key_raw * inv_key, axis=(0, 1, 2))
        grad_key_low = (
            norm_back(key_raw, inv_key, key_gain, grad_key_norm)
            .reshape(row_count, D)
            .astype(jnp.bfloat16)
        )
        full_grads[1] = rows_inner(normed, grad_query_low)
        full_grads[2] = rows_inner(normed, grad_key_low)
        full_grads[3] = rows_inner(normed, grad_value_low)
        grad_normed = (
            times_transposed(grad_query_low, w_query)
            + times_transposed(grad_key_low, w_key)
            + times_transposed(grad_value_low, w_value)
        )
        full_grads[0] = jnp.sum(grad_normed * hidden_in * inv_one, axis=0)
        input_total = grad_middle + norm_back(
            hidden_in, inv_one, gain_one.astype(jnp.float32), grad_normed
        )
        input_grads.append(input_total.reshape(seq_count, tok_count, D).astype(jnp.bfloat16))
        shards = (
            lax.psum_scatter(full_grads[0], ("dp", "seq"), scatter_dimension=0, tiled=True),
            lax.psum_scatter(full_grads[1], ("dp", "seq"), scatter_dimension=0, tiled=True),
            lax.psum_scatter(full_grads[2], ("dp", "seq"), scatter_dimension=0, tiled=True),
            lax.psum_scatter(full_grads[3], ("dp", "seq"), scatter_dimension=0, tiled=True),
            lax.psum_scatter(full_grads[4], ("dp", "seq"), scatter_dimension=0, tiled=True),
            lax.psum_scatter(full_grads[5], ("dp", "seq"), scatter_dimension=0, tiled=True),
            lax.psum_scatter(full_grads[6], ("dp", "seq"), scatter_dimension=0, tiled=True),
            lax.psum_scatter(full_grads[7], ("dp", "seq"), scatter_dimension=0, tiled=True),
            lax.psum_scatter(full_grads[8], ("dp", "seq"), scatter_dimension=0, tiled=True),
        )
        summed = lax.psum((small_grads[0], small_grads[1], small_grads[2]), ("dp", "seq"))
        shards, summed = (list(shards), list(summed))
        if shard_total is None:
            shard_total = shards
            small_total = summed
        else:
            shard_total = [
                earlier_part + later_part for earlier_part, later_part in zip(shard_total, shards)
            ]
            small_total = [
                earlier_part + later_part for earlier_part, later_part in zip(small_total, summed)
            ]
        full_grads = [jnp.zeros_like(member) for member in full_grads]
        small_grads = [jnp.zeros_like(member) for member in small_grads]
    return (
        jnp.stack(outputs_list),
        jnp.stack(input_grads),
        shard_total[0],
        shard_total[1],
        shard_total[2],
        shard_total[3],
        shard_total[4],
        small_total[0],
        small_total[1],
        small_total[2],
        shard_total[5],
        shard_total[6],
        shard_total[7],
        shard_total[8],
    )


def swap_seq(values, mask):
    return lax.ppermute(values, "seq", [(at, at ^ mask) for at in range(8)])


def swap_dp(values, mask):
    return lax.ppermute(values, "dp", [(at, at ^ mask) for at in range(4)])


def pick(pieces, which):
    chosen = pieces[-1]
    for at in range(len(pieces) - 2, -1, -1):
        chosen = jnp.where(which == at, pieces[at], chosen)
    return chosen


def ordered(pieces, own):
    return jnp.stack([pick(pieces, own ^ at) for at in range(len(pieces))])


def at_index(values, index, axis=0):
    return lax.dynamic_index_in_dim(values, index, axis, keepdims=False)


def contract_last(left_side, right_side):
    return lax.dot_general(
        left_side, right_side, (((1,), (1,)), ((), ())), preferred_element_type=jnp.float32
    )


def exact(left_side, right_side):
    return jnp.dot(
        left_side,
        right_side,
        precision=lax.Precision.HIGHEST,
        preferred_element_type=jnp.float32,
    )


def head_block(scale):
    rows = lax.broadcasted_iota(jnp.int32, (128, 128), 0) // HD
    columns = lax.broadcasted_iota(jnp.int32, (128, 128), 1) // HD
    return jnp.where(rows == columns, scale, 0.0).astype(jnp.float32)


def rope_partner(values):
    lane = lax.broadcasted_iota(jnp.int32, values.shape, 1)
    return jnp.where(
        lane % HD < HD // 2, pltpu.roll(values, 128 - HD // 2, 1), pltpu.roll(values, HD // 2, 1)
    )


def three_parts(values):
    first = values.astype(jnp.bfloat16).astype(jnp.float32)
    second = (values - first).astype(jnp.bfloat16).astype(jnp.float32)
    third = (values - first - second).astype(jnp.bfloat16).astype(jnp.float32)
    return first, second, third


BQ = 256
BK = 256
LSE_LANE = 24


def attend_kernel(
    q_in,
    k_in,
    v_in,
    cos_in,
    sin_in,
    hot_in,
    q_gain,
    k_gain,
    bias_in,
    att_out,
    qs_out,
    ks_out,
    vs_out,
    ext_out,
    kx,
    vx,
):
    mean_block = head_block(1.0 / HD)

    def prepare(raw, gain):
        inv = lax.rsqrt(exact(raw * raw, mean_block) + epsilon)
        scaled = raw * inv * gain
        return scaled * cos_in[...] + rope_partner(scaled) * sin_in[...]

    qs_out[...] = (
        prepare(q_in[...], q_gain[...]).astype(jnp.bfloat16).astype(jnp.float32) * HD**-0.5
    ).astype(jnp.bfloat16)
    keys = prepare(k_in[...], k_gain[...]).astype(jnp.bfloat16)
    ks_out[...] = keys
    kx[:, :128] = keys
    kx[:, 128:] = hot_in[...]
    values = v_in[...].astype(jnp.bfloat16)
    vs_out[...] = values
    vx[:, :128] = values
    vx[:, 128:] = jnp.ones(values.shape, jnp.bfloat16)
    lane = lax.broadcasted_iota(jnp.int32, (BQ, 128), 1)

    def step(block, carry):
        rows = pl.ds(pl.multiple_of(block * BQ, BQ), BQ)
        queries = qs_out[rows, :].astype(jnp.float32)
        hot = hot_in[rows, :].astype(jnp.float32)
        results = []
        for head in range(2):
            mine = jnp.where(lane // HD == head, queries, 0.0).astype(jnp.bfloat16)
            extra = hot * bias_in[0, head : head + 1, :]
            scores = contract_last(
                jnp.concatenate([mine, extra.astype(jnp.bfloat16)], axis=1), kx[...]
            )
            weights = jnp.exp(scores).astype(jnp.bfloat16)
            summed = jnp.dot(weights, vx[...], preferred_element_type=jnp.float32)
            total = summed[:, 128:]
            results.append(summed[:, :128] / total)
            first, second, third = three_parts(-jnp.log(total))
            extra = jnp.where(lane == LSE_LANE, first, extra)
            extra = jnp.where(lane == LSE_LANE + 1, second, extra)
            extra = jnp.where(lane == LSE_LANE + 2, third, extra)
            ext_out[head, rows, :] = extra.astype(jnp.bfloat16)
        att_out[rows, :] = jnp.where(lane < HD, results[0], results[1]).astype(jnp.bfloat16)
        return carry

    lax.fori_loop(0, q_in.shape[0] // BQ, step, 0)


def attend_back_kernel(
    q_in,
    k_in,
    qs_in,
    ks_in,
    vs_in,
    ext_in,
    hot_in,
    grad_in,
    att_in,
    cos_in,
    sin_in,
    q_gain,
    k_gain,
    dq_out,
    dk_out,
    dv_out,
    gain_out,
    bias_out,
    kx,
    vx,
    kt,
    qx,
    qg,
    gx,
    dqt,
    dk_sum,
    dv_sum,
):
    tokens = q_in.shape[0]
    lane = lax.broadcasted_iota(jnp.int32, (tokens, 128), 1)
    keys = ks_in[...]
    kx[:, :128] = keys
    kx[:, 128:] = hot_in[...]
    kt[...] = keys.astype(jnp.float32).T.astype(jnp.bfloat16)
    vx[:, :128] = vs_in[...]
    vx[:, 128:] = jnp.where(lane % HD < 3, 1.0, 0.0).astype(jnp.bfloat16)
    grads = grad_in[...].astype(jnp.float32)
    delta = exact(grads * att_in[...].astype(jnp.float32), head_block(1.0))
    first, second, third = three_parts(-delta)
    parts = jnp.where(
        lane % HD == 0,
        first,
        jnp.where(lane % HD == 1, second, jnp.where(lane % HD == 2, third, 0.0)),
    )
    queries = qs_in[...].astype(jnp.float32)
    for head in range(2):
        own = lane // HD == head
        mine = jnp.where(own, queries, 0.0).astype(jnp.bfloat16)
        qx[head, :, :128] = mine
        qx[head, :, 128:] = ext_in[head]
        qg[head, :, :128] = mine
        qg[head, :, 128:] = hot_in[...]
        gx[head, :, :128] = jnp.where(own, grads, 0.0).astype(jnp.bfloat16)
        gx[head, :, 128:] = jnp.where(own, parts, 0.0).astype(jnp.bfloat16)
    dqt[...] = jnp.zeros(dqt.shape, jnp.float32)
    block_lane = lax.broadcasted_iota(jnp.int32, (BK, 128), 1)
    counted = jnp.where((block_lane < 8) | (block_lane == LSE_LANE), 1.0, 0.0)

    def step(block, carry):
        rows = pl.ds(pl.multiple_of(block * BK, BK), BK)
        hot = hot_in[rows, :].astype(jnp.float32) * counted
        dk_parts = []
        dv_parts = []
        bias_parts = []
        for head in range(2):
            probs = jnp.exp(contract_last(kx[rows, :], qx[head]))
            dscores = (probs * contract_last(vx[rows, :], gx[head])).astype(jnp.bfloat16)
            dv_parts.append(
                jnp.dot(
                    probs.astype(jnp.bfloat16), gx[head, :, :128], preferred_element_type=jnp.float32
                )
            )
            wide = jnp.dot(dscores, qg[head], preferred_element_type=jnp.float32)
            dk_parts.append(wide[:, :128])
            bias_parts.append(jnp.sum(wide[:, 128:] * hot, axis=0, keepdims=True))
            head_rows = pl.ds(head * HD, HD)
            dqt[head_rows, :] += jnp.dot(
                kt[head_rows, rows], dscores, preferred_element_type=jnp.float32
            )
        dk_sum[rows, :] = dk_parts[0] + dk_parts[1]
        dv_sum[rows, :] = dv_parts[0] + dv_parts[1]
        return (carry[0] + bias_parts[0], carry[1] + bias_parts[1])

    zero = jnp.zeros((1, 128), jnp.float32)
    sums = lax.fori_loop(0, tokens // BK, step, (zero, zero))
    bias_out[0, 0:1, :] = sums[0]
    bias_out[0, 1:2, :] = sums[1]
    mean_block = head_block(1.0 / HD)

    def finish(raw, upstream, gain):
        inv = lax.rsqrt(exact(raw * raw, mean_block) + epsilon)
        normed = upstream * cos_in[...] - rope_partner(upstream) * sin_in[...]
        gain_grad = jnp.sum(normed * raw * inv, axis=0, keepdims=True)
        weighted = normed * gain
        inner = exact(weighted * raw, mean_block)
        return inv * weighted - raw * (inv * inv * inv) * inner, gain_grad

    dq, dq_gain = finish(q_in[...], dqt[...].T * HD**-0.5, q_gain[...])
    dk, dk_gain = finish(k_in[...], dk_sum[...], k_gain[...])
    dq_out[...] = dq.astype(jnp.bfloat16)
    dk_out[...] = dk.astype(jnp.bfloat16)
    dv_out[...] = dv_sum[...].astype(jnp.bfloat16)
    gain_out[0, 0:1, :] = dq_gain
    gain_out[0, 1:2, :] = dk_gain


def attend(qkv, cos_part, sin_part, hot, q_gain, k_gain, bias_rows):
    tokens = qkv.shape[0]
    column = lambda shift: pl.BlockSpec((tokens, 128), lambda pair: (0, pair + shift))
    whole = pl.BlockSpec((tokens, 128), lambda pair: (0, 0))
    line = pl.BlockSpec((1, 128), lambda pair: (0, 0))
    low = lambda: jax.ShapeDtypeStruct((tokens, 256), jnp.bfloat16)
    return pl.pallas_call(
        attend_kernel,
        grid=(2,),
        in_specs=[
            column(0),
            column(2),
            column(4),
            whole,
            whole,
            whole,
            line,
            line,
            pl.BlockSpec((1, 2, 128), lambda pair: (pair, 0, 0)),
        ],
        out_specs=[
            column(0),
            column(0),
            column(0),
            column(0),
            pl.BlockSpec((2, tokens, 128), lambda pair: (pair, 0, 0)),
        ],
        out_shape=[
            low(),
            low(),
            low(),
            low(),
            jax.ShapeDtypeStruct((4, tokens, 128), jnp.bfloat16),
        ],
        scratch_shapes=[
            pltpu.VMEM((tokens, 256), jnp.bfloat16),
            pltpu.VMEM((tokens, 256), jnp.bfloat16),
        ],
        compiler_params=pltpu.CompilerParams(vmem_limit_bytes=40 << 20),
        cost_estimate=pl.CostEstimate(
            flops=16 * tokens * tokens * 256,
            bytes_accessed=tokens * 256 * 30,
            transcendentals=4 * tokens * tokens,
        ),
        name="attend",
    )(qkv, qkv, qkv, cos_part, sin_part, hot, q_gain, k_gain, bias_rows)


def attend_back(qkv, saved, hot, grads, attended, cos_part, sin_part, q_gain, k_gain):
    queries, keys, values, extra = saved
    tokens = qkv.shape[0]
    column = lambda shift: pl.BlockSpec((tokens, 128), lambda pair: (0, pair + shift))
    whole = pl.BlockSpec((tokens, 128), lambda pair: (0, 0))
    line = pl.BlockSpec((1, 128), lambda pair: (0, 0))
    two = pl.BlockSpec((1, 2, 128), lambda pair: (pair, 0, 0))
    low = lambda: jax.ShapeDtypeStruct((tokens, 256), jnp.bfloat16)
    wide = pltpu.VMEM((tokens, 256), jnp.bfloat16)
    both = pltpu.VMEM((2, tokens, 256), jnp.bfloat16)
    return pl.pallas_call(
        attend_back_kernel,
        grid=(2,),
        in_specs=[
            column(0),
            column(2),
            column(0),
            column(0),
            column(0),
            pl.BlockSpec((2, tokens, 128), lambda pair: (pair, 0, 0)),
            whole,
            column(0),
            column(0),
            whole,
            whole,
            line,
            line,
        ],
        out_specs=[column(0), column(0), column(0), two, two],
        out_shape=[
            low(),
            low(),
            low(),
            jax.ShapeDtypeStruct((2, 2, 128), jnp.float32),
            jax.ShapeDtypeStruct((2, 2, 128), jnp.float32),
        ],
        scratch_shapes=[
            wide,
            wide,
            pltpu.VMEM((128, tokens), jnp.bfloat16),
            both,
            both,
            both,
            pltpu.VMEM((128, tokens), jnp.float32),
            pltpu.VMEM((tokens, 128), jnp.float32),
            pltpu.VMEM((tokens, 128), jnp.float32),
        ],
        compiler_params=pltpu.CompilerParams(vmem_limit_bytes=48 << 20),
        cost_estimate=pl.CostEstimate(
            flops=40 * tokens * tokens * 256,
            bytes_accessed=tokens * 256 * 40,
            transcendentals=4 * tokens * tokens,
        ),
        name="attend_back",
    )(
        qkv,
        qkv,
        queries,
        keys,
        values,
        extra,
        hot,
        grads,
        attended,
        cos_part,
        sin_part,
        q_gain,
        k_gain,
    )


def local_split(
    inputs,
    variate_ids,
    time_ids,
    attn_gain,
    query_weight,
    key_weight,
    value_weight,
    out_weight,
    query_gain,
    key_gain,
    variate_bias,
    ffn_gain,
    gate_weight,
    up_weight,
    down_weight,
    out_grad,
):
    low = jnp.bfloat16
    wide = jnp.float32
    dp_at = lax.axis_index("dp")
    seq_at = lax.axis_index("seq")
    core = seq_at & 1
    level = seq_at >> 1
    batch = level >> 1
    parity = level & 1
    piece = inputs.shape[2]
    tokens = 8 * piece
    swap_core = lambda values: swap_seq(values, 1)
    swap_level = lambda values, mask: swap_seq(values, 2 * mask)

    def gather_sequence(pair):
        mine = at_index(pair, batch)
        other = at_index(pair, 1 - batch)
        far = swap_level(other, 2)
        near = swap_level(mine, 1)
        last = swap_level(far, 1)
        four = jnp.stack([mine, near, far, last])
        return jnp.stack([four, swap_core(four)])

    own_x = inputs[:, 0]
    ids = gather_sequence(jnp.stack([variate_ids[:, 0], time_ids[:, 0]], axis=1))
    sequence = gather_sequence(own_x).reshape(tokens, D)

    gain_low = attn_gain.astype(low).astype(wide)
    weights_low = jnp.stack([query_weight, key_weight, value_weight], axis=1).astype(low)
    scaled = (weights_low.astype(wide) * gain_low[:, None, None]).astype(low)
    scaled = scaled.reshape(32, 3, 2, 2, 256)
    rows = ordered(
        [at_index(scaled, core, 3), swap_core(at_index(scaled, 1 - core, 3))], core
    ).reshape(64, 3, 2, 256)
    same = at_index(rows, parity, 2).reshape(64, 768)
    cross = at_index(rows, 1 - parity, 2).reshape(64, 768)
    rows = ordered(
        [same, swap_level(cross, 1), swap_level(same, 2), swap_level(cross, 3)], level
    ).reshape(256, 768)
    w_qkv = ordered([rows] + [swap_dp(rows, mask) for mask in (1, 2, 3)], dp_at).reshape(D, 768)

    with_gain = jnp.concatenate(
        [out_weight.astype(low), jnp.pad(ffn_gain.astype(low)[:, None], ((0, 0), (0, 127)))], axis=1
    )
    rows = ordered([with_gain] + [swap_level(with_gain, mask) for mask in (1, 2, 3)], level)
    rows = ordered([rows] + [swap_dp(rows, mask) for mask in (1, 2, 3)], dp_at)
    w_out = ordered([rows, swap_core(rows)], core)
    w_out = jnp.transpose(w_out, (1, 2, 0, 3, 4)).reshape(D, D + 128)
    gain_two = w_out[:, D].astype(wide)[None, :]
    w_out = w_out[:, :D]

    own_dy = out_grad[:, 0].reshape(2 * piece, D)
    all_dy = jnp.concatenate([own_dy] + [swap_dp(own_dy, mask) for mask in (1, 2, 3)])

    ffn_local = jnp.stack([gate_weight, up_weight, down_weight]).astype(low)
    w_ffn = lax.all_gather(ffn_local, "seq", axis=1, tiled=True)

    kinds = ids[:, :, 0].reshape(tokens, 1)
    times = ids[:, :, 1].reshape(tokens, 1).astype(wide)
    lane = lax.broadcasted_iota(jnp.int32, (1, 128), 1)
    hot = jnp.where(
        lane < LSE_LANE, (kinds == lane % 8).astype(wide), jnp.where(lane < LSE_LANE + 3, 1.0, 0.0)
    ).astype(low)
    half = HD // 2
    frequency = 10000.0 ** (-(lane % half).astype(wide) / half)
    angles = times * frequency
    cos_part = jnp.cos(angles)
    sin_part = jnp.sin(angles) * jnp.where(lane % HD < half, -1.0, 1.0)
    q_gain = jnp.tile(query_gain, 2)[None, :]
    k_gain = jnp.tile(key_gain, 2)[None, :]
    group = 2 * parity + core
    gaps = at_index((variate_bias[0] - variate_bias[1]).reshape(4, 4), group)
    first, second, third = three_parts(gaps)
    bias_rows = jnp.where(
        lane < 8,
        first[:, None],
        jnp.where(
            lane < 16, second[:, None], jnp.where(lane < LSE_LANE, third[:, None], 0.0)
        ),
    ).reshape(2, 2, 128)

    seq_wide = sequence.astype(wide)
    unit = (seq_wide * rms_scale(seq_wide)).astype(low)
    qkv = product(unit, w_qkv)
    attended, *saved = attend(qkv, cos_part, sin_part, hot, q_gain, k_gain, bias_rows)

    parts = attended.reshape(2, 4, piece, 256)
    both = jnp.stack([parts[0], swap_core(parts[1])], axis=2)
    arrived = [both[0]] + [swap_level(both[mask], mask) for mask in (1, 2, 3)]
    split = jnp.stack(arrived).reshape(2, 2, piece, 2, 256)
    split = jnp.where(batch == 1, split[::-1], split)
    split = jnp.where(parity == 1, split[:, ::-1], split)
    split = jnp.where(core == 1, split[:, :, :, ::-1], split)
    own_att = jnp.transpose(split, (0, 2, 1, 3, 4)).reshape(2 * piece, D)

    own_wide = own_x.reshape(2 * piece, D).astype(wide)
    middle = own_wide + product(own_att, w_out)
    inv_two = rms_scale(middle)
    normed_two = (middle * inv_two * gain_two).astype(low)
    all_two = jnp.concatenate([normed_two] + [swap_dp(normed_two, mask) for mask in (1, 2, 3)])

    w_gate, w_up, w_down = w_ffn[0], w_ffn[1], w_ffn[2]
    gate_pre = times_transposed(all_two, w_gate)
    up_pre = times_transposed(all_two, w_up)
    grad_hidden = times_transposed(all_dy, w_down)
    gate_sig = jax.nn.sigmoid(gate_pre)
    hidden = (gate_pre * gate_sig * up_pre).astype(low)
    grad_gate = (grad_hidden * up_pre * gate_sig * (1.0 + gate_pre * (1.0 - gate_sig))).astype(low)
    grad_up = (grad_hidden * gate_pre * gate_sig).astype(low)

    def scatter_tokens(partial):
        chunks = partial.reshape(4, 2 * piece, D)
        total = chunks[0]
        for mask in (1, 2, 3):
            total = total + swap_dp(chunks[mask].astype(low), mask).astype(wide)
        return total

    grad_two = scatter_tokens(product(grad_gate, w_gate) + product(grad_up, w_up))
    result = middle + scatter_tokens(product(hidden, w_down))
    ffn_grads = jnp.stack(
        [
            rows_inner(grad_gate, all_two).astype(low),
            rows_inner(grad_up, all_two).astype(low),
            rows_inner(hidden, all_dy).astype(low),
        ]
    )
    ffn_grads = lax.psum_scatter(ffn_grads, "seq", scatter_dimension=1, tiled=True).astype(wide)

    dy_wide = own_dy.astype(wide)
    gain_two_part = jnp.sum(grad_two * middle * inv_two, axis=0)
    grad_middle = dy_wide + norm_back(middle, inv_two, gain_two, grad_two)
    middle_low = grad_middle.astype(low)
    grad_att = times_transposed(middle_low, w_out).astype(low)
    out_part = rows_inner(own_att, middle_low)

    split = jnp.transpose(grad_att.reshape(2, piece, 2, 2, 256), (0, 2, 1, 3, 4))
    split = jnp.where(batch == 1, split[::-1], split)
    split = jnp.where(parity == 1, split[:, ::-1], split)
    split = jnp.where(core == 1, split[:, :, :, ::-1], split)
    split = split.reshape(4, piece, 2, 256)
    arrived = jnp.stack([split[0]] + [swap_level(split[mask], mask) for mask in (1, 2, 3)])
    grads = jnp.stack([arrived[:, :, 0], swap_core(arrived[:, :, 1])]).reshape(tokens, 256)

    dq, dk, dv, gain_sums, bias_sums = attend_back(
        qkv, saved, hot, grads, attended, cos_part, sin_part, q_gain, k_gain
    )
    dqkv = jnp.concatenate([dq, dk, dv], axis=1)

    qkv_part = rows_inner(unit, dqkv).astype(low).reshape(4, 4, 2, 32, 768)
    other = swap_core(at_index(qkv_part, 1 - core, 2))
    qkv_part = jnp.stack([at_index(qkv_part, core, 2), other], axis=2)
    total = at_index(qkv_part, dp_at).astype(wide)
    for mask in (1, 2, 3):
        total = total + swap_dp(at_index(qkv_part, dp_at ^ mask), mask).astype(wide)
    total = total.astype(low)
    same = at_index(total, level).astype(wide) + swap_level(at_index(total, level ^ 2), 2).astype(
        wide
    )
    cross = swap_level(at_index(total, level ^ 1), 1).astype(wide) + swap_level(
        at_index(total, level ^ 3), 3
    ).astype(wide)
    split = jnp.stack([same, cross]).reshape(2, 2, 32, 3, 256)
    split = jnp.where(parity == 1, split[::-1], split)
    split = jnp.where(core == 1, split[:, ::-1], split)
    unit_grads = jnp.transpose(split, (3, 2, 0, 1, 4)).reshape(3, 32, D)
    gain_grad = jnp.sum(unit_grads * jnp.transpose(weights_low, (1, 0, 2)).astype(wide), axis=(0, 2))
    qkv_grads = unit_grads * gain_low[None, :, None]

    unit_back = times_transposed(dqkv, w_qkv).reshape(2, 4, piece, D)
    total = unit_back[0] + swap_core(unit_back[1].astype(low)).astype(wide)
    passed = total[2] + swap_level(total[3].astype(low), 1).astype(wide)
    kept = total[0] + swap_level(total[1].astype(low), 1).astype(wide)
    passed = swap_level(passed.astype(low), 2).astype(wide)
    back = jnp.stack([kept, passed])
    back = jnp.where(batch == 1, back[::-1], back).reshape(2 * piece, D)
    inv_one = rms_scale(own_wide)
    inner = jnp.mean(back * own_wide, axis=-1, keepdims=True)
    input_grad = grad_middle + inv_one * back - own_wide * (inv_one * inv_one * inv_one) * inner

    out_part = out_part.reshape(4, 4, 2, 32, D)
    total = at_index(out_part, core, 2) + swap_core(
        at_index(out_part, 1 - core, 2).astype(low)
    ).astype(wide)
    kept = at_index(total, dp_at)
    for mask in (1, 2, 3):
        kept = kept + swap_dp(at_index(total, dp_at ^ mask).astype(low), mask).astype(wide)
    out_grads = at_index(kept, level)
    for mask in (1, 2, 3):
        out_grads = out_grads + swap_level(
            at_index(kept, level ^ mask).astype(low), mask
        ).astype(wide)

    gain_sums = jnp.sum(gain_sums, axis=0).reshape(2, 2, HD)
    gain_sums = jnp.sum(gain_sums, axis=1).reshape(128)
    bias_sums = bias_sums.reshape(4, 128)
    same = jnp.sum(bias_sums[:, :8], axis=1)
    pair = jnp.stack([same, bias_sums[:, LSE_LANE] - same])
    placed = jnp.where(jnp.arange(4)[None, :, None] == group, pair[:, None, :], 0.0).reshape(2 * H)
    small = jnp.concatenate([gain_two_part, gain_sums, placed, jnp.zeros((96,), wide)])
    small = small.reshape(10, 128)
    for swap, masks in ((swap_dp, (1, 2, 3)), (swap_level, (1, 2, 3)), (swap_seq, (1,))):
        moved = [small] + [swap(small, mask) for mask in masks]
        while len(moved) > 1:
            moved = [left + right for left, right in zip(moved[::2], moved[1::2])]
        small = moved[0]
    small = small.reshape(1280)
    gain_two_grad = lax.dynamic_slice_in_dim(small, (dp_at * 8 + seq_at) * 32, 32)

    shape = (2, 1, piece, D)
    return (
        result.astype(low).reshape(shape),
        input_grad.astype(low).reshape(shape),
        gain_grad,
        qkv_grads[0],
        qkv_grads[1],
        qkv_grads[2],
        out_grads,
        small[D : D + HD],
        small[D + HD : D + 2 * HD],
        small[D + 2 * HD : D + 2 * HD + 2 * H].reshape(2, H),
        gain_two_grad,
        ffn_grads[0],
        ffn_grads[1],
        ffn_grads[2],
    )


def solution(mesh):
    placed = (
        P(None, "dp", "seq", None),
        P(None, "dp", "seq"),
        P(None, "dp", "seq"),
        P(("dp", "seq")),
        P(("dp", "seq"), None),
        P(("dp", "seq"), None),
        P(("dp", "seq"), None),
        P(("dp", "seq"), None),
        P(),
        P(),
        P(),
        P(("dp", "seq")),
        P(("dp", "seq"), None),
        P(("dp", "seq"), None),
        P(("dp", "seq"), None),
        P(None, "dp", "seq", None),
    )
    split = mesh.shape["dp"] == 4 and mesh.shape["seq"] == 8
    return jax.shard_map(
        local_split if split else local,
        mesh=mesh,
        in_specs=placed,
        out_specs=(
            P(None, "dp", "seq", None),
            P(None, "dp", "seq", None),
            P(("dp", "seq")),
            P(("dp", "seq"), None),
            P(("dp", "seq"), None),
            P(("dp", "seq"), None),
            P(("dp", "seq"), None),
            P(),
            P(),
            P(),
            P(("dp", "seq")),
            P(("dp", "seq"), None),
            P(("dp", "seq"), None),
            P(("dp", "seq"), None),
        ),
        check_vma=False,
    )
```

```python
import functools
import math

import jax
import jax.numpy as jnp
from jax import lax
from jax.experimental import pallas as pl
from jax.experimental.pallas import tpu as pltpu
from jax.sharding import PartitionSpec as P

D = 1024
H = 16
HD = 64
FF = 4096


epsilon = 1e-06
lowest = -1e30


def rms_scale(values):
    return lax.rsqrt(jnp.mean(values * values, axis=-1, keepdims=True) + epsilon)


def norm_back(values, inv_rms, gain_vec, upstream):
    weighted = upstream * gain_vec
    inner_mean = jnp.mean(weighted * values, axis=-1, keepdims=True)
    return inv_rms * weighted - values * (inv_rms * inv_rms * inv_rms) * inner_mean


def rotation(positions):
    half_dim = HD // 2
    frequency = 10000.0 ** (-jnp.arange(half_dim).astype(jnp.float32) / half_dim)
    angles = positions.astype(jnp.float32)[..., None] * frequency
    return (jnp.cos(angles)[..., None, :], jnp.sin(angles)[..., None, :])


def rotate(values, cos_part, sin_part):
    half_dim = values.shape[-1] // 2
    first_half = values[..., :half_dim]
    second_half = values[..., half_dim:]
    return jnp.concatenate(
        [
            first_half * cos_part - second_half * sin_part,
            first_half * sin_part + second_half * cos_part,
        ],
        axis=-1,
    )


def rotate_back(upstream, cos_part, sin_part):
    half_dim = upstream.shape[-1] // 2
    first_half = upstream[..., :half_dim]
    second_half = upstream[..., half_dim:]
    return jnp.concatenate(
        [
            first_half * cos_part + second_half * sin_part,
            second_half * cos_part - first_half * sin_part,
        ],
        axis=-1,
    )


def product(left_side, right_side):
    return jnp.dot(left_side, right_side, preferred_element_type=jnp.float32)


def times_transposed(left_side, right_side):
    return lax.dot_general(
        left_side, right_side, (((1,), (1,)), ((), ())), preferred_element_type=jnp.float32
    )


def rows_inner(left_side, right_side):
    return lax.dot_general(
        left_side, right_side, (((0,), (0,)), ((), ())), preferred_element_type=jnp.float32
    )


def score_block(queries, key_rows, query_kinds, key_kinds, variate_bias):
    raw_scores = jnp.einsum(
        "sqhe,skhe->shqk", queries, key_rows, preferred_element_type=jnp.float32
    ) * HD ** (-0.5)
    same_kind = query_kinds[:, None, :, None] == key_kinds[:, None, None, :]
    scores = raw_scores + jnp.where(
        same_kind, variate_bias[0][None, :, None, None], variate_bias[1][None, :, None, None]
    )
    return (scores, same_kind)


def forward_piece(queries, query_kinds, variate_bias, carried, pieces):
    piece_keys, piece_values, piece_kinds = pieces
    seq_count = piece_keys.shape[0]
    piece_len = piece_keys.shape[1]
    block_size = math.gcd(piece_len, 512)

    def forward_advance(block_index, totals):
        running_max, running_total, running_sum = totals
        offset = block_index * block_size
        key_rows = lax.dynamic_slice_in_dim(piece_keys, offset, block_size, 1).reshape(
            seq_count, block_size, H, HD
        )
        value_rows = lax.dynamic_slice_in_dim(piece_values, offset, block_size, 1).reshape(
            seq_count, block_size, H, HD
        )
        kind_rows = lax.dynamic_slice_in_dim(piece_kinds, offset, block_size, 1)
        scores, same_kind = score_block(queries, key_rows, query_kinds, kind_rows, variate_bias)
        new_max = jnp.maximum(running_max, jnp.max(scores, axis=-1))
        factor = jnp.exp(running_max - new_max)
        exp_scores = jnp.exp(scores - new_max[..., None])
        running_total = running_total * factor + jnp.sum(exp_scores, axis=-1)
        running_sum = running_sum * factor[..., None] + jnp.einsum(
            "shqk,skhe->shqe",
            exp_scores.astype(jnp.bfloat16),
            value_rows,
            preferred_element_type=jnp.float32,
        )
        return (new_max, running_total, running_sum)

    return lax.fori_loop(0, piece_len // block_size, forward_advance, carried)


def back_piece(context, carried, pieces):
    queries, query_kinds, grad_out, log_total, delta_row, variate_bias = context
    piece_keys, piece_values, piece_kinds = pieces
    seq_count = piece_keys.shape[0]
    piece_len = piece_keys.shape[1]
    block_size = math.gcd(piece_len, 512)
    score_scale = HD ** (-0.5)

    def back_advance(block_index, totals):
        offset = block_index * block_size
        key_rows = lax.dynamic_slice_in_dim(piece_keys, offset, block_size, 1).reshape(
            seq_count, block_size, H, HD
        )
        value_rows = lax.dynamic_slice_in_dim(piece_values, offset, block_size, 1).reshape(
            seq_count, block_size, H, HD
        )
        kind_rows = lax.dynamic_slice_in_dim(piece_kinds, offset, block_size, 1)
        scores, same_kind = score_block(queries, key_rows, query_kinds, kind_rows, variate_bias)
        attn_prob = jnp.exp(scores - log_total[..., None])
        grad_prob = jnp.einsum(
            "sqhe,skhe->shqk", grad_out, value_rows, preferred_element_type=jnp.float32
        )
        grad_score = attn_prob * (grad_prob - delta_row[..., None])
        bias_step = jnp.stack(
            [
                jnp.sum(jnp.where(same_kind, grad_score, 0.0), axis=(0, 2, 3)),
                jnp.sum(jnp.where(same_kind, 0.0, grad_score), axis=(0, 2, 3)),
            ]
        )
        score_low = grad_score.astype(jnp.bfloat16)
        query_grad = (
            totals[0]
            + jnp.einsum("shqk,skhe->shqe", score_low, key_rows, preferred_element_type=jnp.float32)
            * score_scale
        )
        key_part = (
            jnp.einsum("shqk,sqhe->skhe", score_low, queries, preferred_element_type=jnp.float32)
            * score_scale
        ).reshape(seq_count, block_size, D)
        value_part = jnp.einsum(
            "shqk,sqhe->skhe",
            attn_prob.astype(jnp.bfloat16),
            grad_out,
            preferred_element_type=jnp.float32,
        ).reshape(seq_count, block_size, D)
        key_total = lax.dynamic_update_slice_in_dim(
            totals[2],
            lax.dynamic_slice_in_dim(totals[2], offset, block_size, 1) + key_part,
            offset,
            1,
        )
        value_total = lax.dynamic_update_slice_in_dim(
            totals[3],
            lax.dynamic_slice_in_dim(totals[3], offset, block_size, 1) + value_part,
            offset,
            1,
        )
        return (query_grad, totals[1] + bias_step, key_total, value_total)

    return lax.fori_loop(0, piece_len // block_size, back_advance, carried)


def local(
    inputs,
    variate_ids,
    time_ids,
    attn_gain,
    query_weight,
    key_weight,
    value_weight,
    out_weight,
    query_gain,
    key_gain,
    variate_bias,
    ffn_gain,
    gate_weight,
    up_weight,
    down_weight,
    out_grad,
):
    seq_count = inputs.shape[1]
    tok_count = inputs.shape[2]
    row_count = seq_count * tok_count
    full_grads = [
        jnp.zeros(extent, jnp.float32)
        for extent in ((D,), (D, D), (D, D), (D, D), (D, D), (D,), (FF, D), (FF, D), (FF, D))
    ]
    small_grads = [
        jnp.zeros((HD,), jnp.float32),
        jnp.zeros((HD,), jnp.float32),
        jnp.zeros((2, H), jnp.float32),
    ]
    shard_total = None
    small_total = None
    outputs_list = []
    input_grads = []
    weights_now = None
    for micro_index in range(inputs.shape[0]):
        weights_now = (
            lax.all_gather(attn_gain.astype(jnp.bfloat16), ("dp", "seq"), axis=0, tiled=True),
            lax.all_gather(query_weight.astype(jnp.bfloat16), ("dp", "seq"), axis=0, tiled=True),
            lax.all_gather(key_weight.astype(jnp.bfloat16), ("dp", "seq"), axis=0, tiled=True),
            lax.all_gather(value_weight.astype(jnp.bfloat16), ("dp", "seq"), axis=0, tiled=True),
            lax.all_gather(out_weight.astype(jnp.bfloat16), ("dp", "seq"), axis=0, tiled=True),
            lax.all_gather(ffn_gain.astype(jnp.bfloat16), ("dp", "seq"), axis=0, tiled=True),
            lax.all_gather(gate_weight.astype(jnp.bfloat16), ("dp", "seq"), axis=0, tiled=True),
            lax.all_gather(up_weight.astype(jnp.bfloat16), ("dp", "seq"), axis=0, tiled=True),
            lax.all_gather(down_weight.astype(jnp.bfloat16), ("dp", "seq"), axis=0, tiled=True),
        )
        gain_one, w_query, w_key, w_value, w_out, gain_two, w_gate, w_up, w_down = weights_now
        hidden_in = inputs[micro_index].astype(jnp.float32).reshape(row_count, D)
        kinds_now = variate_ids[micro_index].astype(jnp.bfloat16)
        cos_part, sin_part = rotation(time_ids[micro_index])
        inv_one = rms_scale(hidden_in)
        normed = (hidden_in * inv_one * gain_one.astype(jnp.float32)).astype(jnp.bfloat16)
        query_raw = product(normed, w_query).reshape(seq_count, tok_count, H, HD)
        key_raw = product(normed, w_key).reshape(seq_count, tok_count, H, HD)
        value_flat = product(normed, w_value).astype(jnp.bfloat16).reshape(seq_count, tok_count, D)
        inv_query = rms_scale(query_raw)
        query_rot = rotate(query_raw * inv_query * query_gain, cos_part, sin_part).astype(
            jnp.bfloat16
        )
        inv_key = rms_scale(key_raw)
        key_rot = rotate(key_raw * inv_key * key_gain, cos_part, sin_part).astype(jnp.bfloat16)
        key_flat = key_rot.reshape(seq_count, tok_count, D)
        initial = (
            jnp.full((seq_count, H, tok_count), lowest, jnp.float32),
            jnp.zeros((seq_count, H, tok_count), jnp.float32),
            jnp.zeros((seq_count, H, tok_count, HD), jnp.float32),
        )
        final_max, final_total, final_sum = forward_piece(
            query_rot,
            kinds_now,
            variate_bias,
            initial,
            (
                lax.all_gather(key_flat, "seq", axis=1, tiled=True),
                lax.all_gather(value_flat, "seq", axis=1, tiled=True),
                lax.all_gather(kinds_now, "seq", axis=1, tiled=True),
            ),
        )
        log_total = final_max + jnp.log(final_total)
        attended = jnp.transpose(final_sum / final_total[..., None], (0, 2, 1, 3))
        attended_low = attended.reshape(row_count, D).astype(jnp.bfloat16)
        middle = hidden_in + product(attended_low, w_out)
        inv_two = rms_scale(middle)
        normed_two = (middle * inv_two * gain_two.astype(jnp.float32)).astype(jnp.bfloat16)
        gate_pre = times_transposed(normed_two, w_gate)
        up_pre = times_transposed(normed_two, w_up)
        gate_sig = jax.nn.sigmoid(gate_pre)
        hidden_low = (gate_pre * gate_sig * up_pre).astype(jnp.bfloat16)
        result = middle + product(hidden_low, w_down)
        outputs_list.append(result.reshape(seq_count, tok_count, D).astype(jnp.bfloat16))
        gain_one, w_query, w_key, w_value, w_out, gain_two, w_gate, w_up, w_down = (
            lax.all_gather(attn_gain.astype(jnp.bfloat16), ("dp", "seq"), axis=0, tiled=True),
            lax.all_gather(query_weight.astype(jnp.bfloat16), ("dp", "seq"), axis=0, tiled=True),
            lax.all_gather(key_weight.astype(jnp.bfloat16), ("dp", "seq"), axis=0, tiled=True),
            lax.all_gather(value_weight.astype(jnp.bfloat16), ("dp", "seq"), axis=0, tiled=True),
            lax.all_gather(out_weight.astype(jnp.bfloat16), ("dp", "seq"), axis=0, tiled=True),
            lax.all_gather(ffn_gain.astype(jnp.bfloat16), ("dp", "seq"), axis=0, tiled=True),
            lax.all_gather(gate_weight.astype(jnp.bfloat16), ("dp", "seq"), axis=0, tiled=True),
            lax.all_gather(up_weight.astype(jnp.bfloat16), ("dp", "seq"), axis=0, tiled=True),
            lax.all_gather(down_weight.astype(jnp.bfloat16), ("dp", "seq"), axis=0, tiled=True),
        )
        grad_in = out_grad[micro_index].astype(jnp.float32).reshape(row_count, D)
        grad_low = grad_in.astype(jnp.bfloat16)
        full_grads[8] = rows_inner(hidden_low, grad_low)
        grad_hidden = times_transposed(grad_low, w_down)
        grad_gate = (grad_hidden * up_pre * gate_sig * (1.0 + gate_pre * (1.0 - gate_sig))).astype(
            jnp.bfloat16
        )
        grad_up = (grad_hidden * gate_pre * gate_sig).astype(jnp.bfloat16)
        full_grads[6] = rows_inner(grad_gate, normed_two)
        full_grads[7] = rows_inner(grad_up, normed_two)
        grad_normed_two = product(grad_gate, w_gate) + product(grad_up, w_up)
        full_grads[5] = jnp.sum(grad_normed_two * middle * inv_two, axis=0)
        grad_middle = grad_in + norm_back(
            middle, inv_two, gain_two.astype(jnp.float32), grad_normed_two
        )
        grad_middle_low = grad_middle.astype(jnp.bfloat16)
        full_grads[4] = rows_inner(attended_low, grad_middle_low)
        grad_attended = (
            times_transposed(grad_middle_low, w_out)
            .astype(jnp.bfloat16)
            .reshape(seq_count, tok_count, H, HD)
        )
        delta_row = jnp.transpose(
            jnp.sum(grad_attended.astype(jnp.float32) * attended, axis=-1), (0, 2, 1)
        )
        context = (query_rot, kinds_now, grad_attended, log_total, delta_row, variate_bias)
        base_carry = (
            jnp.zeros((seq_count, H, tok_count, HD), jnp.float32),
            jnp.zeros((2, H), jnp.float32),
        )
        length_all = tok_count * lax.axis_size("seq")
        wide_carry = (
            jnp.zeros((seq_count, length_all, D), jnp.float32),
            jnp.zeros((seq_count, length_all, D), jnp.float32),
        )
        grad_query_heads, grad_bias, key_all, value_all = back_piece(
            context,
            base_carry + wide_carry,
            (
                lax.all_gather(key_flat, "seq", axis=1, tiled=True),
                lax.all_gather(value_flat, "seq", axis=1, tiled=True),
                lax.all_gather(kinds_now, "seq", axis=1, tiled=True),
            ),
        )
        grad_key, grad_value = (
            lax.psum_scatter(
                key_all.astype(jnp.bfloat16), "seq", scatter_dimension=1, tiled=True
            ).astype(jnp.float32),
            lax.psum_scatter(
                value_all.astype(jnp.bfloat16), "seq", scatter_dimension=1, tiled=True
            ).astype(jnp.float32),
        )
        grad_key = grad_key.reshape(seq_count, tok_count, H, HD)
        grad_value_low = grad_value.reshape(row_count, D).astype(jnp.bfloat16)
        small_grads[2] = grad_bias
        grad_query = jnp.transpose(grad_query_heads, (0, 2, 1, 3))
        grad_query_norm = rotate_back(grad_query, cos_part, sin_part)
        small_grads[0] = jnp.sum(grad_query_norm * query_raw * inv_query, axis=(0, 1, 2))
        grad_query_low = (
            norm_back(query_raw, inv_query, query_gain, grad_query_norm)
            .reshape(row_count, D)
            .astype(jnp.bfloat16)
        )
        grad_key_norm = rotate_back(grad_key, cos_part, sin_part)
        small_grads[1] = jnp.sum(grad_key_norm * key_raw * inv_key, axis=(0, 1, 2))
        grad_key_low = (
            norm_back(key_raw, inv_key, key_gain, grad_key_norm)
            .reshape(row_count, D)
            .astype(jnp.bfloat16)
        )
        full_grads[1] = rows_inner(normed, grad_query_low)
        full_grads[2] = rows_inner(normed, grad_key_low)
        full_grads[3] = rows_inner(normed, grad_value_low)
        grad_normed = (
            times_transposed(grad_query_low, w_query)
            + times_transposed(grad_key_low, w_key)
            + times_transposed(grad_value_low, w_value)
        )
        full_grads[0] = jnp.sum(grad_normed * hidden_in * inv_one, axis=0)
        input_total = grad_middle + norm_back(
            hidden_in, inv_one, gain_one.astype(jnp.float32), grad_normed
        )
        input_grads.append(input_total.reshape(seq_count, tok_count, D).astype(jnp.bfloat16))
        shards = (
            lax.psum_scatter(full_grads[0], ("dp", "seq"), scatter_dimension=0, tiled=True),
            lax.psum_scatter(full_grads[1], ("dp", "seq"), scatter_dimension=0, tiled=True),
            lax.psum_scatter(full_grads[2], ("dp", "seq"), scatter_dimension=0, tiled=True),
            lax.psum_scatter(full_grads[3], ("dp", "seq"), scatter_dimension=0, tiled=True),
            lax.psum_scatter(full_grads[4], ("dp", "seq"), scatter_dimension=0, tiled=True),
            lax.psum_scatter(full_grads[5], ("dp", "seq"), scatter_dimension=0, tiled=True),
            lax.psum_scatter(full_grads[6], ("dp", "seq"), scatter_dimension=0, tiled=True),
            lax.psum_scatter(full_grads[7], ("dp", "seq"), scatter_dimension=0, tiled=True),
            lax.psum_scatter(full_grads[8], ("dp", "seq"), scatter_dimension=0, tiled=True),
        )
        summed = lax.psum((small_grads[0], small_grads[1], small_grads[2]), ("dp", "seq"))
        shards, summed = (list(shards), list(summed))
        if shard_total is None:
            shard_total = shards
            small_total = summed
        else:
            shard_total = [
                earlier_part + later_part for earlier_part, later_part in zip(shard_total, shards)
            ]
            small_total = [
                earlier_part + later_part for earlier_part, later_part in zip(small_total, summed)
            ]
        full_grads = [jnp.zeros_like(member) for member in full_grads]
        small_grads = [jnp.zeros_like(member) for member in small_grads]
    return (
        jnp.stack(outputs_list),
        jnp.stack(input_grads),
        shard_total[0],
        shard_total[1],
        shard_total[2],
        shard_total[3],
        shard_total[4],
        small_total[0],
        small_total[1],
        small_total[2],
        shard_total[5],
        shard_total[6],
        shard_total[7],
        shard_total[8],
    )


def swap_seq(values, mask):
    return lax.ppermute(values, "seq", [(at, at ^ mask) for at in range(8)])


def swap_dp(values, mask):
    return lax.ppermute(values, "dp", [(at, at ^ mask) for at in range(4)])


def pick(pieces, which):
    chosen = pieces[-1]
    for at in range(len(pieces) - 2, -1, -1):
        chosen = jnp.where(which == at, pieces[at], chosen)
    return chosen


def ordered(pieces, own):
    return jnp.stack([pick(pieces, own ^ at) for at in range(len(pieces))])


def together(*values):
    return lax.optimization_barrier(values)


def at_index(values, index, axis=0):
    return lax.dynamic_index_in_dim(values, index, axis, keepdims=False)


def contract_last(left_side, right_side):
    return lax.dot_general(
        left_side, right_side, (((1,), (1,)), ((), ())), preferred_element_type=jnp.float32
    )


def exact(left_side, right_side):
    return jnp.dot(
        left_side,
        right_side,
        precision=lax.Precision.HIGHEST,
        preferred_element_type=jnp.float32,
    )


def head_block(scale):
    rows = lax.broadcasted_iota(jnp.int32, (128, 128), 0) // HD
    columns = lax.broadcasted_iota(jnp.int32, (128, 128), 1) // HD
    return jnp.where(rows == columns, scale, 0.0).astype(jnp.float32)


def rope_partner(values):
    lane = lax.broadcasted_iota(jnp.int32, values.shape, 1)
    return jnp.where(
        lane % HD < HD // 2, pltpu.roll(values, 128 - HD // 2, 1), pltpu.roll(values, HD // 2, 1)
    )


def three_parts(values):
    first = values.astype(jnp.bfloat16).astype(jnp.float32)
    second = (values - first).astype(jnp.bfloat16).astype(jnp.float32)
    third = (values - first - second).astype(jnp.bfloat16).astype(jnp.float32)
    return first, second, third


GRANT = 60 << 20
BQ = 256
BK = 256
LSE_LANE = 24


def attend_kernel(
    q_in,
    k_in,
    v_in,
    cos_in,
    sin_in,
    hot_in,
    q_gain,
    k_gain,
    bias_in,
    near_out,
    far_out,
    qs_out,
    ks_out,
    vs_out,
    ext_out,
    kx,
    vx,
):
    mean_block = head_block(1.0 / HD)

    def prepare(raw, gain):
        inv = lax.rsqrt(exact(raw * raw, mean_block) + epsilon)
        scaled = raw * inv * gain
        return scaled * cos_in[...] + rope_partner(scaled) * sin_in[...]

    qs_out[...] = (
        prepare(q_in[...], q_gain[...]).astype(jnp.bfloat16).astype(jnp.float32) * HD**-0.5
    ).astype(jnp.bfloat16)
    keys = prepare(k_in[...], k_gain[...]).astype(jnp.bfloat16)
    ks_out[...] = keys
    kx[:, :128] = keys
    kx[:, 128:] = hot_in[...]
    values = v_in[...].astype(jnp.bfloat16)
    vs_out[...] = values
    vx[:, :128] = values
    vx[:, 128:] = jnp.ones(values.shape, jnp.bfloat16)
    lane = lax.broadcasted_iota(jnp.int32, (BQ, 128), 1)

    def step(block, carry):
        rows = pl.ds(pl.multiple_of(block * BQ, BQ), BQ)
        queries = qs_out[rows, :].astype(jnp.float32)
        hot = hot_in[rows, :].astype(jnp.float32)
        results = []
        for head in range(2):
            mine = jnp.where(lane // HD == head, queries, 0.0).astype(jnp.bfloat16)
            extra = hot * bias_in[0, head : head + 1, :]
            scores = contract_last(
                jnp.concatenate([mine, extra.astype(jnp.bfloat16)], axis=1), kx[...]
            )
            weights = jnp.exp(scores).astype(jnp.bfloat16)
            summed = jnp.dot(weights, vx[...], preferred_element_type=jnp.float32)
            total = summed[:, 128:]
            results.append(summed[:, :128] / total)
            first, second, third = three_parts(-jnp.log(total))
            extra = jnp.where(lane == LSE_LANE, first, extra)
            extra = jnp.where(lane == LSE_LANE + 1, second, extra)
            extra = jnp.where(lane == LSE_LANE + 2, third, extra)
            ext_out[head, rows, :] = extra.astype(jnp.bfloat16)
        result = jnp.where(lane < HD, results[0], results[1]).astype(jnp.bfloat16)
        half = near_out.shape[0]

        @pl.when(block < half // BQ)
        def _():
            near_out[pl.ds(pl.multiple_of(block * BQ, BQ), BQ), :] = result

        @pl.when(block >= half // BQ)
        def _():
            far_out[pl.ds(pl.multiple_of(block * BQ - half, BQ), BQ), :] = result

        return carry

    lax.fori_loop(0, q_in.shape[0] // BQ, step, 0)


def attend_back_kernel(
    q_in,
    k_in,
    qs_in,
    ks_in,
    vs_in,
    ext_in,
    hot_in,
    grad_near,
    grad_far,
    att_near,
    att_far,
    cos_in,
    sin_in,
    q_gain,
    k_gain,
    out,
    gain_out,
    bias_out,
    kx,
    vx,
    kt,
    qx,
    qg,
    gx,
    dqt,
    dk_sum,
    dv_sum,
):
    tokens = q_in.shape[0]
    lane = lax.broadcasted_iota(jnp.int32, (tokens, 128), 1)
    keys = ks_in[...]
    kx[:, :128] = keys
    kx[:, 128:] = hot_in[...]
    kt[...] = keys.astype(jnp.float32).T.astype(jnp.bfloat16)
    vx[:, :128] = vs_in[...]
    vx[:, 128:] = jnp.where(lane % HD < 3, 1.0, 0.0).astype(jnp.bfloat16)
    grads = jnp.concatenate([grad_near[...], grad_far[...]]).astype(jnp.float32)
    results = jnp.concatenate([att_near[...], att_far[...]]).astype(jnp.float32)
    delta = exact(grads * results, head_block(1.0))
    first, second, third = three_parts(-delta)
    parts = jnp.where(
        lane % HD == 0,
        first,
        jnp.where(lane % HD == 1, second, jnp.where(lane % HD == 2, third, 0.0)),
    )
    queries = qs_in[...].astype(jnp.float32)
    for head in range(2):
        own = lane // HD == head
        mine = jnp.where(own, queries, 0.0).astype(jnp.bfloat16)
        qx[head, :, :128] = mine
        qx[head, :, 128:] = ext_in[head]
        qg[head, :, :128] = mine
        qg[head, :, 128:] = hot_in[...]
        gx[head, :, :128] = jnp.where(own, grads, 0.0).astype(jnp.bfloat16)
        gx[head, :, 128:] = jnp.where(own, parts, 0.0).astype(jnp.bfloat16)
    dqt[...] = jnp.zeros(dqt.shape, jnp.float32)
    block_lane = lax.broadcasted_iota(jnp.int32, (BK, 128), 1)
    counted = jnp.where((block_lane < 8) | (block_lane == LSE_LANE), 1.0, 0.0)

    def step(block, carry):
        rows = pl.ds(pl.multiple_of(block * BK, BK), BK)
        hot = hot_in[rows, :].astype(jnp.float32) * counted
        dk_parts = []
        dv_parts = []
        bias_parts = []
        for head in range(2):
            probs = jnp.exp(contract_last(kx[rows, :], qx[head]))
            dscores = (probs * contract_last(vx[rows, :], gx[head])).astype(jnp.bfloat16)
            dv_parts.append(
                jnp.dot(
                    probs.astype(jnp.bfloat16), gx[head, :, :128], preferred_element_type=jnp.float32
                )
            )
            wide = jnp.dot(dscores, qg[head], preferred_element_type=jnp.float32)
            dk_parts.append(wide[:, :128])
            bias_parts.append(jnp.sum(wide[:, 128:] * hot, axis=0, keepdims=True))
            head_rows = pl.ds(head * HD, HD)
            dqt[head_rows, :] += jnp.dot(
                kt[head_rows, rows], dscores, preferred_element_type=jnp.float32
            )
        dk_sum[rows, :] = dk_parts[0] + dk_parts[1]
        dv_sum[rows, :] = dv_parts[0] + dv_parts[1]
        return (carry[0] + bias_parts[0], carry[1] + bias_parts[1])

    zero = jnp.zeros((1, 128), jnp.float32)
    sums = lax.fori_loop(0, tokens // BK, step, (zero, zero))
    bias_out[0, 0:1, :] = sums[0]
    bias_out[0, 1:2, :] = sums[1]
    mean_block = head_block(1.0 / HD)

    def finish(raw, upstream, gain):
        inv = lax.rsqrt(exact(raw * raw, mean_block) + epsilon)
        normed = upstream * cos_in[...] - rope_partner(upstream) * sin_in[...]
        gain_grad = jnp.sum(normed * raw * inv, axis=0, keepdims=True)
        weighted = normed * gain
        inner = exact(weighted * raw, mean_block)
        return inv * weighted - raw * (inv * inv * inv) * inner, gain_grad

    dq, dq_gain = finish(q_in[...], dqt[...].T * HD**-0.5, q_gain[...])
    dk, dk_gain = finish(k_in[...], dk_sum[...], k_gain[...])
    out[0] = dq.astype(jnp.bfloat16)
    out[1] = dk.astype(jnp.bfloat16)
    out[2] = dv_sum[...].astype(jnp.bfloat16)
    gain_out[0, 0:1, :] = dq_gain
    gain_out[0, 1:2, :] = dk_gain


def attend(qkv, cos_part, sin_part, hot, q_gain, k_gain, bias_rows):
    tokens = qkv.shape[0]
    column = lambda shift: pl.BlockSpec((tokens, 128), lambda pair: (0, pair + shift))
    half = pl.BlockSpec((tokens // 2, 128), lambda pair: (0, pair))
    whole = pl.BlockSpec((tokens, 128), lambda pair: (0, 0))
    line = pl.BlockSpec((1, 128), lambda pair: (0, 0))
    low = lambda: jax.ShapeDtypeStruct((tokens, 256), jnp.bfloat16)
    return pl.pallas_call(
        attend_kernel,
        grid=(2,),
        in_specs=[
            column(0),
            column(2),
            column(4),
            whole,
            whole,
            whole,
            line,
            line,
            pl.BlockSpec((1, 2, 128), lambda pair: (pair, 0, 0)),
        ],
        out_specs=[
            half,
            half,
            column(0),
            column(0),
            column(0),
            pl.BlockSpec((2, tokens, 128), lambda pair: (pair, 0, 0)),
        ],
        out_shape=[
            jax.ShapeDtypeStruct((tokens // 2, 256), jnp.bfloat16),
            jax.ShapeDtypeStruct((tokens // 2, 256), jnp.bfloat16),
            low(),
            low(),
            low(),
            jax.ShapeDtypeStruct((4, tokens, 128), jnp.bfloat16),
        ],
        scratch_shapes=[
            pltpu.VMEM((tokens, 256), jnp.bfloat16),
            pltpu.VMEM((tokens, 256), jnp.bfloat16),
        ],
        compiler_params=pltpu.CompilerParams(vmem_limit_bytes=GRANT),
        cost_estimate=pl.CostEstimate(
            flops=16 * tokens * tokens * 256,
            bytes_accessed=tokens * 256 * 30,
            transcendentals=4 * tokens * tokens,
        ),
        name="attend",
    )(qkv, qkv, qkv, cos_part, sin_part, hot, q_gain, k_gain, bias_rows)


def attend_back(qkv, saved, hot, grads, attended, cos_part, sin_part, q_gain, k_gain):
    queries, keys, values, extra = saved
    tokens = qkv.shape[0]
    column = lambda shift: pl.BlockSpec((tokens, 128), lambda pair: (0, pair + shift))
    half = pl.BlockSpec((tokens // 2, 128), lambda pair: (0, pair))
    whole = pl.BlockSpec((tokens, 128), lambda pair: (0, 0))
    line = pl.BlockSpec((1, 128), lambda pair: (0, 0))
    two = pl.BlockSpec((1, 2, 128), lambda pair: (pair, 0, 0))
    wide = pltpu.VMEM((tokens, 256), jnp.bfloat16)
    both = pltpu.VMEM((2, tokens, 256), jnp.bfloat16)
    return pl.pallas_call(
        attend_back_kernel,
        grid=(2,),
        in_specs=[
            column(0),
            column(2),
            column(0),
            column(0),
            column(0),
            pl.BlockSpec((2, tokens, 128), lambda pair: (pair, 0, 0)),
            whole,
            half,
            half,
            half,
            half,
            whole,
            whole,
            line,
            line,
        ],
        out_specs=[pl.BlockSpec((3, tokens, 128), lambda pair: (0, 0, pair)), two, two],
        out_shape=[
            jax.ShapeDtypeStruct((3, tokens, 256), jnp.bfloat16),
            jax.ShapeDtypeStruct((2, 2, 128), jnp.float32),
            jax.ShapeDtypeStruct((2, 2, 128), jnp.float32),
        ],
        scratch_shapes=[
            wide,
            wide,
            pltpu.VMEM((128, tokens), jnp.bfloat16),
            both,
            both,
            both,
            pltpu.VMEM((128, tokens), jnp.float32),
            pltpu.VMEM((tokens, 128), jnp.float32),
            pltpu.VMEM((tokens, 128), jnp.float32),
        ],
        compiler_params=pltpu.CompilerParams(vmem_limit_bytes=GRANT),
        cost_estimate=pl.CostEstimate(
            flops=40 * tokens * tokens * 256,
            bytes_accessed=tokens * 256 * 40,
            transcendentals=4 * tokens * tokens,
        ),
        name="attend_back",
    )(
        qkv,
        qkv,
        queries,
        keys,
        values,
        extra,
        hot,
        *grads,
        *attended,
        cos_part,
        sin_part,
        q_gain,
        k_gain,
    )


def front_kernel(place, *refs):
    pieces, crossed, own, other = refs[:4], refs[4], refs[5:9], refs[9]
    weights_out, unit_out, qkv_out = refs[10:]
    dp_at, level, core = place[0], place[1], place[2]
    for at_dp in range(4):
        for at_level in range(4):
            base = ((dp_at ^ at_dp) * 4 + (level ^ at_level)) * 64
            mine = pl.ds(pl.multiple_of(base + core * 32, 32), 32)
            theirs = pl.ds(pl.multiple_of(base + (1 - core) * 32, 32), 32)
            rows = slice(at_level * 32, at_level * 32 + 32)
            for part in range(3):
                lanes = pl.ds(pl.multiple_of(part * 512 + core * 256, 256), 256)
                weights_out[mine, part * 256 : (part + 1) * 256] = pieces[at_dp][rows, lanes]
            weights_out[theirs, :] = crossed[at_dp * 128 + at_level * 32 :][:32, :]

    def norm(values):
        wide = values.astype(jnp.float32)
        return (wide * rms_scale(wide)).astype(jnp.bfloat16)

    for at in range(4):
        unit_out[at * 128 : (at + 1) * 128, :] = norm(own[at][...])
        unit_out[512 + at * 128 : 512 + (at + 1) * 128, :] = norm(other[at])
    for at in range(2):
        rows = slice(at * 512, (at + 1) * 512)
        qkv_out[rows, :] = jnp.dot(
            unit_out[rows, :], weights_out[...], preferred_element_type=jnp.float32
        )


def front(place, pieces, crossed, own, other):
    tokens = 2 * other.shape[0] * other.shape[1]
    quarter = pl.BlockSpec((128, 1536), lambda at: (0, 0))
    piece = pl.BlockSpec((128, D), lambda at: (0, 0))
    return pl.pallas_call(
        front_kernel,
        grid=(1,),
        in_specs=[pl.BlockSpec(memory_space=pltpu.SMEM)]
        + [quarter] * 4
        + [pl.BlockSpec((512, 768), lambda at: (0, 0))]
        + [piece] * 4
        + [pl.BlockSpec((4, 128, D), lambda at: (0, 0, 0))],
        out_specs=[
            pl.BlockSpec((D, 768), lambda at: (0, 0)),
            pl.BlockSpec((tokens, D), lambda at: (0, 0)),
            pl.BlockSpec((tokens, 768), lambda at: (0, 0)),
        ],
        out_shape=[
            jax.ShapeDtypeStruct((D, 768), jnp.bfloat16),
            jax.ShapeDtypeStruct((tokens, D), jnp.bfloat16),
            jax.ShapeDtypeStruct((tokens, 768), jnp.float32),
        ],
        compiler_params=pltpu.CompilerParams(vmem_limit_bytes=GRANT),
        cost_estimate=pl.CostEstimate(
            flops=2 * tokens * D * 768, bytes_accessed=12 * D * D, transcendentals=tokens
        ),
        name="front",
    )(place, *pieces, crossed, *own, other)


def place_kernel(place, *refs):
    out, gain_out = refs[8:]
    gain_out[...] = sum(member[128:, :128].astype(jnp.float32) for member in refs[:8])
    dp_at, level, core = place[0], place[1], place[2]
    for at_dp in range(4):
        for at_level in range(4):
            base = ((dp_at ^ at_dp) * 4 + (level ^ at_level)) * 64
            rows = slice(at_level * 32, at_level * 32 + 32)
            for source, side in ((refs[at_dp], core), (refs[4 + at_dp], 1 - core)):
                to = pl.ds(pl.multiple_of(base + side * 32, 32), 32)
                out[to, :] = source[rows, :]


def place_rows(place, pieces, crossed):
    quarter = pl.BlockSpec((144, D), lambda at: (0, 0))
    return pl.pallas_call(
        place_kernel,
        grid=(1,),
        in_specs=[pl.BlockSpec(memory_space=pltpu.SMEM)] + [quarter] * 8,
        out_specs=[
            pl.BlockSpec((D, D), lambda at: (0, 0)),
            pl.BlockSpec((16, 128), lambda at: (0, 0)),
        ],
        out_shape=[
            jax.ShapeDtypeStruct((D, D), jnp.bfloat16),
            jax.ShapeDtypeStruct((16, 128), jnp.float32),
        ],
        compiler_params=pltpu.CompilerParams(vmem_limit_bytes=GRANT),
        cost_estimate=pl.CostEstimate(flops=0, bytes_accessed=4 * D * D, transcendentals=0),
        name="place_rows",
    )(place, *pieces, *crossed)


def tail_kernel(
    place, dqkv, weights, unit, gains, biases, ffn_gain, back_kept, back_sent, kept, sent, part, small
):
    core, group = place[2], place[3]
    tokens = unit.shape[0]

    def back(rows):
        total = contract_last(dqkv[0, rows, :], weights[:, :256])
        for at in (1, 2):
            total += contract_last(dqkv[at, rows, :], weights[:, at * 256 : (at + 1) * 256])
        return total

    back_kept[...] = back(slice(0, tokens // 2))
    back_sent[...] = back(slice(tokens // 2, tokens)).astype(jnp.bfloat16)
    for at in range(3):
        part[:, at * 256 : (at + 1) * 256] = rows_inner(unit[...], dqkv[at]).astype(jnp.bfloat16)
    for at in range(16):
        rows = slice(at * 32, at * 32 + 32)
        kept[rows, :] = part[pl.ds(pl.multiple_of(at * 64 + core * 32, 32), 32), :]
        sent[rows, :] = part[pl.ds(pl.multiple_of(at * 64 + (1 - core) * 32, 32), 32), :]
    lane = lax.broadcasted_iota(jnp.int32, (1, 128), 1)
    sums = gains[0] + gains[1]
    sums = sums + pltpu.roll(sums, HD, 1)
    placed = jnp.zeros((1, 128), jnp.float32)
    for head in range(4):
        line = biases[head // 2, head % 2 : head % 2 + 1, :]
        same = jnp.sum(jnp.where(lane < 8, line, 0.0), axis=1, keepdims=True)
        total = jnp.sum(jnp.where(lane == LSE_LANE, line, 0.0), axis=1, keepdims=True)
        spot = group * 4 + head
        placed = jnp.where(lane == spot, same, placed)
        placed = jnp.where(lane == spot + H, total - same, placed)
    small[...] = jnp.zeros(small.shape, jnp.float32)
    for at in range(4):
        small[at : at + 1, :256] = ffn_gain[:, at * 256 : (at + 1) * 256]
    small[4:5, :128] = jnp.where(lane < HD, sums[0:1], sums[1:2])
    small[4:5, 128:256] = placed
    kept[512:, :] = small[...].astype(jnp.bfloat16)
    sent[512:, :] = small[...].astype(jnp.bfloat16)


def tail(place, dqkv, weights, unit, gains, biases, ffn_gain):
    tokens = unit.shape[0]
    whole = lambda shape: pl.BlockSpec(shape, lambda at: (0,) * len(shape))
    shapes = [
        ((tokens // 2, D), jnp.float32),
        ((tokens // 2, D), jnp.bfloat16),
        ((528, 768), jnp.bfloat16),
        ((528, 768), jnp.bfloat16),
    ]
    arguments = (dqkv, weights, unit, gains, biases, ffn_gain)
    return pl.pallas_call(
        tail_kernel,
        grid=(1,),
        in_specs=[pl.BlockSpec(memory_space=pltpu.SMEM)]
        + [whole(member.shape) for member in arguments],
        out_specs=[whole(shape) for shape, _ in shapes],
        out_shape=[jax.ShapeDtypeStruct(shape, kind) for shape, kind in shapes],
        scratch_shapes=[pltpu.VMEM((D, 768), jnp.bfloat16), pltpu.VMEM((16, 768), jnp.float32)],
        compiler_params=pltpu.CompilerParams(vmem_limit_bytes=GRANT),
        cost_estimate=pl.CostEstimate(
            flops=4 * tokens * D * 768, bytes_accessed=14 * D * D, transcendentals=0
        ),
        name="tail",
    )(place, *arguments)


def lower_kernel(gate, up, down, out):
    out[0] = gate[...].astype(jnp.bfloat16)
    out[1] = up[...].astype(jnp.bfloat16)
    out[2] = down[...].astype(jnp.bfloat16)


def lower(gate, up, down):
    whole = pl.BlockSpec(gate.shape, lambda at: (0, 0))
    return pl.pallas_call(
        lower_kernel,
        grid=(1,),
        in_specs=[whole] * 3,
        out_specs=pl.BlockSpec((3,) + gate.shape, lambda at: (0, 0, 0)),
        out_shape=jax.ShapeDtypeStruct((3,) + gate.shape, jnp.bfloat16),
        compiler_params=pltpu.CompilerParams(vmem_limit_bytes=GRANT),
        name="lower",
    )(gate, up, down)


def middle_back_kernel(
    kept, near, side, far, dy_in, middle_in, gain_in, weights, grad_out, low_out, att_out, sums_out
):
    wide = jnp.float32
    upstream = (kept[...] + near[...].astype(wide)) + (
        side[...].astype(wide) + far[...].astype(wide)
    )
    middle = middle_in[...]
    inv = rms_scale(middle)
    sums_out[...] = jnp.sum(upstream * middle * inv, axis=0, keepdims=True)
    grad = dy_in[...].astype(wide) + norm_back(middle, inv, gain_in[...], upstream)
    grad_out[...] = grad
    grad_low = grad.astype(jnp.bfloat16)
    low_out[...] = grad_low
    att_out[...] = contract_last(grad_low, weights[...]).astype(jnp.bfloat16)


def middle_back(kept, moved, own_dy, middle, gain_two, w_out):
    rows = kept.shape[0]
    block = pl.BlockSpec((rows, D), lambda at: (0, 0))
    line = pl.BlockSpec((1, D), lambda at: (0, 0))
    return pl.pallas_call(
        middle_back_kernel,
        grid=(1,),
        in_specs=[block] * 6 + [line, pl.BlockSpec((D, D), lambda at: (0, 0))],
        out_specs=[block, block, block, line],
        out_shape=[
            jax.ShapeDtypeStruct((rows, D), jnp.float32),
            jax.ShapeDtypeStruct((rows, D), jnp.bfloat16),
            jax.ShapeDtypeStruct((rows, D), jnp.bfloat16),
            jax.ShapeDtypeStruct((1, D), jnp.float32),
        ],
        compiler_params=pltpu.CompilerParams(vmem_limit_bytes=GRANT),
        cost_estimate=pl.CostEstimate(
            flops=2 * rows * D * D, bytes_accessed=22 * rows * D + 2 * D * D, transcendentals=rows
        ),
        name="middle_back",
    )(kept, *moved, own_dy, middle, gain_two, w_out)


GATED = 512
HIDDEN = 256


def gated_kernel(count, *refs):
    tokens_in, grads_in, weights = refs[:count], refs[count : 2 * count], refs[2 * count]
    hidden_out, back_out = refs[2 * count + 1 : 3 * count + 1], refs[3 * count + 1 : 4 * count + 1]
    totals = refs[4 * count + 1 :]
    step = pl.program_id(0)
    pair = weights[0:2].reshape(2 * GATED, D)
    for at in range(count):
        both = contract_last(tokens_in[at][...], pair)
        gate, up = both[:, :GATED], both[:, GATED:]
        grad_hidden = contract_last(grads_in[at][...], weights[2])
        sig = lax.logistic(gate)
        swished = gate * sig
        hidden_out[at][2] = (swished * up).astype(jnp.bfloat16)
        grad_gate = (grad_hidden * up * sig * (1.0 + gate * (1.0 - sig))).astype(jnp.bfloat16)
        grad_up = (grad_hidden * swished).astype(jnp.bfloat16)
        hidden_out[at][0] = grad_gate
        hidden_out[at][1] = grad_up
        added = jnp.dot(
            jnp.concatenate([grad_gate, grad_up], axis=1), pair, preferred_element_type=jnp.float32
        )
        total = totals[at]

        @pl.when(step == 0)
        def _():
            total[...] = added

        @pl.when(step == pl.num_programs(0) - 1)
        def _():
            back_out[at][...] = (total[...] + added).astype(back_out[at].dtype)


def gated(tokens_in, grads_in, weights, kind):
    count = len(tokens_in)
    chunk = tokens_in[0].shape[0]
    hidden = weights.shape[1]
    assert hidden == 2 * GATED
    whole = pl.BlockSpec((chunk, D), lambda at: (0, 0))
    results = pl.pallas_call(
        functools.partial(gated_kernel, count),
        grid=(2,),
        in_specs=[whole] * (2 * count) + [pl.BlockSpec((3, GATED, D), lambda at: (0, at, 0))],
        out_specs=[pl.BlockSpec((3, chunk, GATED), lambda at: (0, 0, at))] * count
        + [whole] * count,
        out_shape=[jax.ShapeDtypeStruct((3, chunk, hidden), jnp.bfloat16)] * count
        + [jax.ShapeDtypeStruct((chunk, D), kind)] * count,
        scratch_shapes=[pltpu.VMEM((chunk, D), jnp.float32)] * count,
        compiler_params=pltpu.CompilerParams(vmem_limit_bytes=GRANT),
        cost_estimate=pl.CostEstimate(
            flops=10 * count * chunk * D * hidden,
            bytes_accessed=2 * D * (7 * count * chunk + 3 * hidden),
            transcendentals=count * chunk * hidden,
        ),
        name="gated",
    )(*tokens_in, *grads_in, weights)
    return list(zip(results[:count], results[count:]))


def ffn_grads_kernel(*refs):
    tokens_in, grads_in, hidden_in = refs[0:4], refs[4:8], refs[8:12]
    grads_out, tokens_all, grads_all, hidden = refs[12:]
    chunk = tokens_in[0].shape[0]
    rows_of = [slice(at * chunk, (at + 1) * chunk) for at in range(4)]

    @pl.when(pl.program_id(0) == 0)
    def _():
        for at in range(4):
            tokens_all[rows_of[at], :] = tokens_in[at][...]
            grads_all[rows_of[at], :] = grads_in[at][...]

    for which in range(3):
        for at in range(4):
            hidden[which, rows_of[at], :] = hidden_in[at][which]
        other = tokens_all if which < 2 else grads_all
        grads_out[which] = rows_inner(hidden[which], other[...]).astype(jnp.bfloat16)


def ffn_grads(tokens_in, grads_in, hidden_in):
    chunk = tokens_in[0].shape[0]
    tokens = 4 * chunk
    hidden = hidden_in[0].shape[2]
    whole = pl.BlockSpec((chunk, D), lambda at: (0, 0))
    wide_low = pltpu.VMEM((tokens, D), jnp.bfloat16)
    return pl.pallas_call(
        ffn_grads_kernel,
        grid=(hidden // HIDDEN,),
        in_specs=[whole] * 8 + [pl.BlockSpec((3, chunk, HIDDEN), lambda at: (0, 0, at))] * 4,
        out_specs=pl.BlockSpec((3, HIDDEN, D), lambda at: (0, at, 0)),
        out_shape=jax.ShapeDtypeStruct((3, hidden, D), jnp.bfloat16),
        scratch_shapes=[wide_low, wide_low, pltpu.VMEM((3, tokens, HIDDEN), jnp.bfloat16)],
        compiler_params=pltpu.CompilerParams(vmem_limit_bytes=GRANT),
        cost_estimate=pl.CostEstimate(
            flops=6 * tokens * D * hidden,
            bytes_accessed=2 * D * (4 * tokens + 6 * hidden),
            transcendentals=0,
        ),
        name="ffn_grads",
    )(*tokens_in, *grads_in, *hidden_in)


def down_kernel(*refs):
    hidden_in, weights = refs[:4], refs[4]
    outs = refs[5:]
    for at in range(4):
        outs[at][...] = jnp.dot(
            hidden_in[at][0], weights[0], preferred_element_type=jnp.float32
        ).astype(outs[at].dtype)


def down(hidden_in, weights):
    chunk = hidden_in[0].shape[1]
    hidden = weights.shape[1]
    half = D // 2
    block = pl.BlockSpec((chunk, half), lambda at: (0, at))
    return pl.pallas_call(
        down_kernel,
        grid=(2,),
        in_specs=[pl.BlockSpec((1, chunk, hidden), lambda at: (2, 0, 0))] * 4
        + [pl.BlockSpec((1, hidden, half), lambda at: (2, 0, at))],
        out_specs=[block] * 4,
        out_shape=[jax.ShapeDtypeStruct((chunk, D), jnp.float32)]
        + [jax.ShapeDtypeStruct((chunk, D), jnp.bfloat16)] * 3,
        compiler_params=pltpu.CompilerParams(vmem_limit_bytes=GRANT),
        cost_estimate=pl.CostEstimate(
            flops=8 * chunk * D * hidden,
            bytes_accessed=2 * D * (9 * chunk + hidden),
            transcendentals=0,
        ),
        name="down",
    )(*hidden_in, weights)


def local_split(
    inputs,
    variate_ids,
    time_ids,
    attn_gain,
    query_weight,
    key_weight,
    value_weight,
    out_weight,
    query_gain,
    key_gain,
    variate_bias,
    ffn_gain,
    gate_weight,
    up_weight,
    down_weight,
    out_grad,
):
    low = jnp.bfloat16
    wide = jnp.float32
    dp_at = lax.axis_index("dp")
    seq_at = lax.axis_index("seq")
    core = seq_at & 1
    level = seq_at >> 1
    batch = level >> 1
    parity = level & 1
    piece = inputs.shape[2]
    tokens = 8 * piece
    others = (1, 2, 3)
    swap_core = lambda values: swap_seq(values, 1)
    swap_level = lambda values, mask: swap_seq(values, 2 * mask)

    own_dy = out_grad[:, 0].reshape(2 * piece, D)

    gain_low = attn_gain.astype(low).astype(wide)
    weights_low = jnp.stack([query_weight, key_weight, value_weight], axis=1).astype(low)
    scaled = (weights_low.astype(wide) * gain_low[:, None, None]).astype(low)
    scaled = scaled.reshape(32, 3, 2, 512)
    kinds = variate_ids[:, 0]
    times = time_ids[:, 0]
    ids = jnp.stack([kinds, times // 64, times % 64], axis=1).astype(low)
    ids = jnp.concatenate([ids, swap_core(ids)], axis=1)
    ids = jnp.pad(ids, ((0, 0), (0, 26), (0, 0)))

    def with_ids(weights_part, which):
        return jnp.concatenate(
            [weights_part.reshape(32, 1536), at_index(ids, which)], axis=1
        )

    same = with_ids(at_index(scaled, parity, 2), 1 - batch)
    cross_near = with_ids(at_index(scaled, 1 - parity, 2), batch)
    cross_far = with_ids(at_index(scaled, 1 - parity, 2), 1 - batch)
    moved = [swap_level((cross_near, same, cross_far)[mask - 1], mask) for mask in others]
    own_x = inputs[:, 0]
    near, far = at_index(own_x, batch), at_index(own_x, 1 - batch)
    with_gain = jnp.concatenate(
        [
            out_weight.astype(low).reshape(32, D),
            jnp.where(
                jnp.arange(16)[:, None] == dp_at * 4 + level,
                jnp.where(
                    core == 0,
                    jnp.pad(ffn_gain.astype(low)[None, :], ((0, 0), (0, D - 32))),
                    jnp.pad(ffn_gain.astype(low)[None, :], ((0, 0), (32, D - 64))),
                ),
                0.0,
            ).astype(low),
        ]
    )
    near = jnp.concatenate([near, with_gain])
    far = jnp.concatenate([far, with_gain])
    same, near, far, gate_local, up_local, down_local, *moved = together(
        same, near, far, gate_weight, up_weight, down_weight, *moved
    )

    place = jnp.stack([dp_at, level, core, 2 * parity + core]).astype(jnp.int32)
    rows = jnp.concatenate([same[:, :1536]] + [member[:, :1536] for member in moved])
    ids = jnp.stack([at_index(ids, batch)] + [member[:, 1536:] for member in moved])
    moved = [swap_dp(rows, mask) for mask in others]
    from_far = swap_level(far, 2)
    from_near = swap_level(near, 1)
    ffn_local = lower(gate_local, up_local, down_local)
    last = swap_level(from_far, 1)
    ids = jnp.stack([ids[:, :3], ids[:, 3:6]]).astype(wide)

    kinds = ids[:, :, 0].reshape(tokens, 1)
    times = (ids[:, :, 1] * 64.0 + ids[:, :, 2]).reshape(tokens, 1)
    lane = lax.broadcasted_iota(jnp.int32, (1, 128), 1)
    hot = jnp.where(
        lane < LSE_LANE, (kinds == lane % 8).astype(wide), jnp.where(lane < LSE_LANE + 3, 1.0, 0.0)
    ).astype(low)
    half = HD // 2
    frequency = 10000.0 ** (-(lane % half).astype(wide) / half)
    angles = times * frequency
    cos_part = jnp.cos(angles)
    sin_part = jnp.sin(angles) * jnp.where(lane % HD < half, -1.0, 1.0)
    q_gain = jnp.tile(query_gain, 2)[None, :]
    k_gain = jnp.tile(key_gain, 2)[None, :]
    group = 2 * parity + core
    gaps = at_index((variate_bias[0] - variate_bias[1]).reshape(4, 4), group)
    first, second, third = three_parts(gaps)
    bias_rows = jnp.where(
        lane < 8,
        first[:, None],
        jnp.where(
            lane < 16, second[:, None], jnp.where(lane < LSE_LANE, third[:, None], 0.0)
        ),
    ).reshape(2, 2, 128)

    rows, ffn_local, near, from_near, from_far, last, cos_part, sin_part, dy_sent, *moved = together(
        rows, ffn_local, near, from_near, from_far, last, cos_part, sin_part, own_dy, *moved
    )
    w_ffn = lax.all_gather(ffn_local, "seq", axis=1, tiled=True)

    pieces = [rows] + moved
    four = [near, from_near, from_far, last]
    own = [member[:piece] for member in four]
    tiles = [member[piece + 32 :] for member in four]
    out_rows = jnp.concatenate(
        [member[piece : piece + 32] for member in four]
        + [(tiles[0] + tiles[1]) + (tiles[2] + tiles[3])]
    )
    sent = jnp.concatenate(
        [
            jnp.concatenate(
                [
                    jnp.where(
                        core == 0,
                        member[:, at * 512 + 256 : at * 512 + 512],
                        member[:, at * 512 : at * 512 + 256],
                    )
                    for at in range(3)
                ],
                axis=1,
            )
            for member in pieces
        ]
    )
    crossed, rows_crossed, out_rows, dy_sent = together(
        swap_core(jnp.stack(own)), swap_core(sent), out_rows, dy_sent
    )

    w_qkv, unit, qkv = front(place, pieces, rows_crossed, four, crossed)
    att_near, att_far, *saved = attend(qkv, cos_part, sin_part, hot, q_gain, k_gain, bias_rows)
    attended = (att_near, att_far)
    att_near, att_far, dy_near, dy_side, *pieces = together(
        att_near,
        att_far,
        swap_dp(dy_sent, 1),
        swap_dp(dy_sent, 2),
        out_rows,
        *[swap_dp(out_rows, mask) for mask in others],
    )

    part, crossed, *rows_crossed = together(
        att_near, swap_core(att_far), *[swap_core(member) for member in pieces]
    )
    part, crossed = part.reshape(4, piece, 256), crossed.reshape(4, piece, 256)
    both = jnp.concatenate(
        [jnp.where(core == 0, part, crossed), jnp.where(core == 0, crossed, part)], axis=2
    )

    w_out, gain_two = place_rows(place, pieces, rows_crossed)
    w_out, gain_two, dy_far, *arrived = together(
        w_out,
        gain_two,
        swap_dp(dy_sent, 3),
        both[0],
        *[swap_level(both[mask], mask) for mask in others],
    )
    gain_two = gain_two[:, :64].reshape(1, D)
    blocks = [pick(arrived, level ^ at) for at in range(4)]
    own_att = jnp.concatenate(
        [
            jnp.concatenate([blocks[0], blocks[1]], axis=1),
            jnp.concatenate([blocks[2], blocks[3]], axis=1),
        ]
    )

    own_wide = own_x.reshape(2 * piece, D).astype(wide)
    middle = own_wide + product(own_att, w_out)
    inv_two = rms_scale(middle)
    normed_two = (middle * inv_two * gain_two).astype(low)
    dy_pieces = [own_dy, dy_near, dy_side, dy_far]

    own_two, w_ffn, middle, *dy_pieces = together(normed_two, w_ffn, middle, *dy_pieces)
    ((own_hidden, kept),) = gated([own_two], dy_pieces[:1], w_ffn, wide)
    own_two, near_two, side_two, own_hidden, kept = together(
        own_two, swap_dp(own_two, 1), swap_dp(own_two, 2), own_hidden, kept
    )

    (near_hidden, near_back), (side_hidden, side_back) = gated(
        [near_two, side_two], dy_pieces[1:3], w_ffn, low
    )
    far_two, near_hidden, near_back, side_hidden, side_back = together(
        swap_dp(own_two, 3), near_hidden, near_back, side_hidden, side_back
    )

    near_back, side_back = swap_dp(near_back, 1), swap_dp(side_back, 2)
    ((far_hidden, far_back),) = gated([far_two], dy_pieces[3:], w_ffn, low)
    far_hidden, far_back = together(far_hidden, far_back)
    hidden = [own_hidden, near_hidden, side_hidden, far_hidden]
    ffn_part = ffn_grads([own_two, near_two, side_two, far_two], dy_pieces, hidden)
    ffn_part, kept, *moved = together(
        ffn_part, kept, near_back, side_back, swap_dp(far_back, 3)
    )
    ffn_shard = lax.psum_scatter(ffn_part, "seq", scatter_dimension=1, tiled=True)
    grad_middle, middle_low, grad_att, gain_two_part = middle_back(
        kept, moved, own_dy, middle, gain_two, w_out
    )

    blocks = [
        grad_att[at // 2 * piece : (at // 2 + 1) * piece, at % 2 * 512 : (at % 2 + 1) * 512]
        for at in range(4)
    ]
    arrived = [pick(blocks, level)]
    arrived += [swap_level(pick(blocks, level ^ mask), mask) for mask in others]
    out_part = rows_inner(own_att, middle_low).astype(low).reshape(4, 4, 2, 32, D)
    out_kept = at_index(out_part, core, 2)
    out_crossed = swap_core(at_index(out_part, 1 - core, 2))
    down_kept, *down_chunks = down(hidden, w_ffn)
    out_kept, out_crossed, down_kept, *rest = together(
        out_kept, out_crossed, down_kept, *down_chunks, *arrived
    )
    down_chunks, arrived = rest[:3], rest[3:]

    halves = [
        jnp.concatenate([member[:, :256] for member in arrived]),
        jnp.concatenate([member[:, 256:] for member in arrived]),
    ]
    out_half = (out_kept.astype(wide) + out_crossed.astype(wide)).astype(low)
    kept, crossed, out_half, *down_chunks = together(
        pick(halves, core), swap_core(pick(halves, 1 - core)), out_half, *down_chunks
    )
    grads = (kept, crossed)

    out_moved = [swap_dp(at_index(out_half, dp_at ^ mask), mask) for mask in others]
    down_moved = [swap_dp(down_chunks[mask - 1], mask) for mask in (1, 2)]
    dqkv, gain_sums, bias_sums = attend_back(
        qkv, saved, hot, grads, attended, cos_part, sin_part, q_gain, k_gain
    )
    dqkv, last_chunk, *rest = together(dqkv, down_chunks[2], *out_moved, *down_moved)
    out_moved = [member.astype(wide) for member in rest[:3]]
    out_sum = (at_index(out_half, dp_at).astype(wide) + out_moved[0]) + (out_moved[1] + out_moved[2])
    down_moved = rest[3:]

    back_kept, back_sent, kept, sent = tail(
        place, dqkv, w_qkv, unit, gain_sums, bias_sums, gain_two_part
    )
    back_kept, back_crossed, kept, crossed = together(
        back_kept, swap_core(back_sent), kept, swap_core(sent)
    )

    back = (back_kept + back_crossed.astype(wide)).reshape(4, piece, D)
    small_low = (kept[512:].astype(wide) + crossed[512:].astype(wide)).astype(low)

    def dp_message(to):
        return jnp.concatenate(
            [
                lax.dynamic_slice_in_dim(kept, to * 128, 128),
                lax.dynamic_slice_in_dim(crossed, to * 128, 128),
                small_low,
            ]
        )

    moved = [swap_dp(dp_message(dp_at ^ mask), mask) for mask in others]
    back_low = back.astype(low)
    back_moved = [swap_level(back_low[mask], mask) for mask in (2, 3)]
    qkv_kept, kept, near, ffn_shard, middle, down_kept, last_chunk, *rest = together(
        dp_message(dp_at),
        back[0],
        back_low[1],
        ffn_shard,
        middle,
        down_kept,
        last_chunk,
        *down_moved,
        *back_moved,
        *moved,
    )
    down_moved = rest[:2]
    back_moved = [member.astype(wide) for member in rest[2:4]]
    moved = rest[4:]
    ffn_sums = ffn_shard.astype(wide)

    moved = [member.astype(wide) for member in moved]
    total = qkv_kept.astype(wide)
    total = ((total + moved[0]) + (moved[1] + moved[2])).astype(low)
    small_low = total[256:]

    def level_message(to):
        out_block = at_index(out_sum, to).astype(low)
        qkv_block = jnp.concatenate(
            [
                lax.dynamic_slice_in_dim(total, to * 32, 32),
                lax.dynamic_slice_in_dim(total, 128 + to * 32, 32),
            ]
        )
        return jnp.concatenate(
            [qkv_block[:, at * 256 : (at + 1) * 256] for at in range(3)]
            + [out_block[:, at * 256 : (at + 1) * 256] for at in range(4)]
            + [small_low[:, :256]]
        )

    moved = [swap_level(level_message(level ^ mask), mask) for mask in others]
    passed = back_moved[0] + back_moved[1]
    mine, kept, passed, near, last_chunk, *moved = together(
        level_message(level), kept, passed, swap_level(near, 1), swap_dp(last_chunk, 3), *moved
    )
    kept = kept + near.astype(wide)
    down_moved = [member.astype(wide) for member in down_moved + [last_chunk]]
    result = middle + ((down_kept + down_moved[0]) + (down_moved[1] + down_moved[2]))
    result = result.astype(low)
    moved = [member.astype(wide) for member in moved]
    mine = mine.astype(wide)
    back = jnp.concatenate(
        [jnp.where(batch == 0, kept, passed), jnp.where(batch == 0, passed, kept)]
    )
    inv_one = rms_scale(own_wide)
    inner = jnp.mean(back * own_wide, axis=-1, keepdims=True)
    input_grad = grad_middle + inv_one * back - own_wide * (inv_one * inv_one * inv_one) * inner
    input_grad = input_grad.astype(low)

    small = (mine[320:] + moved[0][320:]) + (moved[1][320:] + moved[2][320:])
    small = small[:5].reshape(1280)
    out_grads = (mine[192:320] + moved[0][192:320]) + (moved[1][192:320] + moved[2][192:320])
    out_grads = jnp.concatenate([out_grads[at * 32 : (at + 1) * 32] for at in range(4)], axis=1)
    same = (mine[:192] + moved[1][:192]).reshape(3, 2, 32, 256)
    cross = (moved[0][:192] + moved[2][:192]).reshape(3, 2, 32, 256)
    quarters = []
    for member in (jnp.where(parity == 0, same, cross), jnp.where(parity == 0, cross, same)):
        quarters += [
            jnp.where(core == 0, member[:, 0], member[:, 1]),
            jnp.where(core == 0, member[:, 1], member[:, 0]),
        ]
    unit_grads = jnp.concatenate(quarters, axis=2)
    gain_two_grad = lax.dynamic_slice_in_dim(small, (dp_at * 8 + seq_at) * 32, 32)
    gain_grad = jnp.sum(unit_grads * jnp.transpose(weights_low, (1, 0, 2)).astype(wide), axis=(0, 2))
    qkv_grads = unit_grads * gain_low[None, :, None]

    shape = (2, 1, piece, D)
    return (
        result.reshape(shape),
        input_grad.reshape(shape),
        gain_grad,
        qkv_grads[0],
        qkv_grads[1],
        qkv_grads[2],
        out_grads,
        small[D : D + HD],
        small[D + HD : D + 2 * HD],
        small[D + 2 * HD : D + 2 * HD + 2 * H].reshape(2, H),
        gain_two_grad,
        ffn_sums[0],
        ffn_sums[1],
        ffn_sums[2],
    )


def solution(mesh):
    placed = (
        P(None, "dp", "seq", None),
        P(None, "dp", "seq"),
        P(None, "dp", "seq"),
        P(("dp", "seq")),
        P(("dp", "seq"), None),
        P(("dp", "seq"), None),
        P(("dp", "seq"), None),
        P(("dp", "seq"), None),
        P(),
        P(),
        P(),
        P(("dp", "seq")),
        P(("dp", "seq"), None),
        P(("dp", "seq"), None),
        P(("dp", "seq"), None),
        P(None, "dp", "seq", None),
    )
    split = mesh.shape["dp"] == 4 and mesh.shape["seq"] == 8
    return jax.shard_map(
        local_split if split else local,
        mesh=mesh,
        in_specs=placed,
        out_specs=(
            P(None, "dp", "seq", None),
            P(None, "dp", "seq", None),
            P(("dp", "seq")),
            P(("dp", "seq"), None),
            P(("dp", "seq"), None),
            P(("dp", "seq"), None),
            P(("dp", "seq"), None),
            P(),
            P(),
            P(),
            P(("dp", "seq")),
            P(("dp", "seq"), None),
            P(("dp", "seq"), None),
            P(("dp", "seq"), None),
        ),
        check_vma=False,
    )
```

```python
import functools
import math

import jax
import jax.numpy as jnp
from jax import lax
from jax.experimental import pallas as pl
from jax.experimental.pallas import tpu as pltpu
from jax.sharding import PartitionSpec as P

D = 1024
H = 16
HD = 64
FF = 4096


epsilon = 1e-06
lowest = -1e30


def rms_scale(values):
    return lax.rsqrt(jnp.mean(values * values, axis=-1, keepdims=True) + epsilon)


def norm_back(values, inv_rms, gain_vec, upstream):
    weighted = upstream * gain_vec
    inner_mean = jnp.mean(weighted * values, axis=-1, keepdims=True)
    return inv_rms * weighted - values * (inv_rms * inv_rms * inv_rms) * inner_mean


def rotation(positions):
    half_dim = HD // 2
    frequency = 10000.0 ** (-jnp.arange(half_dim).astype(jnp.float32) / half_dim)
    angles = positions.astype(jnp.float32)[..., None] * frequency
    return (jnp.cos(angles)[..., None, :], jnp.sin(angles)[..., None, :])


def rotate(values, cos_part, sin_part):
    half_dim = values.shape[-1] // 2
    first_half = values[..., :half_dim]
    second_half = values[..., half_dim:]
    return jnp.concatenate(
        [
            first_half * cos_part - second_half * sin_part,
            first_half * sin_part + second_half * cos_part,
        ],
        axis=-1,
    )


def rotate_back(upstream, cos_part, sin_part):
    half_dim = upstream.shape[-1] // 2
    first_half = upstream[..., :half_dim]
    second_half = upstream[..., half_dim:]
    return jnp.concatenate(
        [
            first_half * cos_part + second_half * sin_part,
            second_half * cos_part - first_half * sin_part,
        ],
        axis=-1,
    )


def product(left_side, right_side):
    return jnp.dot(left_side, right_side, preferred_element_type=jnp.float32)


def times_transposed(left_side, right_side):
    return lax.dot_general(
        left_side, right_side, (((1,), (1,)), ((), ())), preferred_element_type=jnp.float32
    )


def rows_inner(left_side, right_side):
    return lax.dot_general(
        left_side, right_side, (((0,), (0,)), ((), ())), preferred_element_type=jnp.float32
    )


def score_block(queries, key_rows, query_kinds, key_kinds, variate_bias):
    raw_scores = jnp.einsum(
        "sqhe,skhe->shqk", queries, key_rows, preferred_element_type=jnp.float32
    ) * HD ** (-0.5)
    same_kind = query_kinds[:, None, :, None] == key_kinds[:, None, None, :]
    scores = raw_scores + jnp.where(
        same_kind, variate_bias[0][None, :, None, None], variate_bias[1][None, :, None, None]
    )
    return (scores, same_kind)


def forward_piece(queries, query_kinds, variate_bias, carried, pieces):
    piece_keys, piece_values, piece_kinds = pieces
    seq_count = piece_keys.shape[0]
    piece_len = piece_keys.shape[1]
    block_size = math.gcd(piece_len, 512)

    def forward_advance(block_index, totals):
        running_max, running_total, running_sum = totals
        offset = block_index * block_size
        key_rows = lax.dynamic_slice_in_dim(piece_keys, offset, block_size, 1).reshape(
            seq_count, block_size, H, HD
        )
        value_rows = lax.dynamic_slice_in_dim(piece_values, offset, block_size, 1).reshape(
            seq_count, block_size, H, HD
        )
        kind_rows = lax.dynamic_slice_in_dim(piece_kinds, offset, block_size, 1)
        scores, same_kind = score_block(queries, key_rows, query_kinds, kind_rows, variate_bias)
        new_max = jnp.maximum(running_max, jnp.max(scores, axis=-1))
        factor = jnp.exp(running_max - new_max)
        exp_scores = jnp.exp(scores - new_max[..., None])
        running_total = running_total * factor + jnp.sum(exp_scores, axis=-1)
        running_sum = running_sum * factor[..., None] + jnp.einsum(
            "shqk,skhe->shqe",
            exp_scores.astype(jnp.bfloat16),
            value_rows,
            preferred_element_type=jnp.float32,
        )
        return (new_max, running_total, running_sum)

    return lax.fori_loop(0, piece_len // block_size, forward_advance, carried)


def back_piece(context, carried, pieces):
    queries, query_kinds, grad_out, log_total, delta_row, variate_bias = context
    piece_keys, piece_values, piece_kinds = pieces
    seq_count = piece_keys.shape[0]
    piece_len = piece_keys.shape[1]
    block_size = math.gcd(piece_len, 512)
    score_scale = HD ** (-0.5)

    def back_advance(block_index, totals):
        offset = block_index * block_size
        key_rows = lax.dynamic_slice_in_dim(piece_keys, offset, block_size, 1).reshape(
            seq_count, block_size, H, HD
        )
        value_rows = lax.dynamic_slice_in_dim(piece_values, offset, block_size, 1).reshape(
            seq_count, block_size, H, HD
        )
        kind_rows = lax.dynamic_slice_in_dim(piece_kinds, offset, block_size, 1)
        scores, same_kind = score_block(queries, key_rows, query_kinds, kind_rows, variate_bias)
        attn_prob = jnp.exp(scores - log_total[..., None])
        grad_prob = jnp.einsum(
            "sqhe,skhe->shqk", grad_out, value_rows, preferred_element_type=jnp.float32
        )
        grad_score = attn_prob * (grad_prob - delta_row[..., None])
        bias_step = jnp.stack(
            [
                jnp.sum(jnp.where(same_kind, grad_score, 0.0), axis=(0, 2, 3)),
                jnp.sum(jnp.where(same_kind, 0.0, grad_score), axis=(0, 2, 3)),
            ]
        )
        score_low = grad_score.astype(jnp.bfloat16)
        query_grad = (
            totals[0]
            + jnp.einsum("shqk,skhe->shqe", score_low, key_rows, preferred_element_type=jnp.float32)
            * score_scale
        )
        key_part = (
            jnp.einsum("shqk,sqhe->skhe", score_low, queries, preferred_element_type=jnp.float32)
            * score_scale
        ).reshape(seq_count, block_size, D)
        value_part = jnp.einsum(
            "shqk,sqhe->skhe",
            attn_prob.astype(jnp.bfloat16),
            grad_out,
            preferred_element_type=jnp.float32,
        ).reshape(seq_count, block_size, D)
        key_total = lax.dynamic_update_slice_in_dim(
            totals[2],
            lax.dynamic_slice_in_dim(totals[2], offset, block_size, 1) + key_part,
            offset,
            1,
        )
        value_total = lax.dynamic_update_slice_in_dim(
            totals[3],
            lax.dynamic_slice_in_dim(totals[3], offset, block_size, 1) + value_part,
            offset,
            1,
        )
        return (query_grad, totals[1] + bias_step, key_total, value_total)

    return lax.fori_loop(0, piece_len // block_size, back_advance, carried)


def local(
    inputs,
    variate_ids,
    time_ids,
    attn_gain,
    query_weight,
    key_weight,
    value_weight,
    out_weight,
    query_gain,
    key_gain,
    variate_bias,
    ffn_gain,
    gate_weight,
    up_weight,
    down_weight,
    out_grad,
):
    seq_count = inputs.shape[1]
    tok_count = inputs.shape[2]
    row_count = seq_count * tok_count
    full_grads = [
        jnp.zeros(extent, jnp.float32)
        for extent in ((D,), (D, D), (D, D), (D, D), (D, D), (D,), (FF, D), (FF, D), (FF, D))
    ]
    small_grads = [
        jnp.zeros((HD,), jnp.float32),
        jnp.zeros((HD,), jnp.float32),
        jnp.zeros((2, H), jnp.float32),
    ]
    shard_total = None
    small_total = None
    outputs_list = []
    input_grads = []
    weights_now = None
    for micro_index in range(inputs.shape[0]):
        weights_now = (
            lax.all_gather(attn_gain.astype(jnp.bfloat16), ("dp", "seq"), axis=0, tiled=True),
            lax.all_gather(query_weight.astype(jnp.bfloat16), ("dp", "seq"), axis=0, tiled=True),
            lax.all_gather(key_weight.astype(jnp.bfloat16), ("dp", "seq"), axis=0, tiled=True),
            lax.all_gather(value_weight.astype(jnp.bfloat16), ("dp", "seq"), axis=0, tiled=True),
            lax.all_gather(out_weight.astype(jnp.bfloat16), ("dp", "seq"), axis=0, tiled=True),
            lax.all_gather(ffn_gain.astype(jnp.bfloat16), ("dp", "seq"), axis=0, tiled=True),
            lax.all_gather(gate_weight.astype(jnp.bfloat16), ("dp", "seq"), axis=0, tiled=True),
            lax.all_gather(up_weight.astype(jnp.bfloat16), ("dp", "seq"), axis=0, tiled=True),
            lax.all_gather(down_weight.astype(jnp.bfloat16), ("dp", "seq"), axis=0, tiled=True),
        )
        gain_one, w_query, w_key, w_value, w_out, gain_two, w_gate, w_up, w_down = weights_now
        hidden_in = inputs[micro_index].astype(jnp.float32).reshape(row_count, D)
        kinds_now = variate_ids[micro_index].astype(jnp.bfloat16)
        cos_part, sin_part = rotation(time_ids[micro_index])
        inv_one = rms_scale(hidden_in)
        normed = (hidden_in * inv_one * gain_one.astype(jnp.float32)).astype(jnp.bfloat16)
        query_raw = product(normed, w_query).reshape(seq_count, tok_count, H, HD)
        key_raw = product(normed, w_key).reshape(seq_count, tok_count, H, HD)
        value_flat = product(normed, w_value).astype(jnp.bfloat16).reshape(seq_count, tok_count, D)
        inv_query = rms_scale(query_raw)
        query_rot = rotate(query_raw * inv_query * query_gain, cos_part, sin_part).astype(
            jnp.bfloat16
        )
        inv_key = rms_scale(key_raw)
        key_rot = rotate(key_raw * inv_key * key_gain, cos_part, sin_part).astype(jnp.bfloat16)
        key_flat = key_rot.reshape(seq_count, tok_count, D)
        initial = (
            jnp.full((seq_count, H, tok_count), lowest, jnp.float32),
            jnp.zeros((seq_count, H, tok_count), jnp.float32),
            jnp.zeros((seq_count, H, tok_count, HD), jnp.float32),
        )
        final_max, final_total, final_sum = forward_piece(
            query_rot,
            kinds_now,
            variate_bias,
            initial,
            (
                lax.all_gather(key_flat, "seq", axis=1, tiled=True),
                lax.all_gather(value_flat, "seq", axis=1, tiled=True),
                lax.all_gather(kinds_now, "seq", axis=1, tiled=True),
            ),
        )
        log_total = final_max + jnp.log(final_total)
        attended = jnp.transpose(final_sum / final_total[..., None], (0, 2, 1, 3))
        attended_low = attended.reshape(row_count, D).astype(jnp.bfloat16)
        middle = hidden_in + product(attended_low, w_out)
        inv_two = rms_scale(middle)
        normed_two = (middle * inv_two * gain_two.astype(jnp.float32)).astype(jnp.bfloat16)
        gate_pre = times_transposed(normed_two, w_gate)
        up_pre = times_transposed(normed_two, w_up)
        gate_sig = jax.nn.sigmoid(gate_pre)
        hidden_low = (gate_pre * gate_sig * up_pre).astype(jnp.bfloat16)
        result = middle + product(hidden_low, w_down)
        outputs_list.append(result.reshape(seq_count, tok_count, D).astype(jnp.bfloat16))
        gain_one, w_query, w_key, w_value, w_out, gain_two, w_gate, w_up, w_down = (
            lax.all_gather(attn_gain.astype(jnp.bfloat16), ("dp", "seq"), axis=0, tiled=True),
            lax.all_gather(query_weight.astype(jnp.bfloat16), ("dp", "seq"), axis=0, tiled=True),
            lax.all_gather(key_weight.astype(jnp.bfloat16), ("dp", "seq"), axis=0, tiled=True),
            lax.all_gather(value_weight.astype(jnp.bfloat16), ("dp", "seq"), axis=0, tiled=True),
            lax.all_gather(out_weight.astype(jnp.bfloat16), ("dp", "seq"), axis=0, tiled=True),
            lax.all_gather(ffn_gain.astype(jnp.bfloat16), ("dp", "seq"), axis=0, tiled=True),
            lax.all_gather(gate_weight.astype(jnp.bfloat16), ("dp", "seq"), axis=0, tiled=True),
            lax.all_gather(up_weight.astype(jnp.bfloat16), ("dp", "seq"), axis=0, tiled=True),
            lax.all_gather(down_weight.astype(jnp.bfloat16), ("dp", "seq"), axis=0, tiled=True),
        )
        grad_in = out_grad[micro_index].astype(jnp.float32).reshape(row_count, D)
        grad_low = grad_in.astype(jnp.bfloat16)
        full_grads[8] = rows_inner(hidden_low, grad_low)
        grad_hidden = times_transposed(grad_low, w_down)
        grad_gate = (grad_hidden * up_pre * gate_sig * (1.0 + gate_pre * (1.0 - gate_sig))).astype(
            jnp.bfloat16
        )
        grad_up = (grad_hidden * gate_pre * gate_sig).astype(jnp.bfloat16)
        full_grads[6] = rows_inner(grad_gate, normed_two)
        full_grads[7] = rows_inner(grad_up, normed_two)
        grad_normed_two = product(grad_gate, w_gate) + product(grad_up, w_up)
        full_grads[5] = jnp.sum(grad_normed_two * middle * inv_two, axis=0)
        grad_middle = grad_in + norm_back(
            middle, inv_two, gain_two.astype(jnp.float32), grad_normed_two
        )
        grad_middle_low = grad_middle.astype(jnp.bfloat16)
        full_grads[4] = rows_inner(attended_low, grad_middle_low)
        grad_attended = (
            times_transposed(grad_middle_low, w_out)
            .astype(jnp.bfloat16)
            .reshape(seq_count, tok_count, H, HD)
        )
        delta_row = jnp.transpose(
            jnp.sum(grad_attended.astype(jnp.float32) * attended, axis=-1), (0, 2, 1)
        )
        context = (query_rot, kinds_now, grad_attended, log_total, delta_row, variate_bias)
        base_carry = (
            jnp.zeros((seq_count, H, tok_count, HD), jnp.float32),
            jnp.zeros((2, H), jnp.float32),
        )
        length_all = tok_count * lax.axis_size("seq")
        wide_carry = (
            jnp.zeros((seq_count, length_all, D), jnp.float32),
            jnp.zeros((seq_count, length_all, D), jnp.float32),
        )
        grad_query_heads, grad_bias, key_all, value_all = back_piece(
            context,
            base_carry + wide_carry,
            (
                lax.all_gather(key_flat, "seq", axis=1, tiled=True),
                lax.all_gather(value_flat, "seq", axis=1, tiled=True),
                lax.all_gather(kinds_now, "seq", axis=1, tiled=True),
            ),
        )
        grad_key, grad_value = (
            lax.psum_scatter(
                key_all.astype(jnp.bfloat16), "seq", scatter_dimension=1, tiled=True
            ).astype(jnp.float32),
            lax.psum_scatter(
                value_all.astype(jnp.bfloat16), "seq", scatter_dimension=1, tiled=True
            ).astype(jnp.float32),
        )
        grad_key = grad_key.reshape(seq_count, tok_count, H, HD)
        grad_value_low = grad_value.reshape(row_count, D).astype(jnp.bfloat16)
        small_grads[2] = grad_bias
        grad_query = jnp.transpose(grad_query_heads, (0, 2, 1, 3))
        grad_query_norm = rotate_back(grad_query, cos_part, sin_part)
        small_grads[0] = jnp.sum(grad_query_norm * query_raw * inv_query, axis=(0, 1, 2))
        grad_query_low = (
            norm_back(query_raw, inv_query, query_gain, grad_query_norm)
            .reshape(row_count, D)
            .astype(jnp.bfloat16)
        )
        grad_key_norm = rotate_back(grad_key, cos_part, sin_part)
        small_grads[1] = jnp.sum(grad_key_norm * key_raw * inv_key, axis=(0, 1, 2))
        grad_key_low = (
            norm_back(key_raw, inv_key, key_gain, grad_key_norm)
            .reshape(row_count, D)
            .astype(jnp.bfloat16)
        )
        full_grads[1] = rows_inner(normed, grad_query_low)
        full_grads[2] = rows_inner(normed, grad_key_low)
        full_grads[3] = rows_inner(normed, grad_value_low)
        grad_normed = (
            times_transposed(grad_query_low, w_query)
            + times_transposed(grad_key_low, w_key)
            + times_transposed(grad_value_low, w_value)
        )
        full_grads[0] = jnp.sum(grad_normed * hidden_in * inv_one, axis=0)
        input_total = grad_middle + norm_back(
            hidden_in, inv_one, gain_one.astype(jnp.float32), grad_normed
        )
        input_grads.append(input_total.reshape(seq_count, tok_count, D).astype(jnp.bfloat16))
        shards = (
            lax.psum_scatter(full_grads[0], ("dp", "seq"), scatter_dimension=0, tiled=True),
            lax.psum_scatter(full_grads[1], ("dp", "seq"), scatter_dimension=0, tiled=True),
            lax.psum_scatter(full_grads[2], ("dp", "seq"), scatter_dimension=0, tiled=True),
            lax.psum_scatter(full_grads[3], ("dp", "seq"), scatter_dimension=0, tiled=True),
            lax.psum_scatter(full_grads[4], ("dp", "seq"), scatter_dimension=0, tiled=True),
            lax.psum_scatter(full_grads[5], ("dp", "seq"), scatter_dimension=0, tiled=True),
            lax.psum_scatter(full_grads[6], ("dp", "seq"), scatter_dimension=0, tiled=True),
            lax.psum_scatter(full_grads[7], ("dp", "seq"), scatter_dimension=0, tiled=True),
            lax.psum_scatter(full_grads[8], ("dp", "seq"), scatter_dimension=0, tiled=True),
        )
        summed = lax.psum((small_grads[0], small_grads[1], small_grads[2]), ("dp", "seq"))
        shards, summed = (list(shards), list(summed))
        if shard_total is None:
            shard_total = shards
            small_total = summed
        else:
            shard_total = [
                earlier_part + later_part for earlier_part, later_part in zip(shard_total, shards)
            ]
            small_total = [
                earlier_part + later_part for earlier_part, later_part in zip(small_total, summed)
            ]
        full_grads = [jnp.zeros_like(member) for member in full_grads]
        small_grads = [jnp.zeros_like(member) for member in small_grads]
    return (
        jnp.stack(outputs_list),
        jnp.stack(input_grads),
        shard_total[0],
        shard_total[1],
        shard_total[2],
        shard_total[3],
        shard_total[4],
        small_total[0],
        small_total[1],
        small_total[2],
        shard_total[5],
        shard_total[6],
        shard_total[7],
        shard_total[8],
    )


def swap_seq(values, mask):
    return lax.ppermute(values, "seq", [(at, at ^ mask) for at in range(8)])


def swap_dp(values, mask):
    return lax.ppermute(values, "dp", [(at, at ^ mask) for at in range(4)])


def pick(pieces, which):
    chosen = pieces[-1]
    for at in range(len(pieces) - 2, -1, -1):
        chosen = jnp.where(which == at, pieces[at], chosen)
    return chosen


def ordered(pieces, own):
    return jnp.stack([pick(pieces, own ^ at) for at in range(len(pieces))])


def together(*values):
    return lax.optimization_barrier(values)


def at_index(values, index, axis=0):
    return lax.dynamic_index_in_dim(values, index, axis, keepdims=False)


def contract_last(left_side, right_side):
    return lax.dot_general(
        left_side, right_side, (((1,), (1,)), ((), ())), preferred_element_type=jnp.float32
    )


def exact(left_side, right_side):
    return jnp.dot(
        left_side,
        right_side,
        precision=lax.Precision.HIGHEST,
        preferred_element_type=jnp.float32,
    )


def head_block(scale):
    rows = lax.broadcasted_iota(jnp.int32, (128, 128), 0) // HD
    columns = lax.broadcasted_iota(jnp.int32, (128, 128), 1) // HD
    return jnp.where(rows == columns, scale, 0.0).astype(jnp.float32)


def rope_partner(values):
    lane = lax.broadcasted_iota(jnp.int32, values.shape, 1)
    return jnp.where(
        lane % HD < HD // 2, pltpu.roll(values, 128 - HD // 2, 1), pltpu.roll(values, HD // 2, 1)
    )


def three_parts(values):
    first = values.astype(jnp.bfloat16).astype(jnp.float32)
    second = (values - first).astype(jnp.bfloat16).astype(jnp.float32)
    third = (values - first - second).astype(jnp.bfloat16).astype(jnp.float32)
    return first, second, third


GRANT = 60 << 20
BQ = 512
BK = 1024
LSE_LANE = 24


def attend_kernel(
    q_in,
    k_in,
    v_in,
    cos_in,
    sin_in,
    hot_in,
    q_gain,
    k_gain,
    bias_in,
    near_out,
    far_out,
    qs_out,
    ks_out,
    vs_out,
    ext_out,
    kx,
    vx,
):
    mean_block = head_block(1.0 / HD)

    def prepare(raw, gain):
        inv = lax.rsqrt(exact(raw * raw, mean_block) + epsilon)
        scaled = raw * inv * gain
        return scaled * cos_in[...] + rope_partner(scaled) * sin_in[...]

    qs_out[...] = (
        prepare(q_in[...], q_gain[...]).astype(jnp.bfloat16).astype(jnp.float32) * HD**-0.5
    ).astype(jnp.bfloat16)
    keys = prepare(k_in[...], k_gain[...]).astype(jnp.bfloat16)
    ks_out[...] = keys
    kx[:, :128] = keys
    kx[:, 128:] = hot_in[...]
    values = v_in[...].astype(jnp.bfloat16)
    vs_out[...] = values
    vx[:, :128] = values
    vx[:, 128:] = jnp.ones(values.shape, jnp.bfloat16)
    lane = lax.broadcasted_iota(jnp.int32, (BQ, 128), 1)

    def step(block, carry):
        rows = pl.ds(pl.multiple_of(block * BQ, BQ), BQ)
        queries = qs_out[rows, :].astype(jnp.float32)
        hot = hot_in[rows, :].astype(jnp.float32)
        results = []
        for head in range(2):
            mine = jnp.where(lane // HD == head, queries, 0.0).astype(jnp.bfloat16)
            extra = hot * bias_in[0, head : head + 1, :]
            scores = contract_last(
                jnp.concatenate([mine, extra.astype(jnp.bfloat16)], axis=1), kx[...]
            )
            weights = jnp.exp(scores).astype(jnp.bfloat16)
            summed = jnp.dot(weights, vx[...], preferred_element_type=jnp.float32)
            total = summed[:, 128:]
            results.append(summed[:, :128] / total)
            first, second, third = three_parts(-jnp.log(total))
            extra = jnp.where(lane == LSE_LANE, first, extra)
            extra = jnp.where(lane == LSE_LANE + 1, second, extra)
            extra = jnp.where(lane == LSE_LANE + 2, third, extra)
            ext_out[head, rows, :] = extra.astype(jnp.bfloat16)
        result = jnp.where(lane < HD, results[0], results[1]).astype(jnp.bfloat16)
        half = near_out.shape[0]

        @pl.when(block < half // BQ)
        def _():
            near_out[pl.ds(pl.multiple_of(block * BQ, BQ), BQ), :] = result

        @pl.when(block >= half // BQ)
        def _():
            far_out[pl.ds(pl.multiple_of(block * BQ - half, BQ), BQ), :] = result

        return carry

    lax.fori_loop(0, q_in.shape[0] // BQ, step, 0)


def attend_back_kernel(
    q_in,
    k_in,
    qs_in,
    ks_in,
    vs_in,
    ext_in,
    hot_in,
    grad_near,
    grad_far,
    att_near,
    att_far,
    cos_in,
    sin_in,
    q_gain,
    k_gain,
    out,
    gain_out,
    bias_out,
    kx,
    vx,
    kt,
    qx,
    qg,
    gx,
    dqt,
    dk_sum,
    dv_sum,
):
    tokens = q_in.shape[0]
    lane = lax.broadcasted_iota(jnp.int32, (tokens, 128), 1)
    keys = ks_in[...]
    kx[:, :128] = keys
    kx[:, 128:] = hot_in[...]
    kt[...] = keys.astype(jnp.float32).T.astype(jnp.bfloat16)
    vx[:, :128] = vs_in[...]
    vx[:, 128:] = jnp.where(lane % HD < 3, 1.0, 0.0).astype(jnp.bfloat16)
    grads = jnp.concatenate([grad_near[...], grad_far[...]]).astype(jnp.float32)
    results = jnp.concatenate([att_near[...], att_far[...]]).astype(jnp.float32)
    delta = exact(grads * results, head_block(1.0))
    first, second, third = three_parts(-delta)
    parts = jnp.where(
        lane % HD == 0,
        first,
        jnp.where(lane % HD == 1, second, jnp.where(lane % HD == 2, third, 0.0)),
    )
    queries = qs_in[...].astype(jnp.float32)
    for head in range(2):
        own = lane // HD == head
        mine = jnp.where(own, queries, 0.0).astype(jnp.bfloat16)
        qx[head, :, :128] = mine
        qx[head, :, 128:] = ext_in[head]
        qg[head, :, :128] = mine
        qg[head, :, 128:] = hot_in[...]
        gx[head, :, :128] = jnp.where(own, grads, 0.0).astype(jnp.bfloat16)
        gx[head, :, 128:] = jnp.where(own, parts, 0.0).astype(jnp.bfloat16)
    dqt[...] = jnp.zeros(dqt.shape, jnp.float32)
    block_lane = lax.broadcasted_iota(jnp.int32, (BK, 128), 1)
    counted = jnp.where((block_lane < 8) | (block_lane == LSE_LANE), 1.0, 0.0)

    def step(block, carry):
        rows = pl.ds(pl.multiple_of(block * BK, BK), BK)
        hot = hot_in[rows, :].astype(jnp.float32) * counted
        dk_parts = []
        dv_parts = []
        bias_parts = []
        for head in range(2):
            probs = jnp.exp(contract_last(kx[rows, :], qx[head]))
            dscores = (probs * contract_last(vx[rows, :], gx[head])).astype(jnp.bfloat16)
            dv_parts.append(
                jnp.dot(
                    probs.astype(jnp.bfloat16), gx[head, :, :128], preferred_element_type=jnp.float32
                )
            )
            wide = jnp.dot(dscores, qg[head], preferred_element_type=jnp.float32)
            dk_parts.append(wide[:, :128])
            bias_parts.append(jnp.sum(wide[:, 128:] * hot, axis=0, keepdims=True))
            head_rows = pl.ds(head * HD, HD)
            dqt[head_rows, :] += jnp.dot(
                kt[head_rows, rows], dscores, preferred_element_type=jnp.float32
            )
        dk_sum[rows, :] = dk_parts[0] + dk_parts[1]
        dv_sum[rows, :] = dv_parts[0] + dv_parts[1]
        return (carry[0] + bias_parts[0], carry[1] + bias_parts[1])

    zero = jnp.zeros((1, 128), jnp.float32)
    sums = lax.fori_loop(0, tokens // BK, step, (zero, zero))
    bias_out[0, 0:1, :] = sums[0]
    bias_out[0, 1:2, :] = sums[1]
    mean_block = head_block(1.0 / HD)

    def finish(raw, upstream, gain):
        inv = lax.rsqrt(exact(raw * raw, mean_block) + epsilon)
        normed = upstream * cos_in[...] - rope_partner(upstream) * sin_in[...]
        gain_grad = jnp.sum(normed * raw * inv, axis=0, keepdims=True)
        weighted = normed * gain
        inner = exact(weighted * raw, mean_block)
        return inv * weighted - raw * (inv * inv * inv) * inner, gain_grad

    dq, dq_gain = finish(q_in[...], dqt[...].T * HD**-0.5, q_gain[...])
    dk, dk_gain = finish(k_in[...], dk_sum[...], k_gain[...])
    out[0] = dq.astype(jnp.bfloat16)
    out[1] = dk.astype(jnp.bfloat16)
    out[2] = dv_sum[...].astype(jnp.bfloat16)
    gain_out[0, 0:1, :] = dq_gain
    gain_out[0, 1:2, :] = dk_gain


def attend(qkv, cos_part, sin_part, hot, q_gain, k_gain, bias_rows):
    tokens = qkv.shape[0]
    column = lambda shift: pl.BlockSpec((tokens, 128), lambda pair: (0, pair + shift))
    half = pl.BlockSpec((tokens // 2, 128), lambda pair: (0, pair))
    whole = pl.BlockSpec((tokens, 128), lambda pair: (0, 0))
    line = pl.BlockSpec((1, 128), lambda pair: (0, 0))
    low = lambda: jax.ShapeDtypeStruct((tokens, 256), jnp.bfloat16)
    return pl.pallas_call(
        attend_kernel,
        grid=(2,),
        in_specs=[
            column(0),
            column(2),
            column(4),
            whole,
            whole,
            whole,
            line,
            line,
            pl.BlockSpec((1, 2, 128), lambda pair: (pair, 0, 0)),
        ],
        out_specs=[
            half,
            half,
            column(0),
            column(0),
            column(0),
            pl.BlockSpec((2, tokens, 128), lambda pair: (pair, 0, 0)),
        ],
        out_shape=[
            jax.ShapeDtypeStruct((tokens // 2, 256), jnp.bfloat16),
            jax.ShapeDtypeStruct((tokens // 2, 256), jnp.bfloat16),
            low(),
            low(),
            low(),
            jax.ShapeDtypeStruct((4, tokens, 128), jnp.bfloat16),
        ],
        scratch_shapes=[
            pltpu.VMEM((tokens, 256), jnp.bfloat16),
            pltpu.VMEM((tokens, 256), jnp.bfloat16),
        ],
        compiler_params=pltpu.CompilerParams(vmem_limit_bytes=GRANT),
        name="attend",
    )(qkv, qkv, qkv, cos_part, sin_part, hot, q_gain, k_gain, bias_rows)


def attend_back(qkv, saved, hot, grads, attended, cos_part, sin_part, q_gain, k_gain):
    queries, keys, values, extra = saved
    tokens = qkv.shape[0]
    column = lambda shift: pl.BlockSpec((tokens, 128), lambda pair: (0, pair + shift))
    half = pl.BlockSpec((tokens // 2, 128), lambda pair: (0, pair))
    whole = pl.BlockSpec((tokens, 128), lambda pair: (0, 0))
    line = pl.BlockSpec((1, 128), lambda pair: (0, 0))
    two = pl.BlockSpec((1, 2, 128), lambda pair: (pair, 0, 0))
    wide = pltpu.VMEM((tokens, 256), jnp.bfloat16)
    both = pltpu.VMEM((2, tokens, 256), jnp.bfloat16)
    return pl.pallas_call(
        attend_back_kernel,
        grid=(2,),
        in_specs=[
            column(0),
            column(2),
            column(0),
            column(0),
            column(0),
            pl.BlockSpec((2, tokens, 128), lambda pair: (pair, 0, 0)),
            whole,
            half,
            half,
            half,
            half,
            whole,
            whole,
            line,
            line,
        ],
        out_specs=[pl.BlockSpec((3, tokens, 128), lambda pair: (0, 0, pair)), two, two],
        out_shape=[
            jax.ShapeDtypeStruct((3, tokens, 256), jnp.bfloat16),
            jax.ShapeDtypeStruct((2, 2, 128), jnp.float32),
            jax.ShapeDtypeStruct((2, 2, 128), jnp.float32),
        ],
        scratch_shapes=[
            wide,
            wide,
            pltpu.VMEM((128, tokens), jnp.bfloat16),
            both,
            both,
            both,
            pltpu.VMEM((128, tokens), jnp.float32),
            pltpu.VMEM((tokens, 128), jnp.float32),
            pltpu.VMEM((tokens, 128), jnp.float32),
        ],
        compiler_params=pltpu.CompilerParams(vmem_limit_bytes=GRANT),
        cost_estimate=pl.CostEstimate(
            flops=40 * tokens * tokens * 256,
            bytes_accessed=tokens * 256 * 40,
            transcendentals=4 * tokens * tokens,
        ),
        name="attend_back",
    )(
        qkv,
        qkv,
        queries,
        keys,
        values,
        extra,
        hot,
        *grads,
        *attended,
        cos_part,
        sin_part,
        q_gain,
        k_gain,
    )


def front_kernel(place, *refs):
    pieces, crossed, own, other = refs[:4], refs[4], refs[5:9], refs[9]
    weights_out, unit_out, qkv_out = refs[10:]
    dp_at, level, core = place[0], place[1], place[2]
    for at_dp in range(4):
        for at_level in range(4):
            base = ((dp_at ^ at_dp) * 4 + (level ^ at_level)) * 64
            mine = pl.ds(pl.multiple_of(base + core * 32, 32), 32)
            theirs = pl.ds(pl.multiple_of(base + (1 - core) * 32, 32), 32)
            rows = slice(at_level * 32, at_level * 32 + 32)
            for part in range(3):
                lanes = pl.ds(pl.multiple_of(part * 512 + core * 256, 256), 256)
                weights_out[mine, part * 256 : (part + 1) * 256] = pieces[at_dp][rows, lanes]
            weights_out[theirs, :] = crossed[at_dp * 128 + at_level * 32 :][:32, :]

    def norm(values):
        wide = values.astype(jnp.float32)
        return (wide * rms_scale(wide)).astype(jnp.bfloat16)

    for at in range(4):
        unit_out[at * 128 : (at + 1) * 128, :] = norm(own[at][...])
        unit_out[512 + at * 128 : 512 + (at + 1) * 128, :] = norm(other[at])
    for at in range(2):
        rows = slice(at * 512, (at + 1) * 512)
        qkv_out[rows, :] = jnp.dot(
            unit_out[rows, :], weights_out[...], preferred_element_type=jnp.float32
        )


def front(place, pieces, crossed, own, other):
    tokens = 2 * other.shape[0] * other.shape[1]
    quarter = pl.BlockSpec((128, 1536), lambda at: (0, 0))
    piece = pl.BlockSpec((128, D), lambda at: (0, 0))
    return pl.pallas_call(
        front_kernel,
        grid=(1,),
        in_specs=[pl.BlockSpec(memory_space=pltpu.SMEM)]
        + [quarter] * 4
        + [pl.BlockSpec((512, 768), lambda at: (0, 0))]
        + [piece] * 4
        + [pl.BlockSpec((4, 128, D), lambda at: (0, 0, 0))],
        out_specs=[
            pl.BlockSpec((D, 768), lambda at: (0, 0)),
            pl.BlockSpec((tokens, D), lambda at: (0, 0)),
            pl.BlockSpec((tokens, 768), lambda at: (0, 0)),
        ],
        out_shape=[
            jax.ShapeDtypeStruct((D, 768), jnp.bfloat16),
            jax.ShapeDtypeStruct((tokens, D), jnp.bfloat16),
            jax.ShapeDtypeStruct((tokens, 768), jnp.float32),
        ],
        compiler_params=pltpu.CompilerParams(vmem_limit_bytes=GRANT),
        name="front",
    )(place, *pieces, crossed, *own, other)


def tail_kernel(
    place, dqkv, weights, unit, gains, biases, ffn_gain, back_kept, back_sent, kept, sent, part, small
):
    core, group = place[2], place[3]
    tokens = unit.shape[0]

    def back(rows):
        total = contract_last(dqkv[0, rows, :], weights[:, :256])
        for at in (1, 2):
            total += contract_last(dqkv[at, rows, :], weights[:, at * 256 : (at + 1) * 256])
        return total

    back_kept[...] = back(slice(0, tokens // 2))
    back_sent[...] = back(slice(tokens // 2, tokens)).astype(jnp.bfloat16)
    for at in range(3):
        part[:, at * 256 : (at + 1) * 256] = rows_inner(unit[...], dqkv[at]).astype(jnp.bfloat16)
    for at in range(16):
        rows = slice(at * 32, at * 32 + 32)
        kept[rows, :] = part[pl.ds(pl.multiple_of(at * 64 + core * 32, 32), 32), :]
        sent[rows, :] = part[pl.ds(pl.multiple_of(at * 64 + (1 - core) * 32, 32), 32), :]
    lane = lax.broadcasted_iota(jnp.int32, (1, 128), 1)
    sums = gains[0] + gains[1]
    sums = sums + pltpu.roll(sums, HD, 1)
    placed = jnp.zeros((1, 128), jnp.float32)
    for head in range(4):
        line = biases[head // 2, head % 2 : head % 2 + 1, :]
        same = jnp.sum(jnp.where(lane < 8, line, 0.0), axis=1, keepdims=True)
        total = jnp.sum(jnp.where(lane == LSE_LANE, line, 0.0), axis=1, keepdims=True)
        spot = group * 4 + head
        placed = jnp.where(lane == spot, same, placed)
        placed = jnp.where(lane == spot + H, total - same, placed)
    small[...] = jnp.zeros(small.shape, jnp.float32)
    for at in range(4):
        small[at : at + 1, :256] = ffn_gain[:, at * 256 : (at + 1) * 256]
    small[4:5, :128] = jnp.where(lane < HD, sums[0:1], sums[1:2])
    small[4:5, 128:256] = placed
    kept[512:, :] = small[...].astype(jnp.bfloat16)
    sent[512:, :] = small[...].astype(jnp.bfloat16)


def tail(place, dqkv, weights, unit, gains, biases, ffn_gain):
    tokens = unit.shape[0]
    whole = lambda shape: pl.BlockSpec(shape, lambda at: (0,) * len(shape))
    shapes = [
        ((tokens // 2, D), jnp.float32),
        ((tokens // 2, D), jnp.bfloat16),
        ((528, 768), jnp.bfloat16),
        ((528, 768), jnp.bfloat16),
    ]
    arguments = (dqkv, weights, unit, gains, biases, ffn_gain)
    return pl.pallas_call(
        tail_kernel,
        grid=(1,),
        in_specs=[pl.BlockSpec(memory_space=pltpu.SMEM)]
        + [whole(member.shape) for member in arguments],
        out_specs=[whole(shape) for shape, _ in shapes],
        out_shape=[jax.ShapeDtypeStruct(shape, kind) for shape, kind in shapes],
        scratch_shapes=[pltpu.VMEM((D, 768), jnp.bfloat16), pltpu.VMEM((16, 768), jnp.float32)],
        compiler_params=pltpu.CompilerParams(vmem_limit_bytes=GRANT),
        cost_estimate=pl.CostEstimate(
            flops=4 * tokens * D * 768, bytes_accessed=14 * D * D, transcendentals=0
        ),
        name="tail",
    )(place, *arguments)


def finish_kernel(place, mine, near, side, far, gain, *refs):
    weights = refs[:3]
    kept, back_near, passed, inputs, upstream = refs[3:8]
    middle, down_kept, down_near, down_side, down_far = refs[8:13]
    grads_out = refs[13:16]
    out_out, input_out, result_out, gain_out, q_out, k_out, bias_out, two_out = refs[16:24]
    wide = jnp.float32
    dp_at, level, core = place[0], place[1], place[2]
    parity, batch = level & 1, level >> 1
    step = pl.program_id(0)

    @pl.when(step == 0)
    def _():
        scale = gain[...].astype(jnp.bfloat16).astype(wide)
        for at in range(3):
            for side_core in range(2):
                rows = slice(at * 64 + side_core * 32, at * 64 + side_core * 32 + 32)
                same = mine[rows, :].astype(wide) + side[rows, :].astype(wide)
                cross = near[rows, :].astype(wide) + far[rows, :].astype(wide)
                for turn, member in ((parity, same), (1 - parity, cross)):
                    lane = (turn * 2 + (core + side_core) % 2) * 256
                    grads_out[at][:, pl.ds(pl.multiple_of(lane, 256), 256)] = member
        total = jnp.zeros((32, 1), wide)
        for at in range(3):
            unscaled = grads_out[at][...]
            total += jnp.sum(
                unscaled * weights[at][...].astype(jnp.bfloat16).astype(wide), axis=1, keepdims=True
            )
            grads_out[at][...] = unscaled * scale
        rows = lax.broadcasted_iota(jnp.int32, (32, 32), 0)
        columns = lax.broadcasted_iota(jnp.int32, (32, 32), 1)
        gain_out[...] = jnp.sum(jnp.where(rows == columns, total, 0.0), axis=0, keepdims=True)

        def summed(rows):
            return (mine[rows, :].astype(wide) + near[rows, :].astype(wide)) + (
                side[rows, :].astype(wide) + far[rows, :].astype(wide)
            )

        for at in range(4):
            out_out[:, at * 256 : (at + 1) * 256] = summed(slice(192 + at * 32, 224 + at * 32))
        small = summed(slice(320, 336))
        q_out[...] = small[4:5, :HD]
        k_out[...] = small[4:5, HD : 2 * HD]
        bias_out[0:1, :] = small[4:5, 2 * HD : 2 * HD + H]
        bias_out[1:2, :] = small[4:5, 2 * HD + H : 2 * HD + 2 * H]
        two = jnp.zeros((1, 32), wide)
        for at_dp in range(4):
            for at_seq in range(8):
                here = (dp_at == at_dp) & (level * 2 + core == at_seq)
                two = jnp.where(here, small[at_dp : at_dp + 1, at_seq * 32 : at_seq * 32 + 32], two)
        two_out[...] = two
    result_out[...] = (
        middle[...]
        + (
            (down_kept[...] + down_near[...].astype(wide))
            + (down_side[...].astype(wide) + down_far[...].astype(wide))
        )
    ).astype(jnp.bfloat16)
    back = jnp.where(
        step == batch, kept[...] + back_near[...].astype(wide), passed[...].astype(wide)
    )
    values = inputs[0].astype(wide)
    inv = rms_scale(values)
    inner = jnp.mean(back * values, axis=-1, keepdims=True)
    input_out[0] = (
        upstream[0] + inv * back - values * (inv * inv * inv) * inner
    ).astype(jnp.bfloat16)


def finish(place, mine, moved, gain, weights, backs, inputs, upstream, outputs):
    whole = lambda shape: pl.BlockSpec(shape, lambda at: (0,) * len(shape))
    arguments = [mine, *moved, gain, *weights, *backs, inputs, upstream, *outputs]
    f32 = jnp.float32
    shapes = [((32, D), f32)] * 4 + [(inputs.shape, jnp.bfloat16)]
    shapes += [(outputs[0].shape, jnp.bfloat16)]
    shapes += [((1, 32), f32), ((1, HD), f32), ((1, HD), f32), ((2, H), f32), ((1, 32), f32)]
    rows, piece = inputs.shape[0] * inputs.shape[1], inputs.shape[1]
    batch_block = pl.BlockSpec((1, piece, D), lambda at: (at, 0, 0))
    row_block = pl.BlockSpec((piece, D), lambda at: (at, 0))

    def spec(shape):
        return {inputs.shape: batch_block, (rows, D): row_block}.get(tuple(shape), whole(shape))

    return pl.pallas_call(
        finish_kernel,
        grid=(2,),
        in_specs=[pl.BlockSpec(memory_space=pltpu.SMEM)]
        + [spec(member.shape) for member in arguments],
        out_specs=[spec(shape) for shape, _ in shapes],
        out_shape=[jax.ShapeDtypeStruct(shape, kind) for shape, kind in shapes],
        compiler_params=pltpu.CompilerParams(vmem_limit_bytes=GRANT),
        name="finish",
    )(place, *arguments)


def lower_kernel(gate, up, down, out):
    out[0] = gate[...].astype(jnp.bfloat16)
    out[1] = up[...].astype(jnp.bfloat16)
    out[2] = down[...].astype(jnp.bfloat16)


def lower(gate, up, down):
    whole = pl.BlockSpec(gate.shape, lambda at: (0, 0))
    return pl.pallas_call(
        lower_kernel,
        grid=(1,),
        in_specs=[whole] * 3,
        out_specs=pl.BlockSpec((3,) + gate.shape, lambda at: (0, 0, 0)),
        out_shape=jax.ShapeDtypeStruct((3,) + gate.shape, jnp.bfloat16),
        compiler_params=pltpu.CompilerParams(vmem_limit_bytes=GRANT),
        name="lower",
    )(gate, up, down)


def middle_back_kernel(
    kept, near, side, far, dy_in, middle_in, gain_in, weights, grad_out, low_out, att_out, sums_out
):
    wide = jnp.float32
    upstream = (kept[...] + near[...].astype(wide)) + (
        side[...].astype(wide) + far[...].astype(wide)
    )
    middle = middle_in[...]
    inv = rms_scale(middle)
    sums_out[...] = jnp.sum(upstream * middle * inv, axis=0, keepdims=True)
    grad = dy_in[...].astype(wide) + norm_back(middle, inv, gain_in[...], upstream)
    grad_out[...] = grad
    grad_low = grad.astype(jnp.bfloat16)
    low_out[...] = grad_low
    att_out[...] = contract_last(grad_low, weights[...]).astype(jnp.bfloat16)


def middle_back(kept, moved, own_dy, middle, gain_two, w_out):
    rows = kept.shape[0]
    block = pl.BlockSpec((rows, D), lambda at: (0, 0))
    line = pl.BlockSpec((1, D), lambda at: (0, 0))
    return pl.pallas_call(
        middle_back_kernel,
        grid=(1,),
        in_specs=[block] * 6 + [line, pl.BlockSpec((D, D), lambda at: (0, 0))],
        out_specs=[block, block, block, line],
        out_shape=[
            jax.ShapeDtypeStruct((rows, D), jnp.float32),
            jax.ShapeDtypeStruct((rows, D), jnp.bfloat16),
            jax.ShapeDtypeStruct((rows, D), jnp.bfloat16),
            jax.ShapeDtypeStruct((1, D), jnp.float32),
        ],
        compiler_params=pltpu.CompilerParams(vmem_limit_bytes=GRANT),
        cost_estimate=pl.CostEstimate(
            flops=2 * rows * D * D, bytes_accessed=22 * rows * D + 2 * D * D, transcendentals=rows
        ),
        name="middle_back",
    )(kept, *moved, own_dy, middle, gain_two, w_out)


GATED = 512
HIDDEN = 256


def load_weights(place, sources, gathered, arrived, which=None):
    level, core = place[1], place[2]
    pieces = [(sources[at], at, core) for at in range(4)]
    pieces += [(sources[4].at[at], at, 1 - core) for at in range(3)]
    pieces += [(sources[5], 3, 1 - core)]
    copies = []
    for at, (source, turn, side) in enumerate(pieces):
        rows = pl.ds(pl.multiple_of(((level ^ turn) * 2 + side) * 128, 128), 128)
        if which is None:
            target = gathered.at[:, rows, :]
        else:
            source, target = source.at[which], gathered.at[rows, :]
        copies.append(pltpu.make_async_copy(source, target, arrived.at[at]))
    for copy in copies:
        copy.start()
    return copies


def gated_kernel(count, place, *refs):
    tokens_in, grads_in, sources = refs[:count], refs[count : 2 * count], refs[2 * count :][:6]
    refs = refs[2 * count + 6 :]
    hidden_out, back_out, totals = refs[:count], refs[count : 2 * count], refs[2 * count :][:count]
    weights, arrived = refs[3 * count :]
    for copy in load_weights(place, sources, weights, arrived):
        copy.wait()

    def half(step, carry):
        units = pl.ds(pl.multiple_of(step * GATED, GATED), GATED)
        pair = jnp.concatenate([weights[0, units, :], weights[1, units, :]])
        third = weights[2, units, :]
        for at in range(count):
            both = contract_last(tokens_in[at][...], pair)
            gate, up = both[:, :GATED], both[:, GATED:]
            grad_hidden = contract_last(grads_in[at][0], third)
            sig = lax.logistic(gate)
            swished = gate * sig
            hidden_out[at][2, :, units] = (swished * up).astype(jnp.bfloat16)
            grad_gate = (grad_hidden * up * sig * (1.0 + gate * (1.0 - sig))).astype(jnp.bfloat16)
            grad_up = (grad_hidden * swished).astype(jnp.bfloat16)
            hidden_out[at][0, :, units] = grad_gate
            hidden_out[at][1, :, units] = grad_up
            added = jnp.dot(
                jnp.concatenate([grad_gate, grad_up], axis=1),
                pair,
                preferred_element_type=jnp.float32,
            )
            total = totals[at]

            @pl.when(step == 0)
            def _():
                total[...] = added

            @pl.when(step == 1)
            def _():
                back_out[at][...] = (total[...] + added).astype(back_out[at].dtype)

        return carry

    lax.fori_loop(0, 2, half, 0)


def dp_block(mask, chunk):
    return pl.BlockSpec((1, chunk, D), lambda at, place: (place[0] ^ mask, 0, 0))


def gated(place, tokens_in, grads_all, masks, weights, kinds):
    count = len(tokens_in)
    chunk = tokens_in[0].shape[0]
    hidden = 8 * weights[0].shape[1]
    assert hidden == 2 * GATED
    whole = pl.BlockSpec((chunk, D), lambda at, place: (0, 0))
    anywhere = pl.BlockSpec(memory_space=pl.ANY)
    results = pl.pallas_call(
        functools.partial(gated_kernel, count),
        grid_spec=pltpu.PrefetchScalarGridSpec(
            num_scalar_prefetch=1,
            grid=(1,),
            in_specs=[whole] * count
            + [dp_block(mask, chunk) for mask in masks]
            + [anywhere] * len(weights),
            out_specs=[pl.BlockSpec((3, chunk, hidden), lambda at, place: (0, 0, 0))] * count
            + [whole] * count,
            scratch_shapes=[pltpu.VMEM((chunk, D), jnp.float32)] * count
            + [pltpu.VMEM((3, hidden, D), jnp.bfloat16), pltpu.SemaphoreType.DMA((8,))],
        ),
        out_shape=[jax.ShapeDtypeStruct((3, chunk, hidden), jnp.bfloat16)] * count
        + [jax.ShapeDtypeStruct((chunk, D), kind) for kind in kinds],
        compiler_params=pltpu.CompilerParams(vmem_limit_bytes=GRANT),
        cost_estimate=pl.CostEstimate(
            flops=10 * count * chunk * D * hidden,
            bytes_accessed=2 * D * (7 * count * chunk + 3 * hidden),
            transcendentals=count * chunk * hidden,
        ),
        name="gated",
    )(place, *tokens_in, *[grads_all] * count, *weights)
    return list(zip(results[:count], results[count:]))


def ffn_grads_kernel(place, *refs):
    tokens_in, grads_in, hidden_in = refs[0:4], refs[4:8], refs[8:12]
    grads_out, tokens_all, grads_all, hidden = refs[12:]
    chunk = tokens_in[0].shape[0]
    rows_of = [slice(at * chunk, (at + 1) * chunk) for at in range(4)]

    @pl.when(pl.program_id(0) == 0)
    def _():
        for at in range(4):
            tokens_all[rows_of[at], :] = tokens_in[at][...]
            grads_all[rows_of[at], :] = grads_in[at][0]

    for which in range(3):
        for at in range(4):
            hidden[which, rows_of[at], :] = hidden_in[at][which]
        other = tokens_all if which < 2 else grads_all
        grads_out[which] = rows_inner(hidden[which], other[...]).astype(jnp.bfloat16)


def ffn_grads(place, tokens_in, grads_in, hidden_in):
    chunk = tokens_in[0].shape[0]
    tokens = 4 * chunk
    hidden = hidden_in[0].shape[2]
    whole = pl.BlockSpec((chunk, D), lambda at, place: (0, 0))
    wide_low = pltpu.VMEM((tokens, D), jnp.bfloat16)
    return pl.pallas_call(
        ffn_grads_kernel,
        grid_spec=pltpu.PrefetchScalarGridSpec(
            num_scalar_prefetch=1,
            grid=(hidden // HIDDEN,),
            in_specs=[whole] * 4
            + [dp_block(mask, chunk) for mask in range(4)]
            + [pl.BlockSpec((3, chunk, HIDDEN), lambda at, place: (0, 0, at))] * 4,
            out_specs=pl.BlockSpec((3, HIDDEN, D), lambda at, place: (0, at, 0)),
            scratch_shapes=[wide_low, wide_low, pltpu.VMEM((3, tokens, HIDDEN), jnp.bfloat16)],
        ),
        out_shape=jax.ShapeDtypeStruct((3, hidden, D), jnp.bfloat16),
        compiler_params=pltpu.CompilerParams(vmem_limit_bytes=GRANT),
        cost_estimate=pl.CostEstimate(
            flops=6 * tokens * D * hidden,
            bytes_accessed=2 * D * (4 * tokens + 6 * hidden),
            transcendentals=0,
        ),
        name="ffn_grads",
    )(place, *tokens_in, *[grads_in] * 4, *hidden_in)


def down_kernel(place, *refs):
    hidden_in, attended, grads, sources = refs[:4], refs[4], refs[5], refs[6:12]
    outs, kept, sent, part, weights, arrived = refs[12:16], *refs[16:]
    core = place[2]
    copies = load_weights(place, sources, weights, arrived, 2)
    part[...] = rows_inner(attended[...], grads[...]).astype(jnp.bfloat16)
    for at in range(16):
        rows = slice(at * 32, at * 32 + 32)
        kept[rows, :] = part[pl.ds(pl.multiple_of(at * 64 + core * 32, 32), 32), :]
        sent[rows, :] = part[pl.ds(pl.multiple_of(at * 64 + (1 - core) * 32, 32), 32), :]
    for copy in copies:
        copy.wait()
    for at in range(4):
        outs[at][...] = jnp.dot(
            hidden_in[at][0], weights[...], preferred_element_type=jnp.float32
        ).astype(outs[at].dtype)


def down(place, hidden_in, weights, attended, grads):
    chunk = hidden_in[0].shape[1]
    hidden = hidden_in[0].shape[2]
    half = D // 2
    whole = pl.BlockSpec((chunk, D), lambda at, place: (0, 0))
    tall = pl.BlockSpec((half, D), lambda at, place: (0, 0))
    return pl.pallas_call(
        down_kernel,
        grid_spec=pltpu.PrefetchScalarGridSpec(
            num_scalar_prefetch=1,
            grid=(1,),
            in_specs=[pl.BlockSpec((1, chunk, hidden), lambda at, place: (2, 0, 0))] * 4
            + [whole] * 2
            + [pl.BlockSpec(memory_space=pl.ANY)] * len(weights),
            out_specs=[whole] * 4 + [tall] * 2,
            scratch_shapes=[
                pltpu.VMEM((D, D), jnp.bfloat16),
                pltpu.VMEM((hidden, D), jnp.bfloat16),
                pltpu.SemaphoreType.DMA((8,)),
            ],
        ),
        out_shape=[jax.ShapeDtypeStruct((chunk, D), jnp.float32)]
        + [jax.ShapeDtypeStruct((chunk, D), jnp.bfloat16)] * 3
        + [jax.ShapeDtypeStruct((half, D), jnp.bfloat16)] * 2,
        compiler_params=pltpu.CompilerParams(vmem_limit_bytes=GRANT),
        cost_estimate=pl.CostEstimate(
            flops=10 * chunk * D * hidden,
            bytes_accessed=2 * D * (11 * chunk + 2 * hidden),
            transcendentals=0,
        ),
        name="down",
    )(place, *hidden_in, attended, grads, *weights)


def local_split(
    inputs,
    variate_ids,
    time_ids,
    attn_gain,
    query_weight,
    key_weight,
    value_weight,
    out_weight,
    query_gain,
    key_gain,
    variate_bias,
    ffn_gain,
    gate_weight,
    up_weight,
    down_weight,
    out_grad,
):
    low = jnp.bfloat16
    wide = jnp.float32
    dp_at = lax.axis_index("dp")
    seq_at = lax.axis_index("seq")
    core = seq_at & 1
    level = seq_at >> 1
    batch = level >> 1
    parity = level & 1
    piece = inputs.shape[2]
    tokens = 8 * piece
    others = (1, 2, 3)
    swap_core = lambda values: swap_seq(values, 1)
    swap_level = lambda values, mask: swap_seq(values, 2 * mask)

    own_dy = out_grad[:, 0].reshape(2 * piece, D)

    gain_low = attn_gain.astype(low).astype(wide)
    weights_low = jnp.stack([query_weight, key_weight, value_weight], axis=1).astype(low)
    scaled = (weights_low.astype(wide) * gain_low[:, None, None]).astype(low)
    scaled = scaled.reshape(32, 3, 2, 512)
    with_gain = jnp.concatenate(
        [out_weight.astype(low), jnp.pad(ffn_gain.astype(low)[:, None], ((0, 0), (0, 127)))], axis=1
    )
    w_out = lax.all_gather(with_gain, ("dp", "seq"), axis=0, tiled=True)
    kinds = variate_ids[:, 0]
    times = time_ids[:, 0]
    ids = jnp.stack([kinds, times // 64, times % 64], axis=1).astype(low)
    ids = jnp.concatenate([ids, swap_core(ids)], axis=1)
    ids = jnp.pad(ids, ((0, 0), (0, 26), (0, 0)))

    def with_ids(weights_part, which):
        return jnp.concatenate(
            [weights_part.reshape(32, 1536), at_index(ids, which)], axis=1
        )

    same = with_ids(at_index(scaled, parity, 2), 1 - batch)
    cross_near = with_ids(at_index(scaled, 1 - parity, 2), batch)
    cross_far = with_ids(at_index(scaled, 1 - parity, 2), 1 - batch)
    moved = [swap_level((cross_near, same, cross_far)[mask - 1], mask) for mask in others]
    own_x = inputs[:, 0]
    near, far = at_index(own_x, batch), at_index(own_x, 1 - batch)
    (
        same,
        near,
        far,
        gate_local,
        up_local,
        down_local,
        query_gain,
        key_gain,
        variate_bias,
        *moved,
    ) = together(
        same,
        near,
        far,
        gate_weight,
        up_weight,
        down_weight,
        query_gain,
        key_gain,
        variate_bias,
        *moved,
    )
    ffn_local = lower(gate_local, up_local, down_local)

    place = jnp.stack([dp_at, level, core, 2 * parity + core]).astype(jnp.int32)
    rows = jnp.concatenate([same[:, :1536]] + [member[:, :1536] for member in moved])
    ids = jnp.stack([at_index(ids, batch)] + [member[:, 1536:] for member in moved])
    moved = [swap_dp(rows, mask) for mask in others]
    from_far = swap_level(far, 2)
    from_near = swap_level(near, 1)
    last = swap_level(from_far, 1)
    ids = jnp.stack([ids[:, :3], ids[:, 3:6]]).astype(wide)

    kinds = ids[:, :, 0].reshape(tokens, 1)
    times = (ids[:, :, 1] * 64.0 + ids[:, :, 2]).reshape(tokens, 1)
    lane = lax.broadcasted_iota(jnp.int32, (1, 128), 1)
    hot = jnp.where(
        lane < LSE_LANE, (kinds == lane % 8).astype(wide), jnp.where(lane < LSE_LANE + 3, 1.0, 0.0)
    ).astype(low)
    half = HD // 2
    frequency = 10000.0 ** (-(lane % half).astype(wide) / half)
    angles = times * frequency
    cos_part = jnp.cos(angles)
    sin_part = jnp.sin(angles) * jnp.where(lane % HD < half, -1.0, 1.0)
    q_gain = jnp.tile(query_gain, 2)[None, :]
    k_gain = jnp.tile(key_gain, 2)[None, :]
    group = 2 * parity + core
    gaps = at_index((variate_bias[0] - variate_bias[1]).reshape(4, 4), group)
    first, second, third = three_parts(gaps)
    bias_rows = jnp.where(
        lane < 8,
        first[:, None],
        jnp.where(
            lane < 16, second[:, None], jnp.where(lane < LSE_LANE, third[:, None], 0.0)
        ),
    ).reshape(2, 2, 128)

    (
        rows,
        ffn_local,
        near,
        from_near,
        from_far,
        last,
        cos_part,
        sin_part,
        dy_sent,
        hot,
        q_gain,
        k_gain,
        bias_rows,
        place,
        *moved,
    ) = together(
        rows,
        ffn_local,
        near,
        from_near,
        from_far,
        last,
        cos_part,
        sin_part,
        own_dy,
        hot,
        q_gain,
        k_gain,
        bias_rows,
        place,
        *moved,
    )

    dy_all = lax.all_gather(dy_sent, "dp", axis=0)

    pieces = [rows] + moved
    own = [near, from_near, from_far, last]
    ffn_near, ffn_far = swap_level(ffn_local, 1), swap_level(ffn_local, 2)
    sent = jnp.concatenate(
        [
            jnp.concatenate(
                [
                    jnp.where(
                        core == 0,
                        member[:, at * 512 + 256 : at * 512 + 512],
                        member[:, at * 512 : at * 512 + 256],
                    )
                    for at in range(3)
                ],
                axis=1,
            )
            for member in pieces
        ]
    )
    crossed, rows_crossed = together(swap_core(jnp.stack(own)), swap_core(sent))

    w_qkv, unit, qkv = front(place, pieces, rows_crossed, own, crossed)
    att_near, att_far, *saved = attend(qkv, cos_part, sin_part, hot, q_gain, k_gain, bias_rows)
    attended = (att_near, att_far)
    att_near, att_far = together(att_near, att_far)

    part, crossed = together(att_near, swap_core(att_far))
    part, crossed = part.reshape(4, piece, 256), crossed.reshape(4, piece, 256)
    both = jnp.concatenate(
        [jnp.where(core == 0, part, crossed), jnp.where(core == 0, crossed, part)], axis=2
    )

    w_out, ffn_near, ffn_far, *arrived = together(
        w_out,
        ffn_near,
        ffn_far,
        both[0],
        *[swap_level(both[mask], mask) for mask in others],
    )
    gain_two = w_out[:, D].astype(wide)[None, :]
    blocks = [pick(arrived, level ^ at) for at in range(4)]
    own_att = jnp.concatenate(
        [
            jnp.concatenate([blocks[0], blocks[1]], axis=1),
            jnp.concatenate([blocks[2], blocks[3]], axis=1),
        ]
    )

    own_wide = own_x.reshape(2 * piece, D).astype(wide)
    middle = own_wide + product(own_att, w_out[:, :D])
    inv_two = rms_scale(middle)
    normed_two = (middle * inv_two * gain_two).astype(low)

    ffn_last, ffn_crossed, near_two, side_two, own_two, middle, own_att, gain_two, dy_all = together(
        swap_level(ffn_far, 1),
        swap_core(jnp.stack([ffn_local, ffn_near, ffn_far])),
        swap_dp(normed_two, 1),
        swap_dp(normed_two, 2),
        normed_two,
        middle,
        own_att,
        gain_two,
        dy_all,
    )

    far_two = swap_dp(own_two, 3)
    w_ffn = [ffn_local, ffn_near, ffn_far, ffn_last, ffn_crossed, swap_core(ffn_last)]
    (near_hidden, near_back), (side_hidden, side_back) = gated(
        place, [near_two, side_two], dy_all, (1, 2), w_ffn, (low, low)
    )
    far_two, near_hidden, near_back, side_hidden, side_back = together(
        far_two, near_hidden, near_back, side_hidden, side_back
    )

    near_back, side_back = swap_dp(near_back, 1), swap_dp(side_back, 2)
    (own_hidden, kept), (far_hidden, far_back) = gated(
        place, [own_two, far_two], dy_all, (0, 3), w_ffn, (wide, low)
    )
    own_hidden, kept, far_hidden, far_back, near_back, side_back = together(
        own_hidden, kept, far_hidden, far_back, near_back, side_back
    )
    hidden = [own_hidden, near_hidden, side_hidden, far_hidden]
    ffn_part = ffn_grads(place, [own_two, near_two, side_two, far_two], dy_all, hidden)
    ffn_part, kept, *moved = together(
        ffn_part, kept, near_back, side_back, swap_dp(far_back, 3)
    )
    ffn_shard = lax.psum_scatter(ffn_part, "seq", scatter_dimension=1, tiled=True)
    grad_middle, middle_low, grad_att, gain_two_part = middle_back(
        kept, moved, own_dy, middle, gain_two, w_out
    )

    blocks = [
        grad_att[at // 2 * piece : (at // 2 + 1) * piece, at % 2 * 512 : (at % 2 + 1) * 512]
        for at in range(4)
    ]
    arrived = [pick(blocks, level)]
    arrived += [swap_level(pick(blocks, level ^ mask), mask) for mask in others]
    down_kept, *rest = down(place, hidden, w_ffn, own_att, middle_low)
    down_chunks, out_kept, out_sent = rest[:3], rest[3], rest[4]
    out_kept, out_sent, down_kept, *rest = together(
        out_kept, out_sent, down_kept, *down_chunks, *arrived
    )
    down_chunks, arrived = rest[:3], rest[3:]

    halves = [
        jnp.concatenate([member[:, :256] for member in arrived]),
        jnp.concatenate([member[:, 256:] for member in arrived]),
    ]

    def out_rows(to):
        rows = [
            lax.dynamic_slice_in_dim(member, to * 128, 128).astype(wide)
            for member in (out_kept, out_crossed)
        ]
        return (rows[0] + rows[1]).astype(low)

    kept, crossed, out_kept, out_crossed, *down_chunks = together(
        pick(halves, core),
        swap_core(pick(halves, 1 - core)),
        out_kept,
        swap_core(out_sent),
        *down_chunks,
    )
    out_parts = [out_rows(dp_at ^ mask) for mask in range(4)]
    grads = (kept, crossed)

    out_moved = [swap_dp(out_parts[mask], mask) for mask in others]
    dqkv, gain_sums, bias_sums = attend_back(
        qkv, saved, hot, grads, attended, cos_part, sin_part, q_gain, k_gain
    )
    dqkv, out_kept, last_chunk, *rest = together(
        dqkv,
        out_parts[0],
        down_chunks[2],
        swap_dp(down_chunks[0], 1),
        swap_dp(down_chunks[1], 2),
        *out_moved,
    )
    down_moved, out_moved = rest[:2], rest[2:]

    out_moved = [member.astype(wide) for member in out_moved]
    out_sum = (out_kept.astype(wide) + out_moved[0]) + (out_moved[1] + out_moved[2])
    back_kept, back_sent, kept, sent = tail(
        place, dqkv, w_qkv, unit, gain_sums, bias_sums, gain_two_part
    )
    back_kept, back_crossed, kept, crossed = together(
        back_kept, swap_core(back_sent), kept, swap_core(sent)
    )

    back = (back_kept + back_crossed.astype(wide)).reshape(4, piece, D)
    small_low = (kept[512:].astype(wide) + crossed[512:].astype(wide)).astype(low)

    def dp_message(to):
        return jnp.concatenate(
            [
                lax.dynamic_slice_in_dim(kept, to * 128, 128),
                lax.dynamic_slice_in_dim(crossed, to * 128, 128),
                small_low,
            ]
        )

    moved = [swap_dp(dp_message(dp_at ^ mask), mask) for mask in others]
    near = swap_level(jnp.stack([back[1], back[3]]).astype(low), 1)
    qkv_kept, kept, passed, near, ffn_shard, last_chunk, *moved = together(
        dp_message(dp_at), back[0], back[2], near, ffn_shard, last_chunk, *moved
    )

    moved = [member.astype(wide) for member in moved]
    total = qkv_kept.astype(wide)
    total = ((total + moved[0]) + (moved[1] + moved[2])).astype(low)
    small_low = total[256:]

    out_sum = out_sum.reshape(4, 32, D)
    ffn_sums = ffn_shard.astype(wide)

    def level_message(to):
        out_block = at_index(out_sum, to).astype(low)
        qkv_block = jnp.concatenate(
            [
                lax.dynamic_slice_in_dim(total, to * 32, 32),
                lax.dynamic_slice_in_dim(total, 128 + to * 32, 32),
            ]
        )
        return jnp.concatenate(
            [qkv_block[:, at * 256 : (at + 1) * 256] for at in range(3)]
            + [out_block[:, at * 256 : (at + 1) * 256] for at in range(4)]
            + [small_low[:, :256]]
        )

    passed = swap_level((passed + near[1].astype(wide)).astype(low), 2)
    mine, kept, near, passed, ffn_sums, last_chunk, *moved = together(
        level_message(level),
        kept,
        near[0],
        passed,
        ffn_sums,
        swap_dp(last_chunk, 3),
        *[swap_level(level_message(level ^ mask), mask) for mask in others],
    )
    *sums, input_grad, result, gain_grad, q_grad, k_grad, bias_grad, gain_two_grad = finish(
        place,
        mine,
        moved,
        attn_gain[:, None],
        [query_weight, key_weight, value_weight],
        [kept, near, passed],
        own_x,
        grad_middle.reshape(2, piece, D),
        [middle, down_kept] + down_moved + [last_chunk],
    )

    shape = (2, 1, piece, D)
    return (
        result.reshape(shape),
        input_grad.reshape(shape),
        gain_grad.reshape(32),
        sums[0],
        sums[1],
        sums[2],
        sums[3],
        q_grad.reshape(HD),
        k_grad.reshape(HD),
        bias_grad,
        gain_two_grad.reshape(32),
        ffn_sums[0],
        ffn_sums[1],
        ffn_sums[2],
    )


def solution(mesh):
    placed = (
        P(None, "dp", "seq", None),
        P(None, "dp", "seq"),
        P(None, "dp", "seq"),
        P(("dp", "seq")),
        P(("dp", "seq"), None),
        P(("dp", "seq"), None),
        P(("dp", "seq"), None),
        P(("dp", "seq"), None),
        P(),
        P(),
        P(),
        P(("dp", "seq")),
        P(("dp", "seq"), None),
        P(("dp", "seq"), None),
        P(("dp", "seq"), None),
        P(None, "dp", "seq", None),
    )
    split = mesh.shape["dp"] == 4 and mesh.shape["seq"] == 8
    return jax.shard_map(
        local_split if split else local,
        mesh=mesh,
        in_specs=placed,
        out_specs=(
            P(None, "dp", "seq", None),
            P(None, "dp", "seq", None),
            P(("dp", "seq")),
            P(("dp", "seq"), None),
            P(("dp", "seq"), None),
            P(("dp", "seq"), None),
            P(("dp", "seq"), None),
            P(),
            P(),
            P(),
            P(("dp", "seq")),
            P(("dp", "seq"), None),
            P(("dp", "seq"), None),
            P(("dp", "seq"), None),
        ),
        check_vma=False,
    )
```

```python
import functools
import math

import jax
import jax.numpy as jnp
from jax import lax
from jax.experimental import pallas as pl
from jax.experimental.pallas import tpu as pltpu
from jax.sharding import PartitionSpec as P

D = 1024
H = 16
HD = 64
FF = 4096


epsilon = 1e-06
lowest = -1e30


def rms_scale(values):
    return lax.rsqrt(jnp.mean(values * values, axis=-1, keepdims=True) + epsilon)


def norm_back(values, inv_rms, gain_vec, upstream):
    weighted = upstream * gain_vec
    inner_mean = jnp.mean(weighted * values, axis=-1, keepdims=True)
    return inv_rms * weighted - values * (inv_rms * inv_rms * inv_rms) * inner_mean


def rotation(positions):
    half_dim = HD // 2
    frequency = 10000.0 ** (-jnp.arange(half_dim).astype(jnp.float32) / half_dim)
    angles = positions.astype(jnp.float32)[..., None] * frequency
    return (jnp.cos(angles)[..., None, :], jnp.sin(angles)[..., None, :])


def rotate(values, cos_part, sin_part):
    half_dim = values.shape[-1] // 2
    first_half = values[..., :half_dim]
    second_half = values[..., half_dim:]
    return jnp.concatenate(
        [
            first_half * cos_part - second_half * sin_part,
            first_half * sin_part + second_half * cos_part,
        ],
        axis=-1,
    )


def rotate_back(upstream, cos_part, sin_part):
    half_dim = upstream.shape[-1] // 2
    first_half = upstream[..., :half_dim]
    second_half = upstream[..., half_dim:]
    return jnp.concatenate(
        [
            first_half * cos_part + second_half * sin_part,
            second_half * cos_part - first_half * sin_part,
        ],
        axis=-1,
    )


def product(left_side, right_side):
    return jnp.dot(left_side, right_side, preferred_element_type=jnp.float32)


def times_transposed(left_side, right_side):
    return lax.dot_general(
        left_side, right_side, (((1,), (1,)), ((), ())), preferred_element_type=jnp.float32
    )


def rows_inner(left_side, right_side):
    return lax.dot_general(
        left_side, right_side, (((0,), (0,)), ((), ())), preferred_element_type=jnp.float32
    )


def score_block(queries, key_rows, query_kinds, key_kinds, variate_bias):
    raw_scores = jnp.einsum(
        "sqhe,skhe->shqk", queries, key_rows, preferred_element_type=jnp.float32
    ) * HD ** (-0.5)
    same_kind = query_kinds[:, None, :, None] == key_kinds[:, None, None, :]
    scores = raw_scores + jnp.where(
        same_kind, variate_bias[0][None, :, None, None], variate_bias[1][None, :, None, None]
    )
    return (scores, same_kind)


def forward_piece(queries, query_kinds, variate_bias, carried, pieces):
    piece_keys, piece_values, piece_kinds = pieces
    seq_count = piece_keys.shape[0]
    piece_len = piece_keys.shape[1]
    block_size = math.gcd(piece_len, 512)

    def forward_advance(block_index, totals):
        running_max, running_total, running_sum = totals
        offset = block_index * block_size
        key_rows = lax.dynamic_slice_in_dim(piece_keys, offset, block_size, 1).reshape(
            seq_count, block_size, H, HD
        )
        value_rows = lax.dynamic_slice_in_dim(piece_values, offset, block_size, 1).reshape(
            seq_count, block_size, H, HD
        )
        kind_rows = lax.dynamic_slice_in_dim(piece_kinds, offset, block_size, 1)
        scores, same_kind = score_block(queries, key_rows, query_kinds, kind_rows, variate_bias)
        new_max = jnp.maximum(running_max, jnp.max(scores, axis=-1))
        factor = jnp.exp(running_max - new_max)
        exp_scores = jnp.exp(scores - new_max[..., None])
        running_total = running_total * factor + jnp.sum(exp_scores, axis=-1)
        running_sum = running_sum * factor[..., None] + jnp.einsum(
            "shqk,skhe->shqe",
            exp_scores.astype(jnp.bfloat16),
            value_rows,
            preferred_element_type=jnp.float32,
        )
        return (new_max, running_total, running_sum)

    return lax.fori_loop(0, piece_len // block_size, forward_advance, carried)


def back_piece(context, carried, pieces):
    queries, query_kinds, grad_out, log_total, delta_row, variate_bias = context
    piece_keys, piece_values, piece_kinds = pieces
    seq_count = piece_keys.shape[0]
    piece_len = piece_keys.shape[1]
    block_size = math.gcd(piece_len, 512)
    score_scale = HD ** (-0.5)

    def back_advance(block_index, totals):
        offset = block_index * block_size
        key_rows = lax.dynamic_slice_in_dim(piece_keys, offset, block_size, 1).reshape(
            seq_count, block_size, H, HD
        )
        value_rows = lax.dynamic_slice_in_dim(piece_values, offset, block_size, 1).reshape(
            seq_count, block_size, H, HD
        )
        kind_rows = lax.dynamic_slice_in_dim(piece_kinds, offset, block_size, 1)
        scores, same_kind = score_block(queries, key_rows, query_kinds, kind_rows, variate_bias)
        attn_prob = jnp.exp(scores - log_total[..., None])
        grad_prob = jnp.einsum(
            "sqhe,skhe->shqk", grad_out, value_rows, preferred_element_type=jnp.float32
        )
        grad_score = attn_prob * (grad_prob - delta_row[..., None])
        bias_step = jnp.stack(
            [
                jnp.sum(jnp.where(same_kind, grad_score, 0.0), axis=(0, 2, 3)),
                jnp.sum(jnp.where(same_kind, 0.0, grad_score), axis=(0, 2, 3)),
            ]
        )
        score_low = grad_score.astype(jnp.bfloat16)
        query_grad = (
            totals[0]
            + jnp.einsum("shqk,skhe->shqe", score_low, key_rows, preferred_element_type=jnp.float32)
            * score_scale
        )
        key_part = (
            jnp.einsum("shqk,sqhe->skhe", score_low, queries, preferred_element_type=jnp.float32)
            * score_scale
        ).reshape(seq_count, block_size, D)
        value_part = jnp.einsum(
            "shqk,sqhe->skhe",
            attn_prob.astype(jnp.bfloat16),
            grad_out,
            preferred_element_type=jnp.float32,
        ).reshape(seq_count, block_size, D)
        key_total = lax.dynamic_update_slice_in_dim(
            totals[2],
            lax.dynamic_slice_in_dim(totals[2], offset, block_size, 1) + key_part,
            offset,
            1,
        )
        value_total = lax.dynamic_update_slice_in_dim(
            totals[3],
            lax.dynamic_slice_in_dim(totals[3], offset, block_size, 1) + value_part,
            offset,
            1,
        )
        return (query_grad, totals[1] + bias_step, key_total, value_total)

    return lax.fori_loop(0, piece_len // block_size, back_advance, carried)


def local(
    inputs,
    variate_ids,
    time_ids,
    attn_gain,
    query_weight,
    key_weight,
    value_weight,
    out_weight,
    query_gain,
    key_gain,
    variate_bias,
    ffn_gain,
    gate_weight,
    up_weight,
    down_weight,
    out_grad,
):
    seq_count = inputs.shape[1]
    tok_count = inputs.shape[2]
    row_count = seq_count * tok_count
    full_grads = [
        jnp.zeros(extent, jnp.float32)
        for extent in ((D,), (D, D), (D, D), (D, D), (D, D), (D,), (FF, D), (FF, D), (FF, D))
    ]
    small_grads = [
        jnp.zeros((HD,), jnp.float32),
        jnp.zeros((HD,), jnp.float32),
        jnp.zeros((2, H), jnp.float32),
    ]
    shard_total = None
    small_total = None
    outputs_list = []
    input_grads = []
    weights_now = None
    for micro_index in range(inputs.shape[0]):
        weights_now = (
            lax.all_gather(attn_gain.astype(jnp.bfloat16), ("dp", "seq"), axis=0, tiled=True),
            lax.all_gather(query_weight.astype(jnp.bfloat16), ("dp", "seq"), axis=0, tiled=True),
            lax.all_gather(key_weight.astype(jnp.bfloat16), ("dp", "seq"), axis=0, tiled=True),
            lax.all_gather(value_weight.astype(jnp.bfloat16), ("dp", "seq"), axis=0, tiled=True),
            lax.all_gather(out_weight.astype(jnp.bfloat16), ("dp", "seq"), axis=0, tiled=True),
            lax.all_gather(ffn_gain.astype(jnp.bfloat16), ("dp", "seq"), axis=0, tiled=True),
            lax.all_gather(gate_weight.astype(jnp.bfloat16), ("dp", "seq"), axis=0, tiled=True),
            lax.all_gather(up_weight.astype(jnp.bfloat16), ("dp", "seq"), axis=0, tiled=True),
            lax.all_gather(down_weight.astype(jnp.bfloat16), ("dp", "seq"), axis=0, tiled=True),
        )
        gain_one, w_query, w_key, w_value, w_out, gain_two, w_gate, w_up, w_down = weights_now
        hidden_in = inputs[micro_index].astype(jnp.float32).reshape(row_count, D)
        kinds_now = variate_ids[micro_index].astype(jnp.bfloat16)
        cos_part, sin_part = rotation(time_ids[micro_index])
        inv_one = rms_scale(hidden_in)
        normed = (hidden_in * inv_one * gain_one.astype(jnp.float32)).astype(jnp.bfloat16)
        query_raw = product(normed, w_query).reshape(seq_count, tok_count, H, HD)
        key_raw = product(normed, w_key).reshape(seq_count, tok_count, H, HD)
        value_flat = product(normed, w_value).astype(jnp.bfloat16).reshape(seq_count, tok_count, D)
        inv_query = rms_scale(query_raw)
        query_rot = rotate(query_raw * inv_query * query_gain, cos_part, sin_part).astype(
            jnp.bfloat16
        )
        inv_key = rms_scale(key_raw)
        key_rot = rotate(key_raw * inv_key * key_gain, cos_part, sin_part).astype(jnp.bfloat16)
        key_flat = key_rot.reshape(seq_count, tok_count, D)
        initial = (
            jnp.full((seq_count, H, tok_count), lowest, jnp.float32),
            jnp.zeros((seq_count, H, tok_count), jnp.float32),
            jnp.zeros((seq_count, H, tok_count, HD), jnp.float32),
        )
        final_max, final_total, final_sum = forward_piece(
            query_rot,
            kinds_now,
            variate_bias,
            initial,
            (
                lax.all_gather(key_flat, "seq", axis=1, tiled=True),
                lax.all_gather(value_flat, "seq", axis=1, tiled=True),
                lax.all_gather(kinds_now, "seq", axis=1, tiled=True),
            ),
        )
        log_total = final_max + jnp.log(final_total)
        attended = jnp.transpose(final_sum / final_total[..., None], (0, 2, 1, 3))
        attended_low = attended.reshape(row_count, D).astype(jnp.bfloat16)
        middle = hidden_in + product(attended_low, w_out)
        inv_two = rms_scale(middle)
        normed_two = (middle * inv_two * gain_two.astype(jnp.float32)).astype(jnp.bfloat16)
        gate_pre = times_transposed(normed_two, w_gate)
        up_pre = times_transposed(normed_two, w_up)
        gate_sig = jax.nn.sigmoid(gate_pre)
        hidden_low = (gate_pre * gate_sig * up_pre).astype(jnp.bfloat16)
        result = middle + product(hidden_low, w_down)
        outputs_list.append(result.reshape(seq_count, tok_count, D).astype(jnp.bfloat16))
        gain_one, w_query, w_key, w_value, w_out, gain_two, w_gate, w_up, w_down = (
            lax.all_gather(attn_gain.astype(jnp.bfloat16), ("dp", "seq"), axis=0, tiled=True),
            lax.all_gather(query_weight.astype(jnp.bfloat16), ("dp", "seq"), axis=0, tiled=True),
            lax.all_gather(key_weight.astype(jnp.bfloat16), ("dp", "seq"), axis=0, tiled=True),
            lax.all_gather(value_weight.astype(jnp.bfloat16), ("dp", "seq"), axis=0, tiled=True),
            lax.all_gather(out_weight.astype(jnp.bfloat16), ("dp", "seq"), axis=0, tiled=True),
            lax.all_gather(ffn_gain.astype(jnp.bfloat16), ("dp", "seq"), axis=0, tiled=True),
            lax.all_gather(gate_weight.astype(jnp.bfloat16), ("dp", "seq"), axis=0, tiled=True),
            lax.all_gather(up_weight.astype(jnp.bfloat16), ("dp", "seq"), axis=0, tiled=True),
            lax.all_gather(down_weight.astype(jnp.bfloat16), ("dp", "seq"), axis=0, tiled=True),
        )
        grad_in = out_grad[micro_index].astype(jnp.float32).reshape(row_count, D)
        grad_low = grad_in.astype(jnp.bfloat16)
        full_grads[8] = rows_inner(hidden_low, grad_low)
        grad_hidden = times_transposed(grad_low, w_down)
        grad_gate = (grad_hidden * up_pre * gate_sig * (1.0 + gate_pre * (1.0 - gate_sig))).astype(
            jnp.bfloat16
        )
        grad_up = (grad_hidden * gate_pre * gate_sig).astype(jnp.bfloat16)
        full_grads[6] = rows_inner(grad_gate, normed_two)
        full_grads[7] = rows_inner(grad_up, normed_two)
        grad_normed_two = product(grad_gate, w_gate) + product(grad_up, w_up)
        full_grads[5] = jnp.sum(grad_normed_two * middle * inv_two, axis=0)
        grad_middle = grad_in + norm_back(
            middle, inv_two, gain_two.astype(jnp.float32), grad_normed_two
        )
        grad_middle_low = grad_middle.astype(jnp.bfloat16)
        full_grads[4] = rows_inner(attended_low, grad_middle_low)
        grad_attended = (
            times_transposed(grad_middle_low, w_out)
            .astype(jnp.bfloat16)
            .reshape(seq_count, tok_count, H, HD)
        )
        delta_row = jnp.transpose(
            jnp.sum(grad_attended.astype(jnp.float32) * attended, axis=-1), (0, 2, 1)
        )
        context = (query_rot, kinds_now, grad_attended, log_total, delta_row, variate_bias)
        base_carry = (
            jnp.zeros((seq_count, H, tok_count, HD), jnp.float32),
            jnp.zeros((2, H), jnp.float32),
        )
        length_all = tok_count * lax.axis_size("seq")
        wide_carry = (
            jnp.zeros((seq_count, length_all, D), jnp.float32),
            jnp.zeros((seq_count, length_all, D), jnp.float32),
        )
        grad_query_heads, grad_bias, key_all, value_all = back_piece(
            context,
            base_carry + wide_carry,
            (
                lax.all_gather(key_flat, "seq", axis=1, tiled=True),
                lax.all_gather(value_flat, "seq", axis=1, tiled=True),
                lax.all_gather(kinds_now, "seq", axis=1, tiled=True),
            ),
        )
        grad_key, grad_value = (
            lax.psum_scatter(
                key_all.astype(jnp.bfloat16), "seq", scatter_dimension=1, tiled=True
            ).astype(jnp.float32),
            lax.psum_scatter(
                value_all.astype(jnp.bfloat16), "seq", scatter_dimension=1, tiled=True
            ).astype(jnp.float32),
        )
        grad_key = grad_key.reshape(seq_count, tok_count, H, HD)
        grad_value_low = grad_value.reshape(row_count, D).astype(jnp.bfloat16)
        small_grads[2] = grad_bias
        grad_query = jnp.transpose(grad_query_heads, (0, 2, 1, 3))
        grad_query_norm = rotate_back(grad_query, cos_part, sin_part)
        small_grads[0] = jnp.sum(grad_query_norm * query_raw * inv_query, axis=(0, 1, 2))
        grad_query_low = (
            norm_back(query_raw, inv_query, query_gain, grad_query_norm)
            .reshape(row_count, D)
            .astype(jnp.bfloat16)
        )
        grad_key_norm = rotate_back(grad_key, cos_part, sin_part)
        small_grads[1] = jnp.sum(grad_key_norm * key_raw * inv_key, axis=(0, 1, 2))
        grad_key_low = (
            norm_back(key_raw, inv_key, key_gain, grad_key_norm)
            .reshape(row_count, D)
            .astype(jnp.bfloat16)
        )
        full_grads[1] = rows_inner(normed, grad_query_low)
        full_grads[2] = rows_inner(normed, grad_key_low)
        full_grads[3] = rows_inner(normed, grad_value_low)
        grad_normed = (
            times_transposed(grad_query_low, w_query)
            + times_transposed(grad_key_low, w_key)
            + times_transposed(grad_value_low, w_value)
        )
        full_grads[0] = jnp.sum(grad_normed * hidden_in * inv_one, axis=0)
        input_total = grad_middle + norm_back(
            hidden_in, inv_one, gain_one.astype(jnp.float32), grad_normed
        )
        input_grads.append(input_total.reshape(seq_count, tok_count, D).astype(jnp.bfloat16))
        shards = (
            lax.psum_scatter(full_grads[0], ("dp", "seq"), scatter_dimension=0, tiled=True),
            lax.psum_scatter(full_grads[1], ("dp", "seq"), scatter_dimension=0, tiled=True),
            lax.psum_scatter(full_grads[2], ("dp", "seq"), scatter_dimension=0, tiled=True),
            lax.psum_scatter(full_grads[3], ("dp", "seq"), scatter_dimension=0, tiled=True),
            lax.psum_scatter(full_grads[4], ("dp", "seq"), scatter_dimension=0, tiled=True),
            lax.psum_scatter(full_grads[5], ("dp", "seq"), scatter_dimension=0, tiled=True),
            lax.psum_scatter(full_grads[6], ("dp", "seq"), scatter_dimension=0, tiled=True),
            lax.psum_scatter(full_grads[7], ("dp", "seq"), scatter_dimension=0, tiled=True),
            lax.psum_scatter(full_grads[8], ("dp", "seq"), scatter_dimension=0, tiled=True),
        )
        summed = lax.psum((small_grads[0], small_grads[1], small_grads[2]), ("dp", "seq"))
        shards, summed = (list(shards), list(summed))
        if shard_total is None:
            shard_total = shards
            small_total = summed
        else:
            shard_total = [
                earlier_part + later_part for earlier_part, later_part in zip(shard_total, shards)
            ]
            small_total = [
                earlier_part + later_part for earlier_part, later_part in zip(small_total, summed)
            ]
        full_grads = [jnp.zeros_like(member) for member in full_grads]
        small_grads = [jnp.zeros_like(member) for member in small_grads]
    return (
        jnp.stack(outputs_list),
        jnp.stack(input_grads),
        shard_total[0],
        shard_total[1],
        shard_total[2],
        shard_total[3],
        shard_total[4],
        small_total[0],
        small_total[1],
        small_total[2],
        shard_total[5],
        shard_total[6],
        shard_total[7],
        shard_total[8],
    )


def swap_seq(values, mask):
    return lax.ppermute(values, "seq", [(at, at ^ mask) for at in range(8)])


def swap_dp(values, mask):
    return lax.ppermute(values, "dp", [(at, at ^ mask) for at in range(4)])


def pick(pieces, which):
    chosen = pieces[-1]
    for at in range(len(pieces) - 2, -1, -1):
        chosen = jnp.where(which == at, pieces[at], chosen)
    return chosen


def ordered(pieces, own):
    return jnp.stack([pick(pieces, own ^ at) for at in range(len(pieces))])


def together(*values):
    return lax.optimization_barrier(values)


def at_index(values, index, axis=0):
    return lax.dynamic_index_in_dim(values, index, axis, keepdims=False)


def contract_last(left_side, right_side):
    return lax.dot_general(
        left_side, right_side, (((1,), (1,)), ((), ())), preferred_element_type=jnp.float32
    )


def head_sums(values, block):
    first = values.astype(jnp.bfloat16)
    second = (values - first.astype(jnp.float32)).astype(jnp.bfloat16)
    return jnp.dot(first, block, preferred_element_type=jnp.float32) + jnp.dot(
        second, block, preferred_element_type=jnp.float32
    )


def head_block(scale):
    rows = lax.broadcasted_iota(jnp.int32, (128, 128), 0) // HD
    columns = lax.broadcasted_iota(jnp.int32, (128, 128), 1) // HD
    return jnp.where(rows == columns, scale, 0.0).astype(jnp.bfloat16)


def rope_partner(values):
    lane = lax.broadcasted_iota(jnp.int32, values.shape, 1)
    return jnp.where(
        lane % HD < HD // 2, pltpu.roll(values, 128 - HD // 2, 1), pltpu.roll(values, HD // 2, 1)
    )


def three_parts(values):
    first = values.astype(jnp.bfloat16).astype(jnp.float32)
    second = (values - first).astype(jnp.bfloat16).astype(jnp.float32)
    third = (values - first - second).astype(jnp.bfloat16).astype(jnp.float32)
    return first, second, third


GRANT = 60 << 20
BQ = 512
BK = 1024
LSE_LANE = 24


def attend_kernel(
    q_in,
    k_in,
    v_in,
    cos_in,
    sin_in,
    hot_in,
    q_gain,
    k_gain,
    bias_in,
    near_out,
    far_out,
    qs_out,
    ks_out,
    vs_out,
    ext_out,
    kx,
    vx,
):
    mean_block = head_block(1.0 / HD)

    def prepare(raw, gain):
        inv = lax.rsqrt(head_sums(raw * raw, mean_block) + epsilon)
        scaled = raw * inv * gain
        return scaled * cos_in[...] + rope_partner(scaled) * sin_in[...]

    qs_out[...] = (
        prepare(q_in[...], q_gain[...]).astype(jnp.bfloat16).astype(jnp.float32) * HD**-0.5
    ).astype(jnp.bfloat16)
    keys = prepare(k_in[...], k_gain[...]).astype(jnp.bfloat16)
    ks_out[...] = keys
    kx[:, :128] = keys
    kx[:, 128:] = hot_in[...]
    values = v_in[...].astype(jnp.bfloat16)
    vs_out[...] = values
    vx[:, :128] = values
    vx[:, 128:] = jnp.ones(values.shape, jnp.bfloat16)
    lane = lax.broadcasted_iota(jnp.int32, (BQ, 128), 1)

    def step(block, carry):
        rows = pl.ds(pl.multiple_of(block * BQ, BQ), BQ)
        queries = qs_out[rows, :].astype(jnp.float32)
        hot = hot_in[rows, :].astype(jnp.float32)
        results = []
        for head in range(2):
            mine = jnp.where(lane // HD == head, queries, 0.0).astype(jnp.bfloat16)
            extra = hot * bias_in[0, head : head + 1, :]
            scores = contract_last(
                jnp.concatenate([mine, extra.astype(jnp.bfloat16)], axis=1), kx[...]
            )
            weights = jnp.exp(scores).astype(jnp.bfloat16)
            summed = jnp.dot(weights, vx[...], preferred_element_type=jnp.float32)
            total = summed[:, 128:]
            results.append(summed[:, :128] / total)
            first, second, third = three_parts(-jnp.log(total))
            extra = jnp.where(lane == LSE_LANE, first, extra)
            extra = jnp.where(lane == LSE_LANE + 1, second, extra)
            extra = jnp.where(lane == LSE_LANE + 2, third, extra)
            ext_out[head, rows, :] = extra.astype(jnp.bfloat16)
        result = jnp.where(lane < HD, results[0], results[1]).astype(jnp.bfloat16)
        half = near_out.shape[0]

        @pl.when(block < half // BQ)
        def _():
            near_out[pl.ds(pl.multiple_of(block * BQ, BQ), BQ), :] = result

        @pl.when(block >= half // BQ)
        def _():
            far_out[pl.ds(pl.multiple_of(block * BQ - half, BQ), BQ), :] = result

        return carry

    lax.fori_loop(0, q_in.shape[0] // BQ, step, 0)


def attend_back_kernel(
    q_in,
    k_in,
    qs_in,
    ks_in,
    vs_in,
    ext_in,
    hot_in,
    grad_near,
    grad_far,
    att_near,
    att_far,
    cos_in,
    sin_in,
    q_gain,
    k_gain,
    out,
    gain_out,
    bias_out,
    kx,
    vx,
    kt,
    qx,
    qg,
    gx,
    dqt,
    dk_sum,
    dv_sum,
):
    tokens = q_in.shape[0]
    lane = lax.broadcasted_iota(jnp.int32, (tokens, 128), 1)
    keys = ks_in[...]
    kx[:, :128] = keys
    kx[:, 128:] = hot_in[...]
    kt[...] = keys.astype(jnp.float32).T.astype(jnp.bfloat16)
    vx[:, :128] = vs_in[...]
    vx[:, 128:] = jnp.where(lane % HD < 3, 1.0, 0.0).astype(jnp.bfloat16)
    grads = jnp.concatenate([grad_near[...], grad_far[...]]).astype(jnp.float32)
    results = jnp.concatenate([att_near[...], att_far[...]]).astype(jnp.float32)
    delta = head_sums(grads * results, head_block(1.0))
    first, second, third = three_parts(-delta)
    parts = jnp.where(
        lane % HD == 0,
        first,
        jnp.where(lane % HD == 1, second, jnp.where(lane % HD == 2, third, 0.0)),
    )
    queries = qs_in[...].astype(jnp.float32)
    for head in range(2):
        own = lane // HD == head
        mine = jnp.where(own, queries, 0.0).astype(jnp.bfloat16)
        qx[head, :, :128] = mine
        qx[head, :, 128:] = ext_in[head]
        qg[head, :, :128] = mine
        qg[head, :, 128:] = hot_in[...]
        gx[head, :, :128] = jnp.where(own, grads, 0.0).astype(jnp.bfloat16)
        gx[head, :, 128:] = jnp.where(own, parts, 0.0).astype(jnp.bfloat16)
    dqt[...] = jnp.zeros(dqt.shape, jnp.float32)
    block_lane = lax.broadcasted_iota(jnp.int32, (BK, 128), 1)
    counted = jnp.where((block_lane < 8) | (block_lane == LSE_LANE), 1.0, 0.0)

    def step(block, carry):
        rows = pl.ds(pl.multiple_of(block * BK, BK), BK)
        hot = hot_in[rows, :].astype(jnp.float32) * counted
        dk_parts = []
        dv_parts = []
        bias_parts = []
        for head in range(2):
            probs = jnp.exp(contract_last(kx[rows, :], qx[head]))
            dscores = (probs * contract_last(vx[rows, :], gx[head])).astype(jnp.bfloat16)
            dv_parts.append(
                jnp.dot(
                    probs.astype(jnp.bfloat16), gx[head, :, :128], preferred_element_type=jnp.float32
                )
            )
            wide = jnp.dot(dscores, qg[head], preferred_element_type=jnp.float32)
            dk_parts.append(wide[:, :128])
            bias_parts.append(jnp.sum(wide[:, 128:] * hot, axis=0, keepdims=True))
            head_rows = pl.ds(head * HD, HD)
            dqt[head_rows, :] += jnp.dot(
                kt[head_rows, rows], dscores, preferred_element_type=jnp.float32
            )
        dk_sum[rows, :] = dk_parts[0] + dk_parts[1]
        dv_sum[rows, :] = dv_parts[0] + dv_parts[1]
        return (carry[0] + bias_parts[0], carry[1] + bias_parts[1])

    zero = jnp.zeros((1, 128), jnp.float32)
    sums = lax.fori_loop(0, tokens // BK, step, (zero, zero))
    bias_out[0, 0:1, :] = sums[0]
    bias_out[0, 1:2, :] = sums[1]
    mean_block = head_block(1.0 / HD)

    def finish(raw, upstream, gain):
        inv = lax.rsqrt(head_sums(raw * raw, mean_block) + epsilon)
        normed = upstream * cos_in[...] - rope_partner(upstream) * sin_in[...]
        gain_grad = jnp.sum(normed * raw * inv, axis=0, keepdims=True)
        weighted = normed * gain
        inner = head_sums(weighted * raw, mean_block)
        return inv * weighted - raw * (inv * inv * inv) * inner, gain_grad

    dq, dq_gain = finish(q_in[...], dqt[...].T * HD**-0.5, q_gain[...])
    dk, dk_gain = finish(k_in[...], dk_sum[...], k_gain[...])
    out[0] = dq.astype(jnp.bfloat16)
    out[1] = dk.astype(jnp.bfloat16)
    out[2] = dv_sum[...].astype(jnp.bfloat16)
    gain_out[0, 0:1, :] = dq_gain
    gain_out[0, 1:2, :] = dk_gain


def attend(qkv, cos_part, sin_part, hot, q_gain, k_gain, bias_rows):
    tokens = qkv.shape[0]
    column = lambda shift: pl.BlockSpec((tokens, 128), lambda pair: (0, pair + shift))
    half = pl.BlockSpec((tokens // 2, 128), lambda pair: (0, pair))
    whole = pl.BlockSpec((tokens, 128), lambda pair: (0, 0))
    line = pl.BlockSpec((1, 128), lambda pair: (0, 0))
    low = lambda: jax.ShapeDtypeStruct((tokens, 256), jnp.bfloat16)
    return pl.pallas_call(
        attend_kernel,
        grid=(2,),
        in_specs=[
            column(0),
            column(2),
            column(4),
            whole,
            whole,
            whole,
            line,
            line,
            pl.BlockSpec((1, 2, 128), lambda pair: (pair, 0, 0)),
        ],
        out_specs=[
            half,
            half,
            column(0),
            column(0),
            column(0),
            pl.BlockSpec((2, tokens, 128), lambda pair: (pair, 0, 0)),
        ],
        out_shape=[
            jax.ShapeDtypeStruct((tokens // 2, 256), jnp.bfloat16),
            jax.ShapeDtypeStruct((tokens // 2, 256), jnp.bfloat16),
            low(),
            low(),
            low(),
            jax.ShapeDtypeStruct((4, tokens, 128), jnp.bfloat16),
        ],
        scratch_shapes=[
            pltpu.VMEM((tokens, 256), jnp.bfloat16),
            pltpu.VMEM((tokens, 256), jnp.bfloat16),
        ],
        compiler_params=pltpu.CompilerParams(vmem_limit_bytes=GRANT),
        name="attend",
    )(qkv, qkv, qkv, cos_part, sin_part, hot, q_gain, k_gain, bias_rows)


def attend_back(qkv, saved, hot, grads, attended, cos_part, sin_part, q_gain, k_gain):
    queries, keys, values, extra = saved
    tokens = qkv.shape[0]
    column = lambda shift: pl.BlockSpec((tokens, 128), lambda pair: (0, pair + shift))
    half = pl.BlockSpec((tokens // 2, 128), lambda pair: (0, pair))
    whole = pl.BlockSpec((tokens, 128), lambda pair: (0, 0))
    line = pl.BlockSpec((1, 128), lambda pair: (0, 0))
    two = pl.BlockSpec((1, 2, 128), lambda pair: (pair, 0, 0))
    wide = pltpu.VMEM((tokens, 256), jnp.bfloat16)
    both = pltpu.VMEM((2, tokens, 256), jnp.bfloat16)
    return pl.pallas_call(
        attend_back_kernel,
        grid=(2,),
        in_specs=[
            column(0),
            column(2),
            column(0),
            column(0),
            column(0),
            pl.BlockSpec((2, tokens, 128), lambda pair: (pair, 0, 0)),
            whole,
            half,
            half,
            half,
            half,
            whole,
            whole,
            line,
            line,
        ],
        out_specs=[pl.BlockSpec((3, tokens, 128), lambda pair: (0, 0, pair)), two, two],
        out_shape=[
            jax.ShapeDtypeStruct((3, tokens, 256), jnp.bfloat16),
            jax.ShapeDtypeStruct((2, 2, 128), jnp.float32),
            jax.ShapeDtypeStruct((2, 2, 128), jnp.float32),
        ],
        scratch_shapes=[
            wide,
            wide,
            pltpu.VMEM((128, tokens), jnp.bfloat16),
            both,
            both,
            both,
            pltpu.VMEM((128, tokens), jnp.float32),
            pltpu.VMEM((tokens, 128), jnp.float32),
            pltpu.VMEM((tokens, 128), jnp.float32),
        ],
        compiler_params=pltpu.CompilerParams(vmem_limit_bytes=GRANT),
        cost_estimate=pl.CostEstimate(
            flops=40 * tokens * tokens * 256,
            bytes_accessed=tokens * 256 * 40,
            transcendentals=4 * tokens * tokens,
        ),
        name="attend_back",
    )(
        qkv,
        qkv,
        queries,
        keys,
        values,
        extra,
        hot,
        *grads,
        *attended,
        cos_part,
        sin_part,
        q_gain,
        k_gain,
    )


def front_kernel(place, *refs):
    pieces, crossed, own, other = refs[:4], refs[4], refs[5:9], refs[9]
    weights_out, unit_out, qkv_out = refs[10:]
    dp_at, level, core = place[0], place[1], place[2]
    step = pl.program_id(0)

    def norm(values):
        wide = values.astype(jnp.float32)
        return (wide * rms_scale(wide)).astype(jnp.bfloat16)

    @pl.when(step == 0)
    def _():
        for at_dp in range(4):
            for at_level in range(4):
                base = ((dp_at ^ at_dp) * 4 + (level ^ at_level)) * 64
                mine = pl.ds(pl.multiple_of(base + core * 32, 32), 32)
                theirs = pl.ds(pl.multiple_of(base + (1 - core) * 32, 32), 32)
                rows = slice(at_level * 32, at_level * 32 + 32)
                for part in range(3):
                    lanes = pl.ds(pl.multiple_of(part * 512 + core * 256, 256), 256)
                    weights_out[mine, part * 256 : (part + 1) * 256] = pieces[at_dp][rows, lanes]
                start = at_dp * 128 + at_level * 32
                weights_out[theirs, :] = crossed[start : start + 32, :]
        for at in range(4):
            unit_out[at * 128 : (at + 1) * 128, :] = norm(own[at][...])

    @pl.when(step == 1)
    def _():
        for at in range(4):
            unit_out[at * 128 : (at + 1) * 128, :] = norm(other[at])

    qkv_out[...] = jnp.dot(unit_out[...], weights_out[...], preferred_element_type=jnp.float32)


def front(place, pieces, crossed, own, other):
    tokens = 2 * other.shape[0] * other.shape[1]
    quarter = pl.BlockSpec((128, 1536), lambda at: (0, 0))
    piece = pl.BlockSpec((128, D), lambda at: (0, 0))
    return pl.pallas_call(
        front_kernel,
        grid=(2,),
        in_specs=[pl.BlockSpec(memory_space=pltpu.SMEM)]
        + [quarter] * 4
        + [pl.BlockSpec((512, 768), lambda at: (0, 0))]
        + [piece] * 4
        + [pl.BlockSpec((4, 128, D), lambda at: (0, 0, 0))],
        out_specs=[
            pl.BlockSpec((D, 768), lambda at: (0, 0)),
            pl.BlockSpec((tokens // 2, D), lambda at: (at, 0)),
            pl.BlockSpec((tokens // 2, 768), lambda at: (at, 0)),
        ],
        out_shape=[
            jax.ShapeDtypeStruct((D, 768), jnp.bfloat16),
            jax.ShapeDtypeStruct((tokens, D), jnp.bfloat16),
            jax.ShapeDtypeStruct((tokens, 768), jnp.float32),
        ],
        compiler_params=pltpu.CompilerParams(vmem_limit_bytes=GRANT),
        name="front",
    )(place, *pieces, crossed, *own, other)


def tail_kernel(
    place, dqkv, weights, unit, gains, biases, ffn_gain, back_kept, back_sent, kept, sent, part, small
):
    core, group = place[2], place[3]
    tokens = unit.shape[0]

    def back(rows):
        total = contract_last(dqkv[0, rows, :], weights[:, :256])
        for at in (1, 2):
            total += contract_last(dqkv[at, rows, :], weights[:, at * 256 : (at + 1) * 256])
        return total

    back_kept[...] = back(slice(0, tokens // 2))
    back_sent[...] = back(slice(tokens // 2, tokens)).astype(jnp.bfloat16)
    for at in range(3):
        part[:, at * 256 : (at + 1) * 256] = rows_inner(unit[...], dqkv[at]).astype(jnp.bfloat16)
    for at in range(16):
        rows = slice(at * 32, at * 32 + 32)
        kept[rows, :] = part[pl.ds(pl.multiple_of(at * 64 + core * 32, 32), 32), :]
        sent[rows, :] = part[pl.ds(pl.multiple_of(at * 64 + (1 - core) * 32, 32), 32), :]
    lane = lax.broadcasted_iota(jnp.int32, (1, 128), 1)
    sums = gains[0] + gains[1]
    sums = sums + pltpu.roll(sums, HD, 1)
    placed = jnp.zeros((1, 128), jnp.float32)
    for head in range(4):
        line = biases[head // 2, head % 2 : head % 2 + 1, :]
        same = jnp.sum(jnp.where(lane < 8, line, 0.0), axis=1, keepdims=True)
        total = jnp.sum(jnp.where(lane == LSE_LANE, line, 0.0), axis=1, keepdims=True)
        spot = group * 4 + head
        placed = jnp.where(lane == spot, same, placed)
        placed = jnp.where(lane == spot + H, total - same, placed)
    small[...] = jnp.zeros(small.shape, jnp.float32)
    for at in range(4):
        small[at : at + 1, :256] = ffn_gain[:, at * 256 : (at + 1) * 256]
    small[4:5, :128] = jnp.where(lane < HD, sums[0:1], sums[1:2])
    small[4:5, 128:256] = placed
    kept[512:, :] = small[...].astype(jnp.bfloat16)
    sent[512:, :] = small[...].astype(jnp.bfloat16)


def tail(place, dqkv, weights, unit, gains, biases, ffn_gain):
    tokens = unit.shape[0]
    whole = lambda shape: pl.BlockSpec(shape, lambda at: (0,) * len(shape))
    shapes = [
        ((tokens // 2, D), jnp.float32),
        ((tokens // 2, D), jnp.bfloat16),
        ((528, 768), jnp.bfloat16),
        ((528, 768), jnp.bfloat16),
    ]
    arguments = (dqkv, weights, unit, gains, biases, ffn_gain)
    return pl.pallas_call(
        tail_kernel,
        grid=(1,),
        in_specs=[pl.BlockSpec(memory_space=pltpu.SMEM)]
        + [whole(member.shape) for member in arguments],
        out_specs=[whole(shape) for shape, _ in shapes],
        out_shape=[jax.ShapeDtypeStruct(shape, kind) for shape, kind in shapes],
        scratch_shapes=[pltpu.VMEM((D, 768), jnp.bfloat16), pltpu.VMEM((16, 768), jnp.float32)],
        compiler_params=pltpu.CompilerParams(vmem_limit_bytes=GRANT),
        cost_estimate=pl.CostEstimate(
            flops=4 * tokens * D * 768, bytes_accessed=14 * D * D, transcendentals=0
        ),
        name="tail",
    )(place, *arguments)


def finish_kernel(place, mine, near, side, far, gain, *refs):
    weights = refs[:3]
    kept, back_near, passed, inputs, upstream = refs[3:8]
    middle, down_kept, down_near, down_side, down_far = refs[8:13]
    grads_out = refs[13:16]
    out_out, input_out, result_out, gain_out, q_out, k_out, bias_out, two_out = refs[16:24]
    wide = jnp.float32
    dp_at, level, core = place[0], place[1], place[2]
    parity, batch = level & 1, level >> 1
    step = pl.program_id(0)

    @pl.when(step == 0)
    def _():
        scale = gain[...].astype(jnp.bfloat16).astype(wide)
        for at in range(3):
            for side_core in range(2):
                rows = slice(at * 64 + side_core * 32, at * 64 + side_core * 32 + 32)
                same = mine[rows, :].astype(wide) + side[rows, :].astype(wide)
                cross = near[rows, :].astype(wide) + far[rows, :].astype(wide)
                for turn, member in ((parity, same), (1 - parity, cross)):
                    lane = (turn * 2 + (core + side_core) % 2) * 256
                    grads_out[at][:, pl.ds(pl.multiple_of(lane, 256), 256)] = member
        total = jnp.zeros((32, 1), wide)
        for at in range(3):
            unscaled = grads_out[at][...]
            total += jnp.sum(
                unscaled * weights[at][...].astype(jnp.bfloat16).astype(wide), axis=1, keepdims=True
            )
            grads_out[at][...] = unscaled * scale
        rows = lax.broadcasted_iota(jnp.int32, (32, 32), 0)
        columns = lax.broadcasted_iota(jnp.int32, (32, 32), 1)
        gain_out[...] = jnp.sum(jnp.where(rows == columns, total, 0.0), axis=0, keepdims=True)

        def summed(rows):
            return (mine[rows, :].astype(wide) + near[rows, :].astype(wide)) + (
                side[rows, :].astype(wide) + far[rows, :].astype(wide)
            )

        for at in range(4):
            out_out[:, at * 256 : (at + 1) * 256] = summed(slice(192 + at * 32, 224 + at * 32))
        small = summed(slice(320, 336))
        q_out[...] = small[4:5, :HD]
        k_out[...] = small[4:5, HD : 2 * HD]
        bias_out[0:1, :] = small[4:5, 2 * HD : 2 * HD + H]
        bias_out[1:2, :] = small[4:5, 2 * HD + H : 2 * HD + 2 * H]
        two = jnp.zeros((1, 32), wide)
        for at_dp in range(4):
            for at_seq in range(8):
                here = (dp_at == at_dp) & (level * 2 + core == at_seq)
                two = jnp.where(here, small[at_dp : at_dp + 1, at_seq * 32 : at_seq * 32 + 32], two)
        two_out[...] = two
    result_out[...] = (
        middle[...]
        + (
            (down_kept[...] + down_near[...].astype(wide))
            + (down_side[...].astype(wide) + down_far[...].astype(wide))
        )
    ).astype(jnp.bfloat16)
    back = jnp.where(
        step == batch, kept[...] + back_near[...].astype(wide), passed[...].astype(wide)
    )
    values = inputs[0].astype(wide)
    inv = rms_scale(values)
    inner = jnp.mean(back * values, axis=-1, keepdims=True)
    input_out[0] = (
        upstream[0] + inv * back - values * (inv * inv * inv) * inner
    ).astype(jnp.bfloat16)


def finish(place, mine, moved, gain, weights, backs, inputs, upstream, outputs):
    whole = lambda shape: pl.BlockSpec(shape, lambda at: (0,) * len(shape))
    arguments = [mine, *moved, gain, *weights, *backs, inputs, upstream, *outputs]
    f32 = jnp.float32
    shapes = [((32, D), f32)] * 4 + [(inputs.shape, jnp.bfloat16)]
    shapes += [(outputs[0].shape, jnp.bfloat16)]
    shapes += [((1, 32), f32), ((1, HD), f32), ((1, HD), f32), ((2, H), f32), ((1, 32), f32)]
    rows, piece = inputs.shape[0] * inputs.shape[1], inputs.shape[1]
    batch_block = pl.BlockSpec((1, piece, D), lambda at: (at, 0, 0))
    row_block = pl.BlockSpec((piece, D), lambda at: (at, 0))

    def spec(shape):
        return {inputs.shape: batch_block, (rows, D): row_block}.get(tuple(shape), whole(shape))

    return pl.pallas_call(
        finish_kernel,
        grid=(2,),
        in_specs=[pl.BlockSpec(memory_space=pltpu.SMEM)]
        + [spec(member.shape) for member in arguments],
        out_specs=[spec(shape) for shape, _ in shapes],
        out_shape=[jax.ShapeDtypeStruct(shape, kind) for shape, kind in shapes],
        compiler_params=pltpu.CompilerParams(vmem_limit_bytes=GRANT),
        name="finish",
    )(place, *arguments)


def lower_kernel(gate, up, down, out):
    out[0] = gate[...].astype(jnp.bfloat16)
    out[1] = up[...].astype(jnp.bfloat16)
    out[2] = down[...].astype(jnp.bfloat16)


def lower(gate, up, down):
    whole = pl.BlockSpec(gate.shape, lambda at: (0, 0))
    return pl.pallas_call(
        lower_kernel,
        grid=(1,),
        in_specs=[whole] * 3,
        out_specs=pl.BlockSpec((3,) + gate.shape, lambda at: (0, 0, 0)),
        out_shape=jax.ShapeDtypeStruct((3,) + gate.shape, jnp.bfloat16),
        compiler_params=pltpu.CompilerParams(vmem_limit_bytes=GRANT),
        name="lower",
    )(gate, up, down)


def middle_back_kernel(
    place, kept, near, side, far, dy_in, middle_in, gain_in, weights, grad_out, low_out, sums_out, *outs
):
    wide = jnp.float32
    step = pl.program_id(0)
    level = place[1]
    upstream = (kept[...] + near[...].astype(wide)) + (
        side[...].astype(wide) + far[...].astype(wide)
    )
    middle = middle_in[...]
    inv = rms_scale(middle)
    sums = jnp.sum(upstream * middle * inv, axis=0, keepdims=True)

    @pl.when(step == 0)
    def _():
        sums_out[...] = sums

    @pl.when(step == 1)
    def _():
        sums_out[...] += sums

    grad = dy_in[...].astype(wide) + norm_back(middle, inv, gain_in[...], upstream)
    grad_out[...] = grad
    grad_low = grad.astype(jnp.bfloat16)
    low_out[...] = grad_low
    halves = [
        contract_last(grad_low, weights[at * 512 : (at + 1) * 512, :D]).astype(jnp.bfloat16)
        for at in range(2)
    ]
    for mask in range(4):
        for parity in range(2):

            @pl.when((level ^ mask) == step * 2 + parity)
            def _():
                outs[mask][...] = halves[parity]


def middle_back(place, kept, moved, own_dy, middle, gain_two, w_out):
    rows = kept.shape[0]
    block = pl.BlockSpec((rows // 2, D), lambda at: (at, 0))
    line = pl.BlockSpec((1, D), lambda at: (0, 0))
    quarter = pl.BlockSpec((rows // 2, D // 2), lambda at: (0, 0))
    return pl.pallas_call(
        middle_back_kernel,
        grid=(2,),
        in_specs=[pl.BlockSpec(memory_space=pltpu.SMEM)]
        + [block] * 6
        + [line, pl.BlockSpec(w_out.shape, lambda at: (0, 0))],
        out_specs=[block, block, line] + [quarter] * 4,
        out_shape=[
            jax.ShapeDtypeStruct((rows, D), jnp.float32),
            jax.ShapeDtypeStruct((rows, D), jnp.bfloat16),
            jax.ShapeDtypeStruct((1, D), jnp.float32),
        ]
        + [jax.ShapeDtypeStruct((rows // 2, D // 2), jnp.bfloat16)] * 4,
        compiler_params=pltpu.CompilerParams(vmem_limit_bytes=GRANT),
        cost_estimate=pl.CostEstimate(
            flops=2 * rows * D * D, bytes_accessed=22 * rows * D + 2 * D * D, transcendentals=rows
        ),
        name="middle_back",
    )(place, kept, *moved, own_dy, middle, gain_two, w_out)


GATED = 512
HIDDEN = 256


def load_weights(place, sources, gathered, arrived, which):
    level, core = place[1], place[2]
    pieces = [(sources[at], at, core) for at in range(4)]
    pieces += [(sources[4 + at], at, 1 - core) for at in range(4)]
    copies = []
    for at, (source, turn, side) in enumerate(pieces):
        rows = pl.ds(pl.multiple_of(((level ^ turn) * 2 + side) * 128, 128), 128)
        copies.append(
            pltpu.make_async_copy(source.at[which], gathered.at[rows, :], arrived.at[at])
        )
    for copy in copies:
        copy.start()
    return copies


def gated_kernel(count, place, *refs):
    tokens_in, grads_in, sources = refs[:count], refs[count : 2 * count], refs[2 * count :][:8]
    refs = refs[2 * count + 8 :]
    hidden_out, back_out, totals = refs[:count], refs[count : 2 * count], refs[2 * count :][:count]
    weights, arrived = refs[3 * count :]
    level, core = place[1], place[2]
    copies = []
    for at in range(8):
        target = weights.at[:, at * 128 : at * 128 + 128, :]
        copies.append(pltpu.make_async_copy(sources[at], target, arrived.at[at]))
        copies[-1].start()
    for step in range(2):
        for at in range(4):
            copies[step * 4 + at].wait()
        units = slice(step * GATED, (step + 1) * GATED)
        side = 1 - core if step else core
        pair = jnp.concatenate([weights[0, units, :], weights[1, units, :]])
        third = weights[2, units, :]
        for at in range(count):
            both = contract_last(tokens_in[at][...], pair)
            gate, up = both[:, :GATED], both[:, GATED:]
            grad_hidden = contract_last(grads_in[at][0], third)
            sig = lax.logistic(gate)
            swished = gate * sig
            hidden = (swished * up).astype(jnp.bfloat16)
            grad_gate = (grad_hidden * up * sig * (1.0 + gate * (1.0 - sig))).astype(jnp.bfloat16)
            grad_up = (grad_hidden * swished).astype(jnp.bfloat16)
            for turn in range(4):
                lanes = pl.ds(pl.multiple_of(((level ^ turn) * 2 + side) * 128, 128), 128)
                part = slice(turn * 128, turn * 128 + 128)
                hidden_out[at][0, :, lanes] = grad_gate[:, part]
                hidden_out[at][1, :, lanes] = grad_up[:, part]
                hidden_out[at][2, :, lanes] = hidden[:, part]
            added = jnp.dot(
                jnp.concatenate([grad_gate, grad_up], axis=1),
                pair,
                preferred_element_type=jnp.float32,
            )
            if step == 0:
                totals[at][...] = added
            else:
                back_out[at][...] = (totals[at][...] + added).astype(back_out[at].dtype)


def dp_block(mask, chunk):
    return pl.BlockSpec((1, chunk, D), lambda at, place: (place[0] ^ mask, 0, 0))


def gated(place, tokens_in, grads_all, masks, weights, kinds):
    count = len(tokens_in)
    chunk = tokens_in[0].shape[0]
    hidden = 8 * weights[0].shape[1]
    assert hidden == 2 * GATED
    whole = pl.BlockSpec((chunk, D), lambda at, place: (0, 0))
    anywhere = pl.BlockSpec(memory_space=pl.ANY)
    results = pl.pallas_call(
        functools.partial(gated_kernel, count),
        grid_spec=pltpu.PrefetchScalarGridSpec(
            num_scalar_prefetch=1,
            grid=(1,),
            in_specs=[whole] * count
            + [dp_block(mask, chunk) for mask in masks]
            + [anywhere] * len(weights),
            out_specs=[pl.BlockSpec((3, chunk, hidden), lambda at, place: (0, 0, 0))] * count
            + [whole] * count,
            scratch_shapes=[pltpu.VMEM((chunk, D), jnp.float32)] * count
            + [pltpu.VMEM((3, hidden, D), jnp.bfloat16), pltpu.SemaphoreType.DMA((8,))],
        ),
        out_shape=[jax.ShapeDtypeStruct((3, chunk, hidden), jnp.bfloat16)] * count
        + [jax.ShapeDtypeStruct((chunk, D), kind) for kind in kinds],
        compiler_params=pltpu.CompilerParams(vmem_limit_bytes=GRANT),
        cost_estimate=pl.CostEstimate(
            flops=10 * count * chunk * D * hidden,
            bytes_accessed=2 * D * (7 * count * chunk + 3 * hidden),
            transcendentals=count * chunk * hidden,
        ),
        name="gated",
    )(place, *tokens_in, *[grads_all] * count, *weights)
    return list(zip(results[:count], results[count:]))


def ffn_grads_kernel(place, *refs):
    tokens_in, grads_in, hidden_in = refs[0:4], refs[4:8], refs[8:12]
    grads_out, tokens_all, grads_all, hidden = refs[12:]
    chunk = tokens_in[0].shape[0]
    rows_of = [slice(at * chunk, (at + 1) * chunk) for at in range(4)]

    @pl.when(pl.program_id(0) == 0)
    def _():
        for at in range(4):
            tokens_all[rows_of[at], :] = tokens_in[at][...]
            grads_all[rows_of[at], :] = grads_in[at][0]

    for which in range(3):
        for at in range(4):
            hidden[which, rows_of[at], :] = hidden_in[at][which]
        other = tokens_all if which < 2 else grads_all
        grads_out[which] = rows_inner(hidden[which], other[...]).astype(jnp.bfloat16)


def ffn_grads(place, tokens_in, grads_in, hidden_in):
    chunk = tokens_in[0].shape[0]
    tokens = 4 * chunk
    hidden = hidden_in[0].shape[2]
    whole = pl.BlockSpec((chunk, D), lambda at, place: (0, 0))
    wide_low = pltpu.VMEM((tokens, D), jnp.bfloat16)
    return pl.pallas_call(
        ffn_grads_kernel,
        grid_spec=pltpu.PrefetchScalarGridSpec(
            num_scalar_prefetch=1,
            grid=(hidden // HIDDEN,),
            in_specs=[whole] * 4
            + [dp_block(mask, chunk) for mask in range(4)]
            + [pl.BlockSpec((3, chunk, HIDDEN), lambda at, place: (0, 0, at))] * 4,
            out_specs=pl.BlockSpec((3, HIDDEN, D), lambda at, place: (0, at, 0)),
            scratch_shapes=[wide_low, wide_low, pltpu.VMEM((3, tokens, HIDDEN), jnp.bfloat16)],
        ),
        out_shape=jax.ShapeDtypeStruct((3, hidden, D), jnp.bfloat16),
        compiler_params=pltpu.CompilerParams(vmem_limit_bytes=GRANT),
        cost_estimate=pl.CostEstimate(
            flops=6 * tokens * D * hidden,
            bytes_accessed=2 * D * (4 * tokens + 6 * hidden),
            transcendentals=0,
        ),
        name="ffn_grads",
    )(place, *tokens_in, *[grads_in] * 4, *hidden_in)


def down_kernel(place, *refs):
    hidden_in, attended, grads, sources = refs[:4], refs[4], refs[5], refs[6:14]
    outs, kept, sent, part, weights, arrived = refs[14:18], *refs[18:]
    core = place[2]
    copies = load_weights(place, sources, weights, arrived, 2)
    part[...] = rows_inner(attended[...], grads[...]).astype(jnp.bfloat16)
    for at in range(16):
        rows = slice(at * 32, at * 32 + 32)
        kept[rows, :] = part[pl.ds(pl.multiple_of(at * 64 + core * 32, 32), 32), :]
        sent[rows, :] = part[pl.ds(pl.multiple_of(at * 64 + (1 - core) * 32, 32), 32), :]
    for copy in copies:
        copy.wait()
    for at in range(4):
        outs[at][...] = jnp.dot(
            hidden_in[at][0], weights[...], preferred_element_type=jnp.float32
        ).astype(outs[at].dtype)


def down(place, hidden_in, weights, attended, grads):
    chunk = hidden_in[0].shape[1]
    hidden = hidden_in[0].shape[2]
    half = D // 2
    whole = pl.BlockSpec((chunk, D), lambda at, place: (0, 0))
    tall = pl.BlockSpec((half, D), lambda at, place: (0, 0))
    return pl.pallas_call(
        down_kernel,
        grid_spec=pltpu.PrefetchScalarGridSpec(
            num_scalar_prefetch=1,
            grid=(1,),
            in_specs=[pl.BlockSpec((1, chunk, hidden), lambda at, place: (2, 0, 0))] * 4
            + [whole] * 2
            + [pl.BlockSpec(memory_space=pl.ANY)] * len(weights),
            out_specs=[whole] * 4 + [tall] * 2,
            scratch_shapes=[
                pltpu.VMEM((D, D), jnp.bfloat16),
                pltpu.VMEM((hidden, D), jnp.bfloat16),
                pltpu.SemaphoreType.DMA((8,)),
            ],
        ),
        out_shape=[jax.ShapeDtypeStruct((chunk, D), jnp.float32)]
        + [jax.ShapeDtypeStruct((chunk, D), jnp.bfloat16)] * 3
        + [jax.ShapeDtypeStruct((half, D), jnp.bfloat16)] * 2,
        compiler_params=pltpu.CompilerParams(vmem_limit_bytes=GRANT),
        cost_estimate=pl.CostEstimate(
            flops=10 * chunk * D * hidden,
            bytes_accessed=2 * D * (11 * chunk + 2 * hidden),
            transcendentals=0,
        ),
        name="down",
    )(place, *hidden_in, attended, grads, *weights)


def local_split(
    inputs,
    variate_ids,
    time_ids,
    attn_gain,
    query_weight,
    key_weight,
    value_weight,
    out_weight,
    query_gain,
    key_gain,
    variate_bias,
    ffn_gain,
    gate_weight,
    up_weight,
    down_weight,
    out_grad,
):
    low = jnp.bfloat16
    wide = jnp.float32
    dp_at = lax.axis_index("dp")
    seq_at = lax.axis_index("seq")
    core = seq_at & 1
    level = seq_at >> 1
    batch = level >> 1
    parity = level & 1
    piece = inputs.shape[2]
    tokens = 8 * piece
    others = (1, 2, 3)
    swap_core = lambda values: swap_seq(values, 1)
    swap_level = lambda values, mask: swap_seq(values, 2 * mask)

    own_dy = out_grad[:, 0].reshape(2 * piece, D)

    gain_low = attn_gain.astype(low).astype(wide)
    weights_low = jnp.stack([query_weight, key_weight, value_weight], axis=1).astype(low)
    scaled = (weights_low.astype(wide) * gain_low[:, None, None]).astype(low)
    scaled = scaled.reshape(32, 3, 2, 512)
    with_gain = jnp.concatenate(
        [out_weight.astype(low), jnp.pad(ffn_gain.astype(low)[:, None], ((0, 0), (0, 127)))], axis=1
    )
    w_out = lax.all_gather(with_gain, ("dp", "seq"), axis=0, tiled=True)
    kinds = variate_ids[:, 0]
    times = time_ids[:, 0]
    ids = jnp.stack([kinds, times // 64, times % 64], axis=1).astype(low)
    ids = jnp.concatenate([ids, swap_core(ids)], axis=1)
    ids = jnp.pad(ids, ((0, 0), (0, 26), (0, 0)))

    def with_ids(weights_part, which):
        return jnp.concatenate(
            [weights_part.reshape(32, 1536), at_index(ids, which)], axis=1
        )

    same = with_ids(at_index(scaled, parity, 2), 1 - batch)
    cross_near = with_ids(at_index(scaled, 1 - parity, 2), batch)
    cross_far = with_ids(at_index(scaled, 1 - parity, 2), 1 - batch)
    moved = [swap_level((cross_near, same, cross_far)[mask - 1], mask) for mask in others]
    own_x = inputs[:, 0]
    near, far = at_index(own_x, batch), at_index(own_x, 1 - batch)
    (
        same,
        near,
        far,
        gate_local,
        up_local,
        down_local,
        query_gain,
        key_gain,
        variate_bias,
        *moved,
    ) = together(
        same,
        near,
        far,
        gate_weight,
        up_weight,
        down_weight,
        query_gain,
        key_gain,
        variate_bias,
        *moved,
    )
    ffn_local = lower(gate_local, up_local, down_local)

    place = jnp.stack([dp_at, level, core, 2 * parity + core]).astype(jnp.int32)
    rows = jnp.concatenate([same[:, :1536]] + [member[:, :1536] for member in moved])
    ids = jnp.stack([at_index(ids, batch)] + [member[:, 1536:] for member in moved])
    moved = [swap_dp(rows, mask) for mask in others]
    from_far = swap_level(far, 2)
    from_near = swap_level(near, 1)
    last = swap_level(from_far, 1)
    ids = jnp.stack([ids[:, :3], ids[:, 3:6]]).astype(wide)

    kinds = ids[:, :, 0].reshape(tokens, 1)
    times = (ids[:, :, 1] * 64.0 + ids[:, :, 2]).reshape(tokens, 1)
    lane = lax.broadcasted_iota(jnp.int32, (1, 128), 1)
    hot = jnp.where(
        lane < LSE_LANE, (kinds == lane % 8).astype(wide), jnp.where(lane < LSE_LANE + 3, 1.0, 0.0)
    ).astype(low)
    half = HD // 2
    frequency = 10000.0 ** (-(lane % half).astype(wide) / half)
    angles = times * frequency
    cos_part = jnp.cos(angles)
    sin_part = jnp.sin(angles) * jnp.where(lane % HD < half, -1.0, 1.0)
    q_gain = jnp.tile(query_gain, 2)[None, :]
    k_gain = jnp.tile(key_gain, 2)[None, :]
    group = 2 * parity + core
    gaps = at_index((variate_bias[0] - variate_bias[1]).reshape(4, 4), group)
    first, second, third = three_parts(gaps)
    bias_rows = jnp.where(
        lane < 8,
        first[:, None],
        jnp.where(
            lane < 16, second[:, None], jnp.where(lane < LSE_LANE, third[:, None], 0.0)
        ),
    ).reshape(2, 2, 128)

    (
        rows,
        ffn_local,
        near,
        from_near,
        from_far,
        last,
        cos_part,
        sin_part,
        dy_sent,
        hot,
        q_gain,
        k_gain,
        bias_rows,
        place,
        *moved,
    ) = together(
        rows,
        ffn_local,
        near,
        from_near,
        from_far,
        last,
        cos_part,
        sin_part,
        own_dy,
        hot,
        q_gain,
        k_gain,
        bias_rows,
        place,
        *moved,
    )

    dy_all = lax.all_gather(dy_sent, "dp", axis=0)

    pieces = [rows] + moved
    own = [near, from_near, from_far, last]
    ffn_near, ffn_far = swap_level(ffn_local, 1), swap_level(ffn_local, 2)
    sent = jnp.concatenate(
        [
            jnp.concatenate(
                [
                    jnp.where(
                        core == 0,
                        member[:, at * 512 + 256 : at * 512 + 512],
                        member[:, at * 512 : at * 512 + 256],
                    )
                    for at in range(3)
                ],
                axis=1,
            )
            for member in pieces
        ]
    )
    crossed, rows_crossed = together(swap_core(jnp.stack(own)), swap_core(sent))

    w_qkv, unit, qkv = front(place, pieces, rows_crossed, own, crossed)
    att_near, att_far, *saved = attend(qkv, cos_part, sin_part, hot, q_gain, k_gain, bias_rows)
    attended = (att_near, att_far)
    att_near, att_far, local_crossed = together(att_near, att_far, swap_core(ffn_local))

    part, crossed = together(att_near, swap_core(att_far))
    part, crossed = part.reshape(4, piece, 256), crossed.reshape(4, piece, 256)
    both = jnp.concatenate(
        [jnp.where(core == 0, part, crossed), jnp.where(core == 0, crossed, part)], axis=2
    )

    w_out, ffn_near, ffn_far, *arrived = together(
        w_out,
        ffn_near,
        ffn_far,
        both[0],
        *[swap_level(both[mask], mask) for mask in others],
    )
    gain_two = w_out[:, D].astype(wide)[None, :]
    blocks = [pick(arrived, level ^ at) for at in range(4)]
    own_att = jnp.concatenate(
        [
            jnp.concatenate([blocks[0], blocks[1]], axis=1),
            jnp.concatenate([blocks[2], blocks[3]], axis=1),
        ]
    )

    own_wide = own_x.reshape(2 * piece, D).astype(wide)
    middle = own_wide + product(own_att, w_out[:, :D])
    inv_two = rms_scale(middle)
    normed_two = (middle * inv_two * gain_two).astype(low)

    ffn_last, near_crossed, far_crossed, near_two, side_two, own_two, middle, own_att, gain_two, dy_all = together(
        swap_level(ffn_far, 1),
        swap_core(ffn_near),
        swap_core(ffn_far),
        swap_dp(normed_two, 1),
        swap_dp(normed_two, 2),
        normed_two,
        middle,
        own_att,
        gain_two,
        dy_all,
    )

    far_two = swap_dp(own_two, 3)
    w_ffn = [ffn_local, ffn_near, ffn_far, ffn_last]
    w_ffn += [local_crossed, near_crossed, far_crossed, swap_core(ffn_last)]
    (near_hidden, near_back), (side_hidden, side_back) = gated(
        place, [near_two, side_two], dy_all, (1, 2), w_ffn, (low, low)
    )
    far_two, near_hidden, near_back, side_hidden, side_back = together(
        far_two, near_hidden, near_back, side_hidden, side_back
    )

    near_back, side_back = swap_dp(near_back, 1), swap_dp(side_back, 2)
    (own_hidden, kept), (far_hidden, far_back) = gated(
        place, [own_two, far_two], dy_all, (0, 3), w_ffn, (wide, low)
    )
    own_hidden, kept, far_hidden, far_back, near_back, side_back = together(
        own_hidden, kept, far_hidden, far_back, near_back, side_back
    )
    hidden = [own_hidden, near_hidden, side_hidden, far_hidden]
    ffn_part = ffn_grads(place, [own_two, near_two, side_two, far_two], dy_all, hidden)
    ffn_part, kept, *moved = together(
        ffn_part, kept, near_back, side_back, swap_dp(far_back, 3)
    )
    ffn_shard = lax.psum_scatter(ffn_part, "seq", scatter_dimension=1, tiled=True)
    grad_middle, middle_low, gain_two_part, *blocks = middle_back(
        place, kept, moved, own_dy, middle, gain_two, w_out
    )

    arrived = [blocks[0]] + [swap_level(blocks[mask], mask) for mask in others]
    down_kept, *rest = down(place, hidden, w_ffn, own_att, middle_low)
    down_chunks, out_kept, out_sent = rest[:3], rest[3], rest[4]
    out_kept, out_sent, down_kept, *rest = together(
        out_kept, out_sent, down_kept, *down_chunks, *arrived
    )
    down_chunks, arrived = rest[:3], rest[3:]

    halves = [
        jnp.concatenate([member[:, :256] for member in arrived]),
        jnp.concatenate([member[:, 256:] for member in arrived]),
    ]

    def out_rows(to):
        rows = [
            lax.dynamic_slice_in_dim(member, to * 128, 128).astype(wide)
            for member in (out_kept, out_crossed)
        ]
        return (rows[0] + rows[1]).astype(low)

    kept, crossed, out_kept, out_crossed, *down_chunks = together(
        pick(halves, core),
        swap_core(pick(halves, 1 - core)),
        out_kept,
        swap_core(out_sent),
        *down_chunks,
    )
    out_parts = [out_rows(dp_at ^ mask) for mask in range(4)]
    grads = (kept, crossed)

    out_moved = [swap_dp(out_parts[mask], mask) for mask in others]
    dqkv, gain_sums, bias_sums = attend_back(
        qkv, saved, hot, grads, attended, cos_part, sin_part, q_gain, k_gain
    )
    dqkv, out_kept, last_chunk, *rest = together(
        dqkv,
        out_parts[0],
        down_chunks[2],
        swap_dp(down_chunks[0], 1),
        swap_dp(down_chunks[1], 2),
        *out_moved,
    )
    down_moved, out_moved = rest[:2], rest[2:]

    out_moved = [member.astype(wide) for member in out_moved]
    out_sum = (out_kept.astype(wide) + out_moved[0]) + (out_moved[1] + out_moved[2])
    back_kept, back_sent, kept, sent = tail(
        place, dqkv, w_qkv, unit, gain_sums, bias_sums, gain_two_part
    )
    back_kept, back_crossed, kept, crossed = together(
        back_kept, swap_core(back_sent), kept, swap_core(sent)
    )

    back = (back_kept + back_crossed.astype(wide)).reshape(4, piece, D)
    small_low = (kept[512:].astype(wide) + crossed[512:].astype(wide)).astype(low)

    def dp_message(to):
        return jnp.concatenate(
            [
                lax.dynamic_slice_in_dim(kept, to * 128, 128),
                lax.dynamic_slice_in_dim(crossed, to * 128, 128),
                small_low,
            ]
        )

    moved = [swap_dp(dp_message(dp_at ^ mask), mask) for mask in others]
    passed = back[2] + swap_level(back[3].astype(low), 1).astype(wide)
    passed = swap_level(passed.astype(low), 2)
    qkv_kept, kept, passed, near, ffn_shard, last_chunk, *moved = together(
        dp_message(dp_at), back[0], passed, back[1].astype(low), ffn_shard, last_chunk, *moved
    )

    moved = [member.astype(wide) for member in moved]
    total = qkv_kept.astype(wide)
    total = ((total + moved[0]) + (moved[1] + moved[2])).astype(low)
    small_low = total[256:]

    out_sum = out_sum.reshape(4, 32, D)
    ffn_sums = ffn_shard.astype(wide)

    def level_message(to):
        out_block = at_index(out_sum, to).astype(low)
        qkv_block = jnp.concatenate(
            [
                lax.dynamic_slice_in_dim(total, to * 32, 32),
                lax.dynamic_slice_in_dim(total, 128 + to * 32, 32),
            ]
        )
        return jnp.concatenate(
            [qkv_block[:, at * 256 : (at + 1) * 256] for at in range(3)]
            + [out_block[:, at * 256 : (at + 1) * 256] for at in range(4)]
            + [small_low[:, :256]]
        )

    mine, kept, near, passed, ffn_sums, last_chunk, *moved = together(
        level_message(level),
        kept,
        swap_level(near, 1),
        passed,
        ffn_sums,
        swap_dp(last_chunk, 3),
        *[swap_level(level_message(level ^ mask), mask) for mask in others],
    )
    *sums, input_grad, result, gain_grad, q_grad, k_grad, bias_grad, gain_two_grad = finish(
        place,
        mine,
        moved,
        attn_gain[:, None],
        [query_weight, key_weight, value_weight],
        [kept, near, passed],
        own_x,
        grad_middle.reshape(2, piece, D),
        [middle, down_kept] + down_moved + [last_chunk],
    )

    shape = (2, 1, piece, D)
    return (
        result.reshape(shape),
        input_grad.reshape(shape),
        gain_grad.reshape(32),
        sums[0],
        sums[1],
        sums[2],
        sums[3],
        q_grad.reshape(HD),
        k_grad.reshape(HD),
        bias_grad,
        gain_two_grad.reshape(32),
        ffn_sums[0],
        ffn_sums[1],
        ffn_sums[2],
    )


def solution(mesh):
    placed = (
        P(None, "dp", "seq", None),
        P(None, "dp", "seq"),
        P(None, "dp", "seq"),
        P(("dp", "seq")),
        P(("dp", "seq"), None),
        P(("dp", "seq"), None),
        P(("dp", "seq"), None),
        P(("dp", "seq"), None),
        P(),
        P(),
        P(),
        P(("dp", "seq")),
        P(("dp", "seq"), None),
        P(("dp", "seq"), None),
        P(("dp", "seq"), None),
        P(None, "dp", "seq", None),
    )
    split = mesh.shape["dp"] == 4 and mesh.shape["seq"] == 8
    return jax.shard_map(
        local_split if split else local,
        mesh=mesh,
        in_specs=placed,
        out_specs=(
            P(None, "dp", "seq", None),
            P(None, "dp", "seq", None),
            P(("dp", "seq")),
            P(("dp", "seq"), None),
            P(("dp", "seq"), None),
            P(("dp", "seq"), None),
            P(("dp", "seq"), None),
            P(),
            P(),
            P(),
            P(("dp", "seq")),
            P(("dp", "seq"), None),
            P(("dp", "seq"), None),
            P(("dp", "seq"), None),
        ),
        check_vma=False,
    )
```

```python
import functools
import math

import jax
import jax.numpy as jnp
from jax import lax
from jax.experimental import pallas as pl
from jax.experimental.pallas import tpu as pltpu
from jax.sharding import PartitionSpec as P

D = 1024
H = 16
HD = 64
FF = 4096


epsilon = 1e-06
lowest = -1e30


def rms_scale(values):
    return lax.rsqrt(jnp.mean(values * values, axis=-1, keepdims=True) + epsilon)


def norm_back(values, inv_rms, gain_vec, upstream):
    weighted = upstream * gain_vec
    inner_mean = jnp.mean(weighted * values, axis=-1, keepdims=True)
    return inv_rms * weighted - values * (inv_rms * inv_rms * inv_rms) * inner_mean


def rotation(positions):
    half_dim = HD // 2
    frequency = 10000.0 ** (-jnp.arange(half_dim).astype(jnp.float32) / half_dim)
    angles = positions.astype(jnp.float32)[..., None] * frequency
    return (jnp.cos(angles)[..., None, :], jnp.sin(angles)[..., None, :])


def rotate(values, cos_part, sin_part):
    half_dim = values.shape[-1] // 2
    first_half = values[..., :half_dim]
    second_half = values[..., half_dim:]
    return jnp.concatenate(
        [
            first_half * cos_part - second_half * sin_part,
            first_half * sin_part + second_half * cos_part,
        ],
        axis=-1,
    )


def rotate_back(upstream, cos_part, sin_part):
    half_dim = upstream.shape[-1] // 2
    first_half = upstream[..., :half_dim]
    second_half = upstream[..., half_dim:]
    return jnp.concatenate(
        [
            first_half * cos_part + second_half * sin_part,
            second_half * cos_part - first_half * sin_part,
        ],
        axis=-1,
    )


def product(left_side, right_side):
    return jnp.dot(left_side, right_side, preferred_element_type=jnp.float32)


def times_transposed(left_side, right_side):
    return lax.dot_general(
        left_side, right_side, (((1,), (1,)), ((), ())), preferred_element_type=jnp.float32
    )


def rows_inner(left_side, right_side):
    return lax.dot_general(
        left_side, right_side, (((0,), (0,)), ((), ())), preferred_element_type=jnp.float32
    )


def score_block(queries, key_rows, query_kinds, key_kinds, variate_bias):
    raw_scores = jnp.einsum(
        "sqhe,skhe->shqk", queries, key_rows, preferred_element_type=jnp.float32
    ) * HD ** (-0.5)
    same_kind = query_kinds[:, None, :, None] == key_kinds[:, None, None, :]
    scores = raw_scores + jnp.where(
        same_kind, variate_bias[0][None, :, None, None], variate_bias[1][None, :, None, None]
    )
    return (scores, same_kind)


def forward_piece(queries, query_kinds, variate_bias, carried, pieces):
    piece_keys, piece_values, piece_kinds = pieces
    seq_count = piece_keys.shape[0]
    piece_len = piece_keys.shape[1]
    block_size = math.gcd(piece_len, 512)

    def forward_advance(block_index, totals):
        running_max, running_total, running_sum = totals
        offset = block_index * block_size
        key_rows = lax.dynamic_slice_in_dim(piece_keys, offset, block_size, 1).reshape(
            seq_count, block_size, H, HD
        )
        value_rows = lax.dynamic_slice_in_dim(piece_values, offset, block_size, 1).reshape(
            seq_count, block_size, H, HD
        )
        kind_rows = lax.dynamic_slice_in_dim(piece_kinds, offset, block_size, 1)
        scores, same_kind = score_block(queries, key_rows, query_kinds, kind_rows, variate_bias)
        new_max = jnp.maximum(running_max, jnp.max(scores, axis=-1))
        factor = jnp.exp(running_max - new_max)
        exp_scores = jnp.exp(scores - new_max[..., None])
        running_total = running_total * factor + jnp.sum(exp_scores, axis=-1)
        running_sum = running_sum * factor[..., None] + jnp.einsum(
            "shqk,skhe->shqe",
            exp_scores.astype(jnp.bfloat16),
            value_rows,
            preferred_element_type=jnp.float32,
        )
        return (new_max, running_total, running_sum)

    return lax.fori_loop(0, piece_len // block_size, forward_advance, carried)


def back_piece(context, carried, pieces):
    queries, query_kinds, grad_out, log_total, delta_row, variate_bias = context
    piece_keys, piece_values, piece_kinds = pieces
    seq_count = piece_keys.shape[0]
    piece_len = piece_keys.shape[1]
    block_size = math.gcd(piece_len, 512)
    score_scale = HD ** (-0.5)

    def back_advance(block_index, totals):
        offset = block_index * block_size
        key_rows = lax.dynamic_slice_in_dim(piece_keys, offset, block_size, 1).reshape(
            seq_count, block_size, H, HD
        )
        value_rows = lax.dynamic_slice_in_dim(piece_values, offset, block_size, 1).reshape(
            seq_count, block_size, H, HD
        )
        kind_rows = lax.dynamic_slice_in_dim(piece_kinds, offset, block_size, 1)
        scores, same_kind = score_block(queries, key_rows, query_kinds, kind_rows, variate_bias)
        attn_prob = jnp.exp(scores - log_total[..., None])
        grad_prob = jnp.einsum(
            "sqhe,skhe->shqk", grad_out, value_rows, preferred_element_type=jnp.float32
        )
        grad_score = attn_prob * (grad_prob - delta_row[..., None])
        bias_step = jnp.stack(
            [
                jnp.sum(jnp.where(same_kind, grad_score, 0.0), axis=(0, 2, 3)),
                jnp.sum(jnp.where(same_kind, 0.0, grad_score), axis=(0, 2, 3)),
            ]
        )
        score_low = grad_score.astype(jnp.bfloat16)
        query_grad = (
            totals[0]
            + jnp.einsum("shqk,skhe->shqe", score_low, key_rows, preferred_element_type=jnp.float32)
            * score_scale
        )
        key_part = (
            jnp.einsum("shqk,sqhe->skhe", score_low, queries, preferred_element_type=jnp.float32)
            * score_scale
        ).reshape(seq_count, block_size, D)
        value_part = jnp.einsum(
            "shqk,sqhe->skhe",
            attn_prob.astype(jnp.bfloat16),
            grad_out,
            preferred_element_type=jnp.float32,
        ).reshape(seq_count, block_size, D)
        key_total = lax.dynamic_update_slice_in_dim(
            totals[2],
            lax.dynamic_slice_in_dim(totals[2], offset, block_size, 1) + key_part,
            offset,
            1,
        )
        value_total = lax.dynamic_update_slice_in_dim(
            totals[3],
            lax.dynamic_slice_in_dim(totals[3], offset, block_size, 1) + value_part,
            offset,
            1,
        )
        return (query_grad, totals[1] + bias_step, key_total, value_total)

    return lax.fori_loop(0, piece_len // block_size, back_advance, carried)


def local(
    inputs,
    variate_ids,
    time_ids,
    attn_gain,
    query_weight,
    key_weight,
    value_weight,
    out_weight,
    query_gain,
    key_gain,
    variate_bias,
    ffn_gain,
    gate_weight,
    up_weight,
    down_weight,
    out_grad,
):
    seq_count = inputs.shape[1]
    tok_count = inputs.shape[2]
    row_count = seq_count * tok_count
    full_grads = [
        jnp.zeros(extent, jnp.float32)
        for extent in ((D,), (D, D), (D, D), (D, D), (D, D), (D,), (FF, D), (FF, D), (FF, D))
    ]
    small_grads = [
        jnp.zeros((HD,), jnp.float32),
        jnp.zeros((HD,), jnp.float32),
        jnp.zeros((2, H), jnp.float32),
    ]
    shard_total = None
    small_total = None
    outputs_list = []
    input_grads = []
    weights_now = None
    for micro_index in range(inputs.shape[0]):
        weights_now = (
            lax.all_gather(attn_gain.astype(jnp.bfloat16), ("dp", "seq"), axis=0, tiled=True),
            lax.all_gather(query_weight.astype(jnp.bfloat16), ("dp", "seq"), axis=0, tiled=True),
            lax.all_gather(key_weight.astype(jnp.bfloat16), ("dp", "seq"), axis=0, tiled=True),
            lax.all_gather(value_weight.astype(jnp.bfloat16), ("dp", "seq"), axis=0, tiled=True),
            lax.all_gather(out_weight.astype(jnp.bfloat16), ("dp", "seq"), axis=0, tiled=True),
            lax.all_gather(ffn_gain.astype(jnp.bfloat16), ("dp", "seq"), axis=0, tiled=True),
            lax.all_gather(gate_weight.astype(jnp.bfloat16), ("dp", "seq"), axis=0, tiled=True),
            lax.all_gather(up_weight.astype(jnp.bfloat16), ("dp", "seq"), axis=0, tiled=True),
            lax.all_gather(down_weight.astype(jnp.bfloat16), ("dp", "seq"), axis=0, tiled=True),
        )
        gain_one, w_query, w_key, w_value, w_out, gain_two, w_gate, w_up, w_down = weights_now
        hidden_in = inputs[micro_index].astype(jnp.float32).reshape(row_count, D)
        kinds_now = variate_ids[micro_index].astype(jnp.bfloat16)
        cos_part, sin_part = rotation(time_ids[micro_index])
        inv_one = rms_scale(hidden_in)
        normed = (hidden_in * inv_one * gain_one.astype(jnp.float32)).astype(jnp.bfloat16)
        query_raw = product(normed, w_query).reshape(seq_count, tok_count, H, HD)
        key_raw = product(normed, w_key).reshape(seq_count, tok_count, H, HD)
        value_flat = product(normed, w_value).astype(jnp.bfloat16).reshape(seq_count, tok_count, D)
        inv_query = rms_scale(query_raw)
        query_rot = rotate(query_raw * inv_query * query_gain, cos_part, sin_part).astype(
            jnp.bfloat16
        )
        inv_key = rms_scale(key_raw)
        key_rot = rotate(key_raw * inv_key * key_gain, cos_part, sin_part).astype(jnp.bfloat16)
        key_flat = key_rot.reshape(seq_count, tok_count, D)
        initial = (
            jnp.full((seq_count, H, tok_count), lowest, jnp.float32),
            jnp.zeros((seq_count, H, tok_count), jnp.float32),
            jnp.zeros((seq_count, H, tok_count, HD), jnp.float32),
        )
        final_max, final_total, final_sum = forward_piece(
            query_rot,
            kinds_now,
            variate_bias,
            initial,
            (
                lax.all_gather(key_flat, "seq", axis=1, tiled=True),
                lax.all_gather(value_flat, "seq", axis=1, tiled=True),
                lax.all_gather(kinds_now, "seq", axis=1, tiled=True),
            ),
        )
        log_total = final_max + jnp.log(final_total)
        attended = jnp.transpose(final_sum / final_total[..., None], (0, 2, 1, 3))
        attended_low = attended.reshape(row_count, D).astype(jnp.bfloat16)
        middle = hidden_in + product(attended_low, w_out)
        inv_two = rms_scale(middle)
        normed_two = (middle * inv_two * gain_two.astype(jnp.float32)).astype(jnp.bfloat16)
        gate_pre = times_transposed(normed_two, w_gate)
        up_pre = times_transposed(normed_two, w_up)
        gate_sig = jax.nn.sigmoid(gate_pre)
        hidden_low = (gate_pre * gate_sig * up_pre).astype(jnp.bfloat16)
        result = middle + product(hidden_low, w_down)
        outputs_list.append(result.reshape(seq_count, tok_count, D).astype(jnp.bfloat16))
        gain_one, w_query, w_key, w_value, w_out, gain_two, w_gate, w_up, w_down = (
            lax.all_gather(attn_gain.astype(jnp.bfloat16), ("dp", "seq"), axis=0, tiled=True),
            lax.all_gather(query_weight.astype(jnp.bfloat16), ("dp", "seq"), axis=0, tiled=True),
            lax.all_gather(key_weight.astype(jnp.bfloat16), ("dp", "seq"), axis=0, tiled=True),
            lax.all_gather(value_weight.astype(jnp.bfloat16), ("dp", "seq"), axis=0, tiled=True),
            lax.all_gather(out_weight.astype(jnp.bfloat16), ("dp", "seq"), axis=0, tiled=True),
            lax.all_gather(ffn_gain.astype(jnp.bfloat16), ("dp", "seq"), axis=0, tiled=True),
            lax.all_gather(gate_weight.astype(jnp.bfloat16), ("dp", "seq"), axis=0, tiled=True),
            lax.all_gather(up_weight.astype(jnp.bfloat16), ("dp", "seq"), axis=0, tiled=True),
            lax.all_gather(down_weight.astype(jnp.bfloat16), ("dp", "seq"), axis=0, tiled=True),
        )
        grad_in = out_grad[micro_index].astype(jnp.float32).reshape(row_count, D)
        grad_low = grad_in.astype(jnp.bfloat16)
        full_grads[8] = rows_inner(hidden_low, grad_low)
        grad_hidden = times_transposed(grad_low, w_down)
        grad_gate = (grad_hidden * up_pre * gate_sig * (1.0 + gate_pre * (1.0 - gate_sig))).astype(
            jnp.bfloat16
        )
        grad_up = (grad_hidden * gate_pre * gate_sig).astype(jnp.bfloat16)
        full_grads[6] = rows_inner(grad_gate, normed_two)
        full_grads[7] = rows_inner(grad_up, normed_two)
        grad_normed_two = product(grad_gate, w_gate) + product(grad_up, w_up)
        full_grads[5] = jnp.sum(grad_normed_two * middle * inv_two, axis=0)
        grad_middle = grad_in + norm_back(
            middle, inv_two, gain_two.astype(jnp.float32), grad_normed_two
        )
        grad_middle_low = grad_middle.astype(jnp.bfloat16)
        full_grads[4] = rows_inner(attended_low, grad_middle_low)
        grad_attended = (
            times_transposed(grad_middle_low, w_out)
            .astype(jnp.bfloat16)
            .reshape(seq_count, tok_count, H, HD)
        )
        delta_row = jnp.transpose(
            jnp.sum(grad_attended.astype(jnp.float32) * attended, axis=-1), (0, 2, 1)
        )
        context = (query_rot, kinds_now, grad_attended, log_total, delta_row, variate_bias)
        base_carry = (
            jnp.zeros((seq_count, H, tok_count, HD), jnp.float32),
            jnp.zeros((2, H), jnp.float32),
        )
        length_all = tok_count * lax.axis_size("seq")
        wide_carry = (
            jnp.zeros((seq_count, length_all, D), jnp.float32),
            jnp.zeros((seq_count, length_all, D), jnp.float32),
        )
        grad_query_heads, grad_bias, key_all, value_all = back_piece(
            context,
            base_carry + wide_carry,
            (
                lax.all_gather(key_flat, "seq", axis=1, tiled=True),
                lax.all_gather(value_flat, "seq", axis=1, tiled=True),
                lax.all_gather(kinds_now, "seq", axis=1, tiled=True),
            ),
        )
        grad_key, grad_value = (
            lax.psum_scatter(
                key_all.astype(jnp.bfloat16), "seq", scatter_dimension=1, tiled=True
            ).astype(jnp.float32),
            lax.psum_scatter(
                value_all.astype(jnp.bfloat16), "seq", scatter_dimension=1, tiled=True
            ).astype(jnp.float32),
        )
        grad_key = grad_key.reshape(seq_count, tok_count, H, HD)
        grad_value_low = grad_value.reshape(row_count, D).astype(jnp.bfloat16)
        small_grads[2] = grad_bias
        grad_query = jnp.transpose(grad_query_heads, (0, 2, 1, 3))
        grad_query_norm = rotate_back(grad_query, cos_part, sin_part)
        small_grads[0] = jnp.sum(grad_query_norm * query_raw * inv_query, axis=(0, 1, 2))
        grad_query_low = (
            norm_back(query_raw, inv_query, query_gain, grad_query_norm)
            .reshape(row_count, D)
            .astype(jnp.bfloat16)
        )
        grad_key_norm = rotate_back(grad_key, cos_part, sin_part)
        small_grads[1] = jnp.sum(grad_key_norm * key_raw * inv_key, axis=(0, 1, 2))
        grad_key_low = (
            norm_back(key_raw, inv_key, key_gain, grad_key_norm)
            .reshape(row_count, D)
            .astype(jnp.bfloat16)
        )
        full_grads[1] = rows_inner(normed, grad_query_low)
        full_grads[2] = rows_inner(normed, grad_key_low)
        full_grads[3] = rows_inner(normed, grad_value_low)
        grad_normed = (
            times_transposed(grad_query_low, w_query)
            + times_transposed(grad_key_low, w_key)
            + times_transposed(grad_value_low, w_value)
        )
        full_grads[0] = jnp.sum(grad_normed * hidden_in * inv_one, axis=0)
        input_total = grad_middle + norm_back(
            hidden_in, inv_one, gain_one.astype(jnp.float32), grad_normed
        )
        input_grads.append(input_total.reshape(seq_count, tok_count, D).astype(jnp.bfloat16))
        shards = (
            lax.psum_scatter(full_grads[0], ("dp", "seq"), scatter_dimension=0, tiled=True),
            lax.psum_scatter(full_grads[1], ("dp", "seq"), scatter_dimension=0, tiled=True),
            lax.psum_scatter(full_grads[2], ("dp", "seq"), scatter_dimension=0, tiled=True),
            lax.psum_scatter(full_grads[3], ("dp", "seq"), scatter_dimension=0, tiled=True),
            lax.psum_scatter(full_grads[4], ("dp", "seq"), scatter_dimension=0, tiled=True),
            lax.psum_scatter(full_grads[5], ("dp", "seq"), scatter_dimension=0, tiled=True),
            lax.psum_scatter(full_grads[6], ("dp", "seq"), scatter_dimension=0, tiled=True),
            lax.psum_scatter(full_grads[7], ("dp", "seq"), scatter_dimension=0, tiled=True),
            lax.psum_scatter(full_grads[8], ("dp", "seq"), scatter_dimension=0, tiled=True),
        )
        summed = lax.psum((small_grads[0], small_grads[1], small_grads[2]), ("dp", "seq"))
        shards, summed = (list(shards), list(summed))
        if shard_total is None:
            shard_total = shards
            small_total = summed
        else:
            shard_total = [
                earlier_part + later_part for earlier_part, later_part in zip(shard_total, shards)
            ]
            small_total = [
                earlier_part + later_part for earlier_part, later_part in zip(small_total, summed)
            ]
        full_grads = [jnp.zeros_like(member) for member in full_grads]
        small_grads = [jnp.zeros_like(member) for member in small_grads]
    return (
        jnp.stack(outputs_list),
        jnp.stack(input_grads),
        shard_total[0],
        shard_total[1],
        shard_total[2],
        shard_total[3],
        shard_total[4],
        small_total[0],
        small_total[1],
        small_total[2],
        shard_total[5],
        shard_total[6],
        shard_total[7],
        shard_total[8],
    )


def swap_seq(values, mask):
    return lax.ppermute(values, "seq", [(at, at ^ mask) for at in range(8)])


def swap_dp(values, mask):
    return lax.ppermute(values, "dp", [(at, at ^ mask) for at in range(4)])


def pick(pieces, which):
    chosen = pieces[-1]
    for at in range(len(pieces) - 2, -1, -1):
        chosen = jnp.where(which == at, pieces[at], chosen)
    return chosen


def ordered(pieces, own):
    return jnp.stack([pick(pieces, own ^ at) for at in range(len(pieces))])


def together(*values):
    return lax.optimization_barrier(values)


def at_index(values, index, axis=0):
    return lax.dynamic_index_in_dim(values, index, axis, keepdims=False)


def contract_last(left_side, right_side):
    return lax.dot_general(
        left_side, right_side, (((1,), (1,)), ((), ())), preferred_element_type=jnp.float32
    )


def head_sums(values, block):
    first = values.astype(jnp.bfloat16)
    second = (values - first.astype(jnp.float32)).astype(jnp.bfloat16)
    return jnp.dot(first, block, preferred_element_type=jnp.float32) + jnp.dot(
        second, block, preferred_element_type=jnp.float32
    )


def head_block(scale):
    rows = lax.broadcasted_iota(jnp.int32, (128, 128), 0) // HD
    columns = lax.broadcasted_iota(jnp.int32, (128, 128), 1) // HD
    return jnp.where(rows == columns, scale, 0.0).astype(jnp.bfloat16)


def rope_partner(values):
    lane = lax.broadcasted_iota(jnp.int32, values.shape, 1)
    return jnp.where(
        lane % HD < HD // 2, pltpu.roll(values, 128 - HD // 2, 1), pltpu.roll(values, HD // 2, 1)
    )


def three_parts(values):
    first = values.astype(jnp.bfloat16).astype(jnp.float32)
    second = (values - first).astype(jnp.bfloat16).astype(jnp.float32)
    third = (values - first - second).astype(jnp.bfloat16).astype(jnp.float32)
    return first, second, third


GRANT = 60 << 20
BQ = 1024
BK = 1024
LSE_LANE = 24


def attend_kernel(
    q_in,
    k_in,
    v_in,
    cos_in,
    sin_in,
    hot_in,
    q_gain,
    k_gain,
    bias_in,
    near_out,
    far_out,
    qs_out,
    ks_out,
    vs_out,
    ext_out,
    kx,
    vx,
):
    mean_block = head_block(1.0 / HD)

    def prepare(raw, gain):
        inv = lax.rsqrt(head_sums(raw * raw, mean_block) + epsilon)
        scaled = raw * inv * gain
        return scaled * cos_in[...] + rope_partner(scaled) * sin_in[...]

    qs_out[...] = (
        prepare(q_in[...], q_gain[...]).astype(jnp.bfloat16).astype(jnp.float32) * HD**-0.5
    ).astype(jnp.bfloat16)
    keys = prepare(k_in[...], k_gain[...]).astype(jnp.bfloat16)
    ks_out[...] = keys
    kx[:, :128] = keys
    kx[:, 128:] = hot_in[...]
    values = v_in[...].astype(jnp.bfloat16)
    vs_out[...] = values
    vx[:, :128] = values
    vx[:, 128:] = jnp.ones(values.shape, jnp.bfloat16)
    lane = lax.broadcasted_iota(jnp.int32, (BQ, 128), 1)

    def step(block, carry):
        rows = pl.ds(pl.multiple_of(block * BQ, BQ), BQ)
        queries = qs_out[rows, :].astype(jnp.float32)
        hot = hot_in[rows, :].astype(jnp.float32)
        results = []
        for head in range(2):
            mine = jnp.where(lane // HD == head, queries, 0.0).astype(jnp.bfloat16)
            extra = hot * bias_in[0, head : head + 1, :]
            scores = contract_last(
                jnp.concatenate([mine, extra.astype(jnp.bfloat16)], axis=1), kx[...]
            )
            weights = jnp.exp(scores).astype(jnp.bfloat16)
            summed = jnp.dot(weights, vx[...], preferred_element_type=jnp.float32)
            total = summed[:, 128:]
            results.append(summed[:, :128] / total)
            first, second, third = three_parts(-jnp.log(total))
            extra = jnp.where(lane == LSE_LANE, first, extra)
            extra = jnp.where(lane == LSE_LANE + 1, second, extra)
            extra = jnp.where(lane == LSE_LANE + 2, third, extra)
            ext_out[head, rows, :] = extra.astype(jnp.bfloat16)
        result = jnp.where(lane < HD, results[0], results[1]).astype(jnp.bfloat16)
        half = near_out.shape[0]
        near_out[...] = result[:half]
        far_out[...] = result[half:]
        return carry

    lax.fori_loop(0, q_in.shape[0] // BQ, step, 0)


def attend_back_kernel(
    q_in,
    k_in,
    qs_in,
    ks_in,
    vs_in,
    ext_in,
    hot_in,
    grad_near,
    grad_far,
    att_near,
    att_far,
    cos_in,
    sin_in,
    q_gain,
    k_gain,
    out,
    gain_out,
    bias_out,
    kx,
    vx,
    kt,
    qx,
    qg,
    gx,
    dqt,
    dk_sum,
    dv_sum,
):
    tokens = q_in.shape[0]
    lane = lax.broadcasted_iota(jnp.int32, (tokens, 128), 1)
    keys = ks_in[...]
    kx[:, :128] = keys
    kx[:, 128:] = hot_in[...]
    kt[...] = keys.astype(jnp.float32).T.astype(jnp.bfloat16)
    vx[:, :128] = vs_in[...]
    vx[:, 128:] = jnp.where(lane % HD < 3, 1.0, 0.0).astype(jnp.bfloat16)
    grads = jnp.concatenate([grad_near[...], grad_far[...]]).astype(jnp.float32)
    results = jnp.concatenate([att_near[...], att_far[...]]).astype(jnp.float32)
    delta = head_sums(grads * results, head_block(1.0))
    first, second, third = three_parts(-delta)
    parts = jnp.where(
        lane % HD == 0,
        first,
        jnp.where(lane % HD == 1, second, jnp.where(lane % HD == 2, third, 0.0)),
    )
    queries = qs_in[...].astype(jnp.float32)
    for head in range(2):
        own = lane // HD == head
        mine = jnp.where(own, queries, 0.0).astype(jnp.bfloat16)
        qx[head, :, :128] = mine
        qx[head, :, 128:] = ext_in[head]
        qg[head, :, :128] = mine
        qg[head, :, 128:] = hot_in[...]
        gx[head, :, :128] = jnp.where(own, grads, 0.0).astype(jnp.bfloat16)
        gx[head, :, 128:] = jnp.where(own, parts, 0.0).astype(jnp.bfloat16)
    dqt[...] = jnp.zeros(dqt.shape, jnp.float32)
    block_lane = lax.broadcasted_iota(jnp.int32, (BK, 128), 1)
    counted = jnp.where((block_lane < 8) | (block_lane == LSE_LANE), 1.0, 0.0)

    def step(block, carry):
        rows = pl.ds(pl.multiple_of(block * BK, BK), BK)
        hot = hot_in[rows, :].astype(jnp.float32) * counted
        dk_parts = []
        dv_parts = []
        bias_parts = []
        for head in range(2):
            probs = jnp.exp(contract_last(kx[rows, :], qx[head]))
            dscores = (probs * contract_last(vx[rows, :], gx[head])).astype(jnp.bfloat16)
            dv_parts.append(
                jnp.dot(
                    probs.astype(jnp.bfloat16), gx[head, :, :128], preferred_element_type=jnp.float32
                )
            )
            wide = jnp.dot(dscores, qg[head], preferred_element_type=jnp.float32)
            dk_parts.append(wide[:, :128])
            bias_parts.append(jnp.sum(wide[:, 128:] * hot, axis=0, keepdims=True))
            head_rows = pl.ds(head * HD, HD)
            dqt[head_rows, :] += jnp.dot(
                kt[head_rows, rows], dscores, preferred_element_type=jnp.float32
            )
        dk_sum[rows, :] = dk_parts[0] + dk_parts[1]
        dv_sum[rows, :] = dv_parts[0] + dv_parts[1]
        return (carry[0] + bias_parts[0], carry[1] + bias_parts[1])

    zero = jnp.zeros((1, 128), jnp.float32)
    sums = lax.fori_loop(0, tokens // BK, step, (zero, zero))
    bias_out[0, 0:1, :] = sums[0]
    bias_out[0, 1:2, :] = sums[1]
    mean_block = head_block(1.0 / HD)

    def finish(raw, upstream, gain):
        inv = lax.rsqrt(head_sums(raw * raw, mean_block) + epsilon)
        normed = upstream * cos_in[...] - rope_partner(upstream) * sin_in[...]
        gain_grad = jnp.sum(normed * raw * inv, axis=0, keepdims=True)
        weighted = normed * gain
        inner = head_sums(weighted * raw, mean_block)
        return inv * weighted - raw * (inv * inv * inv) * inner, gain_grad

    dq, dq_gain = finish(q_in[...], dqt[...].T * HD**-0.5, q_gain[...])
    dk, dk_gain = finish(k_in[...], dk_sum[...], k_gain[...])
    out[0] = dq.astype(jnp.bfloat16)
    out[1] = dk.astype(jnp.bfloat16)
    out[2] = dv_sum[...].astype(jnp.bfloat16)
    gain_out[0, 0:1, :] = dq_gain
    gain_out[0, 1:2, :] = dk_gain


def attend(qkv, cos_part, sin_part, hot, q_gain, k_gain, bias_rows):
    tokens = qkv.shape[0]
    column = lambda shift: pl.BlockSpec((tokens, 128), lambda pair: (0, pair + shift))
    half = pl.BlockSpec((tokens // 2, 128), lambda pair: (0, pair))
    whole = pl.BlockSpec((tokens, 128), lambda pair: (0, 0))
    line = pl.BlockSpec((1, 128), lambda pair: (0, 0))
    low = lambda: jax.ShapeDtypeStruct((tokens, 256), jnp.bfloat16)
    return pl.pallas_call(
        attend_kernel,
        grid=(2,),
        in_specs=[
            column(0),
            column(2),
            column(4),
            whole,
            whole,
            whole,
            line,
            line,
            pl.BlockSpec((1, 2, 128), lambda pair: (pair, 0, 0)),
        ],
        out_specs=[
            half,
            half,
            column(0),
            column(0),
            column(0),
            pl.BlockSpec((2, tokens, 128), lambda pair: (pair, 0, 0)),
        ],
        out_shape=[
            jax.ShapeDtypeStruct((tokens // 2, 256), jnp.bfloat16),
            jax.ShapeDtypeStruct((tokens // 2, 256), jnp.bfloat16),
            low(),
            low(),
            low(),
            jax.ShapeDtypeStruct((4, tokens, 128), jnp.bfloat16),
        ],
        scratch_shapes=[
            pltpu.VMEM((tokens, 256), jnp.bfloat16),
            pltpu.VMEM((tokens, 256), jnp.bfloat16),
        ],
        compiler_params=pltpu.CompilerParams(vmem_limit_bytes=GRANT),
        name="attend",
    )(qkv, qkv, qkv, cos_part, sin_part, hot, q_gain, k_gain, bias_rows)


def attend_back(qkv, saved, hot, grads, attended, cos_part, sin_part, q_gain, k_gain):
    queries, keys, values, extra = saved
    tokens = qkv.shape[0]
    column = lambda shift: pl.BlockSpec((tokens, 128), lambda pair: (0, pair + shift))
    half = pl.BlockSpec((tokens // 2, 128), lambda pair: (0, pair))
    whole = pl.BlockSpec((tokens, 128), lambda pair: (0, 0))
    line = pl.BlockSpec((1, 128), lambda pair: (0, 0))
    two = pl.BlockSpec((1, 2, 128), lambda pair: (pair, 0, 0))
    wide = pltpu.VMEM((tokens, 256), jnp.bfloat16)
    both = pltpu.VMEM((2, tokens, 256), jnp.bfloat16)
    return pl.pallas_call(
        attend_back_kernel,
        grid=(2,),
        in_specs=[
            column(0),
            column(2),
            column(0),
            column(0),
            column(0),
            pl.BlockSpec((2, tokens, 128), lambda pair: (pair, 0, 0)),
            whole,
            half,
            half,
            half,
            half,
            whole,
            whole,
            line,
            line,
        ],
        out_specs=[pl.BlockSpec((3, tokens, 128), lambda pair: (0, 0, pair)), two, two],
        out_shape=[
            jax.ShapeDtypeStruct((3, tokens, 256), jnp.bfloat16),
            jax.ShapeDtypeStruct((2, 2, 128), jnp.float32),
            jax.ShapeDtypeStruct((2, 2, 128), jnp.float32),
        ],
        scratch_shapes=[
            wide,
            wide,
            pltpu.VMEM((128, tokens), jnp.bfloat16),
            both,
            both,
            both,
            pltpu.VMEM((128, tokens), jnp.float32),
            pltpu.VMEM((tokens, 128), jnp.float32),
            pltpu.VMEM((tokens, 128), jnp.float32),
        ],
        compiler_params=pltpu.CompilerParams(vmem_limit_bytes=GRANT),
        cost_estimate=pl.CostEstimate(
            flops=40 * tokens * tokens * 256,
            bytes_accessed=tokens * 256 * 40,
            transcendentals=4 * tokens * tokens,
        ),
        name="attend_back",
    )(
        qkv,
        qkv,
        queries,
        keys,
        values,
        extra,
        hot,
        *grads,
        *attended,
        cos_part,
        sin_part,
        q_gain,
        k_gain,
    )


def as_column(line):
    count = line.shape[1]
    rows = lax.broadcasted_iota(jnp.int32, (count, count), 0)
    columns = lax.broadcasted_iota(jnp.int32, (count, count), 1)
    return jnp.sum(jnp.where(rows == columns, line, 0.0), axis=1, keepdims=True)


def head_kernel(own_ids, other_ids, gain, gain_two, *refs):
    weights, (same_out, near_out, far_out, out_out) = refs[:4], refs[4:]
    out_out[:, :D] = weights[3][...].astype(jnp.bfloat16)
    lane = lax.broadcasted_iota(jnp.int32, (32, 128), 1)
    out_out[:, D:] = jnp.where(lane == 0, as_column(gain_two[...]), 0.0).astype(jnp.bfloat16)
    level = lax.axis_index("seq") >> 1
    batch, parity = level >> 1, level & 1
    scale = as_column(gain[...].astype(jnp.bfloat16).astype(jnp.float32))

    def scaled(at, turn):
        part = weights[at][:, pl.ds(pl.multiple_of(turn * 512, 512), 512)]
        return (part.astype(jnp.bfloat16).astype(jnp.float32) * scale).astype(jnp.bfloat16)

    for at in range(3):
        lanes = slice(at * 512, (at + 1) * 512)
        same_out[:, lanes] = scaled(at, parity)
        crossed = scaled(at, 1 - parity)
        near_out[:, lanes] = crossed
        far_out[:, lanes] = crossed
    rows = lax.broadcasted_iota(jnp.int32, (32, 128), 0)

    def listed(which):
        block = jnp.zeros((32, 128), jnp.int32)
        for side, ids in enumerate((own_ids, other_ids)):
            times = ids[which, 1:2, :]
            for at, line in enumerate((ids[which, 0:1, :], times >> 6, times & 63)):
                block = jnp.where(rows == side * 3 + at, line, block)
        return block.astype(jnp.float32).astype(jnp.bfloat16)

    near_out[:, 1536:] = listed(batch)
    far_ids = listed(1 - batch)
    same_out[:, 1536:] = far_ids
    far_out[:, 1536:] = far_ids


def head(own_ids, other_ids, gain, gain_two, weights):
    whole = lambda shape: pl.BlockSpec(shape, lambda at: (0,) * len(shape))
    arguments = [own_ids, other_ids, gain, gain_two, *weights]
    return pl.pallas_call(
        head_kernel,
        grid=(1,),
        in_specs=[whole(member.shape) for member in arguments],
        out_specs=[whole((32, 1664))] * 3 + [whole((32, D + 128))],
        out_shape=[jax.ShapeDtypeStruct((32, 1664), jnp.bfloat16)] * 3
        + [jax.ShapeDtypeStruct((32, D + 128), jnp.bfloat16)],
        compiler_params=pltpu.CompilerParams(vmem_limit_bytes=GRANT),
        name="head",
    )(*arguments)


def front_kernel(place, *refs):
    pieces, crossed, own, other = refs[:4], refs[4], refs[5:9], refs[9]
    weights_out, unit_out, qkv_out = refs[10:]
    dp_at, level, core = place[0], place[1], place[2]
    step = pl.program_id(0)

    def norm(values):
        wide = values.astype(jnp.float32)
        return (wide * rms_scale(wide)).astype(jnp.bfloat16)

    @pl.when(step == 0)
    def _():
        for at_dp in range(4):
            for at_level in range(4):
                base = ((dp_at ^ at_dp) * 4 + (level ^ at_level)) * 64
                mine = pl.ds(pl.multiple_of(base + core * 32, 32), 32)
                theirs = pl.ds(pl.multiple_of(base + (1 - core) * 32, 32), 32)
                rows = slice(at_level * 32, at_level * 32 + 32)
                for part in range(3):
                    lanes = pl.ds(pl.multiple_of(part * 512 + core * 256, 256), 256)
                    weights_out[mine, part * 256 : (part + 1) * 256] = pieces[at_dp][rows, lanes]
                start = at_dp * 128 + at_level * 32
                weights_out[theirs, :] = crossed[start : start + 32, :]
        for at in range(4):
            unit_out[at * 128 : (at + 1) * 128, :] = norm(own[at][...])

    @pl.when(step == 1)
    def _():
        for at in range(4):
            unit_out[at * 128 : (at + 1) * 128, :] = norm(other[at])

    qkv_out[...] = jnp.dot(unit_out[...], weights_out[...], preferred_element_type=jnp.float32)


def front(place, pieces, crossed, own, other):
    tokens = 2 * other.shape[0] * other.shape[1]
    quarter = pl.BlockSpec((128, 1536), lambda at: (0, 0))
    piece = pl.BlockSpec((128, D), lambda at: (0, 0))
    return pl.pallas_call(
        front_kernel,
        grid=(2,),
        in_specs=[pl.BlockSpec(memory_space=pltpu.SMEM)]
        + [quarter] * 4
        + [pl.BlockSpec((512, 768), lambda at: (0, 0))]
        + [piece] * 4
        + [pl.BlockSpec((4, 128, D), lambda at: (0, 0, 0))],
        out_specs=[
            pl.BlockSpec((D, 768), lambda at: (0, 0)),
            pl.BlockSpec((tokens // 2, D), lambda at: (at, 0)),
            pl.BlockSpec((tokens // 2, 768), lambda at: (at, 0)),
        ],
        out_shape=[
            jax.ShapeDtypeStruct((D, 768), jnp.bfloat16),
            jax.ShapeDtypeStruct((tokens, D), jnp.bfloat16),
            jax.ShapeDtypeStruct((tokens, 768), jnp.float32),
        ],
        compiler_params=pltpu.CompilerParams(vmem_limit_bytes=GRANT),
        name="front",
    )(place, *pieces, crossed, *own, other)


def tail_kernel(
    place, dqkv, weights, unit, gains, biases, ffn_gain, back_kept, back_sent, kept, sent, part, small
):
    core, group = place[2], place[3]
    tokens = unit.shape[0]

    def back(rows):
        total = contract_last(dqkv[0, rows, :], weights[:, :256])
        for at in (1, 2):
            total += contract_last(dqkv[at, rows, :], weights[:, at * 256 : (at + 1) * 256])
        return total

    back_kept[...] = back(slice(0, tokens // 2))
    back_sent[...] = back(slice(tokens // 2, tokens)).astype(jnp.bfloat16)
    for at in range(3):
        part[:, at * 256 : (at + 1) * 256] = rows_inner(unit[...], dqkv[at]).astype(jnp.bfloat16)
    for at in range(16):
        rows = slice(at * 32, at * 32 + 32)
        kept[rows, :] = part[pl.ds(pl.multiple_of(at * 64 + core * 32, 32), 32), :]
        sent[rows, :] = part[pl.ds(pl.multiple_of(at * 64 + (1 - core) * 32, 32), 32), :]
    lane = lax.broadcasted_iota(jnp.int32, (1, 128), 1)
    sums = gains[0] + gains[1]
    sums = sums + pltpu.roll(sums, HD, 1)
    placed = jnp.zeros((1, 128), jnp.float32)
    for head in range(4):
        line = biases[head // 2, head % 2 : head % 2 + 1, :]
        same = jnp.sum(jnp.where(lane < 8, line, 0.0), axis=1, keepdims=True)
        total = jnp.sum(jnp.where(lane == LSE_LANE, line, 0.0), axis=1, keepdims=True)
        spot = group * 4 + head
        placed = jnp.where(lane == spot, same, placed)
        placed = jnp.where(lane == spot + H, total - same, placed)
    small[...] = jnp.zeros(small.shape, jnp.float32)
    for at in range(4):
        small[at : at + 1, :256] = ffn_gain[:, at * 256 : (at + 1) * 256]
    small[4:5, :128] = jnp.where(lane < HD, sums[0:1], sums[1:2])
    small[4:5, 128:256] = placed
    kept[512:, :] = small[...].astype(jnp.bfloat16)
    sent[512:, :] = small[...].astype(jnp.bfloat16)


def tail(place, dqkv, weights, unit, gains, biases, ffn_gain):
    tokens = unit.shape[0]
    whole = lambda shape: pl.BlockSpec(shape, lambda at: (0,) * len(shape))
    shapes = [
        ((tokens // 2, D), jnp.float32),
        ((tokens // 2, D), jnp.bfloat16),
        ((528, 768), jnp.bfloat16),
        ((528, 768), jnp.bfloat16),
    ]
    arguments = (dqkv, weights, unit, gains, biases, ffn_gain)
    return pl.pallas_call(
        tail_kernel,
        grid=(1,),
        in_specs=[pl.BlockSpec(memory_space=pltpu.SMEM)]
        + [whole(member.shape) for member in arguments],
        out_specs=[whole(shape) for shape, _ in shapes],
        out_shape=[jax.ShapeDtypeStruct(shape, kind) for shape, kind in shapes],
        scratch_shapes=[pltpu.VMEM((D, 768), jnp.bfloat16), pltpu.VMEM((16, 768), jnp.float32)],
        compiler_params=pltpu.CompilerParams(vmem_limit_bytes=GRANT),
        cost_estimate=pl.CostEstimate(
            flops=4 * tokens * D * 768, bytes_accessed=14 * D * D, transcendentals=0
        ),
        name="tail",
    )(place, *arguments)


def finish_kernel(place, mine, near, side, far, gain, *refs):
    weights = refs[:3]
    kept, back_near, passed, inputs, upstream = refs[3:8]
    partial, down_far = refs[8:10]
    grads_out = refs[10:13]
    out_out, input_out, result_out, gain_out, q_out, k_out, bias_out, two_out = refs[13:21]
    wide = jnp.float32
    dp_at, level, core = place[0], place[1], place[2]
    parity, batch = level & 1, level >> 1
    step = pl.program_id(0)

    @pl.when(step == 0)
    def _():
        scale = as_column(gain[...].astype(jnp.bfloat16).astype(wide))
        for at in range(3):
            for side_core in range(2):
                rows = slice(at * 64 + side_core * 32, at * 64 + side_core * 32 + 32)
                same = mine[rows, :].astype(wide) + side[rows, :].astype(wide)
                cross = near[rows, :].astype(wide) + far[rows, :].astype(wide)
                for turn, member in ((parity, same), (1 - parity, cross)):
                    lane = (turn * 2 + (core + side_core) % 2) * 256
                    grads_out[at][:, pl.ds(pl.multiple_of(lane, 256), 256)] = member
        total = jnp.zeros((32, 1), wide)
        for at in range(3):
            unscaled = grads_out[at][...]
            total += jnp.sum(
                unscaled * weights[at][...].astype(jnp.bfloat16).astype(wide), axis=1, keepdims=True
            )
            grads_out[at][...] = unscaled * scale
        rows = lax.broadcasted_iota(jnp.int32, (32, 32), 0)
        columns = lax.broadcasted_iota(jnp.int32, (32, 32), 1)
        gain_out[...] = jnp.sum(jnp.where(rows == columns, total, 0.0), axis=0, keepdims=True)

        def summed(rows):
            return (mine[rows, :].astype(wide) + near[rows, :].astype(wide)) + (
                side[rows, :].astype(wide) + far[rows, :].astype(wide)
            )

        for at in range(4):
            out_out[:, at * 256 : (at + 1) * 256] = summed(slice(192 + at * 32, 224 + at * 32))
        small = summed(slice(320, 336))
        q_out[...] = small[4:5, :HD]
        k_out[...] = small[4:5, HD : 2 * HD]
        bias_out[0:1, :] = small[4:5, 2 * HD : 2 * HD + H]
        bias_out[1:2, :] = small[4:5, 2 * HD + H : 2 * HD + 2 * H]
        two = jnp.zeros((1, 32), wide)
        for at_dp in range(4):
            for at_seq in range(8):
                here = (dp_at == at_dp) & (level * 2 + core == at_seq)
                two = jnp.where(here, small[at_dp : at_dp + 1, at_seq * 32 : at_seq * 32 + 32], two)
        two_out[...] = two
    result_out[...] = (partial[...] + down_far[...].astype(wide)).astype(jnp.bfloat16)
    back = jnp.where(
        step == batch, kept[...] + back_near[...].astype(wide), passed[...].astype(wide)
    )
    values = inputs[0].astype(wide)
    inv = rms_scale(values)
    inner = jnp.mean(back * values, axis=-1, keepdims=True)
    input_out[0] = (
        upstream[0] + inv * back - values * (inv * inv * inv) * inner
    ).astype(jnp.bfloat16)


def finish(place, mine, moved, gain, weights, backs, inputs, upstream, outputs):
    whole = lambda shape: pl.BlockSpec(shape, lambda at: (0,) * len(shape))
    arguments = [mine, *moved, gain, *weights, *backs, inputs, upstream, *outputs]
    f32 = jnp.float32
    shapes = [((32, D), f32)] * 4 + [(inputs.shape, jnp.bfloat16)]
    shapes += [(outputs[0].shape, jnp.bfloat16)]
    shapes += [((1, 32), f32), ((1, HD), f32), ((1, HD), f32), ((2, H), f32), ((1, 32), f32)]
    rows, piece = inputs.shape[0] * inputs.shape[1], inputs.shape[1]
    batch_block = pl.BlockSpec((1, piece, D), lambda at: (at, 0, 0))
    row_block = pl.BlockSpec((piece, D), lambda at: (at, 0))

    def spec(shape):
        return {inputs.shape: batch_block, (rows, D): row_block}.get(tuple(shape), whole(shape))

    return pl.pallas_call(
        finish_kernel,
        grid=(2,),
        in_specs=[pl.BlockSpec(memory_space=pltpu.SMEM)]
        + [spec(member.shape) for member in arguments],
        out_specs=[spec(shape) for shape, _ in shapes],
        out_shape=[jax.ShapeDtypeStruct(shape, kind) for shape, kind in shapes],
        compiler_params=pltpu.CompilerParams(vmem_limit_bytes=GRANT),
        name="finish",
    )(place, *arguments)


def lower_kernel(gate, up, down, out):
    out[0] = gate[...].astype(jnp.bfloat16)
    out[1] = up[...].astype(jnp.bfloat16)
    out[2] = down[...].astype(jnp.bfloat16)


def lower(gate, up, down):
    whole = pl.BlockSpec(gate.shape, lambda at: (0, 0))
    return pl.pallas_call(
        lower_kernel,
        grid=(1,),
        in_specs=[whole] * 3,
        out_specs=pl.BlockSpec((3,) + gate.shape, lambda at: (0, 0, 0)),
        out_shape=jax.ShapeDtypeStruct((3,) + gate.shape, jnp.bfloat16),
        compiler_params=pltpu.CompilerParams(vmem_limit_bytes=GRANT),
        name="lower",
    )(gate, up, down)


def middle_back_kernel(
    place, kept, near, side, far, dy_in, middle_in, gain_in, weights, grad_out, low_out, sums_out, *outs
):
    wide = jnp.float32
    step = pl.program_id(0)
    level = place[1]
    upstream = (kept[...] + near[...].astype(wide)) + (
        side[...].astype(wide) + far[...].astype(wide)
    )
    middle = middle_in[...]
    inv = rms_scale(middle)
    sums = jnp.sum(upstream * middle * inv, axis=0, keepdims=True)

    @pl.when(step == 0)
    def _():
        sums_out[...] = sums

    @pl.when(step == 1)
    def _():
        sums_out[...] += sums

    grad = dy_in[...].astype(wide) + norm_back(middle, inv, gain_in[...], upstream)
    grad_out[...] = grad
    grad_low = grad.astype(jnp.bfloat16)
    low_out[...] = grad_low
    halves = [
        contract_last(grad_low, weights[at * 512 : (at + 1) * 512, :D]).astype(jnp.bfloat16)
        for at in range(2)
    ]
    for mask in range(4):
        for parity in range(2):

            @pl.when((level ^ mask) == step * 2 + parity)
            def _():
                outs[mask][...] = halves[parity]


def middle_back(place, kept, moved, own_dy, middle, gain_two, w_out):
    rows = kept.shape[0]
    block = pl.BlockSpec((rows // 2, D), lambda at: (at, 0))
    line = pl.BlockSpec((1, D), lambda at: (0, 0))
    quarter = pl.BlockSpec((rows // 2, D // 2), lambda at: (0, 0))
    return pl.pallas_call(
        middle_back_kernel,
        grid=(2,),
        in_specs=[pl.BlockSpec(memory_space=pltpu.SMEM)]
        + [block] * 6
        + [line, pl.BlockSpec(w_out.shape, lambda at: (0, 0))],
        out_specs=[block, block, line] + [quarter] * 4,
        out_shape=[
            jax.ShapeDtypeStruct((rows, D), jnp.float32),
            jax.ShapeDtypeStruct((rows, D), jnp.bfloat16),
            jax.ShapeDtypeStruct((1, D), jnp.float32),
        ]
        + [jax.ShapeDtypeStruct((rows // 2, D // 2), jnp.bfloat16)] * 4,
        compiler_params=pltpu.CompilerParams(vmem_limit_bytes=GRANT),
        cost_estimate=pl.CostEstimate(
            flops=2 * rows * D * D, bytes_accessed=22 * rows * D + 2 * D * D, transcendentals=rows
        ),
        name="middle_back",
    )(place, kept, *moved, own_dy, middle, gain_two, w_out)


GATED = 512
HIDDEN = 256


def load_weights(place, sources, gathered, arrived, which):
    level, core = place[1], place[2]
    pieces = [(sources[at], at, core) for at in range(4)]
    pieces += [(sources[4 + at], at, 1 - core) for at in range(4)]
    copies = []
    for at, (source, turn, side) in enumerate(pieces):
        rows = pl.ds(pl.multiple_of(((level ^ turn) * 2 + side) * 128, 128), 128)
        copies.append(
            pltpu.make_async_copy(source.at[which], gathered.at[rows, :], arrived.at[at])
        )
    for copy in copies:
        copy.start()
    return copies


def gated_kernel(count, place, *refs):
    tokens_in, grads_in, sources = refs[:count], refs[count : 2 * count], refs[2 * count :][:8]
    refs = refs[2 * count + 8 :]
    hidden_out, back_out, totals = refs[:count], refs[count : 2 * count], refs[2 * count :][:count]
    weights, arrived = refs[3 * count :]
    level, core = place[1], place[2]
    copies = []
    for at in range(8):
        target = weights.at[:, at * 128 : at * 128 + 128, :]
        copies.append(pltpu.make_async_copy(sources[at], target, arrived.at[at]))
        copies[-1].start()
    for step in range(2):
        for at in range(4):
            copies[step * 4 + at].wait()
        units = slice(step * GATED, (step + 1) * GATED)
        side = 1 - core if step else core
        pair = jnp.concatenate([weights[0, units, :], weights[1, units, :]])
        third = weights[2, units, :]
        for at in range(count):
            both = contract_last(tokens_in[at][...], pair)
            gate, up = both[:, :GATED], both[:, GATED:]
            grad_hidden = contract_last(grads_in[at][0], third)
            sig = lax.logistic(gate)
            swished = gate * sig
            hidden = (swished * up).astype(jnp.bfloat16)
            grad_gate = (grad_hidden * up * sig * (1.0 + gate * (1.0 - sig))).astype(jnp.bfloat16)
            grad_up = (grad_hidden * swished).astype(jnp.bfloat16)
            for turn in range(4):
                lanes = pl.ds(pl.multiple_of(((level ^ turn) * 2 + side) * 128, 128), 128)
                part = slice(turn * 128, turn * 128 + 128)
                hidden_out[at][0, :, lanes] = grad_gate[:, part]
                hidden_out[at][1, :, lanes] = grad_up[:, part]
                hidden_out[at][2, :, lanes] = hidden[:, part]
            added = jnp.dot(
                jnp.concatenate([grad_gate, grad_up], axis=1),
                pair,
                preferred_element_type=jnp.float32,
            )
            if step == 0:
                totals[at][...] = added
            else:
                back_out[at][...] = (totals[at][...] + added).astype(back_out[at].dtype)


def dp_block(mask, chunk):
    return pl.BlockSpec((1, chunk, D), lambda at, place: (place[0] ^ mask, 0, 0))


def gated(place, tokens_in, grads_all, masks, weights, kinds):
    count = len(tokens_in)
    chunk = tokens_in[0].shape[0]
    hidden = 8 * weights[0].shape[1]
    assert hidden == 2 * GATED
    whole = pl.BlockSpec((chunk, D), lambda at, place: (0, 0))
    anywhere = pl.BlockSpec(memory_space=pl.ANY)
    results = pl.pallas_call(
        functools.partial(gated_kernel, count),
        grid_spec=pltpu.PrefetchScalarGridSpec(
            num_scalar_prefetch=1,
            grid=(1,),
            in_specs=[whole] * count
            + [dp_block(mask, chunk) for mask in masks]
            + [anywhere] * len(weights),
            out_specs=[pl.BlockSpec((3, chunk, hidden), lambda at, place: (0, 0, 0))] * count
            + [whole] * count,
            scratch_shapes=[pltpu.VMEM((chunk, D), jnp.float32)] * count
            + [pltpu.VMEM((3, hidden, D), jnp.bfloat16), pltpu.SemaphoreType.DMA((8,))],
        ),
        out_shape=[jax.ShapeDtypeStruct((3, chunk, hidden), jnp.bfloat16)] * count
        + [jax.ShapeDtypeStruct((chunk, D), kind) for kind in kinds],
        compiler_params=pltpu.CompilerParams(vmem_limit_bytes=GRANT),
        cost_estimate=pl.CostEstimate(
            flops=10 * count * chunk * D * hidden,
            bytes_accessed=2 * D * (7 * count * chunk + 3 * hidden),
            transcendentals=count * chunk * hidden,
        ),
        name="gated",
    )(place, *tokens_in, *[grads_all] * count, *weights)
    return list(zip(results[:count], results[count:]))


def ffn_grads_kernel(place, *refs):
    tokens_in, grads_in, hidden_in = refs[0:4], refs[4:8], refs[8:12]
    grads_out, tokens_all, grads_all, hidden = refs[12:]
    chunk = tokens_in[0].shape[0]
    rows_of = [slice(at * chunk, (at + 1) * chunk) for at in range(4)]

    @pl.when(pl.program_id(0) == 0)
    def _():
        for at in range(4):
            tokens_all[rows_of[at], :] = tokens_in[at][...]
            grads_all[rows_of[at], :] = grads_in[at][0]

    for which in range(3):
        for at in range(4):
            hidden[which, rows_of[at], :] = hidden_in[at][which]
        other = tokens_all if which < 2 else grads_all
        grads_out[which] = rows_inner(hidden[which], other[...]).astype(jnp.bfloat16)


def ffn_grads(place, tokens_in, grads_in, hidden_in):
    chunk = tokens_in[0].shape[0]
    tokens = 4 * chunk
    hidden = hidden_in[0].shape[2]
    whole = pl.BlockSpec((chunk, D), lambda at, place: (0, 0))
    wide_low = pltpu.VMEM((tokens, D), jnp.bfloat16)
    return pl.pallas_call(
        ffn_grads_kernel,
        grid_spec=pltpu.PrefetchScalarGridSpec(
            num_scalar_prefetch=1,
            grid=(hidden // HIDDEN,),
            in_specs=[whole] * 4
            + [dp_block(mask, chunk) for mask in range(4)]
            + [pl.BlockSpec((3, chunk, HIDDEN), lambda at, place: (0, 0, at))] * 4,
            out_specs=pl.BlockSpec((3, HIDDEN, D), lambda at, place: (0, at, 0)),
            scratch_shapes=[wide_low, wide_low, pltpu.VMEM((3, tokens, HIDDEN), jnp.bfloat16)],
        ),
        out_shape=jax.ShapeDtypeStruct((3, hidden, D), jnp.bfloat16),
        compiler_params=pltpu.CompilerParams(vmem_limit_bytes=GRANT),
        cost_estimate=pl.CostEstimate(
            flops=6 * tokens * D * hidden,
            bytes_accessed=2 * D * (4 * tokens + 6 * hidden),
            transcendentals=0,
        ),
        name="ffn_grads",
    )(place, *tokens_in, *[grads_in] * 4, *hidden_in)


def down_kernel(place, *refs):
    hidden_in, attended, grads, sources = refs[:4], refs[4], refs[5], refs[6:14]
    outs, kept, sent, part, weights, arrived = refs[14:18], *refs[18:]
    core = place[2]
    copies = load_weights(place, sources, weights, arrived, 2)
    part[...] = rows_inner(attended[...], grads[...]).astype(jnp.bfloat16)
    for at in range(16):
        rows = slice(at * 32, at * 32 + 32)
        kept[rows, :] = part[pl.ds(pl.multiple_of(at * 64 + core * 32, 32), 32), :]
        sent[rows, :] = part[pl.ds(pl.multiple_of(at * 64 + (1 - core) * 32, 32), 32), :]
    for copy in copies:
        copy.wait()
    for at in range(4):
        outs[at][...] = jnp.dot(
            hidden_in[at][0], weights[...], preferred_element_type=jnp.float32
        ).astype(outs[at].dtype)


def down(place, hidden_in, weights, attended, grads):
    chunk = hidden_in[0].shape[1]
    hidden = hidden_in[0].shape[2]
    half = D // 2
    whole = pl.BlockSpec((chunk, D), lambda at, place: (0, 0))
    tall = pl.BlockSpec((half, D), lambda at, place: (0, 0))
    return pl.pallas_call(
        down_kernel,
        grid_spec=pltpu.PrefetchScalarGridSpec(
            num_scalar_prefetch=1,
            grid=(1,),
            in_specs=[pl.BlockSpec((1, chunk, hidden), lambda at, place: (2, 0, 0))] * 4
            + [whole] * 2
            + [pl.BlockSpec(memory_space=pl.ANY)] * len(weights),
            out_specs=[whole] * 4 + [tall] * 2,
            scratch_shapes=[
                pltpu.VMEM((D, D), jnp.bfloat16),
                pltpu.VMEM((hidden, D), jnp.bfloat16),
                pltpu.SemaphoreType.DMA((8,)),
            ],
        ),
        out_shape=[jax.ShapeDtypeStruct((chunk, D), jnp.float32)]
        + [jax.ShapeDtypeStruct((chunk, D), jnp.bfloat16)] * 3
        + [jax.ShapeDtypeStruct((half, D), jnp.bfloat16)] * 2,
        compiler_params=pltpu.CompilerParams(vmem_limit_bytes=GRANT),
        cost_estimate=pl.CostEstimate(
            flops=10 * chunk * D * hidden,
            bytes_accessed=2 * D * (11 * chunk + 2 * hidden),
            transcendentals=0,
        ),
        name="down",
    )(place, *hidden_in, attended, grads, *weights)


def local_split(
    inputs,
    variate_ids,
    time_ids,
    attn_gain,
    query_weight,
    key_weight,
    value_weight,
    out_weight,
    query_gain,
    key_gain,
    variate_bias,
    ffn_gain,
    gate_weight,
    up_weight,
    down_weight,
    out_grad,
):
    low = jnp.bfloat16
    wide = jnp.float32
    dp_at = lax.axis_index("dp")
    seq_at = lax.axis_index("seq")
    core = seq_at & 1
    level = seq_at >> 1
    batch = level >> 1
    parity = level & 1
    piece = inputs.shape[2]
    tokens = 8 * piece
    others = (1, 2, 3)
    swap_core = lambda values: swap_seq(values, 1)
    swap_level = lambda values, mask: swap_seq(values, 2 * mask)

    own_dy = out_grad[:, 0].reshape(2 * piece, D)

    ids = jnp.stack([variate_ids[:, 0], time_ids[:, 0]], axis=1)
    same, cross_near, cross_far, with_gain = head(
        ids,
        swap_core(ids),
        attn_gain[None, :],
        ffn_gain[None, :],
        [query_weight, key_weight, value_weight, out_weight],
    )
    w_out = lax.all_gather(with_gain, ("dp", "seq"), axis=0, tiled=True)
    moved = [swap_level((cross_near, same, cross_far)[mask - 1], mask) for mask in others]
    own_x = inputs[:, 0]
    x_late, moved[0] = together(own_x, moved[0])
    near, far = at_index(x_late, batch), at_index(x_late, 1 - batch)
    (
        same,
        near,
        far,
        gate_local,
        up_local,
        down_local,
        query_gain,
        key_gain,
        variate_bias,
        *moved,
    ) = together(
        same,
        near,
        far,
        gate_weight,
        up_weight,
        down_weight,
        query_gain,
        key_gain,
        variate_bias,
        *moved,
    )
    ffn_local = lower(gate_local, up_local, down_local)

    place = jnp.stack([dp_at, level, core, 2 * parity + core]).astype(jnp.int32)
    rows = jnp.concatenate([same[:, :1536]] + [member[:, :1536] for member in moved])
    ids = jnp.stack([cross_near[:, 1536:]] + [member[:, 1536:] for member in moved])
    moved = [swap_dp(rows, mask) for mask in others]
    from_far = swap_level(far, 2)
    from_near = swap_level(near, 1)
    last = swap_level(from_far, 1)
    ids = jnp.stack([ids[:, :3], ids[:, 3:6]]).astype(wide)

    kinds = ids[:, :, 0].reshape(tokens, 1)
    times = (ids[:, :, 1] * 64.0 + ids[:, :, 2]).reshape(tokens, 1)
    lane = lax.broadcasted_iota(jnp.int32, (1, 128), 1)
    hot = jnp.where(
        lane < LSE_LANE, (kinds == lane % 8).astype(wide), jnp.where(lane < LSE_LANE + 3, 1.0, 0.0)
    ).astype(low)
    half = HD // 2
    frequency = 10000.0 ** (-(lane % half).astype(wide) / half)
    angles = times * frequency
    cos_part = jnp.cos(angles)
    sin_part = jnp.sin(angles) * jnp.where(lane % HD < half, -1.0, 1.0)
    q_gain = jnp.tile(query_gain, 2)[None, :]
    k_gain = jnp.tile(key_gain, 2)[None, :]
    group = 2 * parity + core
    gaps = at_index((variate_bias[0] - variate_bias[1]).reshape(4, 4), group)
    first, second, third = three_parts(gaps)
    bias_rows = jnp.where(
        lane < 8,
        first[:, None],
        jnp.where(
            lane < 16, second[:, None], jnp.where(lane < LSE_LANE, third[:, None], 0.0)
        ),
    ).reshape(2, 2, 128)

    (
        rows,
        ffn_local,
        near,
        from_near,
        from_far,
        last,
        cos_part,
        sin_part,
        dy_sent,
        hot,
        q_gain,
        k_gain,
        bias_rows,
        place,
        *moved,
    ) = together(
        rows,
        ffn_local,
        near,
        from_near,
        from_far,
        last,
        cos_part,
        sin_part,
        own_dy,
        hot,
        q_gain,
        k_gain,
        bias_rows,
        place,
        *moved,
    )

    dy_all = lax.all_gather(dy_sent, "dp", axis=0)

    pieces = [rows] + moved
    own = [near, from_near, from_far, last]
    ffn_near, ffn_far = swap_level(ffn_local, 1), swap_level(ffn_local, 2)
    sent = jnp.concatenate(
        [
            jnp.concatenate(
                [
                    jnp.where(
                        core == 0,
                        member[:, at * 512 + 256 : at * 512 + 512],
                        member[:, at * 512 : at * 512 + 256],
                    )
                    for at in range(3)
                ],
                axis=1,
            )
            for member in pieces
        ]
    )
    crossed, rows_crossed = together(swap_core(jnp.stack(own)), swap_core(sent))

    w_qkv, unit, qkv = front(place, pieces, rows_crossed, own, crossed)
    att_near, att_far, *saved = attend(qkv, cos_part, sin_part, hot, q_gain, k_gain, bias_rows)
    attended = (att_near, att_far)
    att_near, att_far, local_crossed = together(att_near, att_far, swap_core(ffn_local))

    part, crossed = together(att_near, swap_core(att_far))
    part, crossed = part.reshape(4, piece, 256), crossed.reshape(4, piece, 256)
    both = jnp.concatenate(
        [jnp.where(core == 0, part, crossed), jnp.where(core == 0, crossed, part)], axis=2
    )

    w_out, gain_two, ffn_near, ffn_far, *arrived = together(
        w_out,
        w_out[:, D].astype(wide)[None, :],
        ffn_near,
        ffn_far,
        both[0],
        *[swap_level(both[mask], mask) for mask in others],
    )
    blocks = [pick(arrived, level ^ at) for at in range(4)]
    own_att = jnp.concatenate(
        [
            jnp.concatenate([blocks[0], blocks[1]], axis=1),
            jnp.concatenate([blocks[2], blocks[3]], axis=1),
        ]
    )

    own_wide = own_x.reshape(2 * piece, D).astype(wide)
    middle = own_wide + product(own_att, w_out[:, :D])
    inv_two = rms_scale(middle)
    normed_two = (middle * inv_two * gain_two).astype(low)

    ffn_last, near_crossed, far_crossed, near_two, side_two, own_two, middle, own_att, gain_two, dy_all = together(
        swap_level(ffn_far, 1),
        swap_core(ffn_near),
        swap_core(ffn_far),
        swap_dp(normed_two, 1),
        swap_dp(normed_two, 2),
        normed_two,
        middle,
        own_att,
        gain_two,
        dy_all,
    )

    far_two = swap_dp(own_two, 3)
    w_ffn = [ffn_local, ffn_near, ffn_far, ffn_last]
    w_ffn += [local_crossed, near_crossed, far_crossed, swap_core(ffn_last)]
    (near_hidden, near_back), (side_hidden, side_back) = gated(
        place, [near_two, side_two], dy_all, (1, 2), w_ffn, (low, low)
    )
    far_two, near_hidden, near_back, side_hidden, side_back = together(
        far_two, near_hidden, near_back, side_hidden, side_back
    )

    near_back, side_back = swap_dp(near_back, 1), swap_dp(side_back, 2)
    (own_hidden, kept), (far_hidden, far_back) = gated(
        place, [own_two, far_two], dy_all, (0, 3), w_ffn, (wide, low)
    )
    own_hidden, kept, far_hidden, far_back, near_back, side_back = together(
        own_hidden, kept, far_hidden, far_back, near_back, side_back
    )
    hidden = [own_hidden, near_hidden, side_hidden, far_hidden]
    ffn_part = ffn_grads(place, [own_two, near_two, side_two, far_two], dy_all, hidden)
    ffn_part, kept, *moved = together(
        ffn_part, kept, near_back, side_back, swap_dp(far_back, 3)
    )
    ffn_shard = lax.psum_scatter(ffn_part, "seq", scatter_dimension=1, tiled=True)
    grad_middle, middle_low, gain_two_part, *blocks = middle_back(
        place, kept, moved, own_dy, middle, gain_two, w_out
    )

    arrived = [blocks[0]] + [swap_level(blocks[mask], mask) for mask in others]
    down_kept, *rest = down(place, hidden, w_ffn, own_att, middle_low)
    down_chunks, out_kept, out_sent = rest[:3], rest[3], rest[4]
    out_kept, out_sent, down_kept, *rest = together(
        out_kept, out_sent, down_kept, *down_chunks, *arrived
    )
    down_chunks, arrived = rest[:3], rest[3:]

    halves = [
        jnp.concatenate([member[:, :256] for member in arrived]),
        jnp.concatenate([member[:, 256:] for member in arrived]),
    ]

    def out_rows(to):
        rows = [
            lax.dynamic_slice_in_dim(member, to * 128, 128).astype(wide)
            for member in (out_kept, out_crossed)
        ]
        return (rows[0] + rows[1]).astype(low)

    kept, crossed, out_kept, out_crossed, *down_chunks = together(
        pick(halves, core),
        swap_core(pick(halves, 1 - core)),
        out_kept,
        swap_core(out_sent),
        *down_chunks,
    )
    out_parts = [out_rows(dp_at ^ mask) for mask in range(4)]
    grads = (kept, crossed)

    out_moved = [swap_dp(out_parts[mask], mask) for mask in others]
    dqkv, gain_sums, bias_sums = attend_back(
        qkv, saved, hot, grads, attended, cos_part, sin_part, q_gain, k_gain
    )
    dqkv, out_kept, last_chunk, *rest = together(
        dqkv,
        out_parts[0],
        down_chunks[2],
        swap_dp(down_chunks[0], 1),
        swap_dp(down_chunks[1], 2),
        *out_moved,
    )
    down_moved, out_moved = rest[:2], rest[2:]

    out_moved = [member.astype(wide) for member in out_moved]
    out_sum = (out_kept.astype(wide) + out_moved[0]) + (out_moved[1] + out_moved[2])
    back_kept, back_sent, kept, sent = tail(
        place, dqkv, w_qkv, unit, gain_sums, bias_sums, gain_two_part
    )
    back_kept, back_crossed, kept, crossed = together(
        back_kept, swap_core(back_sent), kept, swap_core(sent)
    )

    back = (back_kept + back_crossed.astype(wide)).reshape(4, piece, D)
    small_low = (kept[512:].astype(wide) + crossed[512:].astype(wide)).astype(low)

    def dp_message(to):
        return jnp.concatenate(
            [
                lax.dynamic_slice_in_dim(kept, to * 128, 128),
                lax.dynamic_slice_in_dim(crossed, to * 128, 128),
                small_low,
            ]
        )

    moved = [swap_dp(dp_message(dp_at ^ mask), mask) for mask in others]
    passed = back[2] + swap_level(back[3].astype(low), 1).astype(wide)
    passed = swap_level(passed.astype(low), 2)
    down_moved = [member.astype(wide) for member in down_moved]
    partial = (middle + down_kept) + (down_moved[0] + down_moved[1])
    qkv_kept, kept, passed, near, ffn_shard, last_chunk, partial, *moved = together(
        dp_message(dp_at), back[0], passed, back[1].astype(low), ffn_shard, last_chunk, partial, *moved
    )

    moved = [member.astype(wide) for member in moved]
    total = qkv_kept.astype(wide)
    total = ((total + moved[0]) + (moved[1] + moved[2])).astype(low)
    small_low = total[256:]

    out_sum = out_sum.reshape(4, 32, D)
    ffn_sums = ffn_shard.astype(wide)

    def level_message(to):
        out_block = at_index(out_sum, to).astype(low)
        qkv_block = jnp.concatenate(
            [
                lax.dynamic_slice_in_dim(total, to * 32, 32),
                lax.dynamic_slice_in_dim(total, 128 + to * 32, 32),
            ]
        )
        return jnp.concatenate(
            [qkv_block[:, at * 256 : (at + 1) * 256] for at in range(3)]
            + [out_block[:, at * 256 : (at + 1) * 256] for at in range(4)]
            + [small_low[:, :256]]
        )

    mine, kept, near, passed, ffn_sums, last_chunk, *moved = together(
        level_message(level),
        kept,
        swap_level(near, 1),
        passed,
        ffn_sums,
        swap_dp(last_chunk, 3),
        *[swap_level(level_message(level ^ mask), mask) for mask in others],
    )
    *sums, input_grad, result, gain_grad, q_grad, k_grad, bias_grad, gain_two_grad = finish(
        place,
        mine,
        moved,
        attn_gain[None, :],
        [query_weight, key_weight, value_weight],
        [kept, near, passed],
        own_x,
        grad_middle.reshape(2, piece, D),
        [partial, last_chunk],
    )

    shape = (2, 1, piece, D)
    return (
        result.reshape(shape),
        input_grad.reshape(shape),
        gain_grad.reshape(32),
        sums[0],
        sums[1],
        sums[2],
        sums[3],
        q_grad.reshape(HD),
        k_grad.reshape(HD),
        bias_grad,
        gain_two_grad.reshape(32),
        ffn_sums[0],
        ffn_sums[1],
        ffn_sums[2],
    )


def solution(mesh):
    placed = (
        P(None, "dp", "seq", None),
        P(None, "dp", "seq"),
        P(None, "dp", "seq"),
        P(("dp", "seq")),
        P(("dp", "seq"), None),
        P(("dp", "seq"), None),
        P(("dp", "seq"), None),
        P(("dp", "seq"), None),
        P(),
        P(),
        P(),
        P(("dp", "seq")),
        P(("dp", "seq"), None),
        P(("dp", "seq"), None),
        P(("dp", "seq"), None),
        P(None, "dp", "seq", None),
    )
    split = mesh.shape["dp"] == 4 and mesh.shape["seq"] == 8
    return jax.shard_map(
        local_split if split else local,
        mesh=mesh,
        in_specs=placed,
        out_specs=(
            P(None, "dp", "seq", None),
            P(None, "dp", "seq", None),
            P(("dp", "seq")),
            P(("dp", "seq"), None),
            P(("dp", "seq"), None),
            P(("dp", "seq"), None),
            P(("dp", "seq"), None),
            P(),
            P(),
            P(),
            P(("dp", "seq")),
            P(("dp", "seq"), None),
            P(("dp", "seq"), None),
            P(("dp", "seq"), None),
        ),
        check_vma=False,
    )
```

```python
import functools
import math

import jax
import jax.numpy as jnp
from jax import lax
from jax.experimental import pallas as pl
from jax.experimental.pallas import tpu as pltpu
from jax.sharding import PartitionSpec as P

D = 1024
H = 16
HD = 64
FF = 4096


epsilon = 1e-06
lowest = -1e30


def rms_scale(values):
    return lax.rsqrt(jnp.mean(values * values, axis=-1, keepdims=True) + epsilon)


def norm_back(values, inv_rms, gain_vec, upstream):
    weighted = upstream * gain_vec
    inner_mean = jnp.mean(weighted * values, axis=-1, keepdims=True)
    return inv_rms * weighted - values * (inv_rms * inv_rms * inv_rms) * inner_mean


def rotation(positions):
    half_dim = HD // 2
    frequency = 10000.0 ** (-jnp.arange(half_dim).astype(jnp.float32) / half_dim)
    angles = positions.astype(jnp.float32)[..., None] * frequency
    return (jnp.cos(angles)[..., None, :], jnp.sin(angles)[..., None, :])


def rotate(values, cos_part, sin_part):
    half_dim = values.shape[-1] // 2
    first_half = values[..., :half_dim]
    second_half = values[..., half_dim:]
    return jnp.concatenate(
        [
            first_half * cos_part - second_half * sin_part,
            first_half * sin_part + second_half * cos_part,
        ],
        axis=-1,
    )


def rotate_back(upstream, cos_part, sin_part):
    half_dim = upstream.shape[-1] // 2
    first_half = upstream[..., :half_dim]
    second_half = upstream[..., half_dim:]
    return jnp.concatenate(
        [
            first_half * cos_part + second_half * sin_part,
            second_half * cos_part - first_half * sin_part,
        ],
        axis=-1,
    )


def product(left_side, right_side):
    return jnp.dot(left_side, right_side, preferred_element_type=jnp.float32)


def times_transposed(left_side, right_side):
    return lax.dot_general(
        left_side, right_side, (((1,), (1,)), ((), ())), preferred_element_type=jnp.float32
    )


def rows_inner(left_side, right_side):
    return lax.dot_general(
        left_side, right_side, (((0,), (0,)), ((), ())), preferred_element_type=jnp.float32
    )


def score_block(queries, key_rows, query_kinds, key_kinds, variate_bias):
    raw_scores = jnp.einsum(
        "sqhe,skhe->shqk", queries, key_rows, preferred_element_type=jnp.float32
    ) * HD ** (-0.5)
    same_kind = query_kinds[:, None, :, None] == key_kinds[:, None, None, :]
    scores = raw_scores + jnp.where(
        same_kind, variate_bias[0][None, :, None, None], variate_bias[1][None, :, None, None]
    )
    return (scores, same_kind)


def forward_piece(queries, query_kinds, variate_bias, carried, pieces):
    piece_keys, piece_values, piece_kinds = pieces
    seq_count = piece_keys.shape[0]
    piece_len = piece_keys.shape[1]
    block_size = math.gcd(piece_len, 512)

    def forward_advance(block_index, totals):
        running_max, running_total, running_sum = totals
        offset = block_index * block_size
        key_rows = lax.dynamic_slice_in_dim(piece_keys, offset, block_size, 1).reshape(
            seq_count, block_size, H, HD
        )
        value_rows = lax.dynamic_slice_in_dim(piece_values, offset, block_size, 1).reshape(
            seq_count, block_size, H, HD
        )
        kind_rows = lax.dynamic_slice_in_dim(piece_kinds, offset, block_size, 1)
        scores, same_kind = score_block(queries, key_rows, query_kinds, kind_rows, variate_bias)
        new_max = jnp.maximum(running_max, jnp.max(scores, axis=-1))
        factor = jnp.exp(running_max - new_max)
        exp_scores = jnp.exp(scores - new_max[..., None])
        running_total = running_total * factor + jnp.sum(exp_scores, axis=-1)
        running_sum = running_sum * factor[..., None] + jnp.einsum(
            "shqk,skhe->shqe",
            exp_scores.astype(jnp.bfloat16),
            value_rows,
            preferred_element_type=jnp.float32,
        )
        return (new_max, running_total, running_sum)

    return lax.fori_loop(0, piece_len // block_size, forward_advance, carried)


def back_piece(context, carried, pieces):
    queries, query_kinds, grad_out, log_total, delta_row, variate_bias = context
    piece_keys, piece_values, piece_kinds = pieces
    seq_count = piece_keys.shape[0]
    piece_len = piece_keys.shape[1]
    block_size = math.gcd(piece_len, 512)
    score_scale = HD ** (-0.5)

    def back_advance(block_index, totals):
        offset = block_index * block_size
        key_rows = lax.dynamic_slice_in_dim(piece_keys, offset, block_size, 1).reshape(
            seq_count, block_size, H, HD
        )
        value_rows = lax.dynamic_slice_in_dim(piece_values, offset, block_size, 1).reshape(
            seq_count, block_size, H, HD
        )
        kind_rows = lax.dynamic_slice_in_dim(piece_kinds, offset, block_size, 1)
        scores, same_kind = score_block(queries, key_rows, query_kinds, kind_rows, variate_bias)
        attn_prob = jnp.exp(scores - log_total[..., None])
        grad_prob = jnp.einsum(
            "sqhe,skhe->shqk", grad_out, value_rows, preferred_element_type=jnp.float32
        )
        grad_score = attn_prob * (grad_prob - delta_row[..., None])
        bias_step = jnp.stack(
            [
                jnp.sum(jnp.where(same_kind, grad_score, 0.0), axis=(0, 2, 3)),
                jnp.sum(jnp.where(same_kind, 0.0, grad_score), axis=(0, 2, 3)),
            ]
        )
        score_low = grad_score.astype(jnp.bfloat16)
        query_grad = (
            totals[0]
            + jnp.einsum("shqk,skhe->shqe", score_low, key_rows, preferred_element_type=jnp.float32)
            * score_scale
        )
        key_part = (
            jnp.einsum("shqk,sqhe->skhe", score_low, queries, preferred_element_type=jnp.float32)
            * score_scale
        ).reshape(seq_count, block_size, D)
        value_part = jnp.einsum(
            "shqk,sqhe->skhe",
            attn_prob.astype(jnp.bfloat16),
            grad_out,
            preferred_element_type=jnp.float32,
        ).reshape(seq_count, block_size, D)
        key_total = lax.dynamic_update_slice_in_dim(
            totals[2],
            lax.dynamic_slice_in_dim(totals[2], offset, block_size, 1) + key_part,
            offset,
            1,
        )
        value_total = lax.dynamic_update_slice_in_dim(
            totals[3],
            lax.dynamic_slice_in_dim(totals[3], offset, block_size, 1) + value_part,
            offset,
            1,
        )
        return (query_grad, totals[1] + bias_step, key_total, value_total)

    return lax.fori_loop(0, piece_len // block_size, back_advance, carried)


def local(
    inputs,
    variate_ids,
    time_ids,
    attn_gain,
    query_weight,
    key_weight,
    value_weight,
    out_weight,
    query_gain,
    key_gain,
    variate_bias,
    ffn_gain,
    gate_weight,
    up_weight,
    down_weight,
    out_grad,
):
    seq_count = inputs.shape[1]
    tok_count = inputs.shape[2]
    row_count = seq_count * tok_count
    full_grads = [
        jnp.zeros(extent, jnp.float32)
        for extent in ((D,), (D, D), (D, D), (D, D), (D, D), (D,), (FF, D), (FF, D), (FF, D))
    ]
    small_grads = [
        jnp.zeros((HD,), jnp.float32),
        jnp.zeros((HD,), jnp.float32),
        jnp.zeros((2, H), jnp.float32),
    ]
    shard_total = None
    small_total = None
    outputs_list = []
    input_grads = []
    weights_now = None
    for micro_index in range(inputs.shape[0]):
        weights_now = (
            lax.all_gather(attn_gain.astype(jnp.bfloat16), ("dp", "seq"), axis=0, tiled=True),
            lax.all_gather(query_weight.astype(jnp.bfloat16), ("dp", "seq"), axis=0, tiled=True),
            lax.all_gather(key_weight.astype(jnp.bfloat16), ("dp", "seq"), axis=0, tiled=True),
            lax.all_gather(value_weight.astype(jnp.bfloat16), ("dp", "seq"), axis=0, tiled=True),
            lax.all_gather(out_weight.astype(jnp.bfloat16), ("dp", "seq"), axis=0, tiled=True),
            lax.all_gather(ffn_gain.astype(jnp.bfloat16), ("dp", "seq"), axis=0, tiled=True),
            lax.all_gather(gate_weight.astype(jnp.bfloat16), ("dp", "seq"), axis=0, tiled=True),
            lax.all_gather(up_weight.astype(jnp.bfloat16), ("dp", "seq"), axis=0, tiled=True),
            lax.all_gather(down_weight.astype(jnp.bfloat16), ("dp", "seq"), axis=0, tiled=True),
        )
        gain_one, w_query, w_key, w_value, w_out, gain_two, w_gate, w_up, w_down = weights_now
        hidden_in = inputs[micro_index].astype(jnp.float32).reshape(row_count, D)
        kinds_now = variate_ids[micro_index].astype(jnp.bfloat16)
        cos_part, sin_part = rotation(time_ids[micro_index])
        inv_one = rms_scale(hidden_in)
        normed = (hidden_in * inv_one * gain_one.astype(jnp.float32)).astype(jnp.bfloat16)
        query_raw = product(normed, w_query).reshape(seq_count, tok_count, H, HD)
        key_raw = product(normed, w_key).reshape(seq_count, tok_count, H, HD)
        value_flat = product(normed, w_value).astype(jnp.bfloat16).reshape(seq_count, tok_count, D)
        inv_query = rms_scale(query_raw)
        query_rot = rotate(query_raw * inv_query * query_gain, cos_part, sin_part).astype(
            jnp.bfloat16
        )
        inv_key = rms_scale(key_raw)
        key_rot = rotate(key_raw * inv_key * key_gain, cos_part, sin_part).astype(jnp.bfloat16)
        key_flat = key_rot.reshape(seq_count, tok_count, D)
        initial = (
            jnp.full((seq_count, H, tok_count), lowest, jnp.float32),
            jnp.zeros((seq_count, H, tok_count), jnp.float32),
            jnp.zeros((seq_count, H, tok_count, HD), jnp.float32),
        )
        final_max, final_total, final_sum = forward_piece(
            query_rot,
            kinds_now,
            variate_bias,
            initial,
            (
                lax.all_gather(key_flat, "seq", axis=1, tiled=True),
                lax.all_gather(value_flat, "seq", axis=1, tiled=True),
                lax.all_gather(kinds_now, "seq", axis=1, tiled=True),
            ),
        )
        log_total = final_max + jnp.log(final_total)
        attended = jnp.transpose(final_sum / final_total[..., None], (0, 2, 1, 3))
        attended_low = attended.reshape(row_count, D).astype(jnp.bfloat16)
        middle = hidden_in + product(attended_low, w_out)
        inv_two = rms_scale(middle)
        normed_two = (middle * inv_two * gain_two.astype(jnp.float32)).astype(jnp.bfloat16)
        gate_pre = times_transposed(normed_two, w_gate)
        up_pre = times_transposed(normed_two, w_up)
        gate_sig = jax.nn.sigmoid(gate_pre)
        hidden_low = (gate_pre * gate_sig * up_pre).astype(jnp.bfloat16)
        result = middle + product(hidden_low, w_down)
        outputs_list.append(result.reshape(seq_count, tok_count, D).astype(jnp.bfloat16))
        gain_one, w_query, w_key, w_value, w_out, gain_two, w_gate, w_up, w_down = (
            lax.all_gather(attn_gain.astype(jnp.bfloat16), ("dp", "seq"), axis=0, tiled=True),
            lax.all_gather(query_weight.astype(jnp.bfloat16), ("dp", "seq"), axis=0, tiled=True),
            lax.all_gather(key_weight.astype(jnp.bfloat16), ("dp", "seq"), axis=0, tiled=True),
            lax.all_gather(value_weight.astype(jnp.bfloat16), ("dp", "seq"), axis=0, tiled=True),
            lax.all_gather(out_weight.astype(jnp.bfloat16), ("dp", "seq"), axis=0, tiled=True),
            lax.all_gather(ffn_gain.astype(jnp.bfloat16), ("dp", "seq"), axis=0, tiled=True),
            lax.all_gather(gate_weight.astype(jnp.bfloat16), ("dp", "seq"), axis=0, tiled=True),
            lax.all_gather(up_weight.astype(jnp.bfloat16), ("dp", "seq"), axis=0, tiled=True),
            lax.all_gather(down_weight.astype(jnp.bfloat16), ("dp", "seq"), axis=0, tiled=True),
        )
        grad_in = out_grad[micro_index].astype(jnp.float32).reshape(row_count, D)
        grad_low = grad_in.astype(jnp.bfloat16)
        full_grads[8] = rows_inner(hidden_low, grad_low)
        grad_hidden = times_transposed(grad_low, w_down)
        grad_gate = (grad_hidden * up_pre * gate_sig * (1.0 + gate_pre * (1.0 - gate_sig))).astype(
            jnp.bfloat16
        )
        grad_up = (grad_hidden * gate_pre * gate_sig).astype(jnp.bfloat16)
        full_grads[6] = rows_inner(grad_gate, normed_two)
        full_grads[7] = rows_inner(grad_up, normed_two)
        grad_normed_two = product(grad_gate, w_gate) + product(grad_up, w_up)
        full_grads[5] = jnp.sum(grad_normed_two * middle * inv_two, axis=0)
        grad_middle = grad_in + norm_back(
            middle, inv_two, gain_two.astype(jnp.float32), grad_normed_two
        )
        grad_middle_low = grad_middle.astype(jnp.bfloat16)
        full_grads[4] = rows_inner(attended_low, grad_middle_low)
        grad_attended = (
            times_transposed(grad_middle_low, w_out)
            .astype(jnp.bfloat16)
            .reshape(seq_count, tok_count, H, HD)
        )
        delta_row = jnp.transpose(
            jnp.sum(grad_attended.astype(jnp.float32) * attended, axis=-1), (0, 2, 1)
        )
        context = (query_rot, kinds_now, grad_attended, log_total, delta_row, variate_bias)
        base_carry = (
            jnp.zeros((seq_count, H, tok_count, HD), jnp.float32),
            jnp.zeros((2, H), jnp.float32),
        )
        length_all = tok_count * lax.axis_size("seq")
        wide_carry = (
            jnp.zeros((seq_count, length_all, D), jnp.float32),
            jnp.zeros((seq_count, length_all, D), jnp.float32),
        )
        grad_query_heads, grad_bias, key_all, value_all = back_piece(
            context,
            base_carry + wide_carry,
            (
                lax.all_gather(key_flat, "seq", axis=1, tiled=True),
                lax.all_gather(value_flat, "seq", axis=1, tiled=True),
                lax.all_gather(kinds_now, "seq", axis=1, tiled=True),
            ),
        )
        grad_key, grad_value = (
            lax.psum_scatter(
                key_all.astype(jnp.bfloat16), "seq", scatter_dimension=1, tiled=True
            ).astype(jnp.float32),
            lax.psum_scatter(
                value_all.astype(jnp.bfloat16), "seq", scatter_dimension=1, tiled=True
            ).astype(jnp.float32),
        )
        grad_key = grad_key.reshape(seq_count, tok_count, H, HD)
        grad_value_low = grad_value.reshape(row_count, D).astype(jnp.bfloat16)
        small_grads[2] = grad_bias
        grad_query = jnp.transpose(grad_query_heads, (0, 2, 1, 3))
        grad_query_norm = rotate_back(grad_query, cos_part, sin_part)
        small_grads[0] = jnp.sum(grad_query_norm * query_raw * inv_query, axis=(0, 1, 2))
        grad_query_low = (
            norm_back(query_raw, inv_query, query_gain, grad_query_norm)
            .reshape(row_count, D)
            .astype(jnp.bfloat16)
        )
        grad_key_norm = rotate_back(grad_key, cos_part, sin_part)
        small_grads[1] = jnp.sum(grad_key_norm * key_raw * inv_key, axis=(0, 1, 2))
        grad_key_low = (
            norm_back(key_raw, inv_key, key_gain, grad_key_norm)
            .reshape(row_count, D)
            .astype(jnp.bfloat16)
        )
        full_grads[1] = rows_inner(normed, grad_query_low)
        full_grads[2] = rows_inner(normed, grad_key_low)
        full_grads[3] = rows_inner(normed, grad_value_low)
        grad_normed = (
            times_transposed(grad_query_low, w_query)
            + times_transposed(grad_key_low, w_key)
            + times_transposed(grad_value_low, w_value)
        )
        full_grads[0] = jnp.sum(grad_normed * hidden_in * inv_one, axis=0)
        input_total = grad_middle + norm_back(
            hidden_in, inv_one, gain_one.astype(jnp.float32), grad_normed
        )
        input_grads.append(input_total.reshape(seq_count, tok_count, D).astype(jnp.bfloat16))
        shards = (
            lax.psum_scatter(full_grads[0], ("dp", "seq"), scatter_dimension=0, tiled=True),
            lax.psum_scatter(full_grads[1], ("dp", "seq"), scatter_dimension=0, tiled=True),
            lax.psum_scatter(full_grads[2], ("dp", "seq"), scatter_dimension=0, tiled=True),
            lax.psum_scatter(full_grads[3], ("dp", "seq"), scatter_dimension=0, tiled=True),
            lax.psum_scatter(full_grads[4], ("dp", "seq"), scatter_dimension=0, tiled=True),
            lax.psum_scatter(full_grads[5], ("dp", "seq"), scatter_dimension=0, tiled=True),
            lax.psum_scatter(full_grads[6], ("dp", "seq"), scatter_dimension=0, tiled=True),
            lax.psum_scatter(full_grads[7], ("dp", "seq"), scatter_dimension=0, tiled=True),
            lax.psum_scatter(full_grads[8], ("dp", "seq"), scatter_dimension=0, tiled=True),
        )
        summed = lax.psum((small_grads[0], small_grads[1], small_grads[2]), ("dp", "seq"))
        shards, summed = (list(shards), list(summed))
        if shard_total is None:
            shard_total = shards
            small_total = summed
        else:
            shard_total = [
                earlier_part + later_part for earlier_part, later_part in zip(shard_total, shards)
            ]
            small_total = [
                earlier_part + later_part for earlier_part, later_part in zip(small_total, summed)
            ]
        full_grads = [jnp.zeros_like(member) for member in full_grads]
        small_grads = [jnp.zeros_like(member) for member in small_grads]
    return (
        jnp.stack(outputs_list),
        jnp.stack(input_grads),
        shard_total[0],
        shard_total[1],
        shard_total[2],
        shard_total[3],
        shard_total[4],
        small_total[0],
        small_total[1],
        small_total[2],
        shard_total[5],
        shard_total[6],
        shard_total[7],
        shard_total[8],
    )


def swap_seq(values, mask):
    return lax.ppermute(values, "seq", [(at, at ^ mask) for at in range(8)])


def swap_dp(values, mask):
    return lax.ppermute(values, "dp", [(at, at ^ mask) for at in range(4)])


def pick(pieces, which):
    chosen = pieces[-1]
    for at in range(len(pieces) - 2, -1, -1):
        chosen = jnp.where(which == at, pieces[at], chosen)
    return chosen


def ordered(pieces, own):
    return jnp.stack([pick(pieces, own ^ at) for at in range(len(pieces))])


def together(*values):
    return lax.optimization_barrier(values)


def at_index(values, index, axis=0):
    return lax.dynamic_index_in_dim(values, index, axis, keepdims=False)


def contract_last(left_side, right_side):
    return lax.dot_general(
        left_side, right_side, (((1,), (1,)), ((), ())), preferred_element_type=jnp.float32
    )


def head_sums(values, block):
    first = values.astype(jnp.bfloat16)
    second = (values - first.astype(jnp.float32)).astype(jnp.bfloat16)
    return jnp.dot(first, block, preferred_element_type=jnp.float32) + jnp.dot(
        second, block, preferred_element_type=jnp.float32
    )


def head_block(scale):
    rows = lax.broadcasted_iota(jnp.int32, (128, 128), 0) // HD
    columns = lax.broadcasted_iota(jnp.int32, (128, 128), 1) // HD
    return jnp.where(rows == columns, scale, 0.0).astype(jnp.bfloat16)


def rope_partner(values):
    lane = lax.broadcasted_iota(jnp.int32, values.shape, 1)
    return jnp.where(
        lane % HD < HD // 2, pltpu.roll(values, 128 - HD // 2, 1), pltpu.roll(values, HD // 2, 1)
    )


def three_parts(values):
    first = values.astype(jnp.bfloat16).astype(jnp.float32)
    second = (values - first).astype(jnp.bfloat16).astype(jnp.float32)
    third = (values - first - second).astype(jnp.bfloat16).astype(jnp.float32)
    return first, second, third


GRANT = 60 << 20
BQ = 1024
BK = 1024
LSE_LANE = 24


def attend_kernel(
    q_in,
    k_in,
    v_in,
    cos_in,
    sin_in,
    hot_in,
    q_gain,
    k_gain,
    bias_in,
    near_out,
    far_out,
    qs_out,
    ks_out,
    vs_out,
    ext_out,
    kx,
    vx,
):
    mean_block = head_block(1.0 / HD)

    def prepare(raw, gain):
        inv = lax.rsqrt(head_sums(raw * raw, mean_block) + epsilon)
        scaled = raw * inv * gain
        return scaled * cos_in[...] + rope_partner(scaled) * sin_in[...]

    qs_out[...] = (
        prepare(q_in[...], q_gain[...]).astype(jnp.bfloat16).astype(jnp.float32) * HD**-0.5
    ).astype(jnp.bfloat16)
    keys = prepare(k_in[...], k_gain[...]).astype(jnp.bfloat16)
    ks_out[...] = keys
    kx[:, :128] = keys
    kx[:, 128:] = hot_in[...]
    values = v_in[...].astype(jnp.bfloat16)
    vs_out[...] = values
    vx[:, :128] = values
    vx[:, 128:] = jnp.ones(values.shape, jnp.bfloat16)
    lane = lax.broadcasted_iota(jnp.int32, (BQ, 128), 1)

    def step(block, carry):
        rows = pl.ds(pl.multiple_of(block * BQ, BQ), BQ)
        queries = qs_out[rows, :].astype(jnp.float32)
        hot = hot_in[rows, :].astype(jnp.float32)
        results = []
        for head in range(2):
            mine = jnp.where(lane // HD == head, queries, 0.0).astype(jnp.bfloat16)
            extra = hot * bias_in[0, head : head + 1, :]
            scores = contract_last(
                jnp.concatenate([mine, extra.astype(jnp.bfloat16)], axis=1), kx[...]
            )
            weights = jnp.exp(scores).astype(jnp.bfloat16)
            summed = jnp.dot(weights, vx[...], preferred_element_type=jnp.float32)
            total = summed[:, 128:]
            results.append(summed[:, :128] / total)
            first, second, third = three_parts(-jnp.log(total))
            extra = jnp.where(lane == LSE_LANE, first, extra)
            extra = jnp.where(lane == LSE_LANE + 1, second, extra)
            extra = jnp.where(lane == LSE_LANE + 2, third, extra)
            ext_out[head, rows, :] = extra.astype(jnp.bfloat16)
        result = jnp.where(lane < HD, results[0], results[1]).astype(jnp.bfloat16)
        half = near_out.shape[0]
        near_out[...] = result[:half]
        far_out[...] = result[half:]
        return carry

    lax.fori_loop(0, q_in.shape[0] // BQ, step, 0)


def attend_back_kernel(
    q_in,
    k_in,
    qs_in,
    ks_in,
    vs_in,
    ext_in,
    hot_in,
    grad_near,
    grad_far,
    att_near,
    att_far,
    cos_in,
    sin_in,
    q_gain,
    k_gain,
    out,
    gain_out,
    bias_out,
    kx,
    vx,
    kt,
    qx,
    qg,
    gx,
    dqt,
    dk_sum,
    dv_sum,
):
    tokens = q_in.shape[0]
    lane = lax.broadcasted_iota(jnp.int32, (tokens, 128), 1)
    keys = ks_in[...]
    kx[:, :128] = keys
    kx[:, 128:] = hot_in[...]
    kt[...] = keys.astype(jnp.float32).T.astype(jnp.bfloat16)
    vx[:, :128] = vs_in[...]
    vx[:, 128:] = jnp.where(lane % HD < 3, 1.0, 0.0).astype(jnp.bfloat16)
    grads = jnp.concatenate([grad_near[...], grad_far[...]]).astype(jnp.float32)
    results = jnp.concatenate([att_near[...], att_far[...]]).astype(jnp.float32)
    delta = head_sums(grads * results, head_block(1.0))
    first, second, third = three_parts(-delta)
    parts = jnp.where(
        lane % HD == 0,
        first,
        jnp.where(lane % HD == 1, second, jnp.where(lane % HD == 2, third, 0.0)),
    )
    queries = qs_in[...].astype(jnp.float32)
    for head in range(2):
        own = lane // HD == head
        mine = jnp.where(own, queries, 0.0).astype(jnp.bfloat16)
        qx[head, :, :128] = mine
        qx[head, :, 128:] = ext_in[head]
        qg[head, :, :128] = mine
        qg[head, :, 128:] = hot_in[...]
        gx[head, :, :128] = jnp.where(own, grads, 0.0).astype(jnp.bfloat16)
        gx[head, :, 128:] = jnp.where(own, parts, 0.0).astype(jnp.bfloat16)
    dqt[...] = jnp.zeros(dqt.shape, jnp.float32)
    block_lane = lax.broadcasted_iota(jnp.int32, (BK, 128), 1)
    counted = jnp.where((block_lane < 8) | (block_lane == LSE_LANE), 1.0, 0.0)

    def step(block, carry):
        rows = pl.ds(pl.multiple_of(block * BK, BK), BK)
        hot = hot_in[rows, :].astype(jnp.float32) * counted
        dk_parts = []
        dv_parts = []
        bias_parts = []
        for head in range(2):
            probs = jnp.exp(contract_last(kx[rows, :], qx[head]))
            dscores = (probs * contract_last(vx[rows, :], gx[head])).astype(jnp.bfloat16)
            dv_parts.append(
                jnp.dot(
                    probs.astype(jnp.bfloat16), gx[head, :, :128], preferred_element_type=jnp.float32
                )
            )
            wide = jnp.dot(dscores, qg[head], preferred_element_type=jnp.float32)
            dk_parts.append(wide[:, :128])
            bias_parts.append(jnp.sum(wide[:, 128:] * hot, axis=0, keepdims=True))
            head_rows = pl.ds(head * HD, HD)
            dqt[head_rows, :] += jnp.dot(
                kt[head_rows, rows], dscores, preferred_element_type=jnp.float32
            )
        dk_sum[rows, :] = dk_parts[0] + dk_parts[1]
        dv_sum[rows, :] = dv_parts[0] + dv_parts[1]
        return (carry[0] + bias_parts[0], carry[1] + bias_parts[1])

    zero = jnp.zeros((1, 128), jnp.float32)
    sums = lax.fori_loop(0, tokens // BK, step, (zero, zero))
    bias_out[0, 0:1, :] = sums[0]
    bias_out[0, 1:2, :] = sums[1]
    mean_block = head_block(1.0 / HD)

    def finish(raw, upstream, gain):
        inv = lax.rsqrt(head_sums(raw * raw, mean_block) + epsilon)
        normed = upstream * cos_in[...] - rope_partner(upstream) * sin_in[...]
        gain_grad = jnp.sum(normed * raw * inv, axis=0, keepdims=True)
        weighted = normed * gain
        inner = head_sums(weighted * raw, mean_block)
        return inv * weighted - raw * (inv * inv * inv) * inner, gain_grad

    dq, dq_gain = finish(q_in[...], dqt[...].T * HD**-0.5, q_gain[...])
    dk, dk_gain = finish(k_in[...], dk_sum[...], k_gain[...])
    out[0] = dq.astype(jnp.bfloat16)
    out[1] = dk.astype(jnp.bfloat16)
    out[2] = dv_sum[...].astype(jnp.bfloat16)
    gain_out[0, 0:1, :] = dq_gain
    gain_out[0, 1:2, :] = dk_gain


def attend(qkv, cos_part, sin_part, hot, q_gain, k_gain, bias_rows):
    tokens = qkv.shape[0]
    column = lambda shift: pl.BlockSpec((tokens, 128), lambda pair: (0, pair + shift))
    half = pl.BlockSpec((tokens // 2, 128), lambda pair: (0, pair))
    whole = pl.BlockSpec((tokens, 128), lambda pair: (0, 0))
    line = pl.BlockSpec((1, 128), lambda pair: (0, 0))
    low = lambda: jax.ShapeDtypeStruct((tokens, 256), jnp.bfloat16)
    return pl.pallas_call(
        attend_kernel,
        grid=(2,),
        in_specs=[
            column(0),
            column(2),
            column(4),
            whole,
            whole,
            whole,
            line,
            line,
            pl.BlockSpec((1, 2, 128), lambda pair: (pair, 0, 0)),
        ],
        out_specs=[
            half,
            half,
            column(0),
            column(0),
            column(0),
            pl.BlockSpec((2, tokens, 128), lambda pair: (pair, 0, 0)),
        ],
        out_shape=[
            jax.ShapeDtypeStruct((tokens // 2, 256), jnp.bfloat16),
            jax.ShapeDtypeStruct((tokens // 2, 256), jnp.bfloat16),
            low(),
            low(),
            low(),
            jax.ShapeDtypeStruct((4, tokens, 128), jnp.bfloat16),
        ],
        scratch_shapes=[
            pltpu.VMEM((tokens, 256), jnp.bfloat16),
            pltpu.VMEM((tokens, 256), jnp.bfloat16),
        ],
        compiler_params=pltpu.CompilerParams(vmem_limit_bytes=GRANT),
        name="attend",
    )(qkv, qkv, qkv, cos_part, sin_part, hot, q_gain, k_gain, bias_rows)


def attend_back(qkv, saved, hot, grads, attended, cos_part, sin_part, q_gain, k_gain):
    queries, keys, values, extra = saved
    tokens = qkv.shape[0]
    column = lambda shift: pl.BlockSpec((tokens, 128), lambda pair: (0, pair + shift))
    half = pl.BlockSpec((tokens // 2, 128), lambda pair: (0, pair))
    whole = pl.BlockSpec((tokens, 128), lambda pair: (0, 0))
    line = pl.BlockSpec((1, 128), lambda pair: (0, 0))
    two = pl.BlockSpec((1, 2, 128), lambda pair: (pair, 0, 0))
    wide = pltpu.VMEM((tokens, 256), jnp.bfloat16)
    both = pltpu.VMEM((2, tokens, 256), jnp.bfloat16)
    return pl.pallas_call(
        attend_back_kernel,
        grid=(2,),
        in_specs=[
            column(0),
            column(2),
            column(0),
            column(0),
            column(0),
            pl.BlockSpec((2, tokens, 128), lambda pair: (pair, 0, 0)),
            whole,
            half,
            half,
            half,
            half,
            whole,
            whole,
            line,
            line,
        ],
        out_specs=[pl.BlockSpec((3, tokens, 128), lambda pair: (0, 0, pair)), two, two],
        out_shape=[
            jax.ShapeDtypeStruct((3, tokens, 256), jnp.bfloat16),
            jax.ShapeDtypeStruct((2, 2, 128), jnp.float32),
            jax.ShapeDtypeStruct((2, 2, 128), jnp.float32),
        ],
        scratch_shapes=[
            wide,
            wide,
            pltpu.VMEM((128, tokens), jnp.bfloat16),
            both,
            both,
            both,
            pltpu.VMEM((128, tokens), jnp.float32),
            pltpu.VMEM((tokens, 128), jnp.float32),
            pltpu.VMEM((tokens, 128), jnp.float32),
        ],
        compiler_params=pltpu.CompilerParams(vmem_limit_bytes=GRANT),
        cost_estimate=pl.CostEstimate(
            flops=40 * tokens * tokens * 256,
            bytes_accessed=tokens * 256 * 40,
            transcendentals=4 * tokens * tokens,
        ),
        name="attend_back",
    )(
        qkv,
        qkv,
        queries,
        keys,
        values,
        extra,
        hot,
        *grads,
        *attended,
        cos_part,
        sin_part,
        q_gain,
        k_gain,
    )


def as_column(line):
    count = line.shape[1]
    rows = lax.broadcasted_iota(jnp.int32, (count, count), 0)
    columns = lax.broadcasted_iota(jnp.int32, (count, count), 1)
    return jnp.sum(jnp.where(rows == columns, line, 0.0), axis=1, keepdims=True)


def head_kernel(own_ids, other_ids, gain, gain_two, *refs):
    weights, (same_out, near_out, far_out, out_out) = refs[:4], refs[4:]
    out_out[:, :D] = weights[3][...].astype(jnp.bfloat16)
    lane = lax.broadcasted_iota(jnp.int32, (32, 128), 1)
    out_out[:, D:] = jnp.where(lane == 0, as_column(gain_two[...]), 0.0).astype(jnp.bfloat16)
    level = lax.axis_index("seq") >> 1
    batch, parity = level >> 1, level & 1
    scale = as_column(gain[...].astype(jnp.bfloat16).astype(jnp.float32))

    def scaled(at, turn):
        part = weights[at][:, pl.ds(pl.multiple_of(turn * 512, 512), 512)]
        return (part.astype(jnp.bfloat16).astype(jnp.float32) * scale).astype(jnp.bfloat16)

    for at in range(3):
        lanes = slice(at * 512, (at + 1) * 512)
        same_out[:, lanes] = scaled(at, parity)
        crossed = scaled(at, 1 - parity)
        near_out[:, lanes] = crossed
        far_out[:, lanes] = crossed
    rows = lax.broadcasted_iota(jnp.int32, (32, 128), 0)

    def listed(which):
        block = jnp.zeros((32, 128), jnp.int32)
        for side, ids in enumerate((own_ids, other_ids)):
            times = ids[which, 1:2, :]
            for at, line in enumerate((ids[which, 0:1, :], times >> 6, times & 63)):
                block = jnp.where(rows == side * 3 + at, line, block)
        return block.astype(jnp.float32).astype(jnp.bfloat16)

    near_out[:, 1536:] = listed(batch)
    far_ids = listed(1 - batch)
    same_out[:, 1536:] = far_ids
    far_out[:, 1536:] = far_ids


def head(own_ids, other_ids, gain, gain_two, weights):
    whole = lambda shape: pl.BlockSpec(shape, lambda at: (0,) * len(shape))
    arguments = [own_ids, other_ids, gain, gain_two, *weights]
    return pl.pallas_call(
        head_kernel,
        grid=(1,),
        in_specs=[whole(member.shape) for member in arguments],
        out_specs=[whole((32, 1664))] * 3 + [whole((32, D + 128))],
        out_shape=[jax.ShapeDtypeStruct((32, 1664), jnp.bfloat16)] * 3
        + [jax.ShapeDtypeStruct((32, D + 128), jnp.bfloat16)],
        compiler_params=pltpu.CompilerParams(vmem_limit_bytes=GRANT),
        name="head",
    )(*arguments)


def front_kernel(place, *refs):
    pieces, crossed, own, other = refs[:4], refs[4], refs[5:9], refs[9]
    weights_out, unit_out, qkv_out = refs[10:]
    dp_at, level, core = place[0], place[1], place[2]
    step = pl.program_id(0)

    def norm(values):
        wide = values.astype(jnp.float32)
        return (wide * rms_scale(wide)).astype(jnp.bfloat16)

    @pl.when(step == 0)
    def _():
        for at_dp in range(4):
            for at_level in range(4):
                base = ((dp_at ^ at_dp) * 4 + (level ^ at_level)) * 64
                mine = pl.ds(pl.multiple_of(base + core * 32, 32), 32)
                theirs = pl.ds(pl.multiple_of(base + (1 - core) * 32, 32), 32)
                rows = slice(at_level * 32, at_level * 32 + 32)
                for part in range(3):
                    lanes = pl.ds(pl.multiple_of(part * 512 + core * 256, 256), 256)
                    weights_out[mine, part * 256 : (part + 1) * 256] = pieces[at_dp][rows, lanes]
                start = at_dp * 128 + at_level * 32
                weights_out[theirs, :] = crossed[start : start + 32, :]
        for at in range(4):
            unit_out[at * 128 : (at + 1) * 128, :] = norm(own[at][...])

    @pl.when(step == 1)
    def _():
        for at in range(4):
            unit_out[at * 128 : (at + 1) * 128, :] = norm(other[at])

    qkv_out[...] = jnp.dot(unit_out[...], weights_out[...], preferred_element_type=jnp.float32)


def front(place, pieces, crossed, own, other):
    tokens = 2 * other.shape[0] * other.shape[1]
    quarter = pl.BlockSpec((128, 1536), lambda at: (0, 0))
    piece = pl.BlockSpec((128, D), lambda at: (0, 0))
    return pl.pallas_call(
        front_kernel,
        grid=(2,),
        in_specs=[pl.BlockSpec(memory_space=pltpu.SMEM)]
        + [quarter] * 4
        + [pl.BlockSpec((512, 768), lambda at: (0, 0))]
        + [piece] * 4
        + [pl.BlockSpec((4, 128, D), lambda at: (0, 0, 0))],
        out_specs=[
            pl.BlockSpec((D, 768), lambda at: (0, 0)),
            pl.BlockSpec((tokens // 2, D), lambda at: (at, 0)),
            pl.BlockSpec((tokens // 2, 768), lambda at: (at, 0)),
        ],
        out_shape=[
            jax.ShapeDtypeStruct((D, 768), jnp.bfloat16),
            jax.ShapeDtypeStruct((tokens, D), jnp.bfloat16),
            jax.ShapeDtypeStruct((tokens, 768), jnp.float32),
        ],
        compiler_params=pltpu.CompilerParams(vmem_limit_bytes=GRANT),
        name="front",
    )(place, *pieces, crossed, *own, other)


def tail_kernel(
    place, dqkv, weights, unit, gains, biases, ffn_gain, back_kept, back_sent, kept, sent, part, small
):
    core, group = place[2], place[3]
    tokens = unit.shape[0]

    def back(rows):
        total = contract_last(dqkv[0, rows, :], weights[:, :256])
        for at in (1, 2):
            total += contract_last(dqkv[at, rows, :], weights[:, at * 256 : (at + 1) * 256])
        return total

    back_kept[...] = back(slice(0, tokens // 2))
    back_sent[...] = back(slice(tokens // 2, tokens)).astype(jnp.bfloat16)
    for at in range(3):
        part[:, at * 256 : (at + 1) * 256] = rows_inner(unit[...], dqkv[at]).astype(jnp.bfloat16)
    for at in range(16):
        rows = slice(at * 32, at * 32 + 32)
        kept[rows, :] = part[pl.ds(pl.multiple_of(at * 64 + core * 32, 32), 32), :]
        sent[rows, :] = part[pl.ds(pl.multiple_of(at * 64 + (1 - core) * 32, 32), 32), :]
    lane = lax.broadcasted_iota(jnp.int32, (1, 128), 1)
    sums = gains[0] + gains[1]
    sums = sums + pltpu.roll(sums, HD, 1)
    placed = jnp.zeros((1, 128), jnp.float32)
    for head in range(4):
        line = biases[head // 2, head % 2 : head % 2 + 1, :]
        same = jnp.sum(jnp.where(lane < 8, line, 0.0), axis=1, keepdims=True)
        total = jnp.sum(jnp.where(lane == LSE_LANE, line, 0.0), axis=1, keepdims=True)
        spot = group * 4 + head
        placed = jnp.where(lane == spot, same, placed)
        placed = jnp.where(lane == spot + H, total - same, placed)
    small[...] = jnp.zeros(small.shape, jnp.float32)
    for at in range(4):
        small[at : at + 1, :256] = ffn_gain[:, at * 256 : (at + 1) * 256]
    small[4:5, :128] = jnp.where(lane < HD, sums[0:1], sums[1:2])
    small[4:5, 128:256] = placed
    kept[512:, :] = small[...].astype(jnp.bfloat16)
    sent[512:, :] = small[...].astype(jnp.bfloat16)


def tail(place, dqkv, weights, unit, gains, biases, ffn_gain):
    tokens = unit.shape[0]
    whole = lambda shape: pl.BlockSpec(shape, lambda at: (0,) * len(shape))
    shapes = [
        ((tokens // 2, D), jnp.float32),
        ((tokens // 2, D), jnp.bfloat16),
        ((528, 768), jnp.bfloat16),
        ((528, 768), jnp.bfloat16),
    ]
    arguments = (dqkv, weights, unit, gains, biases, ffn_gain)
    return pl.pallas_call(
        tail_kernel,
        grid=(1,),
        in_specs=[pl.BlockSpec(memory_space=pltpu.SMEM)]
        + [whole(member.shape) for member in arguments],
        out_specs=[whole(shape) for shape, _ in shapes],
        out_shape=[jax.ShapeDtypeStruct(shape, kind) for shape, kind in shapes],
        scratch_shapes=[pltpu.VMEM((D, 768), jnp.bfloat16), pltpu.VMEM((16, 768), jnp.float32)],
        compiler_params=pltpu.CompilerParams(vmem_limit_bytes=GRANT),
        cost_estimate=pl.CostEstimate(
            flops=4 * tokens * D * 768, bytes_accessed=14 * D * D, transcendentals=0
        ),
        name="tail",
    )(place, *arguments)


def finish_kernel(place, mine, near, side, far, gain, *refs):
    weights = refs[:3]
    kept, back_near, passed, inputs, upstream = refs[3:8]
    partial, down_far = refs[8:10]
    grads_out = refs[10:13]
    out_out, input_out, result_out, gain_out, q_out, k_out, bias_out, two_out = refs[13:21]
    wide = jnp.float32
    dp_at, level, core = place[0], place[1], place[2]
    parity, batch = level & 1, level >> 1
    step = pl.program_id(0)

    @pl.when(step == 0)
    def _():
        scale = as_column(gain[...].astype(jnp.bfloat16).astype(wide))
        for at in range(3):
            for side_core in range(2):
                rows = slice(at * 64 + side_core * 32, at * 64 + side_core * 32 + 32)
                same = mine[rows, :].astype(wide) + side[rows, :].astype(wide)
                cross = near[rows, :].astype(wide) + far[rows, :].astype(wide)
                for turn, member in ((parity, same), (1 - parity, cross)):
                    lane = (turn * 2 + (core + side_core) % 2) * 256
                    grads_out[at][:, pl.ds(pl.multiple_of(lane, 256), 256)] = member
        total = jnp.zeros((32, 1), wide)
        for at in range(3):
            unscaled = grads_out[at][...]
            total += jnp.sum(
                unscaled * weights[at][...].astype(jnp.bfloat16).astype(wide), axis=1, keepdims=True
            )
            grads_out[at][...] = unscaled * scale
        rows = lax.broadcasted_iota(jnp.int32, (32, 32), 0)
        columns = lax.broadcasted_iota(jnp.int32, (32, 32), 1)
        gain_out[...] = jnp.sum(jnp.where(rows == columns, total, 0.0), axis=0, keepdims=True)

        def summed(rows):
            return (mine[rows, :].astype(wide) + near[rows, :].astype(wide)) + (
                side[rows, :].astype(wide) + far[rows, :].astype(wide)
            )

        for at in range(4):
            out_out[:, at * 256 : (at + 1) * 256] = summed(slice(192 + at * 32, 224 + at * 32))
        small = summed(slice(320, 336))
        q_out[...] = small[4:5, :HD]
        k_out[...] = small[4:5, HD : 2 * HD]
        bias_out[0:1, :] = small[4:5, 2 * HD : 2 * HD + H]
        bias_out[1:2, :] = small[4:5, 2 * HD + H : 2 * HD + 2 * H]
        two = jnp.zeros((1, 32), wide)
        for at_dp in range(4):
            for at_seq in range(8):
                here = (dp_at == at_dp) & (level * 2 + core == at_seq)
                two = jnp.where(here, small[at_dp : at_dp + 1, at_seq * 32 : at_seq * 32 + 32], two)
        two_out[...] = two
    result_out[...] = (partial[...] + down_far[...].astype(wide)).astype(jnp.bfloat16)
    back = jnp.where(
        step == batch, kept[...] + back_near[...].astype(wide), passed[...].astype(wide)
    )
    values = inputs[0].astype(wide)
    inv = rms_scale(values)
    inner = jnp.mean(back * values, axis=-1, keepdims=True)
    input_out[0] = (
        upstream[0] + inv * back - values * (inv * inv * inv) * inner
    ).astype(jnp.bfloat16)


def finish(place, mine, moved, gain, weights, backs, inputs, upstream, outputs):
    whole = lambda shape: pl.BlockSpec(shape, lambda at: (0,) * len(shape))
    arguments = [mine, *moved, gain, *weights, *backs, inputs, upstream, *outputs]
    f32 = jnp.float32
    shapes = [((32, D), f32)] * 4 + [(inputs.shape, jnp.bfloat16)]
    shapes += [(outputs[0].shape, jnp.bfloat16)]
    shapes += [((1, 32), f32), ((1, HD), f32), ((1, HD), f32), ((2, H), f32), ((1, 32), f32)]
    rows, piece = inputs.shape[0] * inputs.shape[1], inputs.shape[1]
    batch_block = pl.BlockSpec((1, piece, D), lambda at: (at, 0, 0))
    row_block = pl.BlockSpec((piece, D), lambda at: (at, 0))

    def spec(shape):
        return {inputs.shape: batch_block, (rows, D): row_block}.get(tuple(shape), whole(shape))

    return pl.pallas_call(
        finish_kernel,
        grid=(2,),
        in_specs=[pl.BlockSpec(memory_space=pltpu.SMEM)]
        + [spec(member.shape) for member in arguments],
        out_specs=[spec(shape) for shape, _ in shapes],
        out_shape=[jax.ShapeDtypeStruct(shape, kind) for shape, kind in shapes],
        compiler_params=pltpu.CompilerParams(vmem_limit_bytes=GRANT),
        name="finish",
    )(place, *arguments)


def lower_kernel(gate, up, down, out):
    out[0] = gate[...].astype(jnp.bfloat16)
    out[1] = up[...].astype(jnp.bfloat16)
    out[2] = down[...].astype(jnp.bfloat16)


def lower(gate, up, down):
    whole = pl.BlockSpec(gate.shape, lambda at: (0, 0))
    return pl.pallas_call(
        lower_kernel,
        grid=(1,),
        in_specs=[whole] * 3,
        out_specs=pl.BlockSpec((3,) + gate.shape, lambda at: (0, 0, 0)),
        out_shape=jax.ShapeDtypeStruct((3,) + gate.shape, jnp.bfloat16),
        compiler_params=pltpu.CompilerParams(vmem_limit_bytes=GRANT),
        name="lower",
    )(gate, up, down)


def middle_back_kernel(
    place, kept, near, side, far, dy_in, middle_in, gain_in, weights, grad_out, low_out, sums_out, *outs
):
    wide = jnp.float32
    step = pl.program_id(0)
    level = place[1]
    upstream = (kept[...] + near[...].astype(wide)) + (
        side[...].astype(wide) + far[...].astype(wide)
    )
    middle = middle_in[...]
    inv = rms_scale(middle)
    sums = jnp.sum(upstream * middle * inv, axis=0, keepdims=True)

    @pl.when(step == 0)
    def _():
        sums_out[...] = sums

    @pl.when(step == 1)
    def _():
        sums_out[...] += sums

    grad = dy_in[...].astype(wide) + norm_back(middle, inv, gain_in[...], upstream)
    grad_out[...] = grad
    grad_low = grad.astype(jnp.bfloat16)
    low_out[...] = grad_low
    halves = [
        contract_last(grad_low, weights[at * 512 : (at + 1) * 512, :D]).astype(jnp.bfloat16)
        for at in range(2)
    ]
    for mask in range(4):
        for parity in range(2):

            @pl.when((level ^ mask) == step * 2 + parity)
            def _():
                outs[mask][...] = halves[parity]


def middle_back(place, kept, moved, own_dy, middle, gain_two, w_out):
    rows = kept.shape[0]
    block = pl.BlockSpec((rows // 2, D), lambda at: (at, 0))
    line = pl.BlockSpec((1, D), lambda at: (0, 0))
    quarter = pl.BlockSpec((rows // 2, D // 2), lambda at: (0, 0))
    return pl.pallas_call(
        middle_back_kernel,
        grid=(2,),
        in_specs=[pl.BlockSpec(memory_space=pltpu.SMEM)]
        + [block] * 6
        + [line, pl.BlockSpec(w_out.shape, lambda at: (0, 0))],
        out_specs=[block, block, line] + [quarter] * 4,
        out_shape=[
            jax.ShapeDtypeStruct((rows, D), jnp.float32),
            jax.ShapeDtypeStruct((rows, D), jnp.bfloat16),
            jax.ShapeDtypeStruct((1, D), jnp.float32),
        ]
        + [jax.ShapeDtypeStruct((rows // 2, D // 2), jnp.bfloat16)] * 4,
        compiler_params=pltpu.CompilerParams(vmem_limit_bytes=GRANT),
        cost_estimate=pl.CostEstimate(
            flops=2 * rows * D * D, bytes_accessed=22 * rows * D + 2 * D * D, transcendentals=rows
        ),
        name="middle_back",
    )(place, kept, *moved, own_dy, middle, gain_two, w_out)


GATED = 512
HIDDEN = 256


def load_weights(place, sources, gathered, arrived, which):
    level, core = place[1], place[2]
    pieces = [(sources[at], at, core) for at in range(4)]
    pieces += [(sources[4 + at], at, 1 - core) for at in range(4)]
    copies = []
    for at, (source, turn, side) in enumerate(pieces):
        rows = pl.ds(pl.multiple_of(((level ^ turn) * 2 + side) * 128, 128), 128)
        copies.append(
            pltpu.make_async_copy(source.at[which], gathered.at[rows, :], arrived.at[at])
        )
    for copy in copies:
        copy.start()
    return copies


def gated_kernel(count, place, *refs):
    tokens_in, grads_in, sources = refs[:count], refs[count : 2 * count], refs[2 * count :][:8]
    refs = refs[2 * count + 8 :]
    hidden_out, back_out, totals = refs[:count], refs[count : 2 * count], refs[2 * count :][:count]
    weights, arrived = refs[3 * count :]
    level, core = place[1], place[2]
    copies = []
    for at in range(8):
        target = weights.at[:, at * 128 : at * 128 + 128, :]
        copies.append(pltpu.make_async_copy(sources[at], target, arrived.at[at]))
        copies[-1].start()
    for step in range(2):
        for at in range(4):
            copies[step * 4 + at].wait()
        units = slice(step * GATED, (step + 1) * GATED)
        side = 1 - core if step else core
        pair = jnp.concatenate([weights[0, units, :], weights[1, units, :]])
        third = weights[2, units, :]
        for at in range(count):
            both = contract_last(tokens_in[at][...], pair)
            gate, up = both[:, :GATED], both[:, GATED:]
            grad_hidden = contract_last(grads_in[at][0], third)
            sig = lax.logistic(gate)
            swished = gate * sig
            hidden = (swished * up).astype(jnp.bfloat16)
            grad_gate = (grad_hidden * up * sig * (1.0 + gate * (1.0 - sig))).astype(jnp.bfloat16)
            grad_up = (grad_hidden * swished).astype(jnp.bfloat16)
            for turn in range(4):
                lanes = pl.ds(pl.multiple_of(((level ^ turn) * 2 + side) * 128, 128), 128)
                part = slice(turn * 128, turn * 128 + 128)
                hidden_out[at][0, :, lanes] = grad_gate[:, part]
                hidden_out[at][1, :, lanes] = grad_up[:, part]
                hidden_out[at][2, :, lanes] = hidden[:, part]
            added = jnp.dot(
                jnp.concatenate([grad_gate, grad_up], axis=1),
                pair,
                preferred_element_type=jnp.float32,
            )
            if step == 0:
                totals[at][...] = added
            else:
                back_out[at][...] = (totals[at][...] + added).astype(back_out[at].dtype)


def dp_block(mask, chunk):
    return pl.BlockSpec((1, chunk, D), lambda at, place: (place[0] ^ mask, 0, 0))


def gated(place, tokens_in, grads_all, masks, weights, kinds):
    count = len(tokens_in)
    chunk = tokens_in[0].shape[0]
    hidden = 8 * weights[0].shape[1]
    assert hidden == 2 * GATED
    whole = pl.BlockSpec((chunk, D), lambda at, place: (0, 0))
    anywhere = pl.BlockSpec(memory_space=pl.ANY)
    results = pl.pallas_call(
        functools.partial(gated_kernel, count),
        grid_spec=pltpu.PrefetchScalarGridSpec(
            num_scalar_prefetch=1,
            grid=(1,),
            in_specs=[whole] * count
            + [dp_block(mask, chunk) for mask in masks]
            + [anywhere] * len(weights),
            out_specs=[pl.BlockSpec((3, chunk, hidden), lambda at, place: (0, 0, 0))] * count
            + [whole] * count,
            scratch_shapes=[pltpu.VMEM((chunk, D), jnp.float32)] * count
            + [pltpu.VMEM((3, hidden, D), jnp.bfloat16), pltpu.SemaphoreType.DMA((8,))],
        ),
        out_shape=[jax.ShapeDtypeStruct((3, chunk, hidden), jnp.bfloat16)] * count
        + [jax.ShapeDtypeStruct((chunk, D), kind) for kind in kinds],
        compiler_params=pltpu.CompilerParams(vmem_limit_bytes=GRANT),
        cost_estimate=pl.CostEstimate(
            flops=10 * count * chunk * D * hidden,
            bytes_accessed=2 * D * (7 * count * chunk + 3 * hidden),
            transcendentals=count * chunk * hidden,
        ),
        name="gated",
    )(place, *tokens_in, *[grads_all] * count, *weights)
    return list(zip(results[:count], results[count:]))


def ffn_grads_kernel(place, *refs):
    tokens_in, grads_in, hidden_in = refs[0:4], refs[4:8], refs[8:12]
    grads_out, tokens_all, grads_all, hidden = refs[12:]
    chunk = tokens_in[0].shape[0]
    rows_of = [slice(at * chunk, (at + 1) * chunk) for at in range(4)]

    @pl.when(pl.program_id(0) == 0)
    def _():
        for at in range(4):
            tokens_all[rows_of[at], :] = tokens_in[at][...]
            grads_all[rows_of[at], :] = grads_in[at][0]

    for which in range(3):
        for at in range(4):
            hidden[which, rows_of[at], :] = hidden_in[at][which]
        other = tokens_all if which < 2 else grads_all
        grads_out[which] = rows_inner(hidden[which], other[...]).astype(jnp.bfloat16)


def ffn_grads(place, tokens_in, grads_in, hidden_in):
    chunk = tokens_in[0].shape[0]
    tokens = 4 * chunk
    hidden = hidden_in[0].shape[2]
    whole = pl.BlockSpec((chunk, D), lambda at, place: (0, 0))
    wide_low = pltpu.VMEM((tokens, D), jnp.bfloat16)
    return pl.pallas_call(
        ffn_grads_kernel,
        grid_spec=pltpu.PrefetchScalarGridSpec(
            num_scalar_prefetch=1,
            grid=(hidden // HIDDEN,),
            in_specs=[whole] * 4
            + [dp_block(mask, chunk) for mask in range(4)]
            + [pl.BlockSpec((3, chunk, HIDDEN), lambda at, place: (0, 0, at))] * 4,
            out_specs=pl.BlockSpec((3, HIDDEN, D), lambda at, place: (0, at, 0)),
            scratch_shapes=[wide_low, wide_low, pltpu.VMEM((3, tokens, HIDDEN), jnp.bfloat16)],
        ),
        out_shape=jax.ShapeDtypeStruct((3, hidden, D), jnp.bfloat16),
        compiler_params=pltpu.CompilerParams(vmem_limit_bytes=GRANT),
        cost_estimate=pl.CostEstimate(
            flops=6 * tokens * D * hidden,
            bytes_accessed=2 * D * (4 * tokens + 6 * hidden),
            transcendentals=0,
        ),
        name="ffn_grads",
    )(place, *tokens_in, *[grads_in] * 4, *hidden_in)


def down_kernel(place, *refs):
    hidden_in, attended, grads, sources = refs[:4], refs[4], refs[5], refs[6:14]
    outs, kept, sent, part, weights, arrived = refs[14:18], *refs[18:]
    core = place[2]
    copies = load_weights(place, sources, weights, arrived, 2)
    part[...] = rows_inner(attended[...], grads[...]).astype(jnp.bfloat16)
    for at in range(16):
        rows = slice(at * 32, at * 32 + 32)
        kept[rows, :] = part[pl.ds(pl.multiple_of(at * 64 + core * 32, 32), 32), :]
        sent[rows, :] = part[pl.ds(pl.multiple_of(at * 64 + (1 - core) * 32, 32), 32), :]
    for copy in copies:
        copy.wait()
    for at in range(4):
        outs[at][...] = jnp.dot(
            hidden_in[at][0], weights[...], preferred_element_type=jnp.float32
        ).astype(outs[at].dtype)


def down(place, hidden_in, weights, attended, grads):
    chunk = hidden_in[0].shape[1]
    hidden = hidden_in[0].shape[2]
    half = D // 2
    whole = pl.BlockSpec((chunk, D), lambda at, place: (0, 0))
    tall = pl.BlockSpec((half, D), lambda at, place: (0, 0))
    return pl.pallas_call(
        down_kernel,
        grid_spec=pltpu.PrefetchScalarGridSpec(
            num_scalar_prefetch=1,
            grid=(1,),
            in_specs=[pl.BlockSpec((1, chunk, hidden), lambda at, place: (2, 0, 0))] * 4
            + [whole] * 2
            + [pl.BlockSpec(memory_space=pl.ANY)] * len(weights),
            out_specs=[whole] * 4 + [tall] * 2,
            scratch_shapes=[
                pltpu.VMEM((D, D), jnp.bfloat16),
                pltpu.VMEM((hidden, D), jnp.bfloat16),
                pltpu.SemaphoreType.DMA((8,)),
            ],
        ),
        out_shape=[jax.ShapeDtypeStruct((chunk, D), jnp.float32)]
        + [jax.ShapeDtypeStruct((chunk, D), jnp.bfloat16)] * 3
        + [jax.ShapeDtypeStruct((half, D), jnp.bfloat16)] * 2,
        compiler_params=pltpu.CompilerParams(vmem_limit_bytes=GRANT),
        cost_estimate=pl.CostEstimate(
            flops=10 * chunk * D * hidden,
            bytes_accessed=2 * D * (11 * chunk + 2 * hidden),
            transcendentals=0,
        ),
        name="down",
    )(place, *hidden_in, attended, grads, *weights)


def local_split(
    inputs,
    variate_ids,
    time_ids,
    attn_gain,
    query_weight,
    key_weight,
    value_weight,
    out_weight,
    query_gain,
    key_gain,
    variate_bias,
    ffn_gain,
    gate_weight,
    up_weight,
    down_weight,
    out_grad,
):
    low = jnp.bfloat16
    wide = jnp.float32
    dp_at = lax.axis_index("dp")
    seq_at = lax.axis_index("seq")
    core = seq_at & 1
    level = seq_at >> 1
    batch = level >> 1
    parity = level & 1
    piece = inputs.shape[2]
    tokens = 8 * piece
    others = (1, 2, 3)
    swap_core = lambda values: swap_seq(values, 1)
    swap_level = lambda values, mask: swap_seq(values, 2 * mask)

    own_dy = out_grad[:, 0].reshape(2 * piece, D)

    ids = jnp.stack([variate_ids[:, 0], time_ids[:, 0]], axis=1)
    same, cross_near, cross_far, with_gain = head(
        ids,
        swap_core(ids),
        attn_gain[None, :],
        ffn_gain[None, :],
        [query_weight, key_weight, value_weight, out_weight],
    )
    w_out = lax.all_gather(with_gain, ("dp", "seq"), axis=0, tiled=True)
    moved = [swap_level((cross_near, same, cross_far)[mask - 1], mask) for mask in others]
    own_x = inputs[:, 0]
    x_late, moved[0] = together(own_x, moved[0])
    near, far = at_index(x_late, batch), at_index(x_late, 1 - batch)
    (
        same,
        near,
        far,
        gate_local,
        up_local,
        down_local,
        query_gain,
        key_gain,
        variate_bias,
        *moved,
    ) = together(
        same,
        near,
        far,
        gate_weight,
        up_weight,
        down_weight,
        query_gain,
        key_gain,
        variate_bias,
        *moved,
    )
    ffn_local = lower(gate_local, up_local, down_local)

    place = jnp.stack([dp_at, level, core, 2 * parity + core]).astype(jnp.int32)
    rows = jnp.concatenate([same[:, :1536]] + [member[:, :1536] for member in moved])
    ids = jnp.stack([cross_near[:, 1536:]] + [member[:, 1536:] for member in moved])
    moved = [swap_dp(rows, mask) for mask in others]
    from_far = swap_level(far, 2)
    from_near = swap_level(near, 1)
    last = swap_level(from_far, 1)
    ids = jnp.stack([ids[:, :3], ids[:, 3:6]]).astype(wide)

    kinds = ids[:, :, 0].reshape(tokens, 1)
    times = (ids[:, :, 1] * 64.0 + ids[:, :, 2]).reshape(tokens, 1)
    lane = lax.broadcasted_iota(jnp.int32, (1, 128), 1)
    hot = jnp.where(
        lane < LSE_LANE, (kinds == lane % 8).astype(wide), jnp.where(lane < LSE_LANE + 3, 1.0, 0.0)
    ).astype(low)
    half = HD // 2
    frequency = 10000.0 ** (-(lane % half).astype(wide) / half)
    angles = times * frequency
    cos_part = jnp.cos(angles)
    sin_part = jnp.sin(angles) * jnp.where(lane % HD < half, -1.0, 1.0)
    q_gain = jnp.tile(query_gain, 2)[None, :]
    k_gain = jnp.tile(key_gain, 2)[None, :]
    group = 2 * parity + core
    gaps = at_index((variate_bias[0] - variate_bias[1]).reshape(4, 4), group)
    first, second, third = three_parts(gaps)
    bias_rows = jnp.where(
        lane < 8,
        first[:, None],
        jnp.where(
            lane < 16, second[:, None], jnp.where(lane < LSE_LANE, third[:, None], 0.0)
        ),
    ).reshape(2, 2, 128)

    (
        rows,
        ffn_local,
        near,
        from_near,
        from_far,
        last,
        cos_part,
        sin_part,
        dy_sent,
        hot,
        q_gain,
        k_gain,
        bias_rows,
        place,
        *moved,
    ) = together(
        rows,
        ffn_local,
        near,
        from_near,
        from_far,
        last,
        cos_part,
        sin_part,
        own_dy,
        hot,
        q_gain,
        k_gain,
        bias_rows,
        place,
        *moved,
    )

    dy_all = lax.all_gather(dy_sent, "dp", axis=0)

    pieces = [rows] + moved
    own = [near, from_near, from_far, last]
    ffn_near, ffn_far = swap_level(ffn_local, 1), swap_level(ffn_local, 2)
    sent = jnp.concatenate(
        [
            jnp.concatenate(
                [
                    jnp.where(
                        core == 0,
                        member[:, at * 512 + 256 : at * 512 + 512],
                        member[:, at * 512 : at * 512 + 256],
                    )
                    for at in range(3)
                ],
                axis=1,
            )
            for member in pieces
        ]
    )
    crossed, rows_crossed = together(swap_core(jnp.stack(own)), swap_core(sent))

    w_qkv, unit, qkv = front(place, pieces, rows_crossed, own, crossed)
    att_near, att_far, *saved = attend(qkv, cos_part, sin_part, hot, q_gain, k_gain, bias_rows)
    attended = (att_near, att_far)
    att_near, att_far, local_crossed = together(att_near, att_far, swap_core(ffn_local))

    part, crossed = together(att_near, swap_core(att_far))
    part, crossed = part.reshape(4, piece, 256), crossed.reshape(4, piece, 256)
    both = jnp.concatenate(
        [jnp.where(core == 0, part, crossed), jnp.where(core == 0, crossed, part)], axis=2
    )

    w_out, gain_two, ffn_near, ffn_far, *arrived = together(
        w_out,
        w_out[:, D].astype(wide)[None, :],
        ffn_near,
        ffn_far,
        both[0],
        *[swap_level(both[mask], mask) for mask in others],
    )
    blocks = [pick(arrived, level ^ at) for at in range(4)]
    own_att = jnp.concatenate(
        [
            jnp.concatenate([blocks[0], blocks[1]], axis=1),
            jnp.concatenate([blocks[2], blocks[3]], axis=1),
        ]
    )

    own_wide = own_x.reshape(2 * piece, D).astype(wide)
    middle = own_wide + product(own_att, w_out[:, :D])
    inv_two = rms_scale(middle)
    normed_two = (middle * inv_two * gain_two).astype(low)

    normed_two, ffn_near, ffn_far = together(normed_two, ffn_near, ffn_far)
    ffn_last, near_crossed, far_crossed, near_two, side_two, own_two, middle, own_att, gain_two, dy_all = together(
        swap_level(ffn_far, 1),
        swap_core(ffn_near),
        swap_core(ffn_far),
        swap_dp(normed_two, 1),
        swap_dp(normed_two, 2),
        normed_two,
        middle,
        own_att,
        gain_two,
        dy_all,
    )

    far_two = swap_dp(own_two, 3)
    w_ffn = [ffn_local, ffn_near, ffn_far, ffn_last]
    w_ffn += [local_crossed, near_crossed, far_crossed, swap_core(ffn_last)]
    (near_hidden, near_back), (side_hidden, side_back) = gated(
        place, [near_two, side_two], dy_all, (1, 2), w_ffn, (low, low)
    )
    far_two, near_hidden, near_back, side_hidden, side_back = together(
        far_two, near_hidden, near_back, side_hidden, side_back
    )

    near_back, side_back = swap_dp(near_back, 1), swap_dp(side_back, 2)
    (own_hidden, kept), (far_hidden, far_back) = gated(
        place, [own_two, far_two], dy_all, (0, 3), w_ffn, (wide, low)
    )
    own_hidden, kept, far_hidden, far_back, near_back, side_back = together(
        own_hidden, kept, far_hidden, far_back, near_back, side_back
    )
    hidden = [own_hidden, near_hidden, side_hidden, far_hidden]
    ffn_part = ffn_grads(place, [own_two, near_two, side_two, far_two], dy_all, hidden)
    ffn_part, kept, *moved = together(
        ffn_part, kept, near_back, side_back, swap_dp(far_back, 3)
    )
    ffn_shard = lax.psum_scatter(ffn_part, "seq", scatter_dimension=1, tiled=True)
    grad_middle, middle_low, gain_two_part, *blocks = middle_back(
        place, kept, moved, own_dy, middle, gain_two, w_out
    )

    arrived = [blocks[0]] + [swap_level(blocks[mask], mask) for mask in others]
    down_kept, *rest = down(place, hidden, w_ffn, own_att, middle_low)
    down_chunks, out_kept, out_sent = rest[:3], rest[3], rest[4]
    out_kept, out_sent, down_kept, *rest = together(
        out_kept, out_sent, down_kept, *down_chunks, *arrived
    )
    down_chunks, arrived = rest[:3], rest[3:]

    halves = [
        jnp.concatenate([member[:, :256] for member in arrived]),
        jnp.concatenate([member[:, 256:] for member in arrived]),
    ]

    def out_rows(to):
        rows = [
            lax.dynamic_slice_in_dim(member, to * 128, 128).astype(wide)
            for member in (out_kept, out_crossed)
        ]
        return (rows[0] + rows[1]).astype(low)

    kept, crossed, out_kept, out_crossed, *down_chunks = together(
        pick(halves, core),
        swap_core(pick(halves, 1 - core)),
        out_kept,
        swap_core(out_sent),
        *down_chunks,
    )
    out_parts = [out_rows(dp_at ^ mask) for mask in range(4)]
    grads = (kept, crossed)

    out_moved = [swap_dp(out_parts[mask], mask) for mask in others]
    dqkv, gain_sums, bias_sums = attend_back(
        qkv, saved, hot, grads, attended, cos_part, sin_part, q_gain, k_gain
    )
    dqkv, out_kept, last_chunk, *rest = together(
        dqkv,
        out_parts[0],
        down_chunks[2],
        swap_dp(down_chunks[0], 1),
        swap_dp(down_chunks[1], 2),
        *out_moved,
    )
    down_moved, out_moved = rest[:2], rest[2:]

    out_moved = [member.astype(wide) for member in out_moved]
    out_sum = (out_kept.astype(wide) + out_moved[0]) + (out_moved[1] + out_moved[2])
    back_kept, back_sent, kept, sent = tail(
        place, dqkv, w_qkv, unit, gain_sums, bias_sums, gain_two_part
    )
    back_kept, back_crossed, kept, crossed = together(
        back_kept, swap_core(back_sent), kept, swap_core(sent)
    )

    back = (back_kept + back_crossed.astype(wide)).reshape(4, piece, D)
    small_low = (kept[512:].astype(wide) + crossed[512:].astype(wide)).astype(low)

    def dp_message(to):
        return jnp.concatenate(
            [
                lax.dynamic_slice_in_dim(kept, to * 128, 128),
                lax.dynamic_slice_in_dim(crossed, to * 128, 128),
                small_low,
            ]
        )

    moved = [swap_dp(dp_message(dp_at ^ mask), mask) for mask in others]
    passed = back[2] + swap_level(back[3].astype(low), 1).astype(wide)
    passed = swap_level(passed.astype(low), 2)
    down_moved = [member.astype(wide) for member in down_moved]
    partial = (middle + down_kept) + (down_moved[0] + down_moved[1])
    qkv_kept, kept, passed, near, ffn_shard, last_chunk, partial, *moved = together(
        dp_message(dp_at), back[0], passed, back[1].astype(low), ffn_shard, last_chunk, partial, *moved
    )

    moved = [member.astype(wide) for member in moved]
    total = qkv_kept.astype(wide)
    total = ((total + moved[0]) + (moved[1] + moved[2])).astype(low)
    small_low = total[256:]

    out_sum = out_sum.reshape(4, 32, D)
    ffn_sums = ffn_shard.astype(wide)

    def level_message(to):
        out_block = at_index(out_sum, to).astype(low)
        qkv_block = jnp.concatenate(
            [
                lax.dynamic_slice_in_dim(total, to * 32, 32),
                lax.dynamic_slice_in_dim(total, 128 + to * 32, 32),
            ]
        )
        return jnp.concatenate(
            [qkv_block[:, at * 256 : (at + 1) * 256] for at in range(3)]
            + [out_block[:, at * 256 : (at + 1) * 256] for at in range(4)]
            + [small_low[:, :256]]
        )

    mine, kept, near, passed, ffn_sums, last_chunk, *moved = together(
        level_message(level),
        kept,
        swap_level(near, 1),
        passed,
        ffn_sums,
        swap_dp(last_chunk, 3),
        *[swap_level(level_message(level ^ mask), mask) for mask in others],
    )
    *sums, input_grad, result, gain_grad, q_grad, k_grad, bias_grad, gain_two_grad = finish(
        place,
        mine,
        moved,
        attn_gain[None, :],
        [query_weight, key_weight, value_weight],
        [kept, near, passed],
        own_x,
        grad_middle.reshape(2, piece, D),
        [partial, last_chunk],
    )

    shape = (2, 1, piece, D)
    return (
        result.reshape(shape),
        input_grad.reshape(shape),
        gain_grad.reshape(32),
        sums[0],
        sums[1],
        sums[2],
        sums[3],
        q_grad.reshape(HD),
        k_grad.reshape(HD),
        bias_grad,
        gain_two_grad.reshape(32),
        ffn_sums[0],
        ffn_sums[1],
        ffn_sums[2],
    )


def solution(mesh):
    placed = (
        P(None, "dp", "seq", None),
        P(None, "dp", "seq"),
        P(None, "dp", "seq"),
        P(("dp", "seq")),
        P(("dp", "seq"), None),
        P(("dp", "seq"), None),
        P(("dp", "seq"), None),
        P(("dp", "seq"), None),
        P(),
        P(),
        P(),
        P(("dp", "seq")),
        P(("dp", "seq"), None),
        P(("dp", "seq"), None),
        P(("dp", "seq"), None),
        P(None, "dp", "seq", None),
    )
    split = mesh.shape["dp"] == 4 and mesh.shape["seq"] == 8
    return jax.shard_map(
        local_split if split else local,
        mesh=mesh,
        in_specs=placed,
        out_specs=(
            P(None, "dp", "seq", None),
            P(None, "dp", "seq", None),
            P(("dp", "seq")),
            P(("dp", "seq"), None),
            P(("dp", "seq"), None),
            P(("dp", "seq"), None),
            P(("dp", "seq"), None),
            P(),
            P(),
            P(),
            P(("dp", "seq")),
            P(("dp", "seq"), None),
            P(("dp", "seq"), None),
            P(("dp", "seq"), None),
        ),
        check_vma=False,
    )
```

```python
import functools
import math

import jax
import jax.numpy as jnp
from jax import lax
from jax.experimental import pallas as pl
from jax.experimental.pallas import tpu as pltpu
from jax.sharding import PartitionSpec as P

D = 1024
H = 16
HD = 64
FF = 4096


epsilon = 1e-06
lowest = -1e30


def rms_scale(values):
    return lax.rsqrt(jnp.mean(values * values, axis=-1, keepdims=True) + epsilon)


def norm_back(values, inv_rms, gain_vec, upstream):
    weighted = upstream * gain_vec
    inner_mean = jnp.mean(weighted * values, axis=-1, keepdims=True)
    return inv_rms * weighted - values * (inv_rms * inv_rms * inv_rms) * inner_mean


def rotation(positions):
    half_dim = HD // 2
    frequency = 10000.0 ** (-jnp.arange(half_dim).astype(jnp.float32) / half_dim)
    angles = positions.astype(jnp.float32)[..., None] * frequency
    return (jnp.cos(angles)[..., None, :], jnp.sin(angles)[..., None, :])


def rotate(values, cos_part, sin_part):
    half_dim = values.shape[-1] // 2
    first_half = values[..., :half_dim]
    second_half = values[..., half_dim:]
    return jnp.concatenate(
        [
            first_half * cos_part - second_half * sin_part,
            first_half * sin_part + second_half * cos_part,
        ],
        axis=-1,
    )


def rotate_back(upstream, cos_part, sin_part):
    half_dim = upstream.shape[-1] // 2
    first_half = upstream[..., :half_dim]
    second_half = upstream[..., half_dim:]
    return jnp.concatenate(
        [
            first_half * cos_part + second_half * sin_part,
            second_half * cos_part - first_half * sin_part,
        ],
        axis=-1,
    )


def product(left_side, right_side):
    return jnp.dot(left_side, right_side, preferred_element_type=jnp.float32)


def times_transposed(left_side, right_side):
    return lax.dot_general(
        left_side, right_side, (((1,), (1,)), ((), ())), preferred_element_type=jnp.float32
    )


def rows_inner(left_side, right_side):
    return lax.dot_general(
        left_side, right_side, (((0,), (0,)), ((), ())), preferred_element_type=jnp.float32
    )


def score_block(queries, key_rows, query_kinds, key_kinds, variate_bias):
    raw_scores = jnp.einsum(
        "sqhe,skhe->shqk", queries, key_rows, preferred_element_type=jnp.float32
    ) * HD ** (-0.5)
    same_kind = query_kinds[:, None, :, None] == key_kinds[:, None, None, :]
    scores = raw_scores + jnp.where(
        same_kind, variate_bias[0][None, :, None, None], variate_bias[1][None, :, None, None]
    )
    return (scores, same_kind)


def forward_piece(queries, query_kinds, variate_bias, carried, pieces):
    piece_keys, piece_values, piece_kinds = pieces
    seq_count = piece_keys.shape[0]
    piece_len = piece_keys.shape[1]
    block_size = math.gcd(piece_len, 512)

    def forward_advance(block_index, totals):
        running_max, running_total, running_sum = totals
        offset = block_index * block_size
        key_rows = lax.dynamic_slice_in_dim(piece_keys, offset, block_size, 1).reshape(
            seq_count, block_size, H, HD
        )
        value_rows = lax.dynamic_slice_in_dim(piece_values, offset, block_size, 1).reshape(
            seq_count, block_size, H, HD
        )
        kind_rows = lax.dynamic_slice_in_dim(piece_kinds, offset, block_size, 1)
        scores, same_kind = score_block(queries, key_rows, query_kinds, kind_rows, variate_bias)
        new_max = jnp.maximum(running_max, jnp.max(scores, axis=-1))
        factor = jnp.exp(running_max - new_max)
        exp_scores = jnp.exp(scores - new_max[..., None])
        running_total = running_total * factor + jnp.sum(exp_scores, axis=-1)
        running_sum = running_sum * factor[..., None] + jnp.einsum(
            "shqk,skhe->shqe",
            exp_scores.astype(jnp.bfloat16),
            value_rows,
            preferred_element_type=jnp.float32,
        )
        return (new_max, running_total, running_sum)

    return lax.fori_loop(0, piece_len // block_size, forward_advance, carried)


def back_piece(context, carried, pieces):
    queries, query_kinds, grad_out, log_total, delta_row, variate_bias = context
    piece_keys, piece_values, piece_kinds = pieces
    seq_count = piece_keys.shape[0]
    piece_len = piece_keys.shape[1]
    block_size = math.gcd(piece_len, 512)
    score_scale = HD ** (-0.5)

    def back_advance(block_index, totals):
        offset = block_index * block_size
        key_rows = lax.dynamic_slice_in_dim(piece_keys, offset, block_size, 1).reshape(
            seq_count, block_size, H, HD
        )
        value_rows = lax.dynamic_slice_in_dim(piece_values, offset, block_size, 1).reshape(
            seq_count, block_size, H, HD
        )
        kind_rows = lax.dynamic_slice_in_dim(piece_kinds, offset, block_size, 1)
        scores, same_kind = score_block(queries, key_rows, query_kinds, kind_rows, variate_bias)
        attn_prob = jnp.exp(scores - log_total[..., None])
        grad_prob = jnp.einsum(
            "sqhe,skhe->shqk", grad_out, value_rows, preferred_element_type=jnp.float32
        )
        grad_score = attn_prob * (grad_prob - delta_row[..., None])
        bias_step = jnp.stack(
            [
                jnp.sum(jnp.where(same_kind, grad_score, 0.0), axis=(0, 2, 3)),
                jnp.sum(jnp.where(same_kind, 0.0, grad_score), axis=(0, 2, 3)),
            ]
        )
        score_low = grad_score.astype(jnp.bfloat16)
        query_grad = (
            totals[0]
            + jnp.einsum("shqk,skhe->shqe", score_low, key_rows, preferred_element_type=jnp.float32)
            * score_scale
        )
        key_part = (
            jnp.einsum("shqk,sqhe->skhe", score_low, queries, preferred_element_type=jnp.float32)
            * score_scale
        ).reshape(seq_count, block_size, D)
        value_part = jnp.einsum(
            "shqk,sqhe->skhe",
            attn_prob.astype(jnp.bfloat16),
            grad_out,
            preferred_element_type=jnp.float32,
        ).reshape(seq_count, block_size, D)
        key_total = lax.dynamic_update_slice_in_dim(
            totals[2],
            lax.dynamic_slice_in_dim(totals[2], offset, block_size, 1) + key_part,
            offset,
            1,
        )
        value_total = lax.dynamic_update_slice_in_dim(
            totals[3],
            lax.dynamic_slice_in_dim(totals[3], offset, block_size, 1) + value_part,
            offset,
            1,
        )
        return (query_grad, totals[1] + bias_step, key_total, value_total)

    return lax.fori_loop(0, piece_len // block_size, back_advance, carried)


def local(
    inputs,
    variate_ids,
    time_ids,
    attn_gain,
    query_weight,
    key_weight,
    value_weight,
    out_weight,
    query_gain,
    key_gain,
    variate_bias,
    ffn_gain,
    gate_weight,
    up_weight,
    down_weight,
    out_grad,
):
    seq_count = inputs.shape[1]
    tok_count = inputs.shape[2]
    row_count = seq_count * tok_count
    full_grads = [
        jnp.zeros(extent, jnp.float32)
        for extent in ((D,), (D, D), (D, D), (D, D), (D, D), (D,), (FF, D), (FF, D), (FF, D))
    ]
    small_grads = [
        jnp.zeros((HD,), jnp.float32),
        jnp.zeros((HD,), jnp.float32),
        jnp.zeros((2, H), jnp.float32),
    ]
    shard_total = None
    small_total = None
    outputs_list = []
    input_grads = []
    weights_now = None
    for micro_index in range(inputs.shape[0]):
        weights_now = (
            lax.all_gather(attn_gain.astype(jnp.bfloat16), ("dp", "seq"), axis=0, tiled=True),
            lax.all_gather(query_weight.astype(jnp.bfloat16), ("dp", "seq"), axis=0, tiled=True),
            lax.all_gather(key_weight.astype(jnp.bfloat16), ("dp", "seq"), axis=0, tiled=True),
            lax.all_gather(value_weight.astype(jnp.bfloat16), ("dp", "seq"), axis=0, tiled=True),
            lax.all_gather(out_weight.astype(jnp.bfloat16), ("dp", "seq"), axis=0, tiled=True),
            lax.all_gather(ffn_gain.astype(jnp.bfloat16), ("dp", "seq"), axis=0, tiled=True),
            lax.all_gather(gate_weight.astype(jnp.bfloat16), ("dp", "seq"), axis=0, tiled=True),
            lax.all_gather(up_weight.astype(jnp.bfloat16), ("dp", "seq"), axis=0, tiled=True),
            lax.all_gather(down_weight.astype(jnp.bfloat16), ("dp", "seq"), axis=0, tiled=True),
        )
        gain_one, w_query, w_key, w_value, w_out, gain_two, w_gate, w_up, w_down = weights_now
        hidden_in = inputs[micro_index].astype(jnp.float32).reshape(row_count, D)
        kinds_now = variate_ids[micro_index].astype(jnp.bfloat16)
        cos_part, sin_part = rotation(time_ids[micro_index])
        inv_one = rms_scale(hidden_in)
        normed = (hidden_in * inv_one * gain_one.astype(jnp.float32)).astype(jnp.bfloat16)
        query_raw = product(normed, w_query).reshape(seq_count, tok_count, H, HD)
        key_raw = product(normed, w_key).reshape(seq_count, tok_count, H, HD)
        value_flat = product(normed, w_value).astype(jnp.bfloat16).reshape(seq_count, tok_count, D)
        inv_query = rms_scale(query_raw)
        query_rot = rotate(query_raw * inv_query * query_gain, cos_part, sin_part).astype(
            jnp.bfloat16
        )
        inv_key = rms_scale(key_raw)
        key_rot = rotate(key_raw * inv_key * key_gain, cos_part, sin_part).astype(jnp.bfloat16)
        key_flat = key_rot.reshape(seq_count, tok_count, D)
        initial = (
            jnp.full((seq_count, H, tok_count), lowest, jnp.float32),
            jnp.zeros((seq_count, H, tok_count), jnp.float32),
            jnp.zeros((seq_count, H, tok_count, HD), jnp.float32),
        )
        final_max, final_total, final_sum = forward_piece(
            query_rot,
            kinds_now,
            variate_bias,
            initial,
            (
                lax.all_gather(key_flat, "seq", axis=1, tiled=True),
                lax.all_gather(value_flat, "seq", axis=1, tiled=True),
                lax.all_gather(kinds_now, "seq", axis=1, tiled=True),
            ),
        )
        log_total = final_max + jnp.log(final_total)
        attended = jnp.transpose(final_sum / final_total[..., None], (0, 2, 1, 3))
        attended_low = attended.reshape(row_count, D).astype(jnp.bfloat16)
        middle = hidden_in + product(attended_low, w_out)
        inv_two = rms_scale(middle)
        normed_two = (middle * inv_two * gain_two.astype(jnp.float32)).astype(jnp.bfloat16)
        gate_pre = times_transposed(normed_two, w_gate)
        up_pre = times_transposed(normed_two, w_up)
        gate_sig = jax.nn.sigmoid(gate_pre)
        hidden_low = (gate_pre * gate_sig * up_pre).astype(jnp.bfloat16)
        result = middle + product(hidden_low, w_down)
        outputs_list.append(result.reshape(seq_count, tok_count, D).astype(jnp.bfloat16))
        gain_one, w_query, w_key, w_value, w_out, gain_two, w_gate, w_up, w_down = (
            lax.all_gather(attn_gain.astype(jnp.bfloat16), ("dp", "seq"), axis=0, tiled=True),
            lax.all_gather(query_weight.astype(jnp.bfloat16), ("dp", "seq"), axis=0, tiled=True),
            lax.all_gather(key_weight.astype(jnp.bfloat16), ("dp", "seq"), axis=0, tiled=True),
            lax.all_gather(value_weight.astype(jnp.bfloat16), ("dp", "seq"), axis=0, tiled=True),
            lax.all_gather(out_weight.astype(jnp.bfloat16), ("dp", "seq"), axis=0, tiled=True),
            lax.all_gather(ffn_gain.astype(jnp.bfloat16), ("dp", "seq"), axis=0, tiled=True),
            lax.all_gather(gate_weight.astype(jnp.bfloat16), ("dp", "seq"), axis=0, tiled=True),
            lax.all_gather(up_weight.astype(jnp.bfloat16), ("dp", "seq"), axis=0, tiled=True),
            lax.all_gather(down_weight.astype(jnp.bfloat16), ("dp", "seq"), axis=0, tiled=True),
        )
        grad_in = out_grad[micro_index].astype(jnp.float32).reshape(row_count, D)
        grad_low = grad_in.astype(jnp.bfloat16)
        full_grads[8] = rows_inner(hidden_low, grad_low)
        grad_hidden = times_transposed(grad_low, w_down)
        grad_gate = (grad_hidden * up_pre * gate_sig * (1.0 + gate_pre * (1.0 - gate_sig))).astype(
            jnp.bfloat16
        )
        grad_up = (grad_hidden * gate_pre * gate_sig).astype(jnp.bfloat16)
        full_grads[6] = rows_inner(grad_gate, normed_two)
        full_grads[7] = rows_inner(grad_up, normed_two)
        grad_normed_two = product(grad_gate, w_gate) + product(grad_up, w_up)
        full_grads[5] = jnp.sum(grad_normed_two * middle * inv_two, axis=0)
        grad_middle = grad_in + norm_back(
            middle, inv_two, gain_two.astype(jnp.float32), grad_normed_two
        )
        grad_middle_low = grad_middle.astype(jnp.bfloat16)
        full_grads[4] = rows_inner(attended_low, grad_middle_low)
        grad_attended = (
            times_transposed(grad_middle_low, w_out)
            .astype(jnp.bfloat16)
            .reshape(seq_count, tok_count, H, HD)
        )
        delta_row = jnp.transpose(
            jnp.sum(grad_attended.astype(jnp.float32) * attended, axis=-1), (0, 2, 1)
        )
        context = (query_rot, kinds_now, grad_attended, log_total, delta_row, variate_bias)
        base_carry = (
            jnp.zeros((seq_count, H, tok_count, HD), jnp.float32),
            jnp.zeros((2, H), jnp.float32),
        )
        length_all = tok_count * lax.axis_size("seq")
        wide_carry = (
            jnp.zeros((seq_count, length_all, D), jnp.float32),
            jnp.zeros((seq_count, length_all, D), jnp.float32),
        )
        grad_query_heads, grad_bias, key_all, value_all = back_piece(
            context,
            base_carry + wide_carry,
            (
                lax.all_gather(key_flat, "seq", axis=1, tiled=True),
                lax.all_gather(value_flat, "seq", axis=1, tiled=True),
                lax.all_gather(kinds_now, "seq", axis=1, tiled=True),
            ),
        )
        grad_key, grad_value = (
            lax.psum_scatter(
                key_all.astype(jnp.bfloat16), "seq", scatter_dimension=1, tiled=True
            ).astype(jnp.float32),
            lax.psum_scatter(
                value_all.astype(jnp.bfloat16), "seq", scatter_dimension=1, tiled=True
            ).astype(jnp.float32),
        )
        grad_key = grad_key.reshape(seq_count, tok_count, H, HD)
        grad_value_low = grad_value.reshape(row_count, D).astype(jnp.bfloat16)
        small_grads[2] = grad_bias
        grad_query = jnp.transpose(grad_query_heads, (0, 2, 1, 3))
        grad_query_norm = rotate_back(grad_query, cos_part, sin_part)
        small_grads[0] = jnp.sum(grad_query_norm * query_raw * inv_query, axis=(0, 1, 2))
        grad_query_low = (
            norm_back(query_raw, inv_query, query_gain, grad_query_norm)
            .reshape(row_count, D)
            .astype(jnp.bfloat16)
        )
        grad_key_norm = rotate_back(grad_key, cos_part, sin_part)
        small_grads[1] = jnp.sum(grad_key_norm * key_raw * inv_key, axis=(0, 1, 2))
        grad_key_low = (
            norm_back(key_raw, inv_key, key_gain, grad_key_norm)
            .reshape(row_count, D)
            .astype(jnp.bfloat16)
        )
        full_grads[1] = rows_inner(normed, grad_query_low)
        full_grads[2] = rows_inner(normed, grad_key_low)
        full_grads[3] = rows_inner(normed, grad_value_low)
        grad_normed = (
            times_transposed(grad_query_low, w_query)
            + times_transposed(grad_key_low, w_key)
            + times_transposed(grad_value_low, w_value)
        )
        full_grads[0] = jnp.sum(grad_normed * hidden_in * inv_one, axis=0)
        input_total = grad_middle + norm_back(
            hidden_in, inv_one, gain_one.astype(jnp.float32), grad_normed
        )
        input_grads.append(input_total.reshape(seq_count, tok_count, D).astype(jnp.bfloat16))
        shards = (
            lax.psum_scatter(full_grads[0], ("dp", "seq"), scatter_dimension=0, tiled=True),
            lax.psum_scatter(full_grads[1], ("dp", "seq"), scatter_dimension=0, tiled=True),
            lax.psum_scatter(full_grads[2], ("dp", "seq"), scatter_dimension=0, tiled=True),
            lax.psum_scatter(full_grads[3], ("dp", "seq"), scatter_dimension=0, tiled=True),
            lax.psum_scatter(full_grads[4], ("dp", "seq"), scatter_dimension=0, tiled=True),
            lax.psum_scatter(full_grads[5], ("dp", "seq"), scatter_dimension=0, tiled=True),
            lax.psum_scatter(full_grads[6], ("dp", "seq"), scatter_dimension=0, tiled=True),
            lax.psum_scatter(full_grads[7], ("dp", "seq"), scatter_dimension=0, tiled=True),
            lax.psum_scatter(full_grads[8], ("dp", "seq"), scatter_dimension=0, tiled=True),
        )
        summed = lax.psum((small_grads[0], small_grads[1], small_grads[2]), ("dp", "seq"))
        shards, summed = (list(shards), list(summed))
        if shard_total is None:
            shard_total = shards
            small_total = summed
        else:
            shard_total = [
                earlier_part + later_part for earlier_part, later_part in zip(shard_total, shards)
            ]
            small_total = [
                earlier_part + later_part for earlier_part, later_part in zip(small_total, summed)
            ]
        full_grads = [jnp.zeros_like(member) for member in full_grads]
        small_grads = [jnp.zeros_like(member) for member in small_grads]
    return (
        jnp.stack(outputs_list),
        jnp.stack(input_grads),
        shard_total[0],
        shard_total[1],
        shard_total[2],
        shard_total[3],
        shard_total[4],
        small_total[0],
        small_total[1],
        small_total[2],
        shard_total[5],
        shard_total[6],
        shard_total[7],
        shard_total[8],
    )


def swap_seq(values, mask):
    return lax.ppermute(values, "seq", [(at, at ^ mask) for at in range(8)])


def swap_dp(values, mask):
    return lax.ppermute(values, "dp", [(at, at ^ mask) for at in range(4)])


def pick(pieces, which):
    chosen = pieces[-1]
    for at in range(len(pieces) - 2, -1, -1):
        chosen = jnp.where(which == at, pieces[at], chosen)
    return chosen


def ordered(pieces, own):
    return jnp.stack([pick(pieces, own ^ at) for at in range(len(pieces))])


def together(*values):
    return lax.optimization_barrier(values)


def at_index(values, index, axis=0):
    return lax.dynamic_index_in_dim(values, index, axis, keepdims=False)


def contract_last(left_side, right_side):
    return lax.dot_general(
        left_side, right_side, (((1,), (1,)), ((), ())), preferred_element_type=jnp.float32
    )


def head_sums(values, block):
    first = values.astype(jnp.bfloat16)
    second = (values - first.astype(jnp.float32)).astype(jnp.bfloat16)
    return jnp.dot(first, block, preferred_element_type=jnp.float32) + jnp.dot(
        second, block, preferred_element_type=jnp.float32
    )


def head_block(scale):
    rows = lax.broadcasted_iota(jnp.int32, (128, 128), 0) // HD
    columns = lax.broadcasted_iota(jnp.int32, (128, 128), 1) // HD
    return jnp.where(rows == columns, scale, 0.0).astype(jnp.bfloat16)


def rope_partner(values):
    lane = lax.broadcasted_iota(jnp.int32, values.shape, 1)
    return jnp.where(
        lane % HD < HD // 2, pltpu.roll(values, 128 - HD // 2, 1), pltpu.roll(values, HD // 2, 1)
    )


def three_parts(values):
    first = values.astype(jnp.bfloat16).astype(jnp.float32)
    second = (values - first).astype(jnp.bfloat16).astype(jnp.float32)
    third = (values - first - second).astype(jnp.bfloat16).astype(jnp.float32)
    return first, second, third


GRANT = 60 << 20
BQ = 1024
BK = 1024
LSE_LANE = 24


def attend_kernel(
    q_in,
    k_in,
    v_in,
    cos_in,
    sin_in,
    hot_in,
    q_gain,
    k_gain,
    bias_in,
    near_out,
    far_out,
    qs_out,
    ks_out,
    vs_out,
    ext_out,
    kx,
    vx,
):
    mean_block = head_block(1.0 / HD)

    def prepare(raw, gain):
        inv = lax.rsqrt(head_sums(raw * raw, mean_block) + epsilon)
        scaled = raw * inv * gain
        return scaled * cos_in[...] + rope_partner(scaled) * sin_in[...]

    qs_out[...] = (
        prepare(q_in[...], q_gain[...]).astype(jnp.bfloat16).astype(jnp.float32) * HD**-0.5
    ).astype(jnp.bfloat16)
    keys = prepare(k_in[...], k_gain[...]).astype(jnp.bfloat16)
    ks_out[...] = keys
    kx[:, :128] = keys
    kx[:, 128:] = hot_in[...]
    values = v_in[...].astype(jnp.bfloat16)
    vs_out[...] = values
    vx[:, :128] = values
    vx[:, 128:] = jnp.ones(values.shape, jnp.bfloat16)
    lane = lax.broadcasted_iota(jnp.int32, (BQ, 128), 1)

    def step(block, carry):
        rows = pl.ds(pl.multiple_of(block * BQ, BQ), BQ)
        queries = qs_out[rows, :].astype(jnp.float32)
        hot = hot_in[rows, :].astype(jnp.float32)
        results = []
        for head in range(2):
            mine = jnp.where(lane // HD == head, queries, 0.0).astype(jnp.bfloat16)
            extra = hot * bias_in[0, head : head + 1, :]
            scores = contract_last(
                jnp.concatenate([mine, extra.astype(jnp.bfloat16)], axis=1), kx[...]
            )
            weights = jnp.exp(scores).astype(jnp.bfloat16)
            summed = jnp.dot(weights, vx[...], preferred_element_type=jnp.float32)
            total = summed[:, 128:]
            results.append(summed[:, :128] / total)
            first, second, third = three_parts(-jnp.log(total))
            extra = jnp.where(lane == LSE_LANE, first, extra)
            extra = jnp.where(lane == LSE_LANE + 1, second, extra)
            extra = jnp.where(lane == LSE_LANE + 2, third, extra)
            ext_out[head, rows, :] = extra.astype(jnp.bfloat16)
        result = jnp.where(lane < HD, results[0], results[1]).astype(jnp.bfloat16)
        half = near_out.shape[0]
        near_out[...] = result[:half]
        far_out[...] = result[half:]
        return carry

    lax.fori_loop(0, q_in.shape[0] // BQ, step, 0)


def attend_back_kernel(
    q_in,
    k_in,
    qs_in,
    ks_in,
    vs_in,
    ext_in,
    hot_in,
    grad_near,
    grad_far,
    att_near,
    att_far,
    cos_in,
    sin_in,
    q_gain,
    k_gain,
    out,
    gain_out,
    bias_out,
    kx,
    vx,
    kt,
    qx,
    qg,
    gx,
    dqt,
    dk_sum,
    dv_sum,
):
    tokens = q_in.shape[0]
    lane = lax.broadcasted_iota(jnp.int32, (tokens, 128), 1)
    keys = ks_in[...]
    kx[:, :128] = keys
    kx[:, 128:] = hot_in[...]
    kt[...] = keys.astype(jnp.float32).T.astype(jnp.bfloat16)
    vx[:, :128] = vs_in[...]
    vx[:, 128:] = jnp.where(lane % HD < 3, 1.0, 0.0).astype(jnp.bfloat16)
    grads = jnp.concatenate([grad_near[...], grad_far[...]]).astype(jnp.float32)
    results = jnp.concatenate([att_near[...], att_far[...]]).astype(jnp.float32)
    delta = head_sums(grads * results, head_block(1.0))
    first, second, third = three_parts(-delta)
    parts = jnp.where(
        lane % HD == 0,
        first,
        jnp.where(lane % HD == 1, second, jnp.where(lane % HD == 2, third, 0.0)),
    )
    queries = qs_in[...].astype(jnp.float32)
    for head in range(2):
        own = lane // HD == head
        mine = jnp.where(own, queries, 0.0).astype(jnp.bfloat16)
        qx[head, :, :128] = mine
        qx[head, :, 128:] = ext_in[head]
        qg[head, :, :128] = mine
        qg[head, :, 128:] = hot_in[...]
        gx[head, :, :128] = jnp.where(own, grads, 0.0).astype(jnp.bfloat16)
        gx[head, :, 128:] = jnp.where(own, parts, 0.0).astype(jnp.bfloat16)
    dqt[...] = jnp.zeros(dqt.shape, jnp.float32)
    block_lane = lax.broadcasted_iota(jnp.int32, (BK, 128), 1)
    counted = jnp.where((block_lane < 8) | (block_lane == LSE_LANE), 1.0, 0.0)

    def step(block, carry):
        rows = pl.ds(pl.multiple_of(block * BK, BK), BK)
        hot = hot_in[rows, :].astype(jnp.float32) * counted
        dk_parts = []
        dv_parts = []
        bias_parts = []
        for head in range(2):
            probs = jnp.exp(contract_last(kx[rows, :], qx[head]))
            dscores = (probs * contract_last(vx[rows, :], gx[head])).astype(jnp.bfloat16)
            dv_parts.append(
                jnp.dot(
                    probs.astype(jnp.bfloat16), gx[head, :, :128], preferred_element_type=jnp.float32
                )
            )
            wide = jnp.dot(dscores, qg[head], preferred_element_type=jnp.float32)
            dk_parts.append(wide[:, :128])
            bias_parts.append(jnp.sum(wide[:, 128:] * hot, axis=0, keepdims=True))
            head_rows = pl.ds(head * HD, HD)
            dqt[head_rows, :] += jnp.dot(
                kt[head_rows, rows], dscores, preferred_element_type=jnp.float32
            )
        dk_sum[rows, :] = dk_parts[0] + dk_parts[1]
        dv_sum[rows, :] = dv_parts[0] + dv_parts[1]
        return (carry[0] + bias_parts[0], carry[1] + bias_parts[1])

    zero = jnp.zeros((1, 128), jnp.float32)
    sums = lax.fori_loop(0, tokens // BK, step, (zero, zero))
    bias_out[0, 0:1, :] = sums[0]
    bias_out[0, 1:2, :] = sums[1]
    mean_block = head_block(1.0 / HD)

    def finish(raw, upstream, gain):
        inv = lax.rsqrt(head_sums(raw * raw, mean_block) + epsilon)
        normed = upstream * cos_in[...] - rope_partner(upstream) * sin_in[...]
        gain_grad = jnp.sum(normed * raw * inv, axis=0, keepdims=True)
        weighted = normed * gain
        inner = head_sums(weighted * raw, mean_block)
        return inv * weighted - raw * (inv * inv * inv) * inner, gain_grad

    dq, dq_gain = finish(q_in[...], dqt[...].T * HD**-0.5, q_gain[...])
    dk, dk_gain = finish(k_in[...], dk_sum[...], k_gain[...])
    out[0] = dq.astype(jnp.bfloat16)
    out[1] = dk.astype(jnp.bfloat16)
    out[2] = dv_sum[...].astype(jnp.bfloat16)
    gain_out[0, 0:1, :] = dq_gain
    gain_out[0, 1:2, :] = dk_gain


def attend(qkv, cos_part, sin_part, hot, q_gain, k_gain, bias_rows):
    tokens = qkv.shape[0]
    column = lambda shift: pl.BlockSpec((tokens, 128), lambda pair: (0, pair + shift))
    half = pl.BlockSpec((tokens // 2, 128), lambda pair: (0, pair))
    whole = pl.BlockSpec((tokens, 128), lambda pair: (0, 0))
    line = pl.BlockSpec((1, 128), lambda pair: (0, 0))
    low = lambda: jax.ShapeDtypeStruct((tokens, 256), jnp.bfloat16)
    return pl.pallas_call(
        attend_kernel,
        grid=(2,),
        in_specs=[
            column(0),
            column(2),
            column(4),
            whole,
            whole,
            whole,
            line,
            line,
            pl.BlockSpec((1, 2, 128), lambda pair: (pair, 0, 0)),
        ],
        out_specs=[
            half,
            half,
            column(0),
            column(0),
            column(0),
            pl.BlockSpec((2, tokens, 128), lambda pair: (pair, 0, 0)),
        ],
        out_shape=[
            jax.ShapeDtypeStruct((tokens // 2, 256), jnp.bfloat16),
            jax.ShapeDtypeStruct((tokens // 2, 256), jnp.bfloat16),
            low(),
            low(),
            low(),
            jax.ShapeDtypeStruct((4, tokens, 128), jnp.bfloat16),
        ],
        scratch_shapes=[
            pltpu.VMEM((tokens, 256), jnp.bfloat16),
            pltpu.VMEM((tokens, 256), jnp.bfloat16),
        ],
        compiler_params=pltpu.CompilerParams(vmem_limit_bytes=GRANT),
        name="attend",
    )(qkv, qkv, qkv, cos_part, sin_part, hot, q_gain, k_gain, bias_rows)


def attend_back(qkv, saved, hot, grads, attended, cos_part, sin_part, q_gain, k_gain):
    queries, keys, values, extra = saved
    tokens = qkv.shape[0]
    column = lambda shift: pl.BlockSpec((tokens, 128), lambda pair: (0, pair + shift))
    half = pl.BlockSpec((tokens // 2, 128), lambda pair: (0, pair))
    whole = pl.BlockSpec((tokens, 128), lambda pair: (0, 0))
    line = pl.BlockSpec((1, 128), lambda pair: (0, 0))
    two = pl.BlockSpec((1, 2, 128), lambda pair: (pair, 0, 0))
    wide = pltpu.VMEM((tokens, 256), jnp.bfloat16)
    both = pltpu.VMEM((2, tokens, 256), jnp.bfloat16)
    return pl.pallas_call(
        attend_back_kernel,
        grid=(2,),
        in_specs=[
            column(0),
            column(2),
            column(0),
            column(0),
            column(0),
            pl.BlockSpec((2, tokens, 128), lambda pair: (pair, 0, 0)),
            whole,
            half,
            half,
            half,
            half,
            whole,
            whole,
            line,
            line,
        ],
        out_specs=[pl.BlockSpec((3, tokens, 128), lambda pair: (0, 0, pair)), two, two],
        out_shape=[
            jax.ShapeDtypeStruct((3, tokens, 256), jnp.bfloat16),
            jax.ShapeDtypeStruct((2, 2, 128), jnp.float32),
            jax.ShapeDtypeStruct((2, 2, 128), jnp.float32),
        ],
        scratch_shapes=[
            wide,
            wide,
            pltpu.VMEM((128, tokens), jnp.bfloat16),
            both,
            both,
            both,
            pltpu.VMEM((128, tokens), jnp.float32),
            pltpu.VMEM((tokens, 128), jnp.float32),
            pltpu.VMEM((tokens, 128), jnp.float32),
        ],
        compiler_params=pltpu.CompilerParams(vmem_limit_bytes=GRANT),
        cost_estimate=pl.CostEstimate(
            flops=40 * tokens * tokens * 256,
            bytes_accessed=tokens * 256 * 40,
            transcendentals=4 * tokens * tokens,
        ),
        name="attend_back",
    )(
        qkv,
        qkv,
        queries,
        keys,
        values,
        extra,
        hot,
        *grads,
        *attended,
        cos_part,
        sin_part,
        q_gain,
        k_gain,
    )


def as_column(line):
    count = line.shape[1]
    rows = lax.broadcasted_iota(jnp.int32, (count, count), 0)
    columns = lax.broadcasted_iota(jnp.int32, (count, count), 1)
    return jnp.sum(jnp.where(rows == columns, line, 0.0), axis=1, keepdims=True)


def head_kernel(own_ids, other_ids, gain, gain_two, *refs):
    weights, (same_out, near_out, far_out, out_out) = refs[:4], refs[4:]
    out_out[:, :D] = weights[3][...].astype(jnp.bfloat16)
    lane = lax.broadcasted_iota(jnp.int32, (32, 128), 1)
    out_out[:, D:] = jnp.where(lane == 0, as_column(gain_two[...]), 0.0).astype(jnp.bfloat16)
    level = lax.axis_index("seq") >> 1
    batch, parity = level >> 1, level & 1
    scale = as_column(gain[...].astype(jnp.bfloat16).astype(jnp.float32))

    def scaled(at, turn):
        part = weights[at][:, pl.ds(pl.multiple_of(turn * 512, 512), 512)]
        return (part.astype(jnp.bfloat16).astype(jnp.float32) * scale).astype(jnp.bfloat16)

    for at in range(3):
        lanes = slice(at * 512, (at + 1) * 512)
        same_out[:, lanes] = scaled(at, parity)
        crossed = scaled(at, 1 - parity)
        near_out[:, lanes] = crossed
        far_out[:, lanes] = crossed
    rows = lax.broadcasted_iota(jnp.int32, (32, 128), 0)

    def listed(which):
        block = jnp.zeros((32, 128), jnp.int32)
        for side, ids in enumerate((own_ids, other_ids)):
            times = ids[which, 1:2, :]
            for at, line in enumerate((ids[which, 0:1, :], times >> 6, times & 63)):
                block = jnp.where(rows == side * 3 + at, line, block)
        return block.astype(jnp.float32).astype(jnp.bfloat16)

    near_out[:, 1536:] = listed(batch)
    far_ids = listed(1 - batch)
    same_out[:, 1536:] = far_ids
    far_out[:, 1536:] = far_ids


def head(own_ids, other_ids, gain, gain_two, weights):
    whole = lambda shape: pl.BlockSpec(shape, lambda at: (0,) * len(shape))
    arguments = [own_ids, other_ids, gain, gain_two, *weights]
    return pl.pallas_call(
        head_kernel,
        grid=(1,),
        in_specs=[whole(member.shape) for member in arguments],
        out_specs=[whole((32, 1664))] * 3 + [whole((32, D + 128))],
        out_shape=[jax.ShapeDtypeStruct((32, 1664), jnp.bfloat16)] * 3
        + [jax.ShapeDtypeStruct((32, D + 128), jnp.bfloat16)],
        compiler_params=pltpu.CompilerParams(vmem_limit_bytes=GRANT),
        name="head",
    )(*arguments)


def front_kernel(place, *refs):
    pieces, crossed, own, other = refs[:4], refs[4], refs[5:9], refs[9]
    weights_out, unit_out, qkv_out = refs[10:]
    dp_at, level, core = place[0], place[1], place[2]
    step = pl.program_id(0)

    def norm(values):
        wide = values.astype(jnp.float32)
        return (wide * rms_scale(wide)).astype(jnp.bfloat16)

    @pl.when(step == 0)
    def _():
        for at_dp in range(4):
            for at_level in range(4):
                base = ((dp_at ^ at_dp) * 4 + (level ^ at_level)) * 64
                mine = pl.ds(pl.multiple_of(base + core * 32, 32), 32)
                theirs = pl.ds(pl.multiple_of(base + (1 - core) * 32, 32), 32)
                rows = slice(at_level * 32, at_level * 32 + 32)
                for part in range(3):
                    lanes = pl.ds(pl.multiple_of(part * 512 + core * 256, 256), 256)
                    weights_out[mine, part * 256 : (part + 1) * 256] = pieces[at_dp][rows, lanes]
                start = at_dp * 128 + at_level * 32
                weights_out[theirs, :] = crossed[start : start + 32, :]
        for at in range(4):
            unit_out[at * 128 : (at + 1) * 128, :] = norm(own[at][...])

    @pl.when(step == 1)
    def _():
        for at in range(4):
            unit_out[at * 128 : (at + 1) * 128, :] = norm(other[at])

    qkv_out[...] = jnp.dot(unit_out[...], weights_out[...], preferred_element_type=jnp.float32)


def front(place, pieces, crossed, own, other):
    tokens = 2 * other.shape[0] * other.shape[1]
    quarter = pl.BlockSpec((128, 1536), lambda at: (0, 0))
    piece = pl.BlockSpec((128, D), lambda at: (0, 0))
    return pl.pallas_call(
        front_kernel,
        grid=(2,),
        in_specs=[pl.BlockSpec(memory_space=pltpu.SMEM)]
        + [quarter] * 4
        + [pl.BlockSpec((512, 768), lambda at: (0, 0))]
        + [piece] * 4
        + [pl.BlockSpec((4, 128, D), lambda at: (0, 0, 0))],
        out_specs=[
            pl.BlockSpec((D, 768), lambda at: (0, 0)),
            pl.BlockSpec((tokens // 2, D), lambda at: (at, 0)),
            pl.BlockSpec((tokens // 2, 768), lambda at: (at, 0)),
        ],
        out_shape=[
            jax.ShapeDtypeStruct((D, 768), jnp.bfloat16),
            jax.ShapeDtypeStruct((tokens, D), jnp.bfloat16),
            jax.ShapeDtypeStruct((tokens, 768), jnp.float32),
        ],
        compiler_params=pltpu.CompilerParams(vmem_limit_bytes=GRANT),
        name="front",
    )(place, *pieces, crossed, *own, other)


def tail_kernel(
    place, dqkv, weights, unit, gains, biases, ffn_gain, back_kept, back_sent, kept, sent, part, small
):
    core, group = place[2], place[3]
    tokens = unit.shape[0]

    def back(rows):
        total = contract_last(dqkv[0, rows, :], weights[:, :256])
        for at in (1, 2):
            total += contract_last(dqkv[at, rows, :], weights[:, at * 256 : (at + 1) * 256])
        return total

    back_kept[...] = back(slice(0, tokens // 2))
    back_sent[...] = back(slice(tokens // 2, tokens)).astype(jnp.bfloat16)
    for at in range(3):
        part[:, at * 256 : (at + 1) * 256] = rows_inner(unit[...], dqkv[at]).astype(jnp.bfloat16)
    for at in range(16):
        rows = slice(at * 32, at * 32 + 32)
        kept[rows, :] = part[pl.ds(pl.multiple_of(at * 64 + core * 32, 32), 32), :]
        sent[rows, :] = part[pl.ds(pl.multiple_of(at * 64 + (1 - core) * 32, 32), 32), :]
    lane = lax.broadcasted_iota(jnp.int32, (1, 128), 1)
    sums = gains[0] + gains[1]
    sums = sums + pltpu.roll(sums, HD, 1)
    placed = jnp.zeros((1, 128), jnp.float32)
    for head in range(4):
        line = biases[head // 2, head % 2 : head % 2 + 1, :]
        same = jnp.sum(jnp.where(lane < 8, line, 0.0), axis=1, keepdims=True)
        total = jnp.sum(jnp.where(lane == LSE_LANE, line, 0.0), axis=1, keepdims=True)
        spot = group * 4 + head
        placed = jnp.where(lane == spot, same, placed)
        placed = jnp.where(lane == spot + H, total - same, placed)
    small[...] = jnp.zeros(small.shape, jnp.float32)
    for at in range(4):
        small[at : at + 1, :256] = ffn_gain[:, at * 256 : (at + 1) * 256]
    small[4:5, :128] = jnp.where(lane < HD, sums[0:1], sums[1:2])
    small[4:5, 128:256] = placed
    kept[512:, :] = small[...].astype(jnp.bfloat16)
    sent[512:, :] = small[...].astype(jnp.bfloat16)


def tail(place, dqkv, weights, unit, gains, biases, ffn_gain):
    tokens = unit.shape[0]
    whole = lambda shape: pl.BlockSpec(shape, lambda at: (0,) * len(shape))
    shapes = [
        ((tokens // 2, D), jnp.float32),
        ((tokens // 2, D), jnp.bfloat16),
        ((528, 768), jnp.bfloat16),
        ((528, 768), jnp.bfloat16),
    ]
    arguments = (dqkv, weights, unit, gains, biases, ffn_gain)
    return pl.pallas_call(
        tail_kernel,
        grid=(1,),
        in_specs=[pl.BlockSpec(memory_space=pltpu.SMEM)]
        + [whole(member.shape) for member in arguments],
        out_specs=[whole(shape) for shape, _ in shapes],
        out_shape=[jax.ShapeDtypeStruct(shape, kind) for shape, kind in shapes],
        scratch_shapes=[pltpu.VMEM((D, 768), jnp.bfloat16), pltpu.VMEM((16, 768), jnp.float32)],
        compiler_params=pltpu.CompilerParams(vmem_limit_bytes=GRANT),
        cost_estimate=pl.CostEstimate(
            flops=4 * tokens * D * 768, bytes_accessed=14 * D * D, transcendentals=0
        ),
        name="tail",
    )(place, *arguments)


def finish_kernel(place, mine, near, side, far, gain, *refs):
    weights = refs[:3]
    kept, back_near, passed, inputs, upstream = refs[3:8]
    partial, down_far = refs[8:10]
    grads_out = refs[10:13]
    out_out, input_out, result_out, gain_out, q_out, k_out, bias_out, two_out = refs[13:21]
    wide = jnp.float32
    dp_at, level, core = place[0], place[1], place[2]
    parity, batch = level & 1, level >> 1
    step = pl.program_id(0)

    @pl.when(step == 0)
    def _():
        scale = as_column(gain[...].astype(jnp.bfloat16).astype(wide))
        for at in range(3):
            for side_core in range(2):
                rows = slice(at * 64 + side_core * 32, at * 64 + side_core * 32 + 32)
                same = mine[rows, :].astype(wide) + side[rows, :].astype(wide)
                cross = near[rows, :].astype(wide) + far[rows, :].astype(wide)
                for turn, member in ((parity, same), (1 - parity, cross)):
                    lane = (turn * 2 + (core + side_core) % 2) * 256
                    grads_out[at][:, pl.ds(pl.multiple_of(lane, 256), 256)] = member
        total = jnp.zeros((32, 1), wide)
        for at in range(3):
            unscaled = grads_out[at][...]
            total += jnp.sum(
                unscaled * weights[at][...].astype(jnp.bfloat16).astype(wide), axis=1, keepdims=True
            )
            grads_out[at][...] = unscaled * scale
        rows = lax.broadcasted_iota(jnp.int32, (32, 32), 0)
        columns = lax.broadcasted_iota(jnp.int32, (32, 32), 1)
        gain_out[...] = jnp.sum(jnp.where(rows == columns, total, 0.0), axis=0, keepdims=True)

        def summed(rows):
            return (mine[rows, :].astype(wide) + near[rows, :].astype(wide)) + (
                side[rows, :].astype(wide) + far[rows, :].astype(wide)
            )

        for at in range(4):
            out_out[:, at * 256 : (at + 1) * 256] = summed(slice(192 + at * 32, 224 + at * 32))
        small = summed(slice(320, 336))
        q_out[...] = small[4:5, :HD]
        k_out[...] = small[4:5, HD : 2 * HD]
        bias_out[0:1, :] = small[4:5, 2 * HD : 2 * HD + H]
        bias_out[1:2, :] = small[4:5, 2 * HD + H : 2 * HD + 2 * H]
        two = jnp.zeros((1, 32), wide)
        for at_dp in range(4):
            for at_seq in range(8):
                here = (dp_at == at_dp) & (level * 2 + core == at_seq)
                two = jnp.where(here, small[at_dp : at_dp + 1, at_seq * 32 : at_seq * 32 + 32], two)
        two_out[...] = two
    result_out[...] = (partial[...] + down_far[...].astype(wide)).astype(jnp.bfloat16)
    back = jnp.where(
        step == batch, kept[...] + back_near[...].astype(wide), passed[...].astype(wide)
    )
    values = inputs[0].astype(wide)
    inv = rms_scale(values)
    inner = jnp.mean(back * values, axis=-1, keepdims=True)
    input_out[0] = (
        upstream[0] + inv * back - values * (inv * inv * inv) * inner
    ).astype(jnp.bfloat16)


def finish(place, mine, moved, gain, weights, backs, inputs, upstream, outputs):
    whole = lambda shape: pl.BlockSpec(shape, lambda at: (0,) * len(shape))
    arguments = [mine, *moved, gain, *weights, *backs, inputs, upstream, *outputs]
    f32 = jnp.float32
    shapes = [((32, D), f32)] * 4 + [(inputs.shape, jnp.bfloat16)]
    shapes += [(outputs[0].shape, jnp.bfloat16)]
    shapes += [((1, 32), f32), ((1, HD), f32), ((1, HD), f32), ((2, H), f32), ((1, 32), f32)]
    rows, piece = inputs.shape[0] * inputs.shape[1], inputs.shape[1]
    batch_block = pl.BlockSpec((1, piece, D), lambda at: (at, 0, 0))
    row_block = pl.BlockSpec((piece, D), lambda at: (at, 0))

    def spec(shape):
        return {inputs.shape: batch_block, (rows, D): row_block}.get(tuple(shape), whole(shape))

    return pl.pallas_call(
        finish_kernel,
        grid=(2,),
        in_specs=[pl.BlockSpec(memory_space=pltpu.SMEM)]
        + [spec(member.shape) for member in arguments],
        out_specs=[spec(shape) for shape, _ in shapes],
        out_shape=[jax.ShapeDtypeStruct(shape, kind) for shape, kind in shapes],
        compiler_params=pltpu.CompilerParams(vmem_limit_bytes=GRANT),
        name="finish",
    )(place, *arguments)


def lower_kernel(gate, up, down, out):
    out[0] = gate[...].astype(jnp.bfloat16)
    out[1] = up[...].astype(jnp.bfloat16)
    out[2] = down[...].astype(jnp.bfloat16)


def lower(gate, up, down):
    whole = pl.BlockSpec(gate.shape, lambda at: (0, 0))
    return pl.pallas_call(
        lower_kernel,
        grid=(1,),
        in_specs=[whole] * 3,
        out_specs=pl.BlockSpec((3,) + gate.shape, lambda at: (0, 0, 0)),
        out_shape=jax.ShapeDtypeStruct((3,) + gate.shape, jnp.bfloat16),
        compiler_params=pltpu.CompilerParams(vmem_limit_bytes=GRANT),
        name="lower",
    )(gate, up, down)


def middle_back_kernel(
    place, kept, near, side, far, dy_in, middle_in, gain_in, weights, grad_out, low_out, sums_out, *outs
):
    wide = jnp.float32
    step = pl.program_id(0)
    level = place[1]
    upstream = (kept[...] + near[...].astype(wide)) + (
        side[...].astype(wide) + far[...].astype(wide)
    )
    middle = middle_in[...]
    inv = rms_scale(middle)
    sums = jnp.sum(upstream * middle * inv, axis=0, keepdims=True)

    @pl.when(step == 0)
    def _():
        sums_out[...] = sums

    @pl.when(step == 1)
    def _():
        sums_out[...] += sums

    grad = dy_in[...].astype(wide) + norm_back(middle, inv, gain_in[...], upstream)
    grad_out[...] = grad
    grad_low = grad.astype(jnp.bfloat16)
    low_out[...] = grad_low
    halves = [
        contract_last(grad_low, weights[at * 512 : (at + 1) * 512, :D]).astype(jnp.bfloat16)
        for at in range(2)
    ]
    for mask in range(4):
        for parity in range(2):

            @pl.when((level ^ mask) == step * 2 + parity)
            def _():
                outs[mask][...] = halves[parity]


def middle_back(place, kept, moved, own_dy, middle, gain_two, w_out):
    rows = kept.shape[0]
    block = pl.BlockSpec((rows // 2, D), lambda at: (at, 0))
    line = pl.BlockSpec((1, D), lambda at: (0, 0))
    quarter = pl.BlockSpec((rows // 2, D // 2), lambda at: (0, 0))
    return pl.pallas_call(
        middle_back_kernel,
        grid=(2,),
        in_specs=[pl.BlockSpec(memory_space=pltpu.SMEM)]
        + [block] * 6
        + [line, pl.BlockSpec(w_out.shape, lambda at: (0, 0))],
        out_specs=[block, block, line] + [quarter] * 4,
        out_shape=[
            jax.ShapeDtypeStruct((rows, D), jnp.float32),
            jax.ShapeDtypeStruct((rows, D), jnp.bfloat16),
            jax.ShapeDtypeStruct((1, D), jnp.float32),
        ]
        + [jax.ShapeDtypeStruct((rows // 2, D // 2), jnp.bfloat16)] * 4,
        compiler_params=pltpu.CompilerParams(vmem_limit_bytes=GRANT),
        cost_estimate=pl.CostEstimate(
            flops=2 * rows * D * D, bytes_accessed=22 * rows * D + 2 * D * D, transcendentals=rows
        ),
        name="middle_back",
    )(place, kept, *moved, own_dy, middle, gain_two, w_out)


GATED = 512
HIDDEN = 256


def load_weights(place, sources, gathered, arrived, which):
    level, core = place[1], place[2]
    pieces = [(sources[at], at, core) for at in range(4)]
    pieces += [(sources[4 + at], at, 1 - core) for at in range(4)]
    copies = []
    for at, (source, turn, side) in enumerate(pieces):
        rows = pl.ds(pl.multiple_of(((level ^ turn) * 2 + side) * 128, 128), 128)
        copies.append(
            pltpu.make_async_copy(source.at[which], gathered.at[rows, :], arrived.at[at])
        )
    for copy in copies:
        copy.start()
    return copies


def gated_kernel(count, place, *refs):
    tokens_in, grads_in, sources = refs[:count], refs[count : 2 * count], refs[2 * count :][:8]
    refs = refs[2 * count + 8 :]
    hidden_out, back_out, totals = refs[:count], refs[count : 2 * count], refs[2 * count :][:count]
    weights, arrived = refs[3 * count :]
    level, core = place[1], place[2]
    copies = []
    for at in range(8):
        target = weights.at[:, at * 128 : at * 128 + 128, :]
        copies.append(pltpu.make_async_copy(sources[at], target, arrived.at[at]))
        copies[-1].start()
    for step in range(2):
        for at in range(4):
            copies[step * 4 + at].wait()
        units = slice(step * GATED, (step + 1) * GATED)
        side = 1 - core if step else core
        pair = jnp.concatenate([weights[0, units, :], weights[1, units, :]])
        third = weights[2, units, :]
        for at in range(count):
            both = contract_last(tokens_in[at][...], pair)
            gate, up = both[:, :GATED], both[:, GATED:]
            grad_hidden = contract_last(grads_in[at][...], third)
            sig = lax.logistic(gate)
            swished = gate * sig
            hidden = (swished * up).astype(jnp.bfloat16)
            grad_gate = (grad_hidden * up * sig * (1.0 + gate * (1.0 - sig))).astype(jnp.bfloat16)
            grad_up = (grad_hidden * swished).astype(jnp.bfloat16)
            for turn in range(4):
                lanes = pl.ds(pl.multiple_of(((level ^ turn) * 2 + side) * 128, 128), 128)
                part = slice(turn * 128, turn * 128 + 128)
                hidden_out[at][0, :, lanes] = grad_gate[:, part]
                hidden_out[at][1, :, lanes] = grad_up[:, part]
                hidden_out[at][2, :, lanes] = hidden[:, part]
            added = jnp.dot(
                jnp.concatenate([grad_gate, grad_up], axis=1),
                pair,
                preferred_element_type=jnp.float32,
            )
            if step == 0:
                totals[at][...] = added
            else:
                back_out[at][...] = (totals[at][...] + added).astype(back_out[at].dtype)


def gated(place, tokens_in, grads_in, weights, kinds):
    count = len(tokens_in)
    chunk = tokens_in[0].shape[0]
    hidden = 8 * weights[0].shape[1]
    assert hidden == 2 * GATED
    whole = pl.BlockSpec((chunk, D), lambda at, place: (0, 0))
    anywhere = pl.BlockSpec(memory_space=pl.ANY)
    results = pl.pallas_call(
        functools.partial(gated_kernel, count),
        grid_spec=pltpu.PrefetchScalarGridSpec(
            num_scalar_prefetch=1,
            grid=(1,),
            in_specs=[whole] * (2 * count)
            + [anywhere] * len(weights),
            out_specs=[pl.BlockSpec((3, chunk, hidden), lambda at, place: (0, 0, 0))] * count
            + [whole] * count,
            scratch_shapes=[pltpu.VMEM((chunk, D), jnp.float32)] * count
            + [pltpu.VMEM((3, hidden, D), jnp.bfloat16), pltpu.SemaphoreType.DMA((8,))],
        ),
        out_shape=[jax.ShapeDtypeStruct((3, chunk, hidden), jnp.bfloat16)] * count
        + [jax.ShapeDtypeStruct((chunk, D), kind) for kind in kinds],
        compiler_params=pltpu.CompilerParams(vmem_limit_bytes=GRANT),
        cost_estimate=pl.CostEstimate(
            flops=10 * count * chunk * D * hidden,
            bytes_accessed=2 * D * (7 * count * chunk + 3 * hidden),
            transcendentals=count * chunk * hidden,
        ),
        name="gated",
    )(place, *tokens_in, *grads_in, *weights)
    return list(zip(results[:count], results[count:]))


def ffn_grads_kernel(place, *refs):
    tokens_in, grads_in, hidden_in = refs[0:4], refs[4:8], refs[8:12]
    grads_out, tokens_all, grads_all, hidden = refs[12:]
    chunk = tokens_in[0].shape[0]
    rows_of = [slice(at * chunk, (at + 1) * chunk) for at in range(4)]

    @pl.when(pl.program_id(0) == 0)
    def _():
        for at in range(4):
            tokens_all[rows_of[at], :] = tokens_in[at][...]
            grads_all[rows_of[at], :] = grads_in[at][...]

    for which in range(3):
        for at in range(4):
            hidden[which, rows_of[at], :] = hidden_in[at][which]
        other = tokens_all if which < 2 else grads_all
        grads_out[which] = rows_inner(hidden[which], other[...]).astype(jnp.bfloat16)


def ffn_grads(place, tokens_in, grads_in, hidden_in):
    chunk = tokens_in[0].shape[0]
    tokens = 4 * chunk
    hidden = hidden_in[0].shape[2]
    whole = pl.BlockSpec((chunk, D), lambda at, place: (0, 0))
    wide_low = pltpu.VMEM((tokens, D), jnp.bfloat16)
    return pl.pallas_call(
        ffn_grads_kernel,
        grid_spec=pltpu.PrefetchScalarGridSpec(
            num_scalar_prefetch=1,
            grid=(hidden // HIDDEN,),
            in_specs=[whole] * 8
            + [pl.BlockSpec((3, chunk, HIDDEN), lambda at, place: (0, 0, at))] * 4,
            out_specs=pl.BlockSpec((3, HIDDEN, D), lambda at, place: (0, at, 0)),
            scratch_shapes=[wide_low, wide_low, pltpu.VMEM((3, tokens, HIDDEN), jnp.bfloat16)],
        ),
        out_shape=jax.ShapeDtypeStruct((3, hidden, D), jnp.bfloat16),
        compiler_params=pltpu.CompilerParams(vmem_limit_bytes=GRANT),
        cost_estimate=pl.CostEstimate(
            flops=6 * tokens * D * hidden,
            bytes_accessed=2 * D * (4 * tokens + 6 * hidden),
            transcendentals=0,
        ),
        name="ffn_grads",
    )(place, *tokens_in, *grads_in, *hidden_in)


def down_kernel(place, *refs):
    hidden_in, attended, grads, sources = refs[:4], refs[4], refs[5], refs[6:14]
    outs, kept, sent, part, weights, arrived = refs[14:18], *refs[18:]
    core = place[2]
    copies = load_weights(place, sources, weights, arrived, 2)
    part[...] = rows_inner(attended[...], grads[...]).astype(jnp.bfloat16)
    for at in range(16):
        rows = slice(at * 32, at * 32 + 32)
        kept[rows, :] = part[pl.ds(pl.multiple_of(at * 64 + core * 32, 32), 32), :]
        sent[rows, :] = part[pl.ds(pl.multiple_of(at * 64 + (1 - core) * 32, 32), 32), :]
    for copy in copies:
        copy.wait()
    for at in range(4):
        outs[at][...] = jnp.dot(
            hidden_in[at][0], weights[...], preferred_element_type=jnp.float32
        ).astype(outs[at].dtype)


def down(place, hidden_in, weights, attended, grads):
    chunk = hidden_in[0].shape[1]
    hidden = hidden_in[0].shape[2]
    half = D // 2
    whole = pl.BlockSpec((chunk, D), lambda at, place: (0, 0))
    tall = pl.BlockSpec((half, D), lambda at, place: (0, 0))
    return pl.pallas_call(
        down_kernel,
        grid_spec=pltpu.PrefetchScalarGridSpec(
            num_scalar_prefetch=1,
            grid=(1,),
            in_specs=[pl.BlockSpec((1, chunk, hidden), lambda at, place: (2, 0, 0))] * 4
            + [whole] * 2
            + [pl.BlockSpec(memory_space=pl.ANY)] * len(weights),
            out_specs=[whole] * 4 + [tall] * 2,
            scratch_shapes=[
                pltpu.VMEM((D, D), jnp.bfloat16),
                pltpu.VMEM((hidden, D), jnp.bfloat16),
                pltpu.SemaphoreType.DMA((8,)),
            ],
        ),
        out_shape=[jax.ShapeDtypeStruct((chunk, D), jnp.float32)]
        + [jax.ShapeDtypeStruct((chunk, D), jnp.bfloat16)] * 3
        + [jax.ShapeDtypeStruct((half, D), jnp.bfloat16)] * 2,
        compiler_params=pltpu.CompilerParams(vmem_limit_bytes=GRANT),
        cost_estimate=pl.CostEstimate(
            flops=10 * chunk * D * hidden,
            bytes_accessed=2 * D * (11 * chunk + 2 * hidden),
            transcendentals=0,
        ),
        name="down",
    )(place, *hidden_in, attended, grads, *weights)


def local_split(
    inputs,
    variate_ids,
    time_ids,
    attn_gain,
    query_weight,
    key_weight,
    value_weight,
    out_weight,
    query_gain,
    key_gain,
    variate_bias,
    ffn_gain,
    gate_weight,
    up_weight,
    down_weight,
    out_grad,
):
    low = jnp.bfloat16
    wide = jnp.float32
    dp_at = lax.axis_index("dp")
    seq_at = lax.axis_index("seq")
    core = seq_at & 1
    level = seq_at >> 1
    batch = level >> 1
    parity = level & 1
    piece = inputs.shape[2]
    tokens = 8 * piece
    others = (1, 2, 3)
    swap_core = lambda values: swap_seq(values, 1)
    swap_level = lambda values, mask: swap_seq(values, 2 * mask)

    own_dy = out_grad[:, 0].reshape(2 * piece, D)

    ids = jnp.stack([variate_ids[:, 0], time_ids[:, 0]], axis=1)
    same, cross_near, cross_far, with_gain = head(
        ids,
        swap_core(ids),
        attn_gain[None, :],
        ffn_gain[None, :],
        [query_weight, key_weight, value_weight, out_weight],
    )
    w_out = lax.all_gather(with_gain, ("dp", "seq"), axis=0, tiled=True)
    moved = [swap_level((cross_near, same, cross_far)[mask - 1], mask) for mask in others]
    own_x = inputs[:, 0]
    dy_near, dy_side = swap_dp(own_dy, 1), swap_dp(own_dy, 2)
    x_late, moved[0] = together(own_x, moved[0])
    near, far = at_index(x_late, batch), at_index(x_late, 1 - batch)
    (
        same,
        dy_near,
        dy_side,
        near,
        far,
        gate_local,
        up_local,
        down_local,
        query_gain,
        key_gain,
        variate_bias,
        *moved,
    ) = together(
        same,
        dy_near,
        dy_side,
        near,
        far,
        gate_weight,
        up_weight,
        down_weight,
        query_gain,
        key_gain,
        variate_bias,
        *moved,
    )
    ffn_local = lower(gate_local, up_local, down_local)

    place = jnp.stack([dp_at, level, core, 2 * parity + core]).astype(jnp.int32)
    rows = jnp.concatenate([same[:, :1536]] + [member[:, :1536] for member in moved])
    ids = jnp.stack([cross_near[:, 1536:]] + [member[:, 1536:] for member in moved])
    moved = [swap_dp(rows, mask) for mask in others]
    from_far = swap_level(far, 2)
    from_near = swap_level(near, 1)
    last = swap_level(from_far, 1)
    ids = jnp.stack([ids[:, :3], ids[:, 3:6]]).astype(wide)

    kinds = ids[:, :, 0].reshape(tokens, 1)
    times = (ids[:, :, 1] * 64.0 + ids[:, :, 2]).reshape(tokens, 1)
    lane = lax.broadcasted_iota(jnp.int32, (1, 128), 1)
    hot = jnp.where(
        lane < LSE_LANE, (kinds == lane % 8).astype(wide), jnp.where(lane < LSE_LANE + 3, 1.0, 0.0)
    ).astype(low)
    half = HD // 2
    frequency = 10000.0 ** (-(lane % half).astype(wide) / half)
    angles = times * frequency
    cos_part = jnp.cos(angles)
    sin_part = jnp.sin(angles) * jnp.where(lane % HD < half, -1.0, 1.0)
    q_gain = jnp.tile(query_gain, 2)[None, :]
    k_gain = jnp.tile(key_gain, 2)[None, :]
    group = 2 * parity + core
    gaps = at_index((variate_bias[0] - variate_bias[1]).reshape(4, 4), group)
    first, second, third = three_parts(gaps)
    bias_rows = jnp.where(
        lane < 8,
        first[:, None],
        jnp.where(
            lane < 16, second[:, None], jnp.where(lane < LSE_LANE, third[:, None], 0.0)
        ),
    ).reshape(2, 2, 128)

    (
        rows,
        ffn_local,
        near,
        from_near,
        from_far,
        last,
        cos_part,
        sin_part,
        dy_sent,
        hot,
        q_gain,
        k_gain,
        bias_rows,
        place,
        *moved,
    ) = together(
        rows,
        ffn_local,
        near,
        from_near,
        from_far,
        last,
        cos_part,
        sin_part,
        own_dy,
        hot,
        q_gain,
        k_gain,
        bias_rows,
        place,
        *moved,
    )

    pieces = [rows] + moved
    own = [near, from_near, from_far, last]
    ffn_near, ffn_far = swap_level(ffn_local, 1), swap_level(ffn_local, 2)
    sent = jnp.concatenate(
        [
            jnp.concatenate(
                [
                    jnp.where(
                        core == 0,
                        member[:, at * 512 + 256 : at * 512 + 512],
                        member[:, at * 512 : at * 512 + 256],
                    )
                    for at in range(3)
                ],
                axis=1,
            )
            for member in pieces
        ]
    )
    crossed, rows_crossed = together(swap_core(jnp.stack(own)), swap_core(sent))

    w_qkv, unit, qkv = front(place, pieces, rows_crossed, own, crossed)
    att_near, att_far, *saved = attend(qkv, cos_part, sin_part, hot, q_gain, k_gain, bias_rows)
    attended = (att_near, att_far)
    att_near, att_far, local_crossed, dy_far = together(
        att_near, att_far, swap_core(ffn_local), swap_dp(dy_sent, 3)
    )

    part, crossed = together(att_near, swap_core(att_far))
    part, crossed = part.reshape(4, piece, 256), crossed.reshape(4, piece, 256)
    both = jnp.concatenate(
        [jnp.where(core == 0, part, crossed), jnp.where(core == 0, crossed, part)], axis=2
    )

    w_out, gain_two, ffn_near, ffn_far, *arrived = together(
        w_out,
        w_out[:, D].astype(wide)[None, :],
        ffn_near,
        ffn_far,
        both[0],
        *[swap_level(both[mask], mask) for mask in others],
    )
    blocks = [pick(arrived, level ^ at) for at in range(4)]
    own_att = jnp.concatenate(
        [
            jnp.concatenate([blocks[0], blocks[1]], axis=1),
            jnp.concatenate([blocks[2], blocks[3]], axis=1),
        ]
    )

    own_wide = own_x.reshape(2 * piece, D).astype(wide)
    middle = own_wide + product(own_att, w_out[:, :D])
    inv_two = rms_scale(middle)
    normed_two = (middle * inv_two * gain_two).astype(low)

    normed_two, ffn_near, ffn_far = together(normed_two, ffn_near, ffn_far)
    ffn_last, near_crossed, far_crossed, near_two, side_two, own_two, middle, own_att, gain_two = together(
        swap_level(ffn_far, 1),
        swap_core(ffn_near),
        swap_core(ffn_far),
        swap_dp(normed_two, 1),
        swap_dp(normed_two, 2),
        normed_two,
        middle,
        own_att,
        gain_two,
    )

    far_two = swap_dp(own_two, 3)
    w_ffn = [ffn_local, ffn_near, ffn_far, ffn_last]
    w_ffn += [local_crossed, near_crossed, far_crossed, swap_core(ffn_last)]
    (near_hidden, near_back), (side_hidden, side_back) = gated(
        place, [near_two, side_two], [dy_near, dy_side], w_ffn, (low, low)
    )
    far_two, near_hidden, near_back, side_hidden, side_back = together(
        far_two, near_hidden, near_back, side_hidden, side_back
    )

    near_back, side_back = swap_dp(near_back, 1), swap_dp(side_back, 2)
    (own_hidden, kept), (far_hidden, far_back) = gated(
        place, [own_two, far_two], [own_dy, dy_far], w_ffn, (wide, low)
    )
    own_hidden, kept, far_hidden, far_back, near_back, side_back = together(
        own_hidden, kept, far_hidden, far_back, near_back, side_back
    )
    hidden = [own_hidden, near_hidden, side_hidden, far_hidden]
    ffn_part = ffn_grads(
        place,
        [own_two, near_two, side_two, far_two],
        [own_dy, dy_near, dy_side, dy_far],
        hidden,
    )
    ffn_part, kept, *moved = together(
        ffn_part, kept, near_back, side_back, swap_dp(far_back, 3)
    )
    ffn_shard = lax.psum_scatter(ffn_part, "seq", scatter_dimension=1, tiled=True)
    grad_middle, middle_low, gain_two_part, *blocks = middle_back(
        place, kept, moved, own_dy, middle, gain_two, w_out
    )

    arrived = [blocks[0]] + [swap_level(blocks[mask], mask) for mask in others]
    down_kept, *rest = down(place, hidden, w_ffn, own_att, middle_low)
    down_chunks, out_kept, out_sent = rest[:3], rest[3], rest[4]
    out_kept, out_sent, down_kept, *rest = together(
        out_kept, out_sent, down_kept, *down_chunks, *arrived
    )
    down_chunks, arrived = rest[:3], rest[3:]

    halves = [
        jnp.concatenate([member[:, :256] for member in arrived]),
        jnp.concatenate([member[:, 256:] for member in arrived]),
    ]

    def out_rows(to):
        rows = [
            lax.dynamic_slice_in_dim(member, to * 128, 128).astype(wide)
            for member in (out_kept, out_crossed)
        ]
        return (rows[0] + rows[1]).astype(low)

    kept, crossed, out_kept, out_crossed, *down_chunks = together(
        pick(halves, core),
        swap_core(pick(halves, 1 - core)),
        out_kept,
        swap_core(out_sent),
        *down_chunks,
    )
    out_parts = [out_rows(dp_at ^ mask) for mask in range(4)]
    grads = (kept, crossed)

    out_moved = [swap_dp(out_parts[mask], mask) for mask in others]
    dqkv, gain_sums, bias_sums = attend_back(
        qkv, saved, hot, grads, attended, cos_part, sin_part, q_gain, k_gain
    )
    dqkv, out_kept, last_chunk, *rest = together(
        dqkv,
        out_parts[0],
        down_chunks[2],
        swap_dp(down_chunks[0], 1),
        swap_dp(down_chunks[1], 2),
        *out_moved,
    )
    down_moved, out_moved = rest[:2], rest[2:]

    out_moved = [member.astype(wide) for member in out_moved]
    out_sum = (out_kept.astype(wide) + out_moved[0]) + (out_moved[1] + out_moved[2])
    back_kept, back_sent, kept, sent = tail(
        place, dqkv, w_qkv, unit, gain_sums, bias_sums, gain_two_part
    )
    back_kept, back_crossed, kept, crossed = together(
        back_kept, swap_core(back_sent), kept, swap_core(sent)
    )

    back = (back_kept + back_crossed.astype(wide)).reshape(4, piece, D)
    small_low = (kept[512:].astype(wide) + crossed[512:].astype(wide)).astype(low)

    def dp_message(to):
        return jnp.concatenate(
            [
                lax.dynamic_slice_in_dim(kept, to * 128, 128),
                lax.dynamic_slice_in_dim(crossed, to * 128, 128),
                small_low,
            ]
        )

    moved = [swap_dp(dp_message(dp_at ^ mask), mask) for mask in others]
    passed = back[2] + swap_level(back[3].astype(low), 1).astype(wide)
    passed = swap_level(passed.astype(low), 2)
    down_moved = [member.astype(wide) for member in down_moved]
    partial = (middle + down_kept) + (down_moved[0] + down_moved[1])
    qkv_kept, kept, passed, near, ffn_shard, last_chunk, partial, *moved = together(
        dp_message(dp_at), back[0], passed, back[1].astype(low), ffn_shard, last_chunk, partial, *moved
    )

    moved = [member.astype(wide) for member in moved]
    total = qkv_kept.astype(wide)
    total = ((total + moved[0]) + (moved[1] + moved[2])).astype(low)
    small_low = total[256:]

    out_sum = out_sum.reshape(4, 32, D)
    ffn_sums = ffn_shard.astype(wide)

    def level_message(to):
        out_block = at_index(out_sum, to).astype(low)
        qkv_block = jnp.concatenate(
            [
                lax.dynamic_slice_in_dim(total, to * 32, 32),
                lax.dynamic_slice_in_dim(total, 128 + to * 32, 32),
            ]
        )
        return jnp.concatenate(
            [qkv_block[:, at * 256 : (at + 1) * 256] for at in range(3)]
            + [out_block[:, at * 256 : (at + 1) * 256] for at in range(4)]
            + [small_low[:, :256]]
        )

    mine, kept, near, passed, ffn_sums, last_chunk, *moved = together(
        level_message(level),
        kept,
        swap_level(near, 1),
        passed,
        ffn_sums,
        swap_dp(last_chunk, 3),
        *[swap_level(level_message(level ^ mask), mask) for mask in others],
    )
    *sums, input_grad, result, gain_grad, q_grad, k_grad, bias_grad, gain_two_grad = finish(
        place,
        mine,
        moved,
        attn_gain[None, :],
        [query_weight, key_weight, value_weight],
        [kept, near, passed],
        own_x,
        grad_middle.reshape(2, piece, D),
        [partial, last_chunk],
    )

    shape = (2, 1, piece, D)
    return (
        result.reshape(shape),
        input_grad.reshape(shape),
        gain_grad.reshape(32),
        sums[0],
        sums[1],
        sums[2],
        sums[3],
        q_grad.reshape(HD),
        k_grad.reshape(HD),
        bias_grad,
        gain_two_grad.reshape(32),
        ffn_sums[0],
        ffn_sums[1],
        ffn_sums[2],
    )


def solution(mesh):
    placed = (
        P(None, "dp", "seq", None),
        P(None, "dp", "seq"),
        P(None, "dp", "seq"),
        P(("dp", "seq")),
        P(("dp", "seq"), None),
        P(("dp", "seq"), None),
        P(("dp", "seq"), None),
        P(("dp", "seq"), None),
        P(),
        P(),
        P(),
        P(("dp", "seq")),
        P(("dp", "seq"), None),
        P(("dp", "seq"), None),
        P(("dp", "seq"), None),
        P(None, "dp", "seq", None),
    )
    split = mesh.shape["dp"] == 4 and mesh.shape["seq"] == 8
    return jax.shard_map(
        local_split if split else local,
        mesh=mesh,
        in_specs=placed,
        out_specs=(
            P(None, "dp", "seq", None),
            P(None, "dp", "seq", None),
            P(("dp", "seq")),
            P(("dp", "seq"), None),
            P(("dp", "seq"), None),
            P(("dp", "seq"), None),
            P(("dp", "seq"), None),
            P(),
            P(),
            P(),
            P(("dp", "seq")),
            P(("dp", "seq"), None),
            P(("dp", "seq"), None),
            P(("dp", "seq"), None),
        ),
        check_vma=False,
    )
```
